32 devices in a mesh: dp: 2 (over y), fsdp: 16 (over z, x, core).
Axes of the slice: x: 2, y: 2, z: 4, core: 2. Of those that a mesh axis runs over, the one named last changes fastest.
Arguments:
- inputs: bfloat16 [2, 32, 256, 768], P(None, ('dp', 'fsdp')), may hold values from -6 to 6
- lengths: int32 [2, 32], P(None, ('dp', 'fsdp')), may hold values from 152 to 256, as said below
- cotangent: bfloat16 [2, 32, 256, 768], P(None, ('dp', 'fsdp')), may hold values from -6 to 6
- w_qkv: bfloat16 [2, 768, 2304], P(None, 'fsdp'), may hold values from -0.21875 to 0.21875
- q_bias: bfloat16 [2, 768], P(None, 'fsdp'), may hold values from -3 to 3
- v_bias: bfloat16 [2, 768], P(None, 'fsdp'), may hold values from -3 to 3
- w_out: bfloat16 [2, 768, 768], P(None, 'fsdp'), may hold values from -0.4375 to 0.4375
- b_out: bfloat16 [2, 768], P(None, 'fsdp'), may hold values from -2 to 2
- gain_one: bfloat16 [2, 768], P(None, 'fsdp'), may hold values from 0.25 to 1.75
- shift_one: bfloat16 [2, 768], P(None, 'fsdp'), may hold values from -2 to 2
- w_gated: bfloat16 [2, 768, 6144], P(None, 'fsdp'), may hold values from -0.21875 to 0.21875
- w_down: bfloat16 [2, 3072, 768], P(None, 'fsdp'), may hold values from -0.15625 to 0.15625
- b_down: bfloat16 [2, 768], P(None, 'fsdp'), may hold values from -2 to 2
- gain_two: bfloat16 [2, 768], P(None, 'fsdp'), may hold values from 0.25 to 1.75
- shift_two: bfloat16 [2, 768], P(None, 'fsdp'), may hold values from -2 to 2
Outputs:
- layer_out: bfloat16 [2, 32, 256, 768], P(None, ('dp', 'fsdp'))
- input_grad: bfloat16 [2, 32, 256, 768], P(None, ('dp', 'fsdp'))
- grad_w_qkv: float32 [2, 768, 2304], P(None, 'fsdp')
- grad_q_bias: float32 [2, 768], P(None, 'fsdp')
- grad_v_bias: float32 [2, 768], P(None, 'fsdp')
- grad_w_out: float32 [2, 768, 768], P(None, 'fsdp')
- grad_b_out: float32 [2, 768], P(None, 'fsdp')
- grad_gain_one: float32 [2, 768], P(None, 'fsdp')
- grad_shift_one: float32 [2, 768], P(None, 'fsdp')
- grad_w_gated: float32 [2, 768, 6144], P(None, 'fsdp')
- grad_w_down: float32 [2, 3072, 768], P(None, 'fsdp')
- grad_b_down: float32 [2, 768], P(None, 'fsdp')
- grad_gain_two: float32 [2, 768], P(None, 'fsdp')
- grad_shift_two: float32 [2, 768], P(None, 'fsdp')
The draws below stay inside these ranges and needn't reach their ends.
Inputs may be any that keep to these rules, and one draw needn't show every extreme that they name: Window s of micro-batch m holds lengths[m, s] real tokens at its start; the slots after them up to 256 are padding.
All inputs are finite; a program needn't handle non-finite values.
Results may differ from the reference program's by a relative error of at most 0.025.
Values may be sent and summed in bfloat16 or wider, within the bound.
A program may use at most 256 MiB of HBM per device.

```python
import math
import jax
import jax.numpy as jnp
from jax import lax

D = 768
HEADS = 12
HEAD_DIM = 64
FF = 3072
LAYERS = 2
MICRO = 2
PAD = 256
SEQS = 32


def draw_lengths(key, part):
    values = jax.random.randint(key, (MICRO, SEQS), PAD * 19 // 32, PAD + 1, dtype=jnp.int32)
    return values.at[0, 0].set(PAD)


def block_scale(key, extent, cuts, smallest, largest):
    def one(dim, shards_of):
        draws = jax.random.uniform(jax.random.fold_in(jax.random.fold_in(key, 6), dim), (shards_of,), jnp.float32, smallest / len(cuts), largest / len(cuts))
        return jnp.repeat(jnp.exp(draws), extent[dim] // shards_of).reshape((-1,) + (1,) * (len(extent) - dim - 1))

    level = one(*cuts[0])
    for cut in cuts[1:]:
        level = level * one(*cut)
    return level


def noise(own_key, dims, scale, bound, cuts=(), held_as=jnp.bfloat16):
    drawn = jax.random.normal(own_key, dims, jnp.float32) * scale
    if len(cuts) > 0:
        drawn = block_scale(own_key, dims, cuts, -0.22, 0.18) * drawn
    return jnp.clip(drawn, min=-bound, max=bound).astype(held_as)


def setup_inputs(seed: int = 0) -> dict:
    streams_of = jax.random.split(jax.random.key(seed), 16)
    inputs = noise(streams_of[0], (MICRO, SEQS, PAD, D), 1.0, 6.0, ((1, 32),))
    lengths = draw_lengths(jax.random.fold_in(streams_of[15], 71), 0)
    cotangent = noise(streams_of[2], (MICRO, SEQS, PAD, D), 1.0, 6.0, ((1, 32),))
    w_qkv = noise(streams_of[3], (LAYERS, D, 3 * D), D ** -0.5, 0.21875, ((1, 16),))
    q_bias = noise(streams_of[4], (LAYERS, D), 0.5, 3.0, ((1, 16),))
    v_bias = noise(streams_of[5], (LAYERS, D), 0.5, 3.0, ((1, 16),))
    w_out = noise(streams_of[6], (LAYERS, D, D), (D // 4) ** -0.5, 0.4375, ((1, 16),))
    b_out = noise(streams_of[7], (LAYERS, D), 0.3, 2.0, ((1, 16),))
    gain_one = jnp.clip(1.0 + 0.15 * jax.random.normal(streams_of[8], (LAYERS, D), jnp.float32), 0.25, 1.75).astype(jnp.bfloat16)
    shift_one = noise(streams_of[9], (LAYERS, D), 0.3, 2.0, ((1, 16),))
    w_gated = noise(streams_of[10], (LAYERS, D, 2 * FF), D ** -0.5, 0.21875, ((1, 16),))
    w_down = noise(streams_of[11], (LAYERS, FF, D), (FF // 2) ** -0.5, 0.15625, ((1, 16),))
    b_down = noise(streams_of[12], (LAYERS, D), 0.3, 2.0, ((1, 16),))
    gain_two = jnp.clip(1.0 + 0.15 * jax.random.normal(streams_of[13], (LAYERS, D), jnp.float32), 0.25, 1.75).astype(jnp.bfloat16)
    shift_two = noise(streams_of[14], (LAYERS, D), 0.3, 2.0, ((1, 16),))
    return dict(inputs=inputs, lengths=lengths, cotangent=cotangent, w_qkv=w_qkv, q_bias=q_bias, v_bias=v_bias, w_out=w_out, b_out=b_out, gain_one=gain_one, shift_one=shift_one, w_gated=w_gated, w_down=w_down, b_down=b_down, gain_two=gain_two, shift_two=shift_two)


EPS = 1e-12
NEG = -1e+30

@jax.custom_vjp
def low(v):
    return lax.optimization_barrier(v.astype(jnp.bfloat16)).astype(jnp.float32)

@jax.custom_vjp
def low_back(v):
    return v

def low_keep(v):
    return (low(v), None)

def low_pass(kept, grad):
    return (grad,)

def back_keep(v):
    return (v, None)

def back_low(kept, grad):
    return (low(grad),)
low.defvjp(low_keep, low_pass)
low_back.defvjp(back_keep, back_low)

def slopes_list(heads_count):
    nearest = 2 ** int(math.floor(math.log2(heads_count)))
    leading = [2.0 ** (-8.0 * (number + 1) / nearest) for number in range(nearest)]
    trailing = [2.0 ** (-8.0 * (number + 1) / (2 * nearest)) for number in range(2 * nearest)][0::2]
    return leading + trailing[:heads_count - nearest]

def alibi_bias(pad_len):
    places = jnp.arange(pad_len).astype(jnp.float32)
    spread = jnp.abs(places[:, None] - places[None, :])
    slopes = jnp.array(slopes_list(HEADS), jnp.float32)
    return -slopes[:, None, None] * spread[None]

def normalize(resid, gain, shift):
    average = lax.optimization_barrier(jnp.mean(resid, axis=-1, keepdims=True))
    centered = resid - average
    variance = lax.optimization_barrier(jnp.mean(centered * centered, axis=-1, keepdims=True))
    return centered * lax.rsqrt(variance + EPS) * gain + shift

def geglu(packed):
    half = packed.shape[-1] // 2
    return jax.nn.gelu(packed[:, :half], approximate=False) * packed[:, half:]

def attend_one(query, keys, values, length):
    scale = HEAD_DIM ** (-0.5)
    scores = jnp.einsum('qhd,khd->hqk', query, keys, precision=lax.Precision.HIGHEST) * scale
    scores = low_back(scores + alibi_bias(query.shape[0]))
    visible = jnp.arange(query.shape[0]).astype(jnp.int32) < length
    scores = jnp.where(visible[None, None, :], scores, NEG)
    attention = low(jax.nn.softmax(scores, axis=-1))
    return jnp.einsum('hqk,khd->qhd', attention, values, precision=lax.Precision.HIGHEST)

def layer_forward(block_in, weights, seq_lengths):
    w_qkv, q_bias, v_bias, w_out, b_out, gain_one, shift_one, w_gated, w_down, b_down, gain_two, shift_two = weights
    seq_count = block_in.shape[0]
    flat_rows = block_in.reshape(-1, D)
    bias_full = jnp.concatenate([q_bias, jnp.zeros_like(q_bias), v_bias])
    qkv = jnp.dot(low(flat_rows), w_qkv, precision=lax.Precision.HIGHEST, preferred_element_type=jnp.float32) + bias_full
    qkv = low_back(low(qkv))
    qkv_split = qkv.reshape(seq_count, -1, 3, HEADS, HEAD_DIM)
    checked = jax.checkpoint(attend_one)
    attended = lax.map(lambda item: checked(item[0], item[1], item[2], item[3]), (qkv_split[:, :, 0], qkv_split[:, :, 1], qkv_split[:, :, 2], seq_lengths))
    attended = low_back(low(attended.reshape(-1, D)))
    branch = low_back(jnp.dot(attended, w_out, precision=lax.Precision.HIGHEST, preferred_element_type=jnp.float32) + b_out)
    hidden = normalize(flat_rows + branch, gain_one, shift_one)
    packed = low_back(jnp.dot(low(hidden), w_gated, precision=lax.Precision.HIGHEST, preferred_element_type=jnp.float32))
    mixed = low(geglu(packed))
    branch_two = low_back(jnp.dot(mixed, w_down, precision=lax.Precision.HIGHEST, preferred_element_type=jnp.float32) + b_down)
    result = normalize(hidden + branch_two, gain_two, shift_two)
    return result.reshape(block_in.shape)

def reference(inputs, lengths, cotangent, w_qkv, q_bias, v_bias, w_out, b_out, gain_one, shift_one, w_gated, w_down, b_down, gain_two, shift_two):
    params = tuple((piece.astype(jnp.float32) for piece in (w_qkv, q_bias, v_bias, w_out, b_out, gain_one, shift_one, w_gated, w_down, b_down, gain_two, shift_two)))

    def micro_step(totals, item):
        block_in, seq_lengths, cot_in = item

        def whole(start_rows, weights):
            current = start_rows
            for layer_at in range(LAYERS):
                current = layer_forward(current, tuple((piece[layer_at] for piece in weights)), seq_lengths)
            return current
        result, back = jax.vjp(whole, block_in.astype(jnp.float32), params)
        grad_in, grad_params = back(cot_in.astype(jnp.float32))
        totals = tuple((total + grad for total, grad in zip(totals, grad_params)))
        return (totals, (result.astype(jnp.bfloat16), grad_in.astype(jnp.bfloat16)))
    start_totals = tuple((jnp.zeros_like(piece) for piece in params))
    totals, (layer_out, input_grad) = lax.scan(micro_step, start_totals, (inputs, lengths, cotangent))
    return (layer_out, input_grad, totals[0], totals[1], totals[2], totals[3], totals[4], totals[5], totals[6], totals[7], totals[8], totals[9], totals[10], totals[11])
```

```python
import functools
import math

import jax
import jax.numpy as jnp
from jax import lax
from jax.experimental import pallas as pl
from jax.experimental.pallas import tpu as pltpu
from jax.sharding import PartitionSpec as P

D = 768
HEADS = 12
HEAD_DIM = 64
FF = 3072
LAYERS = 2


EPS = 1e-12
NEG = -1e30


def slopes_list(heads_count):
    nearest = 2 ** int(math.floor(math.log2(heads_count)))
    leading = [2.0 ** (-8.0 * (number + 1) / nearest) for number in range(nearest)]
    trailing = [2.0 ** (-8.0 * (number + 1) / (2 * nearest)) for number in range(2 * nearest)][0::2]
    return leading + trailing[: heads_count - nearest]


def alibi_bias(pad_len):
    places = jnp.arange(pad_len).astype(jnp.float32)
    spread = jnp.abs(places[:, None] - places[None, :])
    slopes = jnp.array(slopes_list(HEADS), jnp.float32)
    return -slopes[:, None, None] * spread[None]


def normalize(resid, gain, shift):
    average = jnp.mean(resid, axis=-1, keepdims=True)
    centered = resid - average
    variance = jnp.mean(centered * centered, axis=-1, keepdims=True)
    return centered * lax.rsqrt(variance + EPS) * gain + shift


def geglu(packed):
    return jax.nn.gelu(packed[:, :FF], approximate=False) * packed[:, FF:]


def masked_scores(query, keys, length, alibi):
    scale = HEAD_DIM ** (-0.5)
    scores = (
        jnp.einsum("qhd,khd->hqk", query, keys, preferred_element_type=jnp.float32) * scale + alibi
    )
    visible = jnp.arange(query.shape[0]) < length
    return jnp.where(visible[None, None, :], scores, NEG)


def attend_forward(query, keys, values, length, alibi):
    scores = masked_scores(query, keys, length, alibi)
    highest = jnp.max(scores, axis=-1, keepdims=True)
    shifted = jnp.exp(scores - highest)
    row_total = jnp.sum(shifted, axis=-1, keepdims=True)
    attention = (shifted / row_total).astype(jnp.bfloat16)
    log_total = highest + jnp.log(row_total)
    attended = jnp.einsum("hqk,khd->qhd", attention, values, preferred_element_type=jnp.float32)
    return (attended, log_total)


def attend_backward(query, keys, values, grad_att, log_total, length, alibi):
    scale = HEAD_DIM ** (-0.5)
    scores = masked_scores(query, keys, length, alibi)
    attention = jnp.exp(scores - log_total)
    attention_low = attention.astype(jnp.bfloat16)
    d_value = jnp.einsum(
        "hqk,qhd->khd", attention_low, grad_att, preferred_element_type=jnp.float32
    )
    d_attention = jnp.einsum("qhd,khd->hqk", grad_att, values, preferred_element_type=jnp.float32)
    inner = jnp.sum(d_attention * attention, axis=-1, keepdims=True)
    d_scores = (attention * (d_attention - inner)).astype(jnp.bfloat16)
    d_query = jnp.einsum("hqk,khd->qhd", d_scores, keys, preferred_element_type=jnp.float32) * scale
    d_key = jnp.einsum("hqk,qhd->khd", d_scores, query, preferred_element_type=jnp.float32) * scale
    return (d_query, d_key, d_value)


def forward_layer(x_rows, weights, seq_lengths, alibi):
    (
        w_qkv,
        q_bias,
        v_bias,
        w_out,
        b_out,
        gain_one,
        shift_one,
        w_gated,
        w_down,
        b_down,
        gain_two,
        shift_two,
    ) = weights
    seq_count = seq_lengths.shape[0]
    x_low = x_rows.astype(jnp.bfloat16)
    bias_full = jnp.concatenate([q_bias, jnp.zeros_like(q_bias), v_bias]).astype(jnp.float32)
    qkv_low = (jnp.dot(x_low, w_qkv, preferred_element_type=jnp.float32) + bias_full).astype(
        jnp.bfloat16
    )
    qkv_split = qkv_low.reshape(seq_count, -1, 3, HEADS, HEAD_DIM)
    attended, log_total = jax.vmap(attend_forward, in_axes=(0, 0, 0, 0, None))(
        qkv_split[:, :, 0], qkv_split[:, :, 1], qkv_split[:, :, 2], seq_lengths, alibi
    )
    attended_low = attended.reshape(-1, D).astype(jnp.bfloat16)
    resid_one = x_rows + (
        jnp.dot(attended_low, w_out, preferred_element_type=jnp.float32) + b_out.astype(jnp.float32)
    )
    hidden = normalize(resid_one, gain_one.astype(jnp.float32), shift_one.astype(jnp.float32))
    hidden_low = hidden.astype(jnp.bfloat16)
    packed = jnp.dot(hidden_low, w_gated, preferred_element_type=jnp.float32)
    mixed_low = geglu(packed).astype(jnp.bfloat16)
    resid_two = hidden + (
        jnp.dot(mixed_low, w_down, preferred_element_type=jnp.float32) + b_down.astype(jnp.float32)
    )
    result = normalize(resid_two, gain_two.astype(jnp.float32), shift_two.astype(jnp.float32))
    saved = (
        x_low,
        qkv_low,
        log_total,
        attended_low,
        resid_one,
        hidden_low,
        packed,
        mixed_low,
        resid_two,
    )
    return (result, saved)


def backward_layer(grad_out, weights, saved, seq_lengths, alibi):
    (
        w_qkv,
        q_bias,
        v_bias,
        w_out,
        b_out,
        gain_one,
        shift_one,
        w_gated,
        w_down,
        b_down,
        gain_two,
        shift_two,
    ) = weights
    x_low, qkv_low, log_total, attended_low, resid_one, hidden_low, packed, mixed_low, resid_two = (
        saved
    )
    seq_count = seq_lengths.shape[0]
    _, norm_back_two = jax.vjp(
        normalize, resid_two, gain_two.astype(jnp.float32), shift_two.astype(jnp.float32)
    )
    grad_two, d_gain_two, d_shift_two = norm_back_two(grad_out)
    grad_two_low = grad_two.astype(jnp.bfloat16)
    d_w_down = jnp.dot(mixed_low.T, grad_two_low, preferred_element_type=jnp.float32)
    d_b_down = jnp.sum(grad_two_low.astype(jnp.float32), axis=0)
    grad_mixed = jnp.dot(grad_two_low, w_down.T, preferred_element_type=jnp.float32)
    _, geglu_back = jax.vjp(geglu, packed)
    (grad_packed,) = geglu_back(grad_mixed)
    grad_packed_low = grad_packed.astype(jnp.bfloat16)
    d_w_gated = jnp.dot(hidden_low.T, grad_packed_low, preferred_element_type=jnp.float32)
    grad_hidden = grad_two + jnp.dot(grad_packed_low, w_gated.T, preferred_element_type=jnp.float32)
    _, norm_back_one = jax.vjp(
        normalize, resid_one, gain_one.astype(jnp.float32), shift_one.astype(jnp.float32)
    )
    grad_one, d_gain_one, d_shift_one = norm_back_one(grad_hidden)
    grad_one_low = grad_one.astype(jnp.bfloat16)
    d_w_out = jnp.dot(attended_low.T, grad_one_low, preferred_element_type=jnp.float32)
    d_b_out = jnp.sum(grad_one_low.astype(jnp.float32), axis=0)
    grad_att_low = jnp.dot(grad_one_low, w_out.T, preferred_element_type=jnp.float32).astype(
        jnp.bfloat16
    )
    qkv_split = qkv_low.reshape(seq_count, -1, 3, HEADS, HEAD_DIM)
    grad_heads = grad_att_low.reshape(seq_count, -1, HEADS, HEAD_DIM)
    d_query, d_key, d_value = jax.vmap(attend_backward, in_axes=(0, 0, 0, 0, 0, 0, None))(
        qkv_split[:, :, 0],
        qkv_split[:, :, 1],
        qkv_split[:, :, 2],
        grad_heads,
        log_total,
        seq_lengths,
        alibi,
    )
    grad_qkv_low = (
        jnp.stack([d_query, d_key, d_value], axis=2).reshape(-1, 3 * D).astype(jnp.bfloat16)
    )
    d_w_qkv = jnp.dot(x_low.T, grad_qkv_low, preferred_element_type=jnp.float32)
    d_q_bias = jnp.sum(grad_qkv_low[:, :D].astype(jnp.float32), axis=0)
    d_v_bias = jnp.sum(grad_qkv_low[:, 2 * D :].astype(jnp.float32), axis=0)
    grad_in = grad_one + jnp.dot(grad_qkv_low, w_qkv.T, preferred_element_type=jnp.float32)
    grads = (
        d_w_qkv,
        d_q_bias,
        d_v_bias,
        d_w_out,
        d_b_out,
        d_gain_one,
        d_shift_one,
        d_w_gated,
        d_w_down,
        d_b_down,
        d_gain_two,
        d_shift_two,
    )
    return (grad_in, grads)


MESH = pl.DeviceIdType.MESH

def place():
    y = lax.axis_index("dp"); f = lax.axis_index("fsdp")
    z = f // 4; x = lax.rem(f // 2, 2); c = lax.rem(f, 2)
    return z, x, y, c

def dev(z, x, y, c):
    return (y, (z * 2 + x) * 2 + c)

def blk(z, x, c, h):
    return ((z * 2 + x) * 2 + c) * 2 + h

PIECES = [(4, 0), (0, 0), (1, 0), (2, 0), (3, 0), (0, 1), (1, 1), (2, 1), (3, 1)]
XFIRST = [True, False, False, True, False, False, False, True, False]
EVENTS = 25

def gather_kernel(*refs):
    ins, outs = refs[:5], refs[5:10]
    send_sem, recv_sem, local_sem = refs[10:]
    z, x, y, c = place()
    zp = z + 1 - 2 * lax.rem(z, 2)
    zm = 3 - z
    zf = lax.rem(z + 2, 4)
    mid = jnp.logical_and(z >= 1, z <= 2)
    end = jnp.logical_not(mid)
    d_zp, d_zm = dev(zp, x, y, c), dev(zm, x, y, c)
    d_x, d_y, d_c = dev(z, 1 - x, y, c), dev(z, x, 1 - y, c), dev(z, x, y, 1 - c)
    bar = pltpu.get_barrier_semaphore()
    for d in (d_zp, d_zm, d_x, d_y, d_c):
        pl.semaphore_signal(bar, 1, device_id=d, device_id_type=MESH)
    pl.semaphore_wait(bar, 5)

    def at(p, b, n=None):
        t, l = PIECES[p]
        ref = outs[t].at[l]
        return ref.at[b] if n is None else ref.at[pl.ds(b, n)]

    def own(p, h, n=None):
        t, l = PIECES[p]
        ref = ins[t].at[l]
        return ref.at[h] if n is None else ref
    pending = []

    def copy(p, e, src, dst, b, d):
        return pltpu.make_async_remote_copy(src_ref=src, dst_ref=dst, send_sem=send_sem.at[p, e], recv_sem=recv_sem.at[p, b], device_id=d, device_id_type=MESH)

    def send(p, e, b, d, when=None, n=None, mine=False):
        src = at(p, b, n)
        if mine:
            src = own(p, y, n)
        cp = copy(p, e, src, at(p, b, n), b, d)
        if when is None:
            cp.start()
        else:
            pl.when(when)(cp.start)
        pending.append((cp, when))

    def got(p, b, d, when=None, n=None):
        cp = copy(p, 0, at(p, b, n), at(p, b, n), b, d)
        if when is None:
            cp.wait_recv()
        else:
            pl.when(when)(cp.wait_recv)

    def local(p):
        return pltpu.make_async_copy(own(p, 0, 2), at(p, blk(z, x, c, 0), 2), local_sem.at[p])

    def st0(p):
        b = blk(z, x, c, y)
        send(p, 1, b, d_zp, mine=True)
        send(p, 2, b, d_zm, when=mid, mine=True)
        send(p, 3, b, d_x, mine=True)
        send(p, 4, blk(z, x, c, 0), d_c, n=2, mine=True)
        local(p).start()

    def spread(p, k, zz):
        b = blk(zz, x, c, y)
        send(p, 8 + k, b, d_x)
        send(p, 11 + k, b, d_y)

    def relay(p, k, zz):
        bx = blk(zz, 1 - x, c, y)
        by = blk(zz, x, c, 1 - y)
        got(p, bx, d_x)
        if XFIRST[p]:
            send(p, 15 + k, bx, d_y)
        got(p, by, d_y)
        if not XFIRST[p]:
            send(p, 15 + k, by, d_x)
        send(p, 18 + k, blk(zz, x, c, 0), d_c, n=2)

    def diag(p, k, zz):
        b = blk(zz, 1 - x, c, 1 - y)
        got(p, b, d_y if XFIRST[p] else d_x)
        send(p, 22 + k, blk(zz, 1 - x, c, 0), d_c, n=2)

    def st1(p):
        got(p, blk(zp, x, c, y), d_zp)
        send(p, 5, blk(zp, x, c, y), d_zm, when=mid)
        got(p, blk(zm, x, c, y), d_zm, when=mid)
        send(p, 6, blk(zm, x, c, y), d_zp, when=mid)
        spread(p, 0, zp)
        b = blk(z, 1 - x, c, y)
        got(p, b, d_x)
        send(p, 14, b, d_y)

    def st2(p):
        got(p, blk(zf, x, c, y), d_zm, when=mid)
        got(p, blk(zf, x, c, y), d_zp, when=end)
        send(p, 7, blk(zf, x, c, y), d_zp, when=mid)
        spread(p, 1, zf)
        relay(p, 0, zp)
        got(p, blk(z, 1 - x, c, 1 - y), d_y)
        send(p, 21, blk(z, 1 - x, c, 0), d_c, n=2)

    def st3(p):
        got(p, blk(zm, x, c, y), d_zp, when=end)
        spread(p, 2, zm)
        relay(p, 1, zf)
        diag(p, 0, zp)

    def st4(p):
        relay(p, 2, zm)
        diag(p, 1, zf)

    def st5(p):
        diag(p, 2, zm)

    def st6(p):
        local(p).wait()
        for zz in (z, zp, zf, zm):
            for xx in (x, 1 - x):
                got(p, blk(zz, xx, 1 - c, 0), d_c, n=2)

    stages = (st0, st1, st2, st3, st4, st5, st6)
    n = len(PIECES)
    for r in range(n + 6):
        for s in (0, 6, 5, 4, 3, 2, 1):
            p = r - s
            if 0 <= p < n:
                stages[s](p)
    for cp, when in pending:
        if when is None:
            cp.wait_send()
        else:
            pl.when(when)(cp.wait_send)

def gather_all(shards, vec):
    ins = []
    for w in shards:
        l, r, cc = w.shape
        ins.append(w.reshape(l, 2, r // 2, cc))
    ins.append(vec[None])
    outs = [jax.ShapeDtypeStruct((v.shape[0], 32) + v.shape[2:], v.dtype) for v in ins]
    n = len(PIECES)
    hbm = pl.BlockSpec(memory_space=pltpu.HBM)
    res = pl.pallas_call(gather_kernel, out_shape=outs, in_specs=[hbm] * 5, out_specs=[hbm] * 5,
        scratch_shapes=[pltpu.SemaphoreType.DMA((n, EVENTS)), pltpu.SemaphoreType.DMA((n, 32)), pltpu.SemaphoreType.DMA((n,))],
        compiler_params=pltpu.CompilerParams(collective_id=0, has_side_effects=True), name="gather_weights")(*ins)
    full = [o.reshape(o.shape[0], -1, o.shape[-1]) for o in res[:4]]
    return full, res[4][0]

def fetch_all(shards, vectors, fast):
    if fast:
        vec = jnp.stack(vectors, axis=1)
        width = vec.shape[-1]
        vec = jnp.pad(vec, ((0, 0), (0, 0), (0, 128 - width)))
        full, packed = gather_all(shards, vec)
        packed = packed.reshape(-1, LAYERS, 8, 128)[..., :width]
        return full, packed.transpose(1, 2, 0, 3).reshape(LAYERS, 8, -1)
    full = [lax.all_gather(w, "fsdp", axis=1, tiled=True) for w in shards]
    vec = lax.all_gather(jnp.stack(vectors, axis=1), "fsdp", axis=2, tiled=True)
    return full, vec


def reduce_all(grads):
    outs = []
    for g in grads:
        part = lax.psum_scatter(g.astype(jnp.bfloat16), "fsdp", scatter_dimension=0, tiled=True)
        outs.append(lax.psum(part, "dp").astype(jnp.float32))
    return outs


def per_device(fast, inputs, lengths, cotangent, w_qkv, q_bias, v_bias, w_out, b_out, gain_one, shift_one, w_gated, w_down, b_down, gain_two, shift_two):
    micro_count, seq_local, pad_len, _ = inputs.shape
    alibi = alibi_bias(pad_len)
    full, vec = fetch_all(
        (w_qkv, w_out, w_gated, w_down),
        (q_bias, v_bias, b_out, gain_one, shift_one, b_down, gain_two, shift_two),
        fast,
    )
    seq_lengths = lengths.reshape(-1)
    x_rows = inputs.reshape(-1, D).astype(jnp.float32)
    saved_all = []
    weights_all = []
    for l in range(LAYERS):
        v = vec[l]
        weights = (full[0][l], v[0], v[1], full[1][l], v[2], v[3], v[4], full[2][l], full[3][l], v[5], v[6], v[7])
        x_rows, saved = forward_layer(x_rows, weights, seq_lengths, alibi)
        saved_all.append(saved)
        weights_all.append(weights)
    layer_out = x_rows.astype(jnp.bfloat16).reshape(inputs.shape)
    grad_rows = cotangent.reshape(-1, D).astype(jnp.float32)
    mats = [None] * LAYERS
    vecs = [None] * LAYERS
    for l in reversed(range(LAYERS)):
        grad_rows, g = backward_layer(grad_rows, weights_all[l], saved_all[l], seq_lengths, alibi)
        mats[l] = (g[0], g[3], g[7], g[8])
        vecs[l] = jnp.stack([g[1], g[2], g[4], g[5], g[6], g[9], g[10], g[11]], axis=1)
    input_grad = grad_rows.astype(jnp.bfloat16).reshape(inputs.shape)
    flat = []
    for l in range(LAYERS):
        flat += reduce_all(mats[l])
    flat += reduce_all([jnp.concatenate(vecs, axis=1)])
    vs = flat[-1].T.reshape(LAYERS, 8, -1)
    m = [jnp.stack([flat[i], flat[4 + i]]) for i in range(4)]
    return (
        layer_out, input_grad, m[0], vs[:, 0], vs[:, 1], m[1], vs[:, 2], vs[:, 3], vs[:, 4], m[2], m[3], vs[:, 5], vs[:, 6], vs[:, 7],
    )


def solution(mesh):
    placed = (
        P(None, ("dp", "fsdp"), None, None),
        P(None, ("dp", "fsdp")),
        P(None, ("dp", "fsdp"), None, None),
        P(None, "fsdp", None),
        P(None, "fsdp"),
        P(None, "fsdp"),
        P(None, "fsdp", None),
        P(None, "fsdp"),
        P(None, "fsdp"),
        P(None, "fsdp"),
        P(None, "fsdp", None),
        P(None, "fsdp", None),
        P(None, "fsdp"),
        P(None, "fsdp"),
        P(None, "fsdp"),
    )
    return jax.shard_map(
        functools.partial(per_device, dict(mesh.shape) == {"dp": 2, "fsdp": 16}),
        mesh=mesh,
        in_specs=placed,
        out_specs=(
            P(None, ("dp", "fsdp"), None, None),
            P(None, ("dp", "fsdp"), None, None),
            P(None, "fsdp", None),
            P(None, "fsdp"),
            P(None, "fsdp"),
            P(None, "fsdp", None),
            P(None, "fsdp"),
            P(None, "fsdp"),
            P(None, "fsdp"),
            P(None, "fsdp", None),
            P(None, "fsdp", None),
            P(None, "fsdp"),
            P(None, "fsdp"),
            P(None, "fsdp"),
        ),
        check_vma=False,
    )
```

```python
import functools
import math

import jax
import jax.numpy as jnp
from jax import lax
from jax.experimental import pallas as pl
from jax.experimental.pallas import tpu as pltpu
from jax.sharding import PartitionSpec as P

MESH = pl.DeviceIdType.MESH

BF = jnp.bfloat16
F32 = jnp.float32
D, HEADS, HEAD_DIM, FF, LAYERS = 768, 12, 64, 3072, 2
EPS = 1e-12
NEG = -1e30
NT = (((1,), (1,)), ((), ()))


def slopes_list(heads_count):
    nearest = 2 ** int(math.floor(math.log2(heads_count)))
    leading = [2.0 ** (-8.0 * (number + 1) / nearest) for number in range(nearest)]
    trailing = [2.0 ** (-8.0 * (number + 1) / (2 * nearest)) for number in range(2 * nearest)][0::2]
    return leading + trailing[: heads_count - nearest]


def mm(a, b):
    return jnp.dot(a, b, preferred_element_type=F32)


def mm_nt(a, b):
    return lax.dot_general(a, b, NT, preferred_element_type=F32)


def erf(x):
    return lax.erf(x)


def norm_parts(r):
    cent = r - jnp.mean(r, axis=-1, keepdims=True)
    rstd = lax.rsqrt(jnp.mean(cent * cent, axis=-1, keepdims=True) + EPS)
    return cent * rstd, rstd


def norm_back(dy, gain, n, rstd):
    dn = dy * gain
    return rstd * (dn - jnp.mean(dn, axis=-1, keepdims=True) - n * jnp.mean(dn * n, axis=-1, keepdims=True))


def halves(v, axis):
    first = lax.broadcasted_iota(jnp.int32, v.shape, axis) < HEAD_DIM
    zero = jnp.zeros_like(v)
    return jnp.where(first, v, zero), jnp.where(first, zero, v)


def attention_kernel(len_ref, slope_ref, x_ref, wq_ref, wk_ref, wv_ref, vec_ref, q_ref, k_ref, v_ref, att_ref, pt_ref, xt_ref, at_ref, xb_ref, dist_ref):
    i = pl.program_id(0)
    seqs, pad = pt_ref.shape[0], pt_ref.shape[-1]

    @pl.when(i == 0)
    def _():
        xb = x_ref[...].astype(BF)
        xb_ref[...] = xb
        xt_ref[...] = xb.T
        keys = lax.broadcasted_iota(jnp.int32, (pad, pad), 0)
        rows = lax.broadcasted_iota(jnp.int32, (pad, pad), 1)
        dist_ref[...] = jnp.abs(keys - rows).astype(F32)
    xb = xb_ref[...]
    q_ref[...] = (mm(xb, wq_ref[...]) + vec_ref[0:1, :]).astype(BF)
    k_ref[...] = mm(xb, wk_ref[...]).astype(BF)
    v_ref[...] = (mm(xb, wv_ref[...]) + vec_ref[1:2, :]).astype(BF)
    for s in range(seqs):
        rows = slice(s * pad, (s + 1) * pad)
        hidden = jnp.where(lax.broadcasted_iota(jnp.int32, (pad, 1), 0) < len_ref[s], 0.0, NEG)
        for pair in range(2):
            lanes = slice(128 * pair, 128 * pair + 128)
            q2 = q_ref[rows, lanes] * BF(HEAD_DIM ** -0.5)
            k0, k1 = halves(k_ref[rows, lanes], 1)
            v0, v1 = halves(v_ref[rows, lanes].T, 0)
            total = None
            for h, (kh, vh) in enumerate(((k0, v0), (k1, v1))):
                slope = slope_ref[4 * i + 2 * pair + h]
                sc = mm_nt(kh, q2) - slope * dist_ref[...] + hidden
                e = jnp.exp(sc - jnp.max(sc, axis=0, keepdims=True))
                p = (e * (1.0 / jnp.sum(e, axis=0, keepdims=True))).astype(BF)
                pt_ref[s, 2 * pair + h] = p
                part = mm(vh, p)
                total = part if total is None else total + part
            total = total.astype(BF)
            at_ref[lanes, rows] = total
            att_ref[rows, lanes] = total.T


def attention_forward(l, lengths, slopes, x, w_qkv, vec):
    rows = x.shape[0]
    seqs = lengths.shape[0]
    pad = rows // seqs
    col = lambda off: pl.BlockSpec((None, D, 256), lambda i: (l, 0, off + i))
    blk = pl.BlockSpec((rows, 256), lambda i: (0, i))
    smem = pl.BlockSpec(memory_space=pltpu.SMEM)
    act = jax.ShapeDtypeStruct((rows, D), BF)
    return pl.pallas_call(
        attention_kernel,
        grid=(3,),
        in_specs=[smem, smem, pl.BlockSpec((rows, D), lambda i: (0, 0)), col(0), col(3), col(6), pl.BlockSpec((None, 8, 256), lambda i: (l, 0, i))],
        out_specs=[blk, blk, blk, blk, pl.BlockSpec((seqs, 4, pad, pad), lambda i: (0, i, 0, 0)), pl.BlockSpec((D, rows), lambda i: (0, 0)), pl.BlockSpec((256, rows), lambda i: (i, 0))],
        out_shape=[act, act, act, act, jax.ShapeDtypeStruct((seqs, HEADS, pad, pad), BF), jax.ShapeDtypeStruct((D, rows), BF), jax.ShapeDtypeStruct((D, rows), BF)],
        scratch_shapes=[pltpu.VMEM((rows, D), BF), pltpu.VMEM((pad, pad), F32)],
        compiler_params=pltpu.CompilerParams(vmem_limit_bytes=56 * 2**20),
        name="attention_forward",
    )(lengths, slopes, x, w_qkv, w_qkv, w_qkv, vec)


def ff_kernel(att_ref, x_ref, wo_ref, wg_ref, wu_ref, wd_ref, vec_ref, r1_ref, r2_ref, ga_ref, gb_ref, ft_ref, ht_ref, out_ref, h_ref, hb_ref, acc_ref):
    j = pl.program_id(0)

    @pl.when(j == 0)
    def _():
        r1 = x_ref[...].astype(F32) + (mm(att_ref[...], wo_ref[...]) + vec_ref[2:3, :])
        r1_ref[...] = r1
        h = norm_parts(r1)[0] * vec_ref[3:4, :] + vec_ref[4:5, :]
        h_ref[...] = h
        hb = h.astype(BF)
        hb_ref[...] = hb
        ht_ref[...] = hb.T
        acc_ref[...] = jnp.zeros_like(acc_ref)
    hb = hb_ref[...]
    g = mm(hb, wg_ref[...])
    u = mm(hb, wu_ref[...])
    cdf = 0.5 + 0.5 * erf(g * math.sqrt(0.5))
    gelu = g * cdf
    slope = cdf + g * (jnp.exp(-0.5 * (g * g)) * (1.0 / math.sqrt(2.0 * math.pi)))
    ga_ref[...] = gelu.astype(BF)
    gb_ref[...] = (slope * u).astype(BF)
    f = (gelu * u).astype(BF)
    ft_ref[...] = f.T
    acc_ref[...] += mm(f, wd_ref[...])

    @pl.when(j == pl.num_programs(0) - 1)
    def _():
        r2 = h_ref[...] + (acc_ref[...] + vec_ref[5:6, :])
        r2_ref[...] = r2
        out_ref[...] = (norm_parts(r2)[0] * vec_ref[6:7, :] + vec_ref[7:8, :]).astype(out_ref.dtype)


def ff_forward(l, att, x, w_out, w_gated, w_down, vec, out_dtype):
    rows = x.shape[0]
    n = FF // 768
    whole = pl.BlockSpec((rows, D), lambda j: (0, 0))
    blk = pl.BlockSpec((rows, 768), lambda j: (0, j))
    return pl.pallas_call(
        ff_kernel,
        grid=(n,),
        in_specs=[whole, whole, pl.BlockSpec((None, D, D), lambda j: (l, 0, 0)),
                  pl.BlockSpec((None, D, 768), lambda j: (l, 0, j)), pl.BlockSpec((None, D, 768), lambda j: (l, 0, n + j)),
                  pl.BlockSpec((None, 768, D), lambda j: (l, j, 0)), pl.BlockSpec((None, 8, D), lambda j: (l, 0, 0))],
        out_specs=[whole, whole, blk, blk, pl.BlockSpec((768, rows), lambda j: (j, 0)), pl.BlockSpec((D, rows), lambda j: (0, 0)), whole],
        out_shape=[jax.ShapeDtypeStruct((rows, D), F32), jax.ShapeDtypeStruct((rows, D), F32),
                   jax.ShapeDtypeStruct((rows, FF), BF), jax.ShapeDtypeStruct((rows, FF), BF),
                   jax.ShapeDtypeStruct((FF, rows), BF), jax.ShapeDtypeStruct((D, rows), BF), jax.ShapeDtypeStruct((rows, D), out_dtype)],
        scratch_shapes=[pltpu.VMEM((rows, D), F32), pltpu.VMEM((rows, D), BF), pltpu.VMEM((rows, D), F32)],
        compiler_params=pltpu.CompilerParams(vmem_limit_bytes=56 * 2**20),
        name="ff_forward",
    )(att, x, w_out, w_gated, w_gated, w_down, vec)


def colsum(v):
    return jnp.sum(v, axis=0, keepdims=True)


def ff_back_kernel(dy_ref, r1_ref, r2_ref, ga_ref, gb_ref, wo_ref, wg_ref, wu_ref, wd_ref, vec_ref, dm_ref, dg_ref, du_ref, dr1_ref, da_ref, datt_ref, gv_ref, acc_ref):
    j = pl.program_id(0)

    @pl.when(j == 0)
    def _():
        dy = dy_ref[...].astype(F32)
        n, rstd = norm_parts(r2_ref[...])
        dr2 = norm_back(dy, vec_ref[6:7, :], n, rstd)
        acc_ref[...] = dr2
        dm = dr2.astype(BF)
        dm_ref[...] = dm
        gv_ref[5:6, :] = colsum(dm.astype(F32))
        gv_ref[6:7, :] = colsum(dy * n)
        gv_ref[7:8, :] = colsum(dy)
        gv_ref[0:2, :] = jnp.zeros((2, D), F32)
    df = mm_nt(dm_ref[...], wd_ref[...])
    dg = (df * gb_ref[...].astype(F32)).astype(BF)
    du = (df * ga_ref[...].astype(F32)).astype(BF)
    dg_ref[...] = dg
    du_ref[...] = du
    acc_ref[...] += mm_nt(dg, wg_ref[...]) + mm_nt(du, wu_ref[...])

    @pl.when(j == pl.num_programs(0) - 1)
    def _():
        dh = acc_ref[...]
        n, rstd = norm_parts(r1_ref[...])
        dr1 = norm_back(dh, vec_ref[3:4, :], n, rstd)
        dr1_ref[...] = dr1
        da = dr1.astype(BF)
        da_ref[...] = da
        gv_ref[2:3, :] = colsum(da.astype(F32))
        gv_ref[3:4, :] = colsum(dh * n)
        gv_ref[4:5, :] = colsum(dh)
        datt_ref[...] = mm_nt(da, wo_ref[...]).astype(BF)


def ff_backward(l, dy, r1, r2, ga, gb, w_out, w_gated, w_down, vec):
    rows = dy.shape[0]
    n = FF // 768
    whole = pl.BlockSpec((rows, D), lambda j: (0, 0))
    blk = pl.BlockSpec((rows, 768), lambda j: (0, j))
    act = lambda c, t: jax.ShapeDtypeStruct((rows, c), t)
    return pl.pallas_call(
        ff_back_kernel,
        grid=(n,),
        in_specs=[whole, whole, whole, blk, blk, pl.BlockSpec((None, D, D), lambda j: (l, 0, 0)),
                  pl.BlockSpec((None, D, 768), lambda j: (l, 0, j)), pl.BlockSpec((None, D, 768), lambda j: (l, 0, n + j)),
                  pl.BlockSpec((None, 768, D), lambda j: (l, j, 0)), pl.BlockSpec((None, 8, D), lambda j: (l, 0, 0))],
        out_specs=[whole, blk, blk, whole, whole, whole, pl.BlockSpec((8, D), lambda j: (0, 0))],
        out_shape=[act(D, BF), act(FF, BF), act(FF, BF), act(D, F32), act(D, BF), act(D, BF), jax.ShapeDtypeStruct((8, D), F32)],
        scratch_shapes=[pltpu.VMEM((rows, D), F32)],
        compiler_params=pltpu.CompilerParams(vmem_limit_bytes=56 * 2**20),
        name="ff_backward",
    )(dy, r1, r2, ga, gb, w_out, w_gated, w_gated, w_down, vec)


def attention_back_kernel(datt_ref, q_ref, k_ref, v_ref, pt_ref, wq_ref, wk_ref, wv_ref, dr1_ref, dq_ref, dk_ref, dv_ref, dx_ref, gb_ref, acc_ref):
    i = pl.program_id(0)
    seqs, pad = pt_ref.shape[0], pt_ref.shape[-1]
    scale = HEAD_DIM ** -0.5

    @pl.when(i == 0)
    def _():
        acc_ref[...] = dr1_ref[...]
    first = lax.broadcasted_iota(jnp.int32, (pad, 128), 1) < HEAD_DIM
    for s in range(seqs):
        rows = slice(s * pad, (s + 1) * pad)
        for pair in range(2):
            lanes = slice(128 * pair, 128 * pair + 128)
            q2 = q_ref[rows, lanes]
            d2 = datt_ref[rows, lanes]
            vs = halves(v_ref[rows, lanes], 1)
            ks = halves(k_ref[rows, lanes].T, 0)
            dv, dk, dq = [], [], None
            for h in range(2):
                pb = pt_ref[s, 2 * pair + h]
                p = pb.astype(F32)
                dp = mm_nt(vs[h], d2)
                ds = (p * (dp - jnp.sum(dp * p, axis=0, keepdims=True))).astype(BF)
                dv.append(mm(pb, d2))
                dk.append(mm(ds, q2))
                part = mm(ks[h], ds)
                dq = part if dq is None else dq + part
            dv_ref[rows, lanes] = jnp.where(first, dv[0], dv[1]).astype(BF)
            dk_ref[rows, lanes] = (jnp.where(first, dk[0], dk[1]) * scale).astype(BF)
            dq_ref[rows, lanes] = (dq * scale).astype(BF).T
    dq, dk, dv = dq_ref[...], dk_ref[...], dv_ref[...]
    gb_ref[0:1, :] = colsum(dq.astype(F32))
    gb_ref[1:2, :] = colsum(dv.astype(F32))
    gb_ref[2:8, :] = jnp.zeros((6, 256), F32)
    acc_ref[...] += mm_nt(dq, wq_ref[...]) + mm_nt(dk, wk_ref[...]) + mm_nt(dv, wv_ref[...])

    @pl.when(i == pl.num_programs(0) - 1)
    def _():
        dx_ref[...] = acc_ref[...].astype(dx_ref.dtype)


def attention_backward(l, datt, q, k, v, pt, w_qkv, dr1, out_dtype):
    rows = datt.shape[0]
    seqs, _, pad, _ = pt.shape
    col = lambda off: pl.BlockSpec((None, D, 256), lambda i: (l, 0, off + i))
    blk = pl.BlockSpec((rows, 256), lambda i: (0, i))
    whole = pl.BlockSpec((rows, D), lambda i: (0, 0))
    act = jax.ShapeDtypeStruct((rows, D), BF)
    return pl.pallas_call(
        attention_back_kernel,
        grid=(3,),
        in_specs=[blk, blk, blk, blk, pl.BlockSpec((seqs, 4, pad, pad), lambda i: (0, i, 0, 0)), col(0), col(3), col(6), whole],
        out_specs=[blk, blk, blk, whole, pl.BlockSpec((8, 256), lambda i: (0, i))],
        out_shape=[act, act, act, jax.ShapeDtypeStruct((rows, D), out_dtype), jax.ShapeDtypeStruct((8, D), F32)],
        scratch_shapes=[pltpu.VMEM((rows, D), F32)],
        compiler_params=pltpu.CompilerParams(vmem_limit_bytes=56 * 2**20),
        name="attention_backward",
    )(datt, q, k, v, pt, w_qkv, w_qkv, w_qkv, dr1)


def place():
    y = lax.axis_index("dp"); f = lax.axis_index("fsdp")
    z = f // 4; x = lax.rem(f // 2, 2); c = lax.rem(f, 2)
    return z, x, y, c

def dev(z, x, y, c):
    return (y, (z * 2 + x) * 2 + c)

def blk(z, x, c, h):
    return ((z * 2 + x) * 2 + c) * 2 + h

PIECES = [(4, 0), (0, 0), (1, 0), (2, 0), (3, 0), (0, 1), (1, 1), (2, 1), (3, 1)]
XFIRST = [True, False, False, True, False, False, False, True, False]
EVENTS = 25

def gather_kernel(*refs):
    ins, outs = refs[:5], refs[5:10]
    send_sem, recv_sem, local_sem = refs[10:]
    z, x, y, c = place()
    zp = z + 1 - 2 * lax.rem(z, 2)
    zm = 3 - z
    zf = lax.rem(z + 2, 4)
    mid = jnp.logical_and(z >= 1, z <= 2)
    end = jnp.logical_not(mid)
    d_zp, d_zm = dev(zp, x, y, c), dev(zm, x, y, c)
    d_x, d_y, d_c = dev(z, 1 - x, y, c), dev(z, x, 1 - y, c), dev(z, x, y, 1 - c)
    bar = pltpu.get_barrier_semaphore()
    for d in (d_zp, d_zm, d_x, d_y, d_c):
        pl.semaphore_signal(bar, 1, device_id=d, device_id_type=MESH)
    pl.semaphore_wait(bar, 5)

    def at(p, b, n=None):
        t, l = PIECES[p]
        ref = outs[t].at[l]
        return ref.at[b] if n is None else ref.at[pl.ds(b, n)]

    def own(p, h, n=None):
        t, l = PIECES[p]
        ref = ins[t].at[l]
        return ref.at[h] if n is None else ref
    pending = []

    def copy(p, e, src, dst, b, d):
        return pltpu.make_async_remote_copy(src_ref=src, dst_ref=dst, send_sem=send_sem.at[p, e], recv_sem=recv_sem.at[p, b], device_id=d, device_id_type=MESH)

    def send(p, e, b, d, when=None, n=None, mine=False):
        src = at(p, b, n)
        if mine:
            src = own(p, y, n)
        cp = copy(p, e, src, at(p, b, n), b, d)
        if when is None:
            cp.start()
        else:
            pl.when(when)(cp.start)
        pending.append((cp, when))

    def got(p, b, d, when=None, n=None):
        cp = copy(p, 0, at(p, b, n), at(p, b, n), b, d)
        if when is None:
            cp.wait_recv()
        else:
            pl.when(when)(cp.wait_recv)

    def local(p):
        return pltpu.make_async_copy(own(p, 0, 2), at(p, blk(z, x, c, 0), 2), local_sem.at[p])

    def st0(p):
        b = blk(z, x, c, y)
        send(p, 1, b, d_zp, mine=True)
        send(p, 2, b, d_zm, when=mid, mine=True)
        send(p, 3, b, d_x, mine=True)
        send(p, 4, blk(z, x, c, 0), d_c, n=2, mine=True)
        local(p).start()

    def spread(p, k, zz):
        b = blk(zz, x, c, y)
        send(p, 8 + k, b, d_x)
        send(p, 11 + k, b, d_y)

    def relay(p, k, zz):
        bx = blk(zz, 1 - x, c, y)
        by = blk(zz, x, c, 1 - y)
        got(p, bx, d_x)
        if XFIRST[p]:
            send(p, 15 + k, bx, d_y)
        got(p, by, d_y)
        if not XFIRST[p]:
            send(p, 15 + k, by, d_x)
        send(p, 18 + k, blk(zz, x, c, 0), d_c, n=2)

    def diag(p, k, zz):
        b = blk(zz, 1 - x, c, 1 - y)
        got(p, b, d_y if XFIRST[p] else d_x)
        send(p, 22 + k, blk(zz, 1 - x, c, 0), d_c, n=2)

    def st1(p):
        got(p, blk(zp, x, c, y), d_zp)
        send(p, 5, blk(zp, x, c, y), d_zm, when=mid)
        got(p, blk(zm, x, c, y), d_zm, when=mid)
        send(p, 6, blk(zm, x, c, y), d_zp, when=mid)
        spread(p, 0, zp)
        b = blk(z, 1 - x, c, y)
        got(p, b, d_x)
        send(p, 14, b, d_y)

    def st2(p):
        got(p, blk(zf, x, c, y), d_zm, when=mid)
        got(p, blk(zf, x, c, y), d_zp, when=end)
        send(p, 7, blk(zf, x, c, y), d_zp, when=mid)
        spread(p, 1, zf)
        relay(p, 0, zp)
        got(p, blk(z, 1 - x, c, 1 - y), d_y)
        send(p, 21, blk(z, 1 - x, c, 0), d_c, n=2)

    def st3(p):
        got(p, blk(zm, x, c, y), d_zp, when=end)
        spread(p, 2, zm)
        relay(p, 1, zf)
        diag(p, 0, zp)

    def st4(p):
        relay(p, 2, zm)
        diag(p, 1, zf)

    def st5(p):
        diag(p, 2, zm)

    def st6(p):
        local(p).wait()
        for zz in (z, zp, zf, zm):
            for xx in (x, 1 - x):
                got(p, blk(zz, xx, 1 - c, 0), d_c, n=2)

    stages = (st0, st1, st2, st3, st4, st5, st6)
    n = len(PIECES)
    for r in range(n + 6):
        for s in (0, 6, 5, 4, 3, 2, 1):
            p = r - s
            if 0 <= p < n:
                stages[s](p)
    for cp, when in pending:
        if when is None:
            cp.wait_send()
        else:
            pl.when(when)(cp.wait_send)

def gather_all(shards, vec):
    ins = []
    for w in shards:
        l, r, cc = w.shape
        ins.append(w.reshape(l, 2, r // 2, cc))
    ins.append(vec[None])
    outs = [jax.ShapeDtypeStruct((v.shape[0], 32) + v.shape[2:], v.dtype) for v in ins]
    n = len(PIECES)
    hbm = pl.BlockSpec(memory_space=pltpu.HBM)
    res = pl.pallas_call(gather_kernel, out_shape=outs, in_specs=[hbm] * 5, out_specs=[hbm] * 5,
        scratch_shapes=[pltpu.SemaphoreType.DMA((n, EVENTS)), pltpu.SemaphoreType.DMA((n, 32)), pltpu.SemaphoreType.DMA((n,))],
        compiler_params=pltpu.CompilerParams(collective_id=0, has_side_effects=True), name="gather_weights")(*ins)
    full = [o.reshape(o.shape[0], -1, o.shape[-1]) for o in res[:4]]
    return full, res[4][0]


NPIECE = 33
LAG = 2


def piece_first_x(p):
    return lax.rem(p * 5, 8) < 5


def add_into(dst, src):
    dst[...] = (dst[...].astype(F32) + src[...].astype(F32)).astype(BF)


def reduce_kernel(
    vec_ref, *refs
):
    lhs = (refs[0:4], refs[4:8])
    rhs = (refs[8:15], refs[15:22])
    o_qkv, o_out, o_gated, o_down, o_vec = refs[22:27]
    (lbuf, rbuf, sbuf, own, r0, h1, h2, za, zb, yf, stage, r0v, h1v, h2v, zav, zbv, yfv, vown,
     lsem, rsem_l, send_sem, recv_sem, out_sem) = refs[27:]
    z, x, y, c = place()
    zp = z + 1 - 2 * lax.rem(z, 2)
    zm = 3 - z
    zf = lax.rem(z + 2, 4)
    mid = jnp.logical_and(z >= 1, z <= 2)
    end = jnp.logical_not(mid)
    d_zp, d_zm = dev(zp, x, y, c), dev(zm, x, y, c)
    d_x, d_y, d_c = dev(z, 1 - x, y, c), dev(z, x, 1 - y, c), dev(z, x, y, 1 - c)
    bar = pltpu.get_barrier_semaphore()
    for d in (d_zp, d_zm, d_x, d_y, d_c):
        pl.semaphore_signal(bar, 1, device_id=d, device_id_type=MESH)
    pl.semaphore_wait(bar, 5)

    NP = NPIECE - 1

    def load(p, go):
        q = lax.rem(p, 16)
        s = lax.rem(p, 2)

        def left(ref, sub=None):
            for cc in range(2):
                src = ref.at[:, cc] if sub is None else ref.at[:, cc, sub]
                cp = pltpu.make_async_copy(src, lbuf.at[s, cc], lsem.at[s, cc])
                if go:
                    cp.start()
                else:
                    cp.wait()

        def right(ref, col=None):
            src = ref if col is None else ref.at[:, pl.ds(pl.multiple_of(jnp.clip(col, 0, 3) * 768, 768), 768)]
            cp = pltpu.make_async_copy(src, rbuf.at[s], rsem_l.at[s])
            if go:
                cp.start()
            else:
                cp.wait()
        if not go:
            left(lhs[0][1])
            right(rhs[0][0])
            return
        for l in range(LAYERS):
            here = p // 16 == LAYERS - 1 - l
            ft, ht, at, xt = lhs[l]
            dm, dg, du, da, dq, dk, dv = rhs[l]

            @pl.when(jnp.logical_and(here, q < 4))
            def _():
                left(ft, jnp.minimum(q, 3))
                right(dm)

            @pl.when(jnp.logical_and(here, jnp.logical_and(q >= 4, q < 12)))
            def _():
                left(ht)

            @pl.when(jnp.logical_and(here, jnp.logical_and(q >= 4, q < 8)))
            def _():
                right(dg, q - 4)

            @pl.when(jnp.logical_and(here, jnp.logical_and(q >= 8, q < 12)))
            def _():
                right(du, q - 8)

            @pl.when(jnp.logical_and(here, q == 12))
            def _():
                left(at)
                right(da)

            @pl.when(jnp.logical_and(here, q > 12))
            def _():
                left(xt)
            for i, d in enumerate((dq, dk, dv)):
                @pl.when(jnp.logical_and(here, q == 13 + i))
                def _():
                    right(d)

    def rcopy(p, e, src, dst, d):
        return pltpu.make_async_remote_copy(src_ref=src, dst_ref=dst, send_sem=send_sem.at[p, e], recv_sem=recv_sem.at[p, e], device_id=d, device_id_type=MESH)

    def product(s, cc, dst):
        for i in range(4):
            v = jnp.dot(lbuf[s, cc, 2 * i : 2 * i + 2].reshape(96, 512), rbuf[s], preferred_element_type=F32).astype(BF)
            v = v.reshape(2, 48, 768)
            dst[i, :, 0] = v[:, :, :384]
            dst[i, :, 1] = v[:, :, 384:]

    def c_copy(p, s):
        return rcopy(p, 0, sbuf.at[s], r0.at[p], d_c)

    def s0(p):
        s = lax.rem(p, 2)
        load(p, False)

        @pl.when(p >= 2)
        def _():
            c_copy(p - 2, s).wait_send()
        product(s, 1 - c, sbuf.at[s])
        c_copy(p, s).start()
        product(s, c, own.at[lax.rem(p, LAG + 1)])

        @pl.when(p + 1 < NP)
        def _():
            load(p + 1, True)

    class Bufs:
        pass
    main, small = Bufs(), Bufs()
    main.r0, main.h1, main.h2, main.za, main.zb, main.yf = r0, h1, h2, za, zb, yf
    small.r0, small.h1, small.h2, small.za, small.zb, small.yf = r0v, h1v, h2v, zav, zbv, yfv
    zlo = jnp.where(z == 1, 1, 0)
    elo = jnp.where(z == 0, 1, 0)
    mlo = jnp.where(z == 1, 2, 0)
    rlo = jnp.where(z == 1, 0, 2)

    def steps(b, p, i, my):
        fx = piece_first_x(p)
        fy = jnp.logical_not(fx)

        def hop1(go):
            a = rcopy(p, 1, b.r0.at[i, :, 1 - x], b.h1.at[i], d_x)
            bb = rcopy(p, 1, b.r0.at[i, :, :, 1 - y], b.h1.at[i], d_y)
            if go == "start":
                pl.when(fx)(a.start)
                pl.when(fy)(bb.start)
            elif go == "recv":
                a.wait_recv()
            else:
                a.wait_send()

        def hop2(go):
            a = rcopy(p, 2, b.h1.at[i, :, 1 - y], b.h2.at[i], d_y)
            bb = rcopy(p, 2, b.h1.at[i, :, 1 - x], b.h2.at[i], d_x)
            if go == "start":
                pl.when(fx)(a.start)
                pl.when(fy)(bb.start)
            elif go == "recv":
                a.wait_recv()
            else:
                a.wait_send()

        def z1():
            return rcopy(p, 3, b.h2.at[i, pl.ds(elo, 3)], b.za.at[i], d_zp)

        def z2():
            return rcopy(p, 4, b.h2.at[i, pl.ds(mlo, 2)], b.zb.at[i], d_zm)

        def z3():
            return rcopy(p, 5, b.h2.at[i, zp], b.zb.at[i, 0], d_zp)

        def y1():
            return rcopy(p, 6, b.h2.at[i, z], b.yf.at[i], d_y)

        def s1():
            rcopy(p, 0, b.r0.at[i], b.r0.at[i], d_c).wait_recv()
            for k in range(4):
                add_into(b.r0.at[i, k], my.at[k])
            hop1("start")

        def s2():
            hop1("recv")
            for k in range(4):
                @pl.when(fx)
                def _():
                    add_into(b.h1.at[i, k], b.r0.at[i, k, x])

                @pl.when(fy)
                def _():
                    add_into(b.h1.at[i, k], b.r0.at[i, k, :, y])
            hop2("start")

        def s3():
            hop2("recv")
            t = jnp.where(fx, y, x)
            for k in range(4):
                add_into(b.h2.at[i, k], b.h1.at[i, k, t])
            pl.when(end)(z1().start)

        def s4():
            @pl.when(mid)
            def _():
                z1().wait_recv()
                for k in range(3):
                    add_into(b.h2.at[i, zlo + k], b.za.at[i, k])
                z2().start()

        def s5():
            @pl.when(mid)
            def _():
                z2().wait_recv()
                for k in range(2):
                    add_into(b.h2.at[i, rlo + k], b.zb.at[i, k])
                z3().start()

        def s6():
            @pl.when(end)
            def _():
                z3().wait_recv()
                add_into(b.h2.at[i, z], b.zb.at[i, 0])
            y1().start()

        def s7():
            y1().wait_recv()

        def done():
            hop1("send")
            hop2("send")
            pl.when(end)(z1().wait_send)

            @pl.when(mid)
            def _():
                z2().wait_send()
                z3().wait_send()
            y1().wait_send()
        return s1, s2, s3, s4, s5, s6, s7, done

    def out_copy(p, s, go):
        q = lax.rem(p, 16)
        layer = LAYERS - 1 - p // 16

        def one(dst):
            cp = pltpu.make_async_copy(stage.at[s], dst, out_sem.at[s])
            if go:
                cp.start()
            else:
                cp.wait()
        if not go:
            one(o_out.at[0])
            return

        @pl.when(q < 4)
        def _():
            one(o_down.at[layer, pl.ds(pl.multiple_of(jnp.minimum(q, 3) * 48, 48), 48)])

        @pl.when(jnp.logical_and(q >= 4, q < 12))
        def _():
            one(o_gated.at[layer, :, pl.ds(pl.multiple_of(jnp.clip(q - 4, 0, 7) * 768, 768), 768)])

        @pl.when(q == 12)
        def _():
            one(o_out.at[layer])

        @pl.when(q > 12)
        def _():
            one(o_qkv.at[layer, :, pl.ds(pl.multiple_of(jnp.clip(q - 13, 0, 2) * 768, 768), 768)])

    def write(p):
        s = lax.rem(p, 2)

        @pl.when(p >= 2)
        def _():
            out_copy(p - 2, s, False)
        a = h2[p, z].astype(F32)
        b = yf[p].astype(F32)

        @pl.when(y == 0)
        def _():
            stage[s, :, :384] = a
            stage[s, :, 384:] = b

        @pl.when(y == 1)
        def _():
            stage[s, :, :384] = b
            stage[s, :, 384:] = a
        out_copy(p, s, True)

    load(0, True)
    vp = NP
    vload = pltpu.make_async_copy(vec_ref.at[c], vown, out_sem.at[2])
    vload.start()
    vc = rcopy(vp, 0, vec_ref.at[1 - c], r0v.at[0], d_c)
    vc.start()
    vload.wait()
    vsteps = steps(small, vp, 0, vown)

    def body(r, carry):
        def at(k, f):
            p = r - LAG * k

            @pl.when(jnp.logical_and(p >= 0, p < NP))
            def _():
                f(jnp.clip(p, 0, NP - 1))

        def st(k):
            def f(p):
                steps(main, p, p, own.at[lax.rem(p, LAG + 1)])[k - 1]()
                if k == 7:
                    write(p)
            return f
        for k in range(1, 8):
            pl.when(r == LAG * k)(vsteps[k - 1])
        at(0, s0)
        for k in range(7, 0, -1):
            at(k, st(k))
        return carry
    lax.fori_loop(0, NP + 7 * LAG, body, 0)

    for p in (NP - 2, NP - 1):
        c_copy(p, p % 2).wait_send()
        out_copy(p, p % 2, False)

    def fin(p, carry):
        steps(main, p, p, own.at[0])[7]()
        return carry
    lax.fori_loop(0, NP, fin, 0)
    vc.wait_send()
    vsteps[7]()
    va, vb = h2v[0, z].astype(F32), yfv[0].astype(F32)
    o_vec[0] = jnp.where(y == 0, va, vb)
    o_vec[1] = jnp.where(y == 0, vb, va)


def reduce_all(vec, lhs, rhs):
    lhs = [(ft.reshape(8, 2, 4, 48, 512),) + tuple(w.reshape(8, 2, 48, 512) for w in rest) for ft, *rest in lhs]
    hbm = pl.BlockSpec(memory_space=pltpu.HBM)
    out = [
        jax.ShapeDtypeStruct((LAYERS, 48, 2304), F32), jax.ShapeDtypeStruct((LAYERS, 48, 768), F32),
        jax.ShapeDtypeStruct((LAYERS, 48, 6144), F32), jax.ShapeDtypeStruct((LAYERS, 192, 768), F32),
        jax.ShapeDtypeStruct((2, 48, 128), F32),
    ]
    n = NPIECE - 1
    scratch = [
        pltpu.VMEM((2, 2, 8, 48, 512), BF), pltpu.VMEM((2, 512, 768), BF),
        pltpu.VMEM((2, 4, 2, 2, 48, 384), BF), pltpu.VMEM((LAG + 1, 4, 2, 2, 48, 384), BF),
        pltpu.VMEM((n, 4, 2, 2, 48, 384), BF), pltpu.VMEM((n, 4, 2, 48, 384), BF), pltpu.VMEM((n, 4, 48, 384), BF),
        pltpu.VMEM((n, 3, 48, 384), BF), pltpu.VMEM((n, 2, 48, 384), BF), pltpu.VMEM((n, 48, 384), BF),
        pltpu.VMEM((2, 48, 768), F32),
        pltpu.VMEM((1, 4, 2, 2, 48, 128), BF), pltpu.VMEM((1, 4, 2, 48, 128), BF), pltpu.VMEM((1, 4, 48, 128), BF),
        pltpu.VMEM((1, 3, 48, 128), BF), pltpu.VMEM((1, 2, 48, 128), BF), pltpu.VMEM((1, 48, 128), BF),
        pltpu.VMEM((4, 2, 2, 48, 128), BF),
        pltpu.SemaphoreType.DMA((2, 2)), pltpu.SemaphoreType.DMA((2,)),
        pltpu.SemaphoreType.DMA((NPIECE, 7)), pltpu.SemaphoreType.DMA((NPIECE, 7)), pltpu.SemaphoreType.DMA((3,)),
    ]
    return pl.pallas_call(
        reduce_kernel, out_shape=out, in_specs=[hbm] * 23,
        out_specs=[hbm] * 4 + [pl.BlockSpec(memory_space=pltpu.VMEM)],
        scratch_shapes=scratch,
        compiler_params=pltpu.CompilerParams(collective_id=1, has_side_effects=True, vmem_limit_bytes=62 * 2**20), name="reduce_grads",
    )(vec, *lhs[0], *lhs[1], *rhs[0], *rhs[1])


def fetch_all(shards, vectors, fast):
    vec = jnp.stack(vectors, axis=1)
    if not fast:
        full = [lax.all_gather(w, "fsdp", axis=1, tiled=True) for w in shards]
        return full, lax.all_gather(vec, "fsdp", axis=2, tiled=True).astype(F32)
    width = vec.shape[-1]
    full, packed = gather_all(shards, jnp.pad(vec, ((0, 0), (0, 0), (0, 128 - width))))
    packed = packed.reshape(-1, LAYERS, 8, 128)[..., :width]
    return full, packed.transpose(1, 2, 0, 3).reshape(LAYERS, 8, -1).astype(F32)


def sum_grads(lhs, rhs, vecs, fast):
    vec = jnp.stack(vecs)
    if fast:
        v = vec.reshape(LAYERS, 8, 8, 2, 48).transpose(3, 2, 0, 4, 1)
        v = jnp.pad(v, ((0, 0),) * 4 + ((0, 120),)).reshape(2, 4, 2, LAYERS, 48, 128)
        *mats, v = reduce_all(v.astype(BF), lhs, rhs)
        return mats, v[:, :, :8].transpose(0, 2, 1)

    def one(g, dim):
        part = lax.psum_scatter(g.astype(BF), "fsdp", scatter_dimension=dim, tiled=True)
        return lax.psum(part, "dp").astype(F32)
    mats = [[], [], [], []]
    for (ft, ht, at, xt), (dm, dg, du, da, dq, dk, dv) in zip(lhs, rhs):
        mats[0].append(one(mm(xt, jnp.concatenate([dq, dk, dv], axis=1)), 0))
        mats[1].append(one(mm(at, da), 0))
        mats[2].append(one(mm(ht, jnp.concatenate([dg, du], axis=1)), 0))
        mats[3].append(one(mm(ft, dm), 0))
    return [jnp.stack(m) for m in mats], one(vec, 2)


def per_device(fast, inputs, lengths, cotangent, w_qkv, q_bias, v_bias, w_out, b_out, gain_one, shift_one, w_gated, w_down, b_down, gain_two, shift_two):
    (wq, wo, wg, wd), vec = fetch_all(
        (w_qkv, w_out, w_gated, w_down),
        (q_bias, v_bias, b_out, gain_one, shift_one, b_down, gain_two, shift_two),
        fast,
    )
    seq_lengths = lengths.reshape(-1)
    slopes = jnp.array(slopes_list(HEADS), F32)
    x = inputs.reshape(-1, D)
    kept = []
    for l in range(LAYERS):
        q, k, v, att, pt, xt, at = attention_forward(l, seq_lengths, slopes, x, wq, vec)
        out_dtype = BF if l == LAYERS - 1 else F32
        r1, r2, ga, gb, ft, ht, x = ff_forward(l, att, x, wo, wg, wd, vec, out_dtype)
        kept.append((q, k, v, pt, r1, r2, ga, gb, (ft, ht, at, xt)))
    dy = cotangent.reshape(-1, D)
    rhs, vecs = [None] * LAYERS, [None] * LAYERS
    for l in reversed(range(LAYERS)):
        q, k, v, pt, r1, r2, ga, gb, _ = kept[l]
        dm, dg, du, dr1, da, datt, gv = ff_backward(l, dy, r1, r2, ga, gb, wo, wg, wd, vec)
        dq, dk, dv, dy, gbias = attention_backward(l, datt, q, k, v, pt, wq, dr1, BF if l == 0 else F32)
        rhs[l] = (dm, dg, du, da, dq, dk, dv)
        vecs[l] = gv + gbias
    m, vs = sum_grads([k[8] for k in kept], rhs, vecs, fast)
    return (
        x.reshape(inputs.shape), dy.reshape(inputs.shape), m[0], vs[:, 0], vs[:, 1], m[1], vs[:, 2], vs[:, 3], vs[:, 4], m[2], m[3], vs[:, 5], vs[:, 6], vs[:, 7],
    )


def solution(mesh):
    placed = (
        P(None, ("dp", "fsdp"), None, None),
        P(None, ("dp", "fsdp")),
        P(None, ("dp", "fsdp"), None, None),
        P(None, "fsdp", None),
        P(None, "fsdp"),
        P(None, "fsdp"),
        P(None, "fsdp", None),
        P(None, "fsdp"),
        P(None, "fsdp"),
        P(None, "fsdp"),
        P(None, "fsdp", None),
        P(None, "fsdp", None),
        P(None, "fsdp"),
        P(None, "fsdp"),
        P(None, "fsdp"),
    )
    return jax.shard_map(
        functools.partial(per_device, dict(mesh.shape) == {"dp": 2, "fsdp": 16}),
        mesh=mesh,
        in_specs=placed,
        out_specs=(
            P(None, ("dp", "fsdp"), None, None),
            P(None, ("dp", "fsdp"), None, None),
            P(None, "fsdp", None),
            P(None, "fsdp"),
            P(None, "fsdp"),
            P(None, "fsdp", None),
            P(None, "fsdp"),
            P(None, "fsdp"),
            P(None, "fsdp"),
            P(None, "fsdp", None),
            P(None, "fsdp", None),
            P(None, "fsdp"),
            P(None, "fsdp"),
            P(None, "fsdp"),
        ),
        check_vma=False,
    )
```

```python
import functools
import math

import jax
import jax.numpy as jnp
from jax import lax
from jax.experimental import pallas as pl
from jax.experimental.pallas import tpu as pltpu
from jax.sharding import PartitionSpec as P

MESH = pl.DeviceIdType.MESH

BF = jnp.bfloat16
F32 = jnp.float32
D, HEADS, HEAD_DIM, FF, LAYERS = 768, 12, 64, 3072, 2
EPS = 1e-12
NEG = -1e30
NT = (((1,), (1,)), ((), ()))


def slopes_list(heads_count):
    nearest = 2 ** int(math.floor(math.log2(heads_count)))
    leading = [2.0 ** (-8.0 * (number + 1) / nearest) for number in range(nearest)]
    trailing = [2.0 ** (-8.0 * (number + 1) / (2 * nearest)) for number in range(2 * nearest)][0::2]
    return leading + trailing[: heads_count - nearest]


def mm(a, b):
    return jnp.dot(a, b, preferred_element_type=F32)


def mm_nt(a, b):
    return lax.dot_general(a, b, NT, preferred_element_type=F32)


def erf(x):
    return lax.erf(x)


def norm_parts(r):
    cent = r - jnp.mean(r, axis=-1, keepdims=True)
    rstd = lax.rsqrt(jnp.mean(cent * cent, axis=-1, keepdims=True) + EPS)
    return cent * rstd, rstd


def norm_back(dy, gain, n, rstd):
    dn = dy * gain
    return rstd * (dn - jnp.mean(dn, axis=-1, keepdims=True) - n * jnp.mean(dn * n, axis=-1, keepdims=True))


def halves(v, axis):
    first = lax.broadcasted_iota(jnp.int32, v.shape, axis) < HEAD_DIM
    zero = jnp.zeros_like(v)
    return jnp.where(first, v, zero), jnp.where(first, zero, v)


def attention_kernel(len_ref, slope_ref, x_ref, wq_ref, wk_ref, wv_ref, vec_ref, q_ref, k_ref, v_ref, att_ref, pt_ref, xt_ref, at_ref, xb_ref, dist_ref):
    i = pl.program_id(0)
    seqs, pad = pt_ref.shape[0], pt_ref.shape[-1]

    @pl.when(i == 0)
    def _():
        xb = x_ref[...].astype(BF)
        xb_ref[...] = xb
        xt_ref[...] = xb.T
        keys = lax.broadcasted_iota(jnp.int32, (pad, pad), 0)
        rows = lax.broadcasted_iota(jnp.int32, (pad, pad), 1)
        dist_ref[...] = jnp.abs(keys - rows).astype(F32)
    xb = xb_ref[...]
    q_ref[...] = (mm(xb, wq_ref[...]) + vec_ref[0:1, :]).astype(BF)
    k_ref[...] = mm(xb, wk_ref[...]).astype(BF)
    v_ref[...] = (mm(xb, wv_ref[...]) + vec_ref[1:2, :]).astype(BF)
    for s in range(seqs):
        rows = slice(s * pad, (s + 1) * pad)
        hidden = jnp.where(lax.broadcasted_iota(jnp.int32, (pad, 1), 0) < len_ref[s], 0.0, NEG)
        for pair in range(2):
            lanes = slice(128 * pair, 128 * pair + 128)
            q2 = q_ref[rows, lanes] * BF(HEAD_DIM ** -0.5)
            k0, k1 = halves(k_ref[rows, lanes], 1)
            v0, v1 = halves(v_ref[rows, lanes].T, 0)
            total = None
            for h, (kh, vh) in enumerate(((k0, v0), (k1, v1))):
                slope = slope_ref[4 * i + 2 * pair + h]
                sc = mm_nt(kh, q2) - slope * dist_ref[...] + hidden
                e = jnp.exp(sc - jnp.max(sc, axis=0, keepdims=True))
                p = (e * (1.0 / jnp.sum(e, axis=0, keepdims=True))).astype(BF)
                pt_ref[s, 2 * pair + h] = p
                part = mm(vh, p)
                total = part if total is None else total + part
            total = total.astype(BF)
            at_ref[lanes, rows] = total
            att_ref[rows, lanes] = total.T


def attention_forward(l, lengths, slopes, x, w_qkv, vec):
    rows = x.shape[0]
    seqs = lengths.shape[0]
    pad = rows // seqs
    col = lambda off: pl.BlockSpec((None, D, 256), lambda i: (l, 0, off + i))
    blk = pl.BlockSpec((rows, 256), lambda i: (0, i))
    smem = pl.BlockSpec(memory_space=pltpu.SMEM)
    act = jax.ShapeDtypeStruct((rows, D), BF)
    return pl.pallas_call(
        attention_kernel,
        grid=(3,),
        in_specs=[smem, smem, pl.BlockSpec((rows, D), lambda i: (0, 0)), col(0), col(3), col(6), pl.BlockSpec((None, 8, 256), lambda i: (l, 0, i))],
        out_specs=[blk, blk, blk, blk, pl.BlockSpec((seqs, 4, pad, pad), lambda i: (0, i, 0, 0)), pl.BlockSpec((D, rows), lambda i: (0, 0)), pl.BlockSpec((256, rows), lambda i: (i, 0))],
        out_shape=[act, act, act, act, jax.ShapeDtypeStruct((seqs, HEADS, pad, pad), BF), jax.ShapeDtypeStruct((D, rows), BF), jax.ShapeDtypeStruct((D, rows), BF)],
        scratch_shapes=[pltpu.VMEM((rows, D), BF), pltpu.VMEM((pad, pad), F32)],
        compiler_params=pltpu.CompilerParams(vmem_limit_bytes=56 * 2**20),
        name="attention_forward",
    )(lengths, slopes, x, w_qkv, w_qkv, w_qkv, vec)


def ff_kernel(att_ref, x_ref, wo_ref, wg_ref, wu_ref, wd_ref, vec_ref, r1_ref, r2_ref, ga_ref, gb_ref, ft_ref, ht_ref, out_ref, h_ref, hb_ref, acc_ref):
    j = pl.program_id(0)

    @pl.when(j == 0)
    def _():
        r1 = x_ref[...].astype(F32) + (mm(att_ref[...], wo_ref[...]) + vec_ref[2:3, :])
        r1_ref[...] = r1
        h = norm_parts(r1)[0] * vec_ref[3:4, :] + vec_ref[4:5, :]
        h_ref[...] = h
        hb = h.astype(BF)
        hb_ref[...] = hb
        ht_ref[...] = hb.T
        acc_ref[...] = jnp.zeros_like(acc_ref)
    hb = hb_ref[...]
    g = mm(hb, wg_ref[...])
    u = mm(hb, wu_ref[...])
    cdf = 0.5 + 0.5 * erf(g * math.sqrt(0.5))
    gelu = g * cdf
    slope = cdf + g * (jnp.exp(-0.5 * (g * g)) * (1.0 / math.sqrt(2.0 * math.pi)))
    ga_ref[...] = gelu.astype(BF)
    gb_ref[...] = (slope * u).astype(BF)
    f = (gelu * u).astype(BF)
    ft_ref[...] = f.T
    acc_ref[...] += mm(f, wd_ref[...])

    @pl.when(j == pl.num_programs(0) - 1)
    def _():
        r2 = h_ref[...] + (acc_ref[...] + vec_ref[5:6, :])
        r2_ref[...] = r2
        out_ref[...] = (norm_parts(r2)[0] * vec_ref[6:7, :] + vec_ref[7:8, :]).astype(out_ref.dtype)


def ff_forward(l, att, x, w_out, w_gated, w_down, vec, out_dtype):
    rows = x.shape[0]
    n = FF // 768
    whole = pl.BlockSpec((rows, D), lambda j: (0, 0))
    blk = pl.BlockSpec((rows, 768), lambda j: (0, j))
    return pl.pallas_call(
        ff_kernel,
        grid=(n,),
        in_specs=[whole, whole, pl.BlockSpec((None, D, D), lambda j: (l, 0, 0)),
                  pl.BlockSpec((None, D, 768), lambda j: (l, 0, j)), pl.BlockSpec((None, D, 768), lambda j: (l, 0, n + j)),
                  pl.BlockSpec((None, 768, D), lambda j: (l, j, 0)), pl.BlockSpec((None, 8, D), lambda j: (l, 0, 0))],
        out_specs=[whole, whole, blk, blk, pl.BlockSpec((768, rows), lambda j: (j, 0)), pl.BlockSpec((D, rows), lambda j: (0, 0)), whole],
        out_shape=[jax.ShapeDtypeStruct((rows, D), F32), jax.ShapeDtypeStruct((rows, D), F32),
                   jax.ShapeDtypeStruct((rows, FF), BF), jax.ShapeDtypeStruct((rows, FF), BF),
                   jax.ShapeDtypeStruct((FF, rows), BF), jax.ShapeDtypeStruct((D, rows), BF), jax.ShapeDtypeStruct((rows, D), out_dtype)],
        scratch_shapes=[pltpu.VMEM((rows, D), F32), pltpu.VMEM((rows, D), BF), pltpu.VMEM((rows, D), F32)],
        compiler_params=pltpu.CompilerParams(vmem_limit_bytes=56 * 2**20),
        name="ff_forward",
    )(att, x, w_out, w_gated, w_gated, w_down, vec)


def colsum(v):
    return jnp.sum(v, axis=0, keepdims=True)


def ff_back_kernel(dy_ref, r1_ref, r2_ref, ga_ref, gb_ref, wo_ref, wg_ref, wu_ref, wd_ref, vec_ref, dm_ref, dg_ref, du_ref, dr1_ref, da_ref, datt_ref, gv_ref, acc_ref):
    j = pl.program_id(0)

    @pl.when(j == 0)
    def _():
        dy = dy_ref[...].astype(F32)
        n, rstd = norm_parts(r2_ref[...])
        dr2 = norm_back(dy, vec_ref[6:7, :], n, rstd)
        acc_ref[...] = dr2
        dm = dr2.astype(BF)
        dm_ref[...] = dm
        gv_ref[5:6, :] = colsum(dm.astype(F32))
        gv_ref[6:7, :] = colsum(dy * n)
        gv_ref[7:8, :] = colsum(dy)
        gv_ref[0:2, :] = jnp.zeros((2, D), F32)
    df = mm_nt(dm_ref[...], wd_ref[...])
    dg = (df * gb_ref[...].astype(F32)).astype(BF)
    du = (df * ga_ref[...].astype(F32)).astype(BF)
    dg_ref[...] = dg
    du_ref[...] = du
    acc_ref[...] += mm_nt(dg, wg_ref[...]) + mm_nt(du, wu_ref[...])

    @pl.when(j == pl.num_programs(0) - 1)
    def _():
        dh = acc_ref[...]
        n, rstd = norm_parts(r1_ref[...])
        dr1 = norm_back(dh, vec_ref[3:4, :], n, rstd)
        dr1_ref[...] = dr1
        da = dr1.astype(BF)
        da_ref[...] = da
        gv_ref[2:3, :] = colsum(da.astype(F32))
        gv_ref[3:4, :] = colsum(dh * n)
        gv_ref[4:5, :] = colsum(dh)
        datt_ref[...] = mm_nt(da, wo_ref[...]).astype(BF)


def ff_backward(l, dy, r1, r2, ga, gb, w_out, w_gated, w_down, vec):
    rows = dy.shape[0]
    n = FF // 768
    whole = pl.BlockSpec((rows, D), lambda j: (0, 0))
    blk = pl.BlockSpec((rows, 768), lambda j: (0, j))
    act = lambda c, t: jax.ShapeDtypeStruct((rows, c), t)
    return pl.pallas_call(
        ff_back_kernel,
        grid=(n,),
        in_specs=[whole, whole, whole, blk, blk, pl.BlockSpec((None, D, D), lambda j: (l, 0, 0)),
                  pl.BlockSpec((None, D, 768), lambda j: (l, 0, j)), pl.BlockSpec((None, D, 768), lambda j: (l, 0, n + j)),
                  pl.BlockSpec((None, 768, D), lambda j: (l, j, 0)), pl.BlockSpec((None, 8, D), lambda j: (l, 0, 0))],
        out_specs=[whole, blk, blk, whole, whole, whole, pl.BlockSpec((8, D), lambda j: (0, 0))],
        out_shape=[act(D, BF), act(FF, BF), act(FF, BF), act(D, F32), act(D, BF), act(D, BF), jax.ShapeDtypeStruct((8, D), F32)],
        scratch_shapes=[pltpu.VMEM((rows, D), F32)],
        compiler_params=pltpu.CompilerParams(vmem_limit_bytes=56 * 2**20),
        name="ff_backward",
    )(dy, r1, r2, ga, gb, w_out, w_gated, w_gated, w_down, vec)


def attention_back_kernel(datt_ref, q_ref, k_ref, v_ref, pt_ref, wq_ref, wk_ref, wv_ref, dr1_ref, dq_ref, dk_ref, dv_ref, dx_ref, gb_ref, acc_ref):
    i = pl.program_id(0)
    seqs, pad = pt_ref.shape[0], pt_ref.shape[-1]
    scale = HEAD_DIM ** -0.5

    @pl.when(i == 0)
    def _():
        acc_ref[...] = dr1_ref[...]
    first = lax.broadcasted_iota(jnp.int32, (pad, 128), 1) < HEAD_DIM
    for s in range(seqs):
        rows = slice(s * pad, (s + 1) * pad)
        for pair in range(2):
            lanes = slice(128 * pair, 128 * pair + 128)
            q2 = q_ref[rows, lanes]
            d2 = datt_ref[rows, lanes]
            vs = halves(v_ref[rows, lanes], 1)
            ks = halves(k_ref[rows, lanes].T, 0)
            dv, dk, dq = [], [], None
            for h in range(2):
                pb = pt_ref[s, 2 * pair + h]
                p = pb.astype(F32)
                dp = mm_nt(vs[h], d2)
                ds = (p * (dp - jnp.sum(dp * p, axis=0, keepdims=True))).astype(BF)
                dv.append(mm(pb, d2))
                dk.append(mm(ds, q2))
                part = mm(ks[h], ds)
                dq = part if dq is None else dq + part
            dv_ref[rows, lanes] = jnp.where(first, dv[0], dv[1]).astype(BF)
            dk_ref[rows, lanes] = (jnp.where(first, dk[0], dk[1]) * scale).astype(BF)
            dq_ref[rows, lanes] = (dq * scale).astype(BF).T
    dq, dk, dv = dq_ref[...], dk_ref[...], dv_ref[...]
    gb_ref[0:1, :] = colsum(dq.astype(F32))
    gb_ref[1:2, :] = colsum(dv.astype(F32))
    gb_ref[2:8, :] = jnp.zeros((6, 256), F32)
    acc_ref[...] += mm_nt(dq, wq_ref[...]) + mm_nt(dk, wk_ref[...]) + mm_nt(dv, wv_ref[...])

    @pl.when(i == pl.num_programs(0) - 1)
    def _():
        dx_ref[...] = acc_ref[...].astype(dx_ref.dtype)


def attention_backward(l, datt, q, k, v, pt, w_qkv, dr1, out_dtype):
    rows = datt.shape[0]
    seqs, _, pad, _ = pt.shape
    col = lambda off: pl.BlockSpec((None, D, 256), lambda i: (l, 0, off + i))
    blk = pl.BlockSpec((rows, 256), lambda i: (0, i))
    whole = pl.BlockSpec((rows, D), lambda i: (0, 0))
    act = jax.ShapeDtypeStruct((rows, D), BF)
    return pl.pallas_call(
        attention_back_kernel,
        grid=(3,),
        in_specs=[blk, blk, blk, blk, pl.BlockSpec((seqs, 4, pad, pad), lambda i: (0, i, 0, 0)), col(0), col(3), col(6), whole],
        out_specs=[blk, blk, blk, whole, pl.BlockSpec((8, 256), lambda i: (0, i))],
        out_shape=[act, act, act, jax.ShapeDtypeStruct((rows, D), out_dtype), jax.ShapeDtypeStruct((8, D), F32)],
        scratch_shapes=[pltpu.VMEM((rows, D), F32)],
        compiler_params=pltpu.CompilerParams(vmem_limit_bytes=56 * 2**20),
        name="attention_backward",
    )(datt, q, k, v, pt, w_qkv, w_qkv, w_qkv, dr1)


def place():
    y = lax.axis_index("dp"); f = lax.axis_index("fsdp")
    z = f // 4; x = lax.rem(f // 2, 2); c = lax.rem(f, 2)
    return z, x, y, c

def dev(z, x, y, c):
    return (y, (z * 2 + x) * 2 + c)

def blk(z, x, c, h):
    return ((z * 2 + x) * 2 + c) * 2 + h

PIECES = [(4, 0), (0, 0), (1, 0), (2, 0), (3, 0), (0, 1), (1, 1), (2, 1), (3, 1)]
XFIRST = [True, False, False, True, False, False, False, True, False]
EVENTS = 25

def gather_kernel(*refs):
    ins, outs = refs[:5], refs[5:10]
    send_sem, recv_sem, local_sem = refs[10:]
    z, x, y, c = place()
    zp = z + 1 - 2 * lax.rem(z, 2)
    zm = 3 - z
    zf = lax.rem(z + 2, 4)
    mid = jnp.logical_and(z >= 1, z <= 2)
    end = jnp.logical_not(mid)
    d_zp, d_zm = dev(zp, x, y, c), dev(zm, x, y, c)
    d_x, d_y, d_c = dev(z, 1 - x, y, c), dev(z, x, 1 - y, c), dev(z, x, y, 1 - c)
    bar = pltpu.get_barrier_semaphore()
    for d in (d_zp, d_zm, d_x, d_y, d_c):
        pl.semaphore_signal(bar, 1, device_id=d, device_id_type=MESH)
    pl.semaphore_wait(bar, 5)

    def at(p, b, n=None):
        t, l = PIECES[p]
        ref = outs[t].at[l]
        return ref.at[b] if n is None else ref.at[pl.ds(b, n)]

    def own(p, h, n=None):
        t, l = PIECES[p]
        ref = ins[t].at[l]
        return ref.at[h] if n is None else ref
    pending = []

    def copy(p, e, src, dst, b, d):
        return pltpu.make_async_remote_copy(src_ref=src, dst_ref=dst, send_sem=send_sem.at[p, e], recv_sem=recv_sem.at[p, b], device_id=d, device_id_type=MESH)

    def send(p, e, b, d, when=None, n=None, mine=False):
        src = at(p, b, n)
        if mine:
            src = own(p, y, n)
        cp = copy(p, e, src, at(p, b, n), b, d)
        if when is None:
            cp.start()
        else:
            pl.when(when)(cp.start)
        pending.append((cp, when))

    def got(p, b, d, when=None, n=None):
        cp = copy(p, 0, at(p, b, n), at(p, b, n), b, d)
        if when is None:
            cp.wait_recv()
        else:
            pl.when(when)(cp.wait_recv)

    def local(p):
        return pltpu.make_async_copy(own(p, 0, 2), at(p, blk(z, x, c, 0), 2), local_sem.at[p])

    def st0(p):
        b = blk(z, x, c, y)
        send(p, 1, b, d_zp, mine=True)
        send(p, 2, b, d_zm, when=mid, mine=True)
        send(p, 3, b, d_x, mine=True)
        send(p, 4, blk(z, x, c, 0), d_c, n=2, mine=True)
        local(p).start()

    def spread(p, k, zz):
        b = blk(zz, x, c, y)
        send(p, 8 + k, b, d_x)
        send(p, 11 + k, b, d_y)

    def relay(p, k, zz):
        bx = blk(zz, 1 - x, c, y)
        by = blk(zz, x, c, 1 - y)
        got(p, bx, d_x)
        if XFIRST[p]:
            send(p, 15 + k, bx, d_y)
        got(p, by, d_y)
        if not XFIRST[p]:
            send(p, 15 + k, by, d_x)
        send(p, 18 + k, blk(zz, x, c, 0), d_c, n=2)

    def diag(p, k, zz):
        b = blk(zz, 1 - x, c, 1 - y)
        got(p, b, d_y if XFIRST[p] else d_x)
        send(p, 22 + k, blk(zz, 1 - x, c, 0), d_c, n=2)

    def st1(p):
        got(p, blk(zp, x, c, y), d_zp)
        send(p, 5, blk(zp, x, c, y), d_zm, when=mid)
        got(p, blk(zm, x, c, y), d_zm, when=mid)
        send(p, 6, blk(zm, x, c, y), d_zp, when=mid)
        spread(p, 0, zp)
        b = blk(z, 1 - x, c, y)
        got(p, b, d_x)
        send(p, 14, b, d_y)

    def st2(p):
        got(p, blk(zf, x, c, y), d_zm, when=mid)
        got(p, blk(zf, x, c, y), d_zp, when=end)
        send(p, 7, blk(zf, x, c, y), d_zp, when=mid)
        spread(p, 1, zf)
        relay(p, 0, zp)
        got(p, blk(z, 1 - x, c, 1 - y), d_y)
        send(p, 21, blk(z, 1 - x, c, 0), d_c, n=2)

    def st3(p):
        got(p, blk(zm, x, c, y), d_zp, when=end)
        spread(p, 2, zm)
        relay(p, 1, zf)
        diag(p, 0, zp)

    def st4(p):
        relay(p, 2, zm)
        diag(p, 1, zf)

    def st5(p):
        diag(p, 2, zm)

    def st6(p):
        local(p).wait()
        for zz in (z, zp, zf, zm):
            for xx in (x, 1 - x):
                got(p, blk(zz, xx, 1 - c, 0), d_c, n=2)

    stages = (st0, st1, st2, st3, st4, st5, st6)
    n = len(PIECES)
    for r in range(n + 6):
        for s in (0, 6, 5, 4, 3, 2, 1):
            p = r - s
            if 0 <= p < n:
                stages[s](p)
    for cp, when in pending:
        if when is None:
            cp.wait_send()
        else:
            pl.when(when)(cp.wait_send)

def gather_all(shards, vec):
    ins = []
    for w in shards:
        l, r, cc = w.shape
        ins.append(w.reshape(l, 2, r // 2, cc))
    ins.append(vec[None])
    outs = [jax.ShapeDtypeStruct((v.shape[0], 32) + v.shape[2:], v.dtype) for v in ins]
    n = len(PIECES)
    hbm = pl.BlockSpec(memory_space=pltpu.HBM)
    res = pl.pallas_call(gather_kernel, out_shape=outs, in_specs=[hbm] * 5, out_specs=[hbm] * 5,
        scratch_shapes=[pltpu.SemaphoreType.DMA((n, EVENTS)), pltpu.SemaphoreType.DMA((n, 32)), pltpu.SemaphoreType.DMA((n,))],
        compiler_params=pltpu.CompilerParams(collective_id=0, has_side_effects=True), name="gather_weights")(*ins)
    full = [o.reshape(o.shape[0], -1, o.shape[-1]) for o in res[:4]]
    return full, res[4][0]


NPIECE = 33
LAG = 2
SLOTS = 16


def piece_first_x(p):
    return lax.rem(p * 5, 8) < 5


def add_into(dst, src):
    dst[...] = (dst[...].astype(F32) + src[...].astype(F32)).astype(BF)


class Group:
    def __init__(self, names, refs):
        for name, ref in zip(names, refs):
            setattr(self, name, ref)


KEPT = ("r1", "r2", "ga", "gb", "q", "k", "v", "pt", "ft", "ht", "at", "xt")
MATS = ("wq", "wo", "wg", "wd")
GRADS = ("dm", "dg", "du", "da", "dq", "dk", "dv")


def backward_kernel(*refs):
    refs = list(refs)

    def take(names):
        n = len(names)
        g = Group(names, refs[:n])
        del refs[:n]
        return g
    cot, vec = refs[:2]
    del refs[:2]
    kept = [take(KEPT) for _ in range(LAYERS)]
    w = take(MATS)
    o = take(("qkv", "out", "gated", "down", "vec", "dx"))
    g = take(GRADS)
    s = take(("lbuf", "rbuf", "sbuf", "own", "stage", "r0v", "h1v", "h2v", "zav", "zbv", "yfv", "vall"))
    c_ = take(("r0", "h1", "h2", "za", "zb", "yf"))
    t_ = take(("acc", "res", "wd", "wg", "wu", "ga", "gb", "wo", "dm", "dg", "du", "da", "datt", "q", "k", "v", "pt", "wq", "wk", "wv", "dq", "dk", "dv", "gv", "cot"))
    m_ = take(("lsem", "rsem", "send", "recv", "out", "vload", "fsem", "asem", "osem"))
    pad = kept[0].pt.shape[-1]
    seqs = kept[0].pt.shape[0]

    z, x, y, c = place()
    zp = z + 1 - 2 * lax.rem(z, 2)
    zm = 3 - z
    mid = jnp.logical_and(z >= 1, z <= 2)
    end = jnp.logical_not(mid)
    d_zp, d_zm = dev(zp, x, y, c), dev(zm, x, y, c)
    d_x, d_y, d_c = dev(z, 1 - x, y, c), dev(z, x, 1 - y, c), dev(z, x, y, 1 - c)
    bar = pltpu.get_barrier_semaphore()
    for d in (d_zp, d_zm, d_x, d_y, d_c):
        pl.semaphore_signal(bar, 1, device_id=d, device_id_type=MESH)
    pl.semaphore_wait(bar, 5)
    NP = NPIECE - 1


    def run(cp, go):
        if go:
            cp.start()
        else:
            cp.wait()

    def cols(ref, j, width):
        return ref.at[:, pl.ds(pl.multiple_of(j * width, width), width)]

    def load_ff(l, j, go):
        def one(i, src, dst):
            run(pltpu.make_async_copy(src, dst, m_.fsem.at[i]), go)
        one(0, w.wd.at[l, pl.ds(pl.multiple_of(j * 768, 768), 768)], t_.wd)
        one(1, cols(w.wg.at[l], j, 768), t_.wg)
        one(2, cols(w.wg.at[l], j + 4, 768), t_.wu)

        def acts(kl):
            one(3, cols(kl.ga, j, 768), t_.ga)
            one(4, cols(kl.gb, j, 768), t_.gb)

            @pl.when(j == 0)
            def _():
                one(5, kl.r2, t_.res)

            @pl.when(j == 3)
            def _():
                one(5, kl.r1, t_.res)
        if go:
            for i in range(LAYERS):
                @pl.when(l == i)
                def _():
                    acts(kept[i])
        else:
            one(3, cols(kept[0].ga, j, 768), t_.ga)
            one(4, cols(kept[0].gb, j, 768), t_.gb)

            @pl.when(jnp.logical_or(j == 0, j == 3))
            def _():
                one(5, kept[0].r1, t_.res)

        @pl.when(j == 3)
        def _():
            one(6, w.wo.at[l], t_.wo)

    def load_att(l, i, go):
        def one(n, src, dst):
            run(pltpu.make_async_copy(src, dst, m_.asem.at[n]), go)

        def acts(kl):
            one(0, cols(kl.q, i, 256), t_.q)
            one(1, cols(kl.k, i, 256), t_.k)
            one(2, cols(kl.v, i, 256), t_.v)
            one(3, kl.pt.at[:, pl.ds(4 * i, 4)], t_.pt)
        if go:
            for n in range(LAYERS):
                @pl.when(l == n)
                def _():
                    acts(kept[n])
        else:
            acts(kept[0])
        one(4, cols(w.wq.at[l], i, 256), t_.wq)
        one(5, cols(w.wq.at[l], i + 3, 256), t_.wk)
        one(6, cols(w.wq.at[l], i + 6, 256), t_.wv)

    def ff_task(l, j):
        load_ff(l, j, False)

        @pl.when(j == 0)
        def _():
            dy = t_.acc[...]
            n, rstd = norm_parts(t_.res[...])
            dr2 = norm_back(dy, vec[l, 6:7, :], n, rstd)
            t_.acc[...] = dr2
            dm = dr2.astype(BF)
            t_.dm[...] = dm
            t_.gv[l, 5:6, :] = colsum(dm.astype(F32))
            t_.gv[l, 6:7, :] = colsum(dy * n)
            t_.gv[l, 7:8, :] = colsum(dy)
        df = mm_nt(t_.dm[...], t_.wd[...])
        dg = (df * t_.gb[...].astype(F32)).astype(BF)
        du = (df * t_.ga[...].astype(F32)).astype(BF)
        t_.dg[...] = dg
        t_.du[...] = du
        t_.acc[...] += mm_nt(dg, t_.wg[...]) + mm_nt(du, t_.wu[...])

        @pl.when(j == 3)
        def _():
            dh = t_.acc[...]
            n, rstd = norm_parts(t_.res[...])
            dr1 = norm_back(dh, vec[l, 3:4, :], n, rstd)
            t_.acc[...] = dr1
            da = dr1.astype(BF)
            t_.da[...] = da
            t_.gv[l, 2:3, :] = colsum(da.astype(F32))
            t_.gv[l, 3:4, :] = colsum(dh * n)
            t_.gv[l, 4:5, :] = colsum(dh)
            datt = mm_nt(da, t_.wo[...]).astype(BF)
            for i in range(3):
                t_.datt[i] = datt[:, 256 * i : 256 * i + 256]
        store_ff(l, j, True)

        @pl.when(j < 3)
        def _():
            load_ff(l, j + 1, True)

        @pl.when(j == 3)
        def _():
            load_att(l, 0, True)

    def store_ff(l, j, go):
        def one(i, src, dst):
            run(pltpu.make_async_copy(src, dst, m_.osem.at[i]), go)
        one(0, t_.dg, cols(g.dg.at[l], j, 768))
        one(1, t_.du, cols(g.du.at[l], j, 768))

        @pl.when(j == 0)
        def _():
            one(2, t_.dm, g.dm.at[l])

        @pl.when(j == 3)
        def _():
            one(3, t_.da, g.da.at[l])

    def att_task(l, i):
        load_att(l, i, False)
        scale = HEAD_DIM ** -0.5
        first = lax.broadcasted_iota(jnp.int32, (pad, 128), 1) < HEAD_DIM
        for sq in range(seqs):
            rows = slice(sq * pad, (sq + 1) * pad)
            for pair in range(2):
                lanes = slice(128 * pair, 128 * pair + 128)
                q2 = t_.q[rows, lanes]
                d2 = t_.datt[i, rows, lanes]
                vs = halves(t_.v[rows, lanes], 1)
                ks = halves(t_.k[rows, lanes].T, 0)
                dv, dk, dq = [], [], None
                for h in range(2):
                    pb = t_.pt[sq, 2 * pair + h]
                    p = pb.astype(F32)
                    dp = mm_nt(vs[h], d2)
                    ds = (p * (dp - jnp.sum(dp * p, axis=0, keepdims=True))).astype(BF)
                    dv.append(mm(pb, d2))
                    dk.append(mm(ds, q2))
                    part = mm(ks[h], ds)
                    dq = part if dq is None else dq + part
                t_.dv[rows, lanes] = jnp.where(first, dv[0], dv[1]).astype(BF)
                t_.dk[rows, lanes] = (jnp.where(first, dk[0], dk[1]) * scale).astype(BF)
                t_.dq[rows, lanes] = (dq * scale).astype(BF).T
        dq, dk, dv = t_.dq[...], t_.dk[...], t_.dv[...]
        at = pl.ds(pl.multiple_of(i * 256, 256), 256)
        t_.gv[l, 0:1, at] = colsum(dq.astype(F32))
        t_.gv[l, 1:2, at] = colsum(dv.astype(F32))
        t_.acc[...] += mm_nt(dq, t_.wq[...]) + mm_nt(dk, t_.wk[...]) + mm_nt(dv, t_.wv[...])
        store_att(l, i, True)

        @pl.when(i < 2)
        def _():
            load_att(l, i + 1, True)

        @pl.when(jnp.logical_and(i == 2, l > 0))
        def _():
            load_ff(jnp.maximum(l - 1, 0), 0, True)

        @pl.when(jnp.logical_and(i == 2, l == 0))
        def _():
            t_.cot[...] = t_.acc[...].astype(BF)
            pltpu.make_async_copy(t_.cot, o.dx, m_.osem.at[7]).start()

    def store_att(l, i, go):
        def one(n, src, dst):
            run(pltpu.make_async_copy(src, dst, m_.osem.at[n]), go)
        one(4, t_.dq, cols(g.dq.at[l], i, 256))
        one(5, t_.dk, cols(g.dk.at[l], i, 256))
        one(6, t_.dv, cols(g.dv.at[l], i, 256))

    def task(t, ff, att):
        l = LAYERS - 1 - t // 7
        u = lax.rem(t, 7)

        @pl.when(u < 4)
        def _():
            ff(l, jnp.minimum(u, 3))

        @pl.when(u >= 4)
        def _():
            att(l, jnp.clip(u - 4, 0, 2))


    def load(p, go):
        q = lax.rem(p, 16)
        n = lax.rem(p, 2)
        layer = LAYERS - 1 - p // 16

        def left(ref, sub=None):
            for cc in range(2):
                src = ref.at[:, cc] if sub is None else ref.at[:, cc, sub]
                run(pltpu.make_async_copy(src, s.lbuf.at[n, cc], m_.lsem.at[n, cc]), go)

        def right(ref, col=None):
            src = ref.at[layer] if col is None else cols(ref.at[layer], jnp.clip(col, 0, 3), 768)
            run(pltpu.make_async_copy(src, s.rbuf.at[n], m_.rsem.at[n]), go)
        if not go:
            left(kept[0].ht)
            right(g.dm)
            return
        for l in range(LAYERS):
            here = layer == l
            kl = kept[l]

            @pl.when(jnp.logical_and(here, q < 4))
            def _():
                left(kl.ft, jnp.minimum(q, 3))

            @pl.when(jnp.logical_and(here, jnp.logical_and(q >= 4, q < 12)))
            def _():
                left(kl.ht)

            @pl.when(jnp.logical_and(here, q == 12))
            def _():
                left(kl.at)

            @pl.when(jnp.logical_and(here, q > 12))
            def _():
                left(kl.xt)

        @pl.when(q < 4)
        def _():
            right(g.dm)

        @pl.when(jnp.logical_and(q >= 4, q < 8))
        def _():
            right(g.dg, q - 4)

        @pl.when(jnp.logical_and(q >= 8, q < 12))
        def _():
            right(g.du, q - 8)
        for i, d in enumerate((g.da, g.dq, g.dk, g.dv)):
            @pl.when(q == 12 + i)
            def _():
                right(d)

    def rcopy(p, e, src, dst, d):
        return pltpu.make_async_remote_copy(src_ref=src, dst_ref=dst, send_sem=m_.send.at[p, e], recv_sem=m_.recv.at[p, e], device_id=d, device_id_type=MESH)

    def product(n, cc, dst):
        for i in range(4):
            v = mm(s.lbuf[n, cc, 2 * i : 2 * i + 2].reshape(96, 512), s.rbuf[n]).astype(BF)
            v = v.reshape(2, 48, 768)
            dst[i, :, 0] = v[:, :, :384]
            dst[i, :, 1] = v[:, :, 384:]

    def c_copy(p, n):
        return rcopy(p, 0, s.sbuf.at[n], c_.r0.at[lax.rem(p, SLOTS)], d_c)

    def s0(p):
        n = lax.rem(p, 2)
        load(p, False)

        @pl.when(p >= 2)
        def _():
            c_copy(jnp.maximum(p - 2, 0), n).wait_send()
        product(n, 1 - c, s.sbuf.at[n])
        c_copy(p, n).start()
        product(n, c, s.own.at[lax.rem(p, LAG + 1)])

        @pl.when(p + 1 < NP)
        def _():
            load(jnp.minimum(p + 1, NP - 1), True)
    small = Group(("r0", "h1", "h2", "za", "zb", "yf"), (s.r0v, s.h1v, s.h2v, s.zav, s.zbv, s.yfv))
    zlo = jnp.where(z == 1, 1, 0)
    elo = jnp.where(z == 0, 1, 0)
    mlo = jnp.where(z == 1, 2, 0)
    rlo = jnp.where(z == 1, 0, 2)

    def steps(b, p, i, my):
        fx = piece_first_x(p)
        fy = jnp.logical_not(fx)

        def hop1(go):
            a = rcopy(p, 1, b.r0.at[i, :, 1 - x], b.h1.at[i], d_x)
            if go == "start":
                pl.when(fx)(a.start)
                pl.when(fy)(rcopy(p, 1, b.r0.at[i, :, :, 1 - y], b.h1.at[i], d_y).start)
            elif go == "recv":
                a.wait_recv()
            else:
                a.wait_send()

        def hop2(go):
            a = rcopy(p, 2, b.h1.at[i, :, 1 - y], b.h2.at[i], d_y)
            if go == "start":
                pl.when(fx)(a.start)
                pl.when(fy)(rcopy(p, 2, b.h1.at[i, :, 1 - x], b.h2.at[i], d_x).start)
            elif go == "recv":
                a.wait_recv()
            else:
                a.wait_send()

        def z1():
            return rcopy(p, 3, b.h2.at[i, pl.ds(elo, 3)], b.za.at[i], d_zp)

        def z2():
            return rcopy(p, 4, b.h2.at[i, pl.ds(mlo, 2)], b.zb.at[i], d_zm)

        def z3():
            return rcopy(p, 5, b.h2.at[i, zp], b.zb.at[i, 0], d_zp)

        def y1():
            return rcopy(p, 6, b.h2.at[i, z], b.yf.at[i], d_y)

        def s1():
            rcopy(p, 0, b.r0.at[i], b.r0.at[i], d_c).wait_recv()
            for k in range(4):
                add_into(b.r0.at[i, k], my.at[k])
            hop1("start")

        def s2():
            hop1("recv")
            for k in range(4):
                @pl.when(fx)
                def _():
                    add_into(b.h1.at[i, k], b.r0.at[i, k, x])

                @pl.when(fy)
                def _():
                    add_into(b.h1.at[i, k], b.r0.at[i, k, :, y])
            hop2("start")

        def s3():
            hop1("send")
            hop2("recv")
            t = jnp.where(fx, y, x)
            for k in range(4):
                add_into(b.h2.at[i, k], b.h1.at[i, k, t])
            pl.when(end)(z1().start)

        def s4():
            hop2("send")

            @pl.when(mid)
            def _():
                z1().wait_recv()
                for k in range(3):
                    add_into(b.h2.at[i, zlo + k], b.za.at[i, k])
                z2().start()

        def s5():
            pl.when(end)(z1().wait_send)

            @pl.when(mid)
            def _():
                z2().wait_recv()
                for k in range(2):
                    add_into(b.h2.at[i, rlo + k], b.zb.at[i, k])
                z3().start()

        def s6():
            pl.when(mid)(z2().wait_send)

            @pl.when(end)
            def _():
                z3().wait_recv()
                add_into(b.h2.at[i, z], b.zb.at[i, 0])
            y1().start()

        def s7():
            pl.when(mid)(z3().wait_send)
            y1().wait_send()
            y1().wait_recv()
        return s1, s2, s3, s4, s5, s6, s7

    def out_copy(p, n, go):
        q = lax.rem(p, 16)
        layer = LAYERS - 1 - p // 16

        def one(dst):
            run(pltpu.make_async_copy(s.stage.at[n], dst, m_.out.at[n]), go)
        if not go:
            one(o.out.at[0])
            return

        @pl.when(q < 4)
        def _():
            one(o.down.at[layer, pl.ds(pl.multiple_of(jnp.minimum(q, 3) * 48, 48), 48)])

        @pl.when(jnp.logical_and(q >= 4, q < 12))
        def _():
            one(cols(o.gated.at[layer], jnp.clip(q - 4, 0, 7), 768))

        @pl.when(q == 12)
        def _():
            one(o.out.at[layer])

        @pl.when(q > 12)
        def _():
            one(cols(o.qkv.at[layer], jnp.clip(q - 13, 0, 2), 768))

    def write(p):
        n = lax.rem(p, 2)

        @pl.when(p >= 2)
        def _():
            out_copy(p, n, False)
        i = lax.rem(p, SLOTS)
        a = c_.h2[i, z].astype(F32)
        b = c_.yf[i].astype(F32)

        @pl.when(y == 0)
        def _():
            s.stage[n, :, :384] = a
            s.stage[n, :, 384:] = b

        @pl.when(y == 1)
        def _():
            s.stage[n, :, :384] = b
            s.stage[n, :, 384:] = a
        out_copy(p, n, True)


    vp = NP
    vc = rcopy(vp, 0, s.vall.at[1 - c], s.r0v.at[0], d_c)
    vsteps = steps(small, vp, 0, s.vall.at[c])
    VSTART = 27

    def pack_vectors():
        for l in range(LAYERS):
            v = jnp.concatenate([t_.gv[l], jnp.zeros((120, D), F32)], axis=0).T.astype(BF)
            for k in range(16):
                s.vall[k % 2, k // 4, (k // 2) % 2, l] = v[48 * k : 48 * k + 48]
        vc.start()


    top = LAYERS - 1
    first = pltpu.make_async_copy(cot, t_.cot, m_.vload)
    first.start()
    load_ff(top, 0, True)
    first.wait()
    t_.acc[...] = t_.cot[...].astype(F32)
    ff_task(top, 0)
    store_ff(top, 0, False)
    load(0, True)

    def body(r, carry):
        def at(k, f):
            p = r - LAG * k

            @pl.when(jnp.logical_and(p >= 0, p < NP))
            def _():
                f(jnp.clip(p, 0, NP - 1))

        def st(k):
            def f(p):
                steps(c_, p, lax.rem(p, SLOTS), s.own.at[lax.rem(p, LAG + 1)])[k - 1]()
                if k == 7:
                    write(p)
            return f
        even = lax.rem(r, 2) == 0

        @pl.when(jnp.logical_and(even, jnp.logical_and(r >= 2, r < 28)))
        def _():
            task(jnp.clip(r // 2, 1, 13), lambda l, j: store_ff(l, j, False), lambda l, i: store_att(l, i, False))
        for k in range(1, 8):
            pl.when(r == VSTART + LAG * k)(vsteps[k - 1])
        at(0, s0)
        for k in range(7, 0, -1):
            at(k, st(k))
        pl.when(r == VSTART)(pack_vectors)

        @pl.when(jnp.logical_and(jnp.logical_not(even), r < 26))
        def _():
            task(jnp.clip((r + 1) // 2, 1, 13), ff_task, att_task)
        return carry
    lax.fori_loop(0, NP + 7 * LAG, body, 0)

    for p in (NP - 2, NP - 1):
        c_copy(p, p % 2).wait_send()
        out_copy(p, p % 2, False)
    vc.wait_send()
    pltpu.make_async_copy(t_.cot, o.dx, m_.osem.at[7]).wait()
    va, vb = s.h2v[0, z].astype(F32), s.yfv[0].astype(F32)
    o.vec[0] = jnp.where(y == 0, va, vb)
    o.vec[1] = jnp.where(y == 0, vb, va)


def backward_all(cot, vec, kept, mats):
    rows = cot.shape[0]
    hbm = pl.BlockSpec(memory_space=pltpu.HBM)
    vmem = pl.BlockSpec(memory_space=pltpu.VMEM)
    kept = [k[:8] + (k[8].reshape(8, 2, 4, 48, rows),) + tuple(a.reshape(8, 2, 48, rows) for a in k[9:]) for k in kept]
    act = lambda c, t: jax.ShapeDtypeStruct((rows, c), t)
    out = [
        jax.ShapeDtypeStruct((LAYERS, 48, 3 * D), F32), jax.ShapeDtypeStruct((LAYERS, 48, D), F32),
        jax.ShapeDtypeStruct((LAYERS, 48, 2 * FF), F32), jax.ShapeDtypeStruct((LAYERS, 192, D), F32),
        jax.ShapeDtypeStruct((2, 48, 128), F32), act(D, BF),
    ]
    both = lambda c: jax.ShapeDtypeStruct((LAYERS, rows, c), BF)
    scratch_out = [both(D), both(FF), both(FF), both(D), both(D), both(D), both(D)]
    seqs, _, pad, _ = kept[0][7].shape
    v = pltpu.VMEM
    dma = pltpu.SemaphoreType.DMA
    n = SLOTS
    scratch = [
        v((2, 2, 8, 48, rows), BF), v((2, rows, 768), BF), v((2, 4, 2, 2, 48, 384), BF), v((LAG + 1, 4, 2, 2, 48, 384), BF), v((2, 48, 768), F32),
        v((1, 4, 2, 2, 48, 128), BF), v((1, 4, 2, 48, 128), BF), v((1, 4, 48, 128), BF),
        v((1, 3, 48, 128), BF), v((1, 2, 48, 128), BF), v((1, 48, 128), BF), v((2, 4, 2, 2, 48, 128), BF),
        v((n, 4, 2, 2, 48, 384), BF), v((n, 4, 2, 48, 384), BF), v((n, 4, 48, 384), BF), v((n, 3, 48, 384), BF), v((n, 2, 48, 384), BF), v((n, 48, 384), BF),
        v((rows, D), F32), v((rows, D), F32), v((768, D), BF), v((D, 768), BF), v((D, 768), BF), v((rows, 768), BF), v((rows, 768), BF), v((D, D), BF),
        v((rows, D), BF), v((rows, 768), BF), v((rows, 768), BF), v((rows, D), BF), v((3, rows, 256), BF),
        v((rows, 256), BF), v((rows, 256), BF), v((rows, 256), BF), v((seqs, 4, pad, pad), BF), v((D, 256), BF), v((D, 256), BF), v((D, 256), BF),
        v((rows, 256), BF), v((rows, 256), BF), v((rows, 256), BF), v((LAYERS, 8, D), F32), v((rows, D), BF),
        dma((2, 2)), dma((2,)), dma((NPIECE, 7)), dma((NPIECE, 7)), dma((2,)), dma, dma((7,)), dma((7,)), dma((8,)),
    ]
    res = pl.pallas_call(
        backward_kernel, out_shape=out + scratch_out,
        in_specs=[hbm, vmem] + [hbm] * 28,
        out_specs=[hbm] * 4 + [vmem] + [hbm] * 8,
        scratch_shapes=scratch,
        compiler_params=pltpu.CompilerParams(collective_id=1, has_side_effects=True, vmem_limit_bytes=62 * 2**20), name="backward_reduce",
    )(cot, vec, *kept[0], *kept[1], *mats)
    return res[:4], res[4], res[5]


def fetch_all(shards, vectors, fast):
    vec = jnp.stack(vectors, axis=1)
    if not fast:
        full = [lax.all_gather(w, "fsdp", axis=1, tiled=True) for w in shards]
        return full, lax.all_gather(vec, "fsdp", axis=2, tiled=True).astype(F32)
    width = vec.shape[-1]
    full, packed = gather_all(shards, jnp.pad(vec, ((0, 0), (0, 0), (0, 128 - width))))
    packed = packed.reshape(-1, LAYERS, 8, 128)[..., :width]
    return full, packed.transpose(1, 2, 0, 3).reshape(LAYERS, 8, -1).astype(F32)


def backward_plain(dy, vec, kept, mats):
    wq, wo, wg, wd = mats

    def one(g, dim):
        part = lax.psum_scatter(g.astype(BF), "fsdp", scatter_dimension=dim, tiled=True)
        return lax.psum(part, "dp").astype(F32)
    sums, vecs = [None] * LAYERS, [None] * LAYERS
    for l in reversed(range(LAYERS)):
        r1, r2, ga, gb, q, k, v, pt, ft, ht, at, xt = kept[l]
        dm, dg, du, dr1, da, datt, gv = ff_backward(l, dy, r1, r2, ga, gb, wo, wg, wd, vec)
        dq, dk, dv, dy, gbias = attention_backward(l, datt, q, k, v, pt, wq, dr1, BF if l == 0 else F32)
        pairs = ((xt, jnp.concatenate([dq, dk, dv], axis=1)), (at, da), (ht, jnp.concatenate([dg, du], axis=1)), (ft, dm))
        sums[l] = [one(mm(a, b), 0) for a, b in pairs]
        vecs[l] = gv + gbias
    return [jnp.stack(m) for m in zip(*sums)], one(jnp.stack(vecs), 2), dy


def per_device(fast, inputs, lengths, cotangent, w_qkv, q_bias, v_bias, w_out, b_out, gain_one, shift_one, w_gated, w_down, b_down, gain_two, shift_two):
    mats, vec = fetch_all(
        (w_qkv, w_out, w_gated, w_down),
        (q_bias, v_bias, b_out, gain_one, shift_one, b_down, gain_two, shift_two),
        fast,
    )
    wq, wo, wg, wd = mats
    seq_lengths = lengths.reshape(-1)
    slopes = jnp.array(slopes_list(HEADS), F32)
    x = inputs.reshape(-1, D)
    kept = []
    for l in range(LAYERS):
        q, k, v, att, pt, xt, at = attention_forward(l, seq_lengths, slopes, x, wq, vec)
        out_dtype = BF if l == LAYERS - 1 else F32
        r1, r2, ga, gb, ft, ht, x = ff_forward(l, att, x, wo, wg, wd, vec, out_dtype)
        kept.append((r1, r2, ga, gb, q, k, v, pt, ft, ht, at, xt))
    dy = cotangent.reshape(-1, D)
    if fast:
        m, packed, dx = backward_all(dy, vec, kept, mats)
        vs = packed[:, :, :8].transpose(0, 2, 1)
    else:
        m, vs, dx = backward_plain(dy, vec, kept, mats)
    return (
        x.reshape(inputs.shape), dx.reshape(inputs.shape), m[0], vs[:, 0], vs[:, 1], m[1], vs[:, 2], vs[:, 3], vs[:, 4], m[2], m[3], vs[:, 5], vs[:, 6], vs[:, 7],
    )


def solution(mesh):
    placed = (
        P(None, ("dp", "fsdp"), None, None),
        P(None, ("dp", "fsdp")),
        P(None, ("dp", "fsdp"), None, None),
        P(None, "fsdp", None),
        P(None, "fsdp"),
        P(None, "fsdp"),
        P(None, "fsdp", None),
        P(None, "fsdp"),
        P(None, "fsdp"),
        P(None, "fsdp"),
        P(None, "fsdp", None),
        P(None, "fsdp", None),
        P(None, "fsdp"),
        P(None, "fsdp"),
        P(None, "fsdp"),
    )
    return jax.shard_map(
        functools.partial(per_device, dict(mesh.shape) == {"dp": 2, "fsdp": 16}),
        mesh=mesh,
        in_specs=placed,
        out_specs=(
            P(None, ("dp", "fsdp"), None, None),
            P(None, ("dp", "fsdp"), None, None),
            P(None, "fsdp", None),
            P(None, "fsdp"),
            P(None, "fsdp"),
            P(None, "fsdp", None),
            P(None, "fsdp"),
            P(None, "fsdp"),
            P(None, "fsdp"),
            P(None, "fsdp", None),
            P(None, "fsdp", None),
            P(None, "fsdp"),
            P(None, "fsdp"),
            P(None, "fsdp"),
        ),
        check_vma=False,
    )
```

```python
import functools
import math

import jax
import jax.numpy as jnp
from jax import lax
from jax.experimental import pallas as pl
from jax.experimental.pallas import tpu as pltpu
from jax.sharding import PartitionSpec as P

MESH = pl.DeviceIdType.MESH

BF = jnp.bfloat16
F32 = jnp.float32
D, HEADS, HEAD_DIM, FF, LAYERS = 768, 12, 64, 3072, 2
EPS = 1e-12
NEG = -1e30
NT = (((1,), (1,)), ((), ()))


def slopes_list(heads_count):
    nearest = 2 ** int(math.floor(math.log2(heads_count)))
    leading = [2.0 ** (-8.0 * (number + 1) / nearest) for number in range(nearest)]
    trailing = [2.0 ** (-8.0 * (number + 1) / (2 * nearest)) for number in range(2 * nearest)][0::2]
    return leading + trailing[: heads_count - nearest]


def mm(a, b):
    return jnp.dot(a, b, preferred_element_type=F32)


def mm_nt(a, b):
    return lax.dot_general(a, b, NT, preferred_element_type=F32)


def erf(x):
    return lax.erf(x)


def norm_parts(r):
    cent = r - jnp.mean(r, axis=-1, keepdims=True)
    rstd = lax.rsqrt(jnp.mean(cent * cent, axis=-1, keepdims=True) + EPS)
    return cent * rstd, rstd


def norm_back(dy, gain, n, rstd):
    dn = dy * gain
    return rstd * (dn - jnp.mean(dn, axis=-1, keepdims=True) - n * jnp.mean(dn * n, axis=-1, keepdims=True))


def halves(v, axis):
    first = lax.broadcasted_iota(jnp.int32, v.shape, axis) < HEAD_DIM
    zero = jnp.zeros_like(v)
    return jnp.where(first, v, zero), jnp.where(first, zero, v)


def attention_kernel(len_ref, slope_ref, x_ref, wq_ref, wk_ref, wv_ref, vec_ref, q_ref, k_ref, v_ref, att_ref, pt_ref, xt_ref, at_ref, xb_ref, dist_ref):
    i = pl.program_id(0)
    seqs, pad = pt_ref.shape[0], pt_ref.shape[-1]

    @pl.when(i == 0)
    def _():
        xb = x_ref[...].astype(BF)
        xb_ref[...] = xb
        xt_ref[...] = xb.T
        keys = lax.broadcasted_iota(jnp.int32, (pad, pad), 0)
        rows = lax.broadcasted_iota(jnp.int32, (pad, pad), 1)
        dist_ref[...] = jnp.abs(keys - rows).astype(F32)
    xb = xb_ref[...]
    q_ref[...] = (mm(xb, wq_ref[...]) + vec_ref[0:1, :]).astype(BF)
    k_ref[...] = mm(xb, wk_ref[...]).astype(BF)
    v_ref[...] = (mm(xb, wv_ref[...]) + vec_ref[1:2, :]).astype(BF)
    for s in range(seqs):
        rows = slice(s * pad, (s + 1) * pad)
        hidden = jnp.where(lax.broadcasted_iota(jnp.int32, (pad, 1), 0) < len_ref[s], 0.0, NEG)
        for pair in range(2):
            lanes = slice(128 * pair, 128 * pair + 128)
            q2 = q_ref[rows, lanes] * BF(HEAD_DIM ** -0.5)
            k0, k1 = halves(k_ref[rows, lanes], 1)
            v0, v1 = halves(v_ref[rows, lanes].T, 0)
            total = None
            for h, (kh, vh) in enumerate(((k0, v0), (k1, v1))):
                slope = slope_ref[4 * i + 2 * pair + h]
                sc = mm_nt(kh, q2) - slope * dist_ref[...] + hidden
                e = jnp.exp(sc - jnp.max(sc, axis=0, keepdims=True))
                p = (e * (1.0 / jnp.sum(e, axis=0, keepdims=True))).astype(BF)
                pt_ref[s, 2 * pair + h] = p
                part = mm(vh, p)
                total = part if total is None else total + part
            total = total.astype(BF)
            at_ref[lanes, rows] = total
            att_ref[rows, lanes] = total.T


def attention_forward(l, lengths, slopes, x, w_qkv, vec):
    rows = x.shape[0]
    seqs = lengths.shape[0]
    pad = rows // seqs
    col = lambda off: pl.BlockSpec((None, D, 256), lambda i: (l, 0, off + i))
    blk = pl.BlockSpec((rows, 256), lambda i: (0, i))
    smem = pl.BlockSpec(memory_space=pltpu.SMEM)
    act = jax.ShapeDtypeStruct((rows, D), BF)
    return pl.pallas_call(
        attention_kernel,
        grid=(3,),
        in_specs=[smem, smem, pl.BlockSpec((rows, D), lambda i: (0, 0)), col(0), col(3), col(6), pl.BlockSpec((None, 8, 256), lambda i: (l, 0, i))],
        out_specs=[blk, blk, blk, blk, pl.BlockSpec((seqs, 4, pad, pad), lambda i: (0, i, 0, 0)), pl.BlockSpec((D, rows), lambda i: (0, 0)), pl.BlockSpec((256, rows), lambda i: (i, 0))],
        out_shape=[act, act, act, act, jax.ShapeDtypeStruct((seqs, HEADS, pad, pad), BF), jax.ShapeDtypeStruct((D, rows), BF), jax.ShapeDtypeStruct((D, rows), BF)],
        scratch_shapes=[pltpu.VMEM((rows, D), BF), pltpu.VMEM((pad, pad), F32)],
        compiler_params=pltpu.CompilerParams(vmem_limit_bytes=56 * 2**20),
        name="attention_forward",
    )(lengths, slopes, x, w_qkv, w_qkv, w_qkv, vec)


def ff_kernel(att_ref, x_ref, wo_ref, wg_ref, wu_ref, wd_ref, vec_ref, r1_ref, r2_ref, ga_ref, gb_ref, ft_ref, ht_ref, out_ref, h_ref, hb_ref, acc_ref):
    j = pl.program_id(0)

    @pl.when(j == 0)
    def _():
        r1 = x_ref[...].astype(F32) + (mm(att_ref[...], wo_ref[...]) + vec_ref[2:3, :])
        r1_ref[...] = r1
        h = norm_parts(r1)[0] * vec_ref[3:4, :] + vec_ref[4:5, :]
        h_ref[...] = h
        hb = h.astype(BF)
        hb_ref[...] = hb
        ht_ref[...] = hb.T
        acc_ref[...] = jnp.zeros_like(acc_ref)
    hb = hb_ref[...]
    g = mm(hb, wg_ref[...])
    u = mm(hb, wu_ref[...])
    cdf = 0.5 + 0.5 * erf(g * math.sqrt(0.5))
    gelu = g * cdf
    slope = cdf + g * (jnp.exp(-0.5 * (g * g)) * (1.0 / math.sqrt(2.0 * math.pi)))
    ga_ref[...] = gelu.astype(BF)
    gb_ref[...] = (slope * u).astype(BF)
    f = (gelu * u).astype(BF)
    ft_ref[...] = f.T
    acc_ref[...] += mm(f, wd_ref[...])

    @pl.when(j == pl.num_programs(0) - 1)
    def _():
        r2 = h_ref[...] + (acc_ref[...] + vec_ref[5:6, :])
        r2_ref[...] = r2
        out_ref[...] = (norm_parts(r2)[0] * vec_ref[6:7, :] + vec_ref[7:8, :]).astype(out_ref.dtype)


def ff_forward(l, att, x, w_out, w_gated, w_down, vec, out_dtype):
    rows = x.shape[0]
    n = FF // 768
    whole = pl.BlockSpec((rows, D), lambda j: (0, 0))
    blk = pl.BlockSpec((rows, 768), lambda j: (0, j))
    return pl.pallas_call(
        ff_kernel,
        grid=(n,),
        in_specs=[whole, whole, pl.BlockSpec((None, D, D), lambda j: (l, 0, 0)),
                  pl.BlockSpec((None, D, 768), lambda j: (l, 0, j)), pl.BlockSpec((None, D, 768), lambda j: (l, 0, n + j)),
                  pl.BlockSpec((None, 768, D), lambda j: (l, j, 0)), pl.BlockSpec((None, 8, D), lambda j: (l, 0, 0))],
        out_specs=[whole, whole, blk, blk, pl.BlockSpec((768, rows), lambda j: (j, 0)), pl.BlockSpec((D, rows), lambda j: (0, 0)), whole],
        out_shape=[jax.ShapeDtypeStruct((rows, D), F32), jax.ShapeDtypeStruct((rows, D), F32),
                   jax.ShapeDtypeStruct((rows, FF), BF), jax.ShapeDtypeStruct((rows, FF), BF),
                   jax.ShapeDtypeStruct((FF, rows), BF), jax.ShapeDtypeStruct((D, rows), BF), jax.ShapeDtypeStruct((rows, D), out_dtype)],
        scratch_shapes=[pltpu.VMEM((rows, D), F32), pltpu.VMEM((rows, D), BF), pltpu.VMEM((rows, D), F32)],
        compiler_params=pltpu.CompilerParams(vmem_limit_bytes=56 * 2**20),
        name="ff_forward",
    )(att, x, w_out, w_gated, w_gated, w_down, vec)


def colsum(v):
    return jnp.sum(v, axis=0, keepdims=True)


def ff_back_kernel(dy_ref, r1_ref, r2_ref, ga_ref, gb_ref, wo_ref, wg_ref, wu_ref, wd_ref, vec_ref, dm_ref, dg_ref, du_ref, dr1_ref, da_ref, datt_ref, gv_ref, acc_ref):
    j = pl.program_id(0)

    @pl.when(j == 0)
    def _():
        dy = dy_ref[...].astype(F32)
        n, rstd = norm_parts(r2_ref[...])
        dr2 = norm_back(dy, vec_ref[6:7, :], n, rstd)
        acc_ref[...] = dr2
        dm = dr2.astype(BF)
        dm_ref[...] = dm
        gv_ref[5:6, :] = colsum(dm.astype(F32))
        gv_ref[6:7, :] = colsum(dy * n)
        gv_ref[7:8, :] = colsum(dy)
        gv_ref[0:2, :] = jnp.zeros((2, D), F32)
    df = mm_nt(dm_ref[...], wd_ref[...])
    dg = (df * gb_ref[...].astype(F32)).astype(BF)
    du = (df * ga_ref[...].astype(F32)).astype(BF)
    dg_ref[...] = dg
    du_ref[...] = du
    acc_ref[...] += mm_nt(dg, wg_ref[...]) + mm_nt(du, wu_ref[...])

    @pl.when(j == pl.num_programs(0) - 1)
    def _():
        dh = acc_ref[...]
        n, rstd = norm_parts(r1_ref[...])
        dr1 = norm_back(dh, vec_ref[3:4, :], n, rstd)
        dr1_ref[...] = dr1
        da = dr1.astype(BF)
        da_ref[...] = da
        gv_ref[2:3, :] = colsum(da.astype(F32))
        gv_ref[3:4, :] = colsum(dh * n)
        gv_ref[4:5, :] = colsum(dh)
        datt_ref[...] = mm_nt(da, wo_ref[...]).astype(BF)


def ff_backward(l, dy, r1, r2, ga, gb, w_out, w_gated, w_down, vec):
    rows = dy.shape[0]
    n = FF // 768
    whole = pl.BlockSpec((rows, D), lambda j: (0, 0))
    blk = pl.BlockSpec((rows, 768), lambda j: (0, j))
    act = lambda c, t: jax.ShapeDtypeStruct((rows, c), t)
    return pl.pallas_call(
        ff_back_kernel,
        grid=(n,),
        in_specs=[whole, whole, whole, blk, blk, pl.BlockSpec((None, D, D), lambda j: (l, 0, 0)),
                  pl.BlockSpec((None, D, 768), lambda j: (l, 0, j)), pl.BlockSpec((None, D, 768), lambda j: (l, 0, n + j)),
                  pl.BlockSpec((None, 768, D), lambda j: (l, j, 0)), pl.BlockSpec((None, 8, D), lambda j: (l, 0, 0))],
        out_specs=[whole, blk, blk, whole, whole, whole, pl.BlockSpec((8, D), lambda j: (0, 0))],
        out_shape=[act(D, BF), act(FF, BF), act(FF, BF), act(D, F32), act(D, BF), act(D, BF), jax.ShapeDtypeStruct((8, D), F32)],
        scratch_shapes=[pltpu.VMEM((rows, D), F32)],
        compiler_params=pltpu.CompilerParams(vmem_limit_bytes=56 * 2**20),
        name="ff_backward",
    )(dy, r1, r2, ga, gb, w_out, w_gated, w_gated, w_down, vec)


def attention_back_kernel(datt_ref, q_ref, k_ref, v_ref, pt_ref, wq_ref, wk_ref, wv_ref, dr1_ref, dq_ref, dk_ref, dv_ref, dx_ref, gb_ref, acc_ref):
    i = pl.program_id(0)
    seqs, pad = pt_ref.shape[0], pt_ref.shape[-1]
    scale = HEAD_DIM ** -0.5

    @pl.when(i == 0)
    def _():
        acc_ref[...] = dr1_ref[...]
    first = lax.broadcasted_iota(jnp.int32, (pad, 128), 1) < HEAD_DIM
    for s in range(seqs):
        rows = slice(s * pad, (s + 1) * pad)
        for pair in range(2):
            lanes = slice(128 * pair, 128 * pair + 128)
            q2 = q_ref[rows, lanes]
            d2 = datt_ref[rows, lanes]
            vs = halves(v_ref[rows, lanes], 1)
            ks = halves(k_ref[rows, lanes].T, 0)
            dv, dk, dq = [], [], None
            for h in range(2):
                pb = pt_ref[s, 2 * pair + h]
                p = pb.astype(F32)
                dp = mm_nt(vs[h], d2)
                ds = (p * (dp - jnp.sum(dp * p, axis=0, keepdims=True))).astype(BF)
                dv.append(mm(pb, d2))
                dk.append(mm(ds, q2))
                part = mm(ks[h], ds)
                dq = part if dq is None else dq + part
            dv_ref[rows, lanes] = jnp.where(first, dv[0], dv[1]).astype(BF)
            dk_ref[rows, lanes] = (jnp.where(first, dk[0], dk[1]) * scale).astype(BF)
            dq_ref[rows, lanes] = (dq * scale).astype(BF).T
    dq, dk, dv = dq_ref[...], dk_ref[...], dv_ref[...]
    gb_ref[0:1, :] = colsum(dq.astype(F32))
    gb_ref[1:2, :] = colsum(dv.astype(F32))
    gb_ref[2:8, :] = jnp.zeros((6, 256), F32)
    acc_ref[...] += mm_nt(dq, wq_ref[...]) + mm_nt(dk, wk_ref[...]) + mm_nt(dv, wv_ref[...])

    @pl.when(i == pl.num_programs(0) - 1)
    def _():
        dx_ref[...] = acc_ref[...].astype(dx_ref.dtype)


def attention_backward(l, datt, q, k, v, pt, w_qkv, dr1, out_dtype):
    rows = datt.shape[0]
    seqs, _, pad, _ = pt.shape
    col = lambda off: pl.BlockSpec((None, D, 256), lambda i: (l, 0, off + i))
    blk = pl.BlockSpec((rows, 256), lambda i: (0, i))
    whole = pl.BlockSpec((rows, D), lambda i: (0, 0))
    act = jax.ShapeDtypeStruct((rows, D), BF)
    return pl.pallas_call(
        attention_back_kernel,
        grid=(3,),
        in_specs=[blk, blk, blk, blk, pl.BlockSpec((seqs, 4, pad, pad), lambda i: (0, i, 0, 0)), col(0), col(3), col(6), whole],
        out_specs=[blk, blk, blk, whole, pl.BlockSpec((8, 256), lambda i: (0, i))],
        out_shape=[act, act, act, jax.ShapeDtypeStruct((rows, D), out_dtype), jax.ShapeDtypeStruct((8, D), F32)],
        scratch_shapes=[pltpu.VMEM((rows, D), F32)],
        compiler_params=pltpu.CompilerParams(vmem_limit_bytes=56 * 2**20),
        name="attention_backward",
    )(datt, q, k, v, pt, w_qkv, w_qkv, w_qkv, dr1)


def place():
    y = lax.axis_index("dp"); f = lax.axis_index("fsdp")
    z = f // 4; x = lax.rem(f // 2, 2); c = lax.rem(f, 2)
    return z, x, y, c

def dev(z, x, y, c):
    return (y, (z * 2 + x) * 2 + c)

PIECES = 8 * LAYERS
GLAG = 1
KEPT = ("r1", "r2", "ga", "gb", "q", "k", "v", "pt", "ft", "ht", "at", "xt")


class Group:
    def __init__(self, names, refs):
        for name, ref in zip(names, refs):
            setattr(self, name, ref)


def taker(refs):
    refs = list(refs)

    def take(*names):
        g = Group(names, refs[: len(names)])
        del refs[: len(names)]
        return g
    return take


def run(cp, go):
    if go:
        cp.start()
    else:
        cp.wait()


def cols(ref, j, width):
    return ref.at[:, pl.ds(pl.multiple_of(j * width, width), width)]


def matrix_loads(w, p, k, dst, sem):
    return [pltpu.make_async_copy(w.at[p, :, :, :, h, k], dst.at[:, :, :, :, pl.ds(384 * h, 384)], sem) for h in range(2)]


def wait_all(dst, sem):
    pltpu.make_async_copy(dst, dst, sem).wait()


def forward_kernel(*refs):
    take = taker(refs)
    i_ = take("lens", "slopes", "x", "qkv", "out", "gated", "down", *["v%d" % i for i in range(8)])
    o_ = take("w", "v", "vec", "last")
    kept = [take(*KEPT) for _ in range(LAYERS)]
    t_ = take("x", "xb", "dist", "q", "k", "v", "att", "pt", "at", "xt", "wq", "wk", "wv", "wo", "wg", "wu", "wd", "h", "hb", "f", "ga", "gb", "ft", "res", "last", "vown", "vwide", "vec_in")
    m_ = take("local", "zsend", "fsend", "xysend", "rsend", "csend", "recv", "crecv", "vlocal", "vload", "load", "wload", "store")
    pad = t_.pt.shape[-1]
    seqs = t_.pt.shape[0]

    z, x, y, c = place()
    zp = z + 1 - 2 * lax.rem(z, 2)
    zm = 3 - z
    zf = lax.rem(z + 2, 4)
    mid = jnp.logical_and(z >= 1, z <= 2)
    end = jnp.logical_not(mid)
    d_zp, d_zm = dev(zp, x, y, c), dev(zm, x, y, c)
    d_x, d_y, d_c = dev(z, 1 - x, y, c), dev(z, x, 1 - y, c), dev(z, x, y, 1 - c)
    bar = pltpu.get_barrier_semaphore()
    for d in (d_zp, d_zm, d_x, d_y, d_c):
        pl.semaphore_signal(bar, 1, device_id=d, device_id_type=MESH)


    def local(p):
        u = lax.rem(p, 8)
        l = p // 8

        def put(h, k, src):
            pltpu.make_async_copy(src, o_.w.at[p, z, x, c, h, k], m_.local.at[p]).start()

        def part(ref, off):
            return ref.at[l, :, pl.ds(pl.multiple_of(off, 128), 384)]
        for h in range(2):
            @pl.when(u == 0)
            def _():
                put(h, 0, part(i_.qkv, 384 * h))
                put(h, 1, part(i_.qkv, 768 + 384 * h))

            @pl.when(u == 1)
            def _():
                put(h, 0, part(i_.qkv, 1536 + 384 * h))
                put(h, 1, part(i_.out, 384 * h))

            @pl.when(jnp.logical_and(u >= 2, u < 6))
            def _():
                j = jnp.clip(u - 2, 0, 3) * 768
                put(h, 0, part(i_.gated, j + 384 * h))
                put(h, 1, part(i_.gated, j + FF + 384 * h))

            @pl.when(u >= 6)
            def _():
                for k in range(2):
                    r = pl.multiple_of(jnp.clip(2 * (u - 6) + k, 0, 3) * 48, 48)
                    put(h, k, i_.down.at[l, pl.ds(r, 48), pl.ds(384 * h, 384)])

    def locals_from(p, carry):
        local(p)
        return carry
    local(0)
    t_.vwide[...] = jnp.zeros_like(t_.vwide)
    for n in range(8):
        row = getattr(i_, "v%d" % n)[...].astype(F32)
        for l in range(LAYERS):
            t_.vwide[l, n : n + 1, 0:48] = row[l : l + 1, :]
    t_.vown[...] = t_.vwide[...].astype(BF)
    vplace = pltpu.make_async_copy(t_.vown, o_.v.at[z, x, c], m_.vlocal.at[0])
    vplace.start()
    xload = pltpu.make_async_copy(i_.x, t_.last, m_.vlocal.at[1])
    xload.start()
    lax.fori_loop(1, PIECES, locals_from, 0)
    pl.semaphore_wait(bar, 5)


    def stages(b, s):
        def copy(zz, xx, hh, sem, d):
            u = b(zz, xx, c, hh)
            return pltpu.make_async_remote_copy(src_ref=u, dst_ref=u, send_sem=sem.at[s], recv_sem=m_.recv.at[s, (zz * 2 + xx) * 2 + hh], device_id=d, device_id_type=MESH)

        def zsend(zz, d, sem=m_.fsend):
            copy(zz, x, y, sem, d).start()

        def got(zz, xx, hh, d):
            copy(zz, xx, hh, m_.zsend, d).wait_recv()

        def plane(zz, cc=c):
            u = b(zz, slice(None), cc, slice(None))
            return pltpu.make_async_remote_copy(src_ref=u, dst_ref=u, send_sem=m_.csend.at[s], recv_sem=m_.crecv.at[s, zz], device_id=d_c, device_id_type=MESH)

        def spread(zz):
            copy(zz, x, y, m_.xysend, d_x).start()
            copy(zz, x, y, m_.xysend, d_y).start()

        def relay(zz, first_x):
            got(zz, 1 - x, y, d_x)
            got(zz, x, 1 - y, d_y)

            def through_y():
                copy(zz, 1 - x, y, m_.rsend, d_y).start()

            def through_x():
                copy(zz, x, 1 - y, m_.rsend, d_x).start()
            if first_x is True:
                through_y()
            elif first_x is False:
                through_x()
            else:
                pl.when(first_x)(through_y)
                pl.when(jnp.logical_not(first_x))(through_x)

        def diagonal(zz):
            got(zz, 1 - x, 1 - y, d_y)
            plane(zz).start()

        def st0():
            zsend(z, d_zp, m_.zsend)
            pl.when(mid)(lambda: zsend(z, d_zm, m_.zsend))
            copy(z, x, y, m_.xysend, d_x).start()

        def st1():
            got(zp, x, y, d_zp)

            @pl.when(mid)
            def _():
                zsend(zp, d_zm)
                got(zm, x, y, d_zm)
                zsend(zm, d_zp)
            spread(zp)
            got(z, 1 - x, y, d_x)
            copy(z, 1 - x, y, m_.xysend, d_y).start()

        def st2():
            got(zf, x, y, d_zp)
            pl.when(mid)(lambda: zsend(zf, d_zp))
            spread(zf)
            relay(zp, True)
            diagonal(z)

        def st3():
            pl.when(end)(lambda: got(zm, x, y, d_zp))
            spread(zm)
            relay(zf, False)
            diagonal(zp)

        def st4():
            relay(zm, lax.rem(s, 2) == 0)
            diagonal(zf)

        def st5():
            diagonal(zm)

        def st6():
            for zz in (z, zp, zf, zm):
                plane(zz, 1 - c).wait_recv()
        return st0, st1, st2, st3, st4, st5, st6

    def sent(b, s, many):
        wait_all(many(8), m_.xysend.at[s])
        wait_all(many(3), m_.rsend.at[s])
        wait_all(many(16), m_.csend.at[s])
        pl.when(end)(lambda: wait_all(many(1), m_.zsend.at[s]))

        @pl.when(mid)
        def _():
            wait_all(many(2), m_.zsend.at[s])
            wait_all(many(3), m_.fsend.at[s])

    def unit(p):
        return lambda zz, xx, cc, hh: o_.w.at[p, zz, xx, cc, hh]

    def vunit(zz, xx, cc, hh):
        return o_.v.at[zz, xx, cc, hh]

    def many_w(n):
        if n == 8:
            return o_.w.at[0, 0]
        if n == 16:
            return o_.w.at[0, :, :, 0]
        return o_.w.at[0:n, 0, 0, 0, 0]

    def many_v(n):
        if n == 8:
            return o_.v.at[0]
        if n == 16:
            return o_.v.at[:, :, 0]
        return o_.v.at[0:n, 0, 0, 0]


    def load_att(l):
        for cp in matrix_loads(o_.w, 8 * l, 0, t_.wq, m_.wload.at[0]) + matrix_loads(o_.w, 8 * l, 1, t_.wk, m_.wload.at[1]) + matrix_loads(o_.w, 8 * l + 1, 0, t_.wv, m_.wload.at[2]) + matrix_loads(o_.w, 8 * l + 1, 1, t_.wo, m_.wload.at[3]):
            cp.start()

    def load_gated(l, j):
        for cp in matrix_loads(o_.w, 8 * l + 2 + j, 0, t_.wg, m_.wload.at[4]) + matrix_loads(o_.w, 8 * l + 2 + j, 1, t_.wu, m_.wload.at[5]):
            cp.start()

    def load_down(l):
        for s in range(4):
            for h in range(2):
                pltpu.make_async_copy(o_.w.at[8 * l + 6 + s // 2, :, :, :, h, s % 2], t_.wd.at[:, :, :, s, :, pl.ds(384 * h, 384)], m_.wload.at[6]).start()

    def store(i, src, dst, go):
        run(pltpu.make_async_copy(src, dst, m_.store.at[i]), go)

    def per_layer(l, f):
        for n in range(LAYERS):
            @pl.when(l == n)
            def _():
                f(kept[n])

    def vrow(l, n):
        return o_.vec[l, n : n + 1, :]

    def store_att(kl, i, go):
        store(0, t_.q, cols(kl.q, i, 256), go)
        store(1, t_.k, cols(kl.k, i, 256), go)
        store(2, t_.v, cols(kl.v, i, 256), go)
        store(3, t_.pt, kl.pt.at[:, pl.ds(4 * i, 4)], go)
        store(4, t_.at, kl.at.at[pl.ds(pl.multiple_of(256 * i, 256), 256)], go)

        @pl.when(i == 0)
        def _():
            store(5, t_.xt, kl.xt, go)

    def att_task(l, i):
        @pl.when(i == 0)
        def _():
            wait_all(t_.wq, m_.wload.at[0])
            wait_all(t_.wk, m_.wload.at[1])
            wait_all(t_.wv, m_.wload.at[2])
            xb = t_.x[...].astype(BF)
            t_.xb[...] = xb
            t_.xt[...] = xb.T
        xb = t_.xb[...]
        lane = pl.multiple_of(256 * i, 256)
        at = pl.ds(lane, 256)
        t_.q[...] = (mm(xb, t_.wq[:, :, :, :, at].reshape(D, 256)) + o_.vec[l, 0:1, at]).astype(BF)
        t_.k[...] = mm(xb, t_.wk[:, :, :, :, at].reshape(D, 256)).astype(BF)
        t_.v[...] = (mm(xb, t_.wv[:, :, :, :, at].reshape(D, 256)) + o_.vec[l, 1:2, at]).astype(BF)
        for s in range(seqs):
            rows = slice(s * pad, (s + 1) * pad)
            hidden = jnp.where(lax.broadcasted_iota(jnp.int32, (pad, 1), 0) < i_.lens[s], 0.0, NEG)
            for pair in range(2):
                lanes = slice(128 * pair, 128 * pair + 128)
                q2 = t_.q[rows, lanes] * BF(HEAD_DIM ** -0.5)
                ks = halves(t_.k[rows, lanes], 1)
                vs = halves(t_.v[rows, lanes].T, 0)
                total = None
                for h in range(2):
                    slope = i_.slopes[4 * i + 2 * pair + h]
                    sc = mm_nt(ks[h], q2) - slope * t_.dist[...] + hidden
                    e = jnp.exp(sc - jnp.max(sc, axis=0, keepdims=True))
                    p = (e * (1.0 / jnp.sum(e, axis=0, keepdims=True))).astype(BF)
                    t_.pt[s, 2 * pair + h] = p
                    part = mm(vs[h], p)
                    total = part if total is None else total + part
                total = total.astype(BF)
                t_.at[lanes, rows] = total
                t_.att[rows, pl.ds(pl.multiple_of(lane + 128 * pair, 128), 128)] = total.T
        per_layer(l, lambda kl: store_att(kl, i, True))

    def store_ff(kl, j, go):
        store(6, t_.ga, cols(kl.ga, j, 768), go)
        store(7, t_.gb, cols(kl.gb, j, 768), go)
        store(8, t_.ft, kl.ft.at[pl.ds(pl.multiple_of(768 * j, 768), 768)], go)

        @pl.when(j == 0)
        def _():
            store(9, t_.res, kl.r1, go)
            store(10, t_.xt, kl.ht, go)

    def ff_task(l, j):
        @pl.when(j == 0)
        def _():
            wait_all(t_.wo, m_.wload.at[3])
            r1 = t_.x[...] + (mm(t_.att[...], t_.wo[...].reshape(D, D)) + vrow(l, 2))
            t_.res[...] = r1
            h = norm_parts(r1)[0] * vrow(l, 3) + vrow(l, 4)
            t_.h[...] = h
            hb = h.astype(BF)
            t_.hb[...] = hb
            t_.xt[...] = hb.T
        wait_all(t_.wg, m_.wload.at[4])
        wait_all(t_.wu, m_.wload.at[5])
        hb = t_.hb[...]
        g = mm(hb, t_.wg[...].reshape(D, 768))
        u = mm(hb, t_.wu[...].reshape(D, 768))
        cdf = 0.5 + 0.5 * erf(g * math.sqrt(0.5))
        gelu = g * cdf
        slope = cdf + g * (jnp.exp(-0.5 * (g * g)) * (1.0 / math.sqrt(2.0 * math.pi)))
        t_.ga[...] = gelu.astype(BF)
        t_.gb[...] = (slope * u).astype(BF)
        f = (gelu * u).astype(BF)
        t_.f[j] = f
        t_.ft[...] = f.T
        per_layer(l, lambda kl: store_ff(kl, j, True))

    def down_task(l):
        wait_all(t_.wd, m_.wload.at[6])
        total = t_.h[...] + vrow(l, 5)
        for j in range(4):
            total = total + mm(t_.f[j], t_.wd[j].reshape(768, D))
        t_.res[...] = total
        out = norm_parts(total)[0] * vrow(l, 6) + vrow(l, 7)
        t_.x[...] = out
        per_layer(l, lambda kl: store(9, t_.res, kl.r2, True))

        @pl.when(l == LAYERS - 1)
        def _():
            t_.last[...] = out.astype(BF)
            store(11, t_.last, o_.last, True)

    def task(t, att, ff, down):
        l = t // 8
        u = lax.rem(t, 8)
        pl.when(u < 3)(lambda: att(l, jnp.minimum(u, 2)))
        pl.when(jnp.logical_and(u >= 3, u < 7))(lambda: ff(l, jnp.clip(u - 3, 0, 3)))
        pl.when(u == 7)(lambda: down(l))

    def stored(t):
        task(t, lambda l, i: store_att(kept[0], i, False), lambda l, j: store_ff(kept[0], j, False), lambda l: store(9, t_.res, kept[0].r2, False))

    def fetch(t):
        def att(l, i):
            pl.when(i == 0)(lambda: load_att(l))
        task(t, att, load_gated, load_down)


    first_task = 7 * GLAG + 1
    last_round = first_task + 8 * LAYERS
    vst = stages(vunit, PIECES)

    def body(r, carry):
        def at(k):
            p = r - GLAG * k

            @pl.when(jnp.logical_and(p >= 0, p < PIECES))
            def _():
                q = jnp.clip(p, 0, PIECES - 1)
                if k == 0:
                    wait_all(o_.w.at[q, z, x, c], m_.local.at[q])
                stages(unit(q), q)[k]()
        for k in range(7):
            @pl.when(r == GLAG * k)
            def _():
                if k == 0:
                    vplace.wait()
                vst[k]()
        for k in (0, 6, 5, 4, 3, 2, 1):
            at(k)

        @pl.when(r == first_task - 1)
        def _():
            cp = pltpu.make_async_copy(o_.v, t_.vec_in, m_.vload)
            cp.start()
            xload.wait()
            t_.x[...] = t_.last[...].astype(F32)
            keys = lax.broadcasted_iota(jnp.int32, (pad, pad), 0)
            rows = lax.broadcasted_iota(jnp.int32, (pad, pad), 1)
            t_.dist[...] = jnp.abs(keys - rows).astype(F32)
            cp.wait()
            unpack_vectors()
        t = r - first_task

        @pl.when(t >= 1)
        def _():
            stored(jnp.clip(t - 1, 0, 8 * LAYERS - 1))

        @pl.when(t >= 0)
        def _():
            task(jnp.clip(t, 0, 8 * LAYERS - 1), att_task, ff_task, down_task)

        @pl.when(jnp.logical_and(t >= -1, t + 1 < 8 * LAYERS))
        def _():
            fetch(jnp.clip(t + 1, 0, 8 * LAYERS - 1))
        return carry

    def unpack_vectors():
        for l in range(LAYERS):
            parts = [t_.vec_in[b // 4, (b // 2) % 2, b % 2, l].astype(F32)[:, 0:48] for b in range(16)]
            o_.vec[l] = jnp.concatenate(parts, axis=1)
    lax.fori_loop(0, last_round, body, 0)
    stored(8 * LAYERS - 1)
    store(11, t_.last, o_.last, False)

    def finish(p, carry):
        sent(unit(p), p, many_w)
        return carry
    lax.fori_loop(0, PIECES, finish, 0)
    sent(vunit, PIECES, many_v)


def forward_all(lengths, slopes, x, shards, vectors):
    rows = x.shape[0]
    seqs = lengths.shape[0]
    pad = rows // seqs
    hbm = pl.BlockSpec(memory_space=pltpu.HBM)
    vmem = pl.BlockSpec(memory_space=pltpu.VMEM)
    smem = pl.BlockSpec(memory_space=pltpu.SMEM)
    S = jax.ShapeDtypeStruct
    act = lambda n, t: S((rows, n), t)
    one = [act(D, F32), act(D, F32), act(FF, BF), act(FF, BF), act(D, BF), act(D, BF), act(D, BF), S((seqs, HEADS, pad, pad), BF), S((FF, rows), BF), S((D, rows), BF), S((D, rows), BF), S((D, rows), BF)]
    out = [S((PIECES, 4, 2, 2, 2, 2, 48, 384), BF), S((4, 2, 2, 2, 8, 128), BF), S((LAYERS, 8, D), F32), act(D, BF)] + one * LAYERS
    v = pltpu.VMEM
    dma = pltpu.SemaphoreType.DMA
    mat = v((4, 2, 2, 48, D), BF)
    n = PIECES + 1
    scratch = [
        v((rows, D), F32), v((rows, D), BF), v((pad, pad), F32), v((rows, 256), BF), v((rows, 256), BF), v((rows, 256), BF), v((rows, D), BF),
        v((seqs, 4, pad, pad), BF), v((256, rows), BF), v((D, rows), BF), mat, mat, mat, mat, mat, mat, v((4, 2, 2, 4, 48, D), BF),
        v((rows, D), F32), v((rows, D), BF), v((4, rows, 768), BF), v((rows, 768), BF), v((rows, 768), BF), v((768, rows), BF), v((rows, D), F32), v((rows, D), BF),
        v((2, 8, 128), BF), v((2, 8, 128), F32), v((4, 2, 2, 2, 8, 128), BF),
        dma((PIECES,)), dma((n,)), dma((n,)), dma((n,)), dma((n,)), dma((n,)), dma((n, 16)), dma((n, 4)), dma((2,)), dma, dma, dma((7,)), dma((12,)),
    ]
    res = pl.pallas_call(
        forward_kernel, out_shape=out,
        in_specs=[smem, smem, hbm] + [hbm] * 4 + [vmem] * 8,
        out_specs=[hbm, hbm, vmem, hbm] + [hbm] * (12 * LAYERS),
        scratch_shapes=scratch,
        compiler_params=pltpu.CompilerParams(collective_id=0, has_side_effects=True, vmem_limit_bytes=60 * 2**20), name="gather_forward",
    )(lengths, slopes, x, *shards, *vectors)
    return res[0], res[2], res[3], [res[4 + 12 * l : 16 + 12 * l] for l in range(LAYERS)]


NPIECE = 33
LAG = 2
SLOTS = 16


def piece_first_x(p):
    return lax.rem(p * 5, 8) < 5


def add_into(dst, src):
    dst[...] = (dst[...].astype(F32) + src[...].astype(F32)).astype(BF)


GRADS = ("dm", "dg", "du", "da", "dq", "dk", "dv")


def backward_kernel(*refs):
    take = taker(refs)
    i_ = take("cot", "vec")
    cot, vec = i_.cot, i_.vec
    kept = [take(*KEPT) for _ in range(LAYERS)]
    w = take("w").w
    o = take("qkv", "out", "gated", "down", "vec", "dx")
    g = take(*GRADS)
    s = take("lbuf", "rbuf", "sbuf", "own", "stage", "r0v", "h1v", "h2v", "zav", "zbv", "yfv", "vall")
    c_ = take("r0", "h1", "h2", "za", "zb", "yf")
    t_ = take("acc", "res", "wd", "wg", "wu", "ga", "gb", "wo", "dm", "dg", "du", "da", "datt", "q", "k", "v", "pt", "wq", "wk", "wv", "dq", "dk", "dv", "gv", "cot")
    m_ = take("lsem", "rsem", "send", "recv", "out", "vload", "fsem", "asem", "osem")
    pad = kept[0].pt.shape[-1]
    seqs = kept[0].pt.shape[0]

    z, x, y, c = place()
    zp = z + 1 - 2 * lax.rem(z, 2)
    zm = 3 - z
    mid = jnp.logical_and(z >= 1, z <= 2)
    end = jnp.logical_not(mid)
    d_zp, d_zm = dev(zp, x, y, c), dev(zm, x, y, c)
    d_x, d_y, d_c = dev(z, 1 - x, y, c), dev(z, x, 1 - y, c), dev(z, x, y, 1 - c)
    bar = pltpu.get_barrier_semaphore()
    for d in (d_zp, d_zm, d_x, d_y, d_c):
        pl.semaphore_signal(bar, 1, device_id=d, device_id_type=MESH)
    pl.semaphore_wait(bar, 5)
    NP = NPIECE - 1


    def load_ff(l, j, go):
        def one(i, src, dst):
            run(pltpu.make_async_copy(src, dst, m_.fsem.at[i]), go)
        if go:
            for n in range(4):
                for h in range(2):
                    one(0, w.at[8 * l + 6 + n // 2, j, :, :, h, n % 2], t_.wd.at[:, :, n, :, pl.ds(384 * h, 384)])
            for cp in matrix_loads(w, 8 * l + 2 + j, 0, t_.wg, m_.fsem.at[1]) + matrix_loads(w, 8 * l + 2 + j, 1, t_.wu, m_.fsem.at[2]):
                cp.start()
        else:
            wait_all(t_.wd, m_.fsem.at[0])
            wait_all(t_.wg, m_.fsem.at[1])
            wait_all(t_.wu, m_.fsem.at[2])

        def acts(kl):
            one(3, cols(kl.ga, j, 768), t_.ga)
            one(4, cols(kl.gb, j, 768), t_.gb)

            @pl.when(j == 0)
            def _():
                one(5, kl.r2, t_.res)

            @pl.when(j == 3)
            def _():
                one(5, kl.r1, t_.res)
        if go:
            for i in range(LAYERS):
                @pl.when(l == i)
                def _():
                    acts(kept[i])
        else:
            one(3, cols(kept[0].ga, j, 768), t_.ga)
            one(4, cols(kept[0].gb, j, 768), t_.gb)

            @pl.when(jnp.logical_or(j == 0, j == 3))
            def _():
                one(5, kept[0].r1, t_.res)

        @pl.when(j == 3)
        def _():
            if go:
                for cp in matrix_loads(w, 8 * l + 1, 1, t_.wo, m_.fsem.at[6]):
                    cp.start()
            else:
                wait_all(t_.wo, m_.fsem.at[6])

    def load_att(l, i, go):
        def one(n, src, dst):
            run(pltpu.make_async_copy(src, dst, m_.asem.at[n]), go)

        def acts(kl):
            one(0, cols(kl.q, i, 256), t_.q)
            one(1, cols(kl.k, i, 256), t_.k)
            one(2, cols(kl.v, i, 256), t_.v)
            one(3, kl.pt.at[:, pl.ds(4 * i, 4)], t_.pt)
        if go:
            for n in range(LAYERS):
                @pl.when(l == n)
                def _():
                    acts(kept[n])
        else:
            acts(kept[0])
        @pl.when(i == 0)
        def _():
            for n, dst in enumerate((t_.wq, t_.wk, t_.wv)):
                if go:
                    for cp in matrix_loads(w, 8 * l + n // 2, n % 2, dst, m_.asem.at[4 + n]):
                        cp.start()
                else:
                    wait_all(dst, m_.asem.at[4 + n])

    def ff_task(l, j):
        load_ff(l, j, False)

        @pl.when(j == 0)
        def _():
            dy = t_.acc[...]
            n, rstd = norm_parts(t_.res[...])
            dr2 = norm_back(dy, vec[l, 6:7, :], n, rstd)
            t_.acc[...] = dr2
            dm = dr2.astype(BF)
            t_.dm[...] = dm
            t_.gv[l, 5:6, :] = colsum(dm.astype(F32))
            t_.gv[l, 6:7, :] = colsum(dy * n)
            t_.gv[l, 7:8, :] = colsum(dy)
        df = mm_nt(t_.dm[...], t_.wd[...].reshape(768, D))
        dg = (df * t_.gb[...].astype(F32)).astype(BF)
        du = (df * t_.ga[...].astype(F32)).astype(BF)
        t_.dg[...] = dg
        t_.du[...] = du
        t_.acc[...] += mm_nt(dg, t_.wg[...].reshape(D, 768)) + mm_nt(du, t_.wu[...].reshape(D, 768))

        @pl.when(j == 3)
        def _():
            dh = t_.acc[...]
            n, rstd = norm_parts(t_.res[...])
            dr1 = norm_back(dh, vec[l, 3:4, :], n, rstd)
            t_.acc[...] = dr1
            da = dr1.astype(BF)
            t_.da[...] = da
            t_.gv[l, 2:3, :] = colsum(da.astype(F32))
            t_.gv[l, 3:4, :] = colsum(dh * n)
            t_.gv[l, 4:5, :] = colsum(dh)
            datt = mm_nt(da, t_.wo[...].reshape(D, D)).astype(BF)
            for i in range(3):
                t_.datt[i] = datt[:, 256 * i : 256 * i + 256]
        store_ff(l, j, True)

        @pl.when(j < 3)
        def _():
            load_ff(l, j + 1, True)

        @pl.when(j == 3)
        def _():
            load_att(l, 0, True)

    def store_ff(l, j, go):
        def one(i, src, dst):
            run(pltpu.make_async_copy(src, dst, m_.osem.at[i]), go)
        one(0, t_.dg, cols(g.dg.at[l], j, 768))
        one(1, t_.du, cols(g.du.at[l], j, 768))

        @pl.when(j == 0)
        def _():
            one(2, t_.dm, g.dm.at[l])

        @pl.when(j == 3)
        def _():
            one(3, t_.da, g.da.at[l])

    def att_task(l, i):
        load_att(l, i, False)
        scale = HEAD_DIM ** -0.5
        first = lax.broadcasted_iota(jnp.int32, (pad, 128), 1) < HEAD_DIM
        for sq in range(seqs):
            rows = slice(sq * pad, (sq + 1) * pad)
            for pair in range(2):
                lanes = slice(128 * pair, 128 * pair + 128)
                q2 = t_.q[rows, lanes]
                d2 = t_.datt[i, rows, lanes]
                vs = halves(t_.v[rows, lanes], 1)
                ks = halves(t_.k[rows, lanes].T, 0)
                dv, dk, dq = [], [], None
                for h in range(2):
                    pb = t_.pt[sq, 2 * pair + h]
                    p = pb.astype(F32)
                    dp = mm_nt(vs[h], d2)
                    ds = (p * (dp - jnp.sum(dp * p, axis=0, keepdims=True))).astype(BF)
                    dv.append(mm(pb, d2))
                    dk.append(mm(ds, q2))
                    part = mm(ks[h], ds)
                    dq = part if dq is None else dq + part
                t_.dv[rows, lanes] = jnp.where(first, dv[0], dv[1]).astype(BF)
                t_.dk[rows, lanes] = (jnp.where(first, dk[0], dk[1]) * scale).astype(BF)
                t_.dq[rows, lanes] = (dq * scale).astype(BF).T
        dq, dk, dv = t_.dq[...], t_.dk[...], t_.dv[...]
        at = pl.ds(pl.multiple_of(i * 256, 256), 256)
        t_.gv[l, 0:1, at] = colsum(dq.astype(F32))
        t_.gv[l, 1:2, at] = colsum(dv.astype(F32))
        t_.acc[...] += (
            mm_nt(dq, t_.wq[:, :, :, :, at].reshape(D, 256)) + mm_nt(dk, t_.wk[:, :, :, :, at].reshape(D, 256)) + mm_nt(dv, t_.wv[:, :, :, :, at].reshape(D, 256))
        )
        store_att(l, i, True)

        @pl.when(i < 2)
        def _():
            load_att(l, i + 1, True)

        @pl.when(jnp.logical_and(i == 2, l > 0))
        def _():
            load_ff(jnp.maximum(l - 1, 0), 0, True)

        @pl.when(jnp.logical_and(i == 2, l == 0))
        def _():
            t_.cot[...] = t_.acc[...].astype(BF)
            pltpu.make_async_copy(t_.cot, o.dx, m_.osem.at[7]).start()

    def store_att(l, i, go):
        def one(n, src, dst):
            run(pltpu.make_async_copy(src, dst, m_.osem.at[n]), go)
        one(4, t_.dq, cols(g.dq.at[l], i, 256))
        one(5, t_.dk, cols(g.dk.at[l], i, 256))
        one(6, t_.dv, cols(g.dv.at[l], i, 256))

    def task(t, ff, att):
        l = LAYERS - 1 - t // 7
        u = lax.rem(t, 7)

        @pl.when(u < 4)
        def _():
            ff(l, jnp.minimum(u, 3))

        @pl.when(u >= 4)
        def _():
            att(l, jnp.clip(u - 4, 0, 2))


    def load(p, go):
        q = lax.rem(p, 16)
        n = lax.rem(p, 2)
        layer = LAYERS - 1 - p // 16

        def left(ref, sub=None):
            for cc in range(2):
                src = ref.at[:, cc] if sub is None else ref.at[:, cc, sub]
                run(pltpu.make_async_copy(src, s.lbuf.at[n, cc], m_.lsem.at[n, cc]), go)

        def right(ref, col=None):
            src = ref.at[layer] if col is None else cols(ref.at[layer], jnp.clip(col, 0, 3), 768)
            run(pltpu.make_async_copy(src, s.rbuf.at[n], m_.rsem.at[n]), go)
        if not go:
            left(kept[0].ht)
            right(g.dm)
            return
        for l in range(LAYERS):
            here = layer == l
            kl = kept[l]

            @pl.when(jnp.logical_and(here, q < 4))
            def _():
                left(kl.ft, jnp.minimum(q, 3))

            @pl.when(jnp.logical_and(here, jnp.logical_and(q >= 4, q < 12)))
            def _():
                left(kl.ht)

            @pl.when(jnp.logical_and(here, q == 12))
            def _():
                left(kl.at)

            @pl.when(jnp.logical_and(here, q > 12))
            def _():
                left(kl.xt)

        @pl.when(q < 4)
        def _():
            right(g.dm)

        @pl.when(jnp.logical_and(q >= 4, q < 8))
        def _():
            right(g.dg, q - 4)

        @pl.when(jnp.logical_and(q >= 8, q < 12))
        def _():
            right(g.du, q - 8)
        for i, d in enumerate((g.da, g.dq, g.dk, g.dv)):
            @pl.when(q == 12 + i)
            def _():
                right(d)

    def rcopy(p, e, src, dst, d):
        return pltpu.make_async_remote_copy(src_ref=src, dst_ref=dst, send_sem=m_.send.at[p, e], recv_sem=m_.recv.at[p, e], device_id=d, device_id_type=MESH)

    def product(n, cc, dst):
        for i in range(4):
            v = mm(s.lbuf[n, cc, 2 * i : 2 * i + 2].reshape(96, 512), s.rbuf[n]).astype(BF)
            v = v.reshape(2, 48, 768)
            dst[i, :, 0] = v[:, :, :384]
            dst[i, :, 1] = v[:, :, 384:]

    def c_copy(p, n):
        return rcopy(p, 0, s.sbuf.at[n], c_.r0.at[lax.rem(p, SLOTS)], d_c)

    def s0(p):
        n = lax.rem(p, 2)
        load(p, False)

        @pl.when(p >= 2)
        def _():
            c_copy(jnp.maximum(p - 2, 0), n).wait_send()
        product(n, 1 - c, s.sbuf.at[n])
        c_copy(p, n).start()
        product(n, c, s.own.at[lax.rem(p, LAG + 1)])

        @pl.when(p + 1 < NP)
        def _():
            load(jnp.minimum(p + 1, NP - 1), True)
    small = Group(("r0", "h1", "h2", "za", "zb", "yf"), (s.r0v, s.h1v, s.h2v, s.zav, s.zbv, s.yfv))
    zlo = jnp.where(z == 1, 1, 0)
    elo = jnp.where(z == 0, 1, 0)
    mlo = jnp.where(z == 1, 2, 0)
    rlo = jnp.where(z == 1, 0, 2)

    def steps(b, p, i, my):
        fx = piece_first_x(p)
        fy = jnp.logical_not(fx)

        def hop1(go):
            a = rcopy(p, 1, b.r0.at[i, :, 1 - x], b.h1.at[i], d_x)
            if go == "start":
                pl.when(fx)(a.start)
                pl.when(fy)(rcopy(p, 1, b.r0.at[i, :, :, 1 - y], b.h1.at[i], d_y).start)
            elif go == "recv":
                a.wait_recv()
            else:
                a.wait_send()

        def hop2(go):
            a = rcopy(p, 2, b.h1.at[i, :, 1 - y], b.h2.at[i], d_y)
            if go == "start":
                pl.when(fx)(a.start)
                pl.when(fy)(rcopy(p, 2, b.h1.at[i, :, 1 - x], b.h2.at[i], d_x).start)
            elif go == "recv":
                a.wait_recv()
            else:
                a.wait_send()

        def z1():
            return rcopy(p, 3, b.h2.at[i, pl.ds(elo, 3)], b.za.at[i], d_zp)

        def z2():
            return rcopy(p, 4, b.h2.at[i, pl.ds(mlo, 2)], b.zb.at[i], d_zm)

        def z3():
            return rcopy(p, 5, b.h2.at[i, zp], b.zb.at[i, 0], d_zp)

        def y1():
            return rcopy(p, 6, b.h2.at[i, z], b.yf.at[i], d_y)

        def s1():
            rcopy(p, 0, b.r0.at[i], b.r0.at[i], d_c).wait_recv()
            for k in range(4):
                add_into(b.r0.at[i, k], my.at[k])
            hop1("start")

        def s2():
            hop1("recv")
            for k in range(4):
                @pl.when(fx)
                def _():
                    add_into(b.h1.at[i, k], b.r0.at[i, k, x])

                @pl.when(fy)
                def _():
                    add_into(b.h1.at[i, k], b.r0.at[i, k, :, y])
            hop2("start")

        def s3():
            hop1("send")
            hop2("recv")
            t = jnp.where(fx, y, x)
            for k in range(4):
                add_into(b.h2.at[i, k], b.h1.at[i, k, t])
            pl.when(end)(z1().start)

        def s4():
            hop2("send")

            @pl.when(mid)
            def _():
                z1().wait_recv()
                for k in range(3):
                    add_into(b.h2.at[i, zlo + k], b.za.at[i, k])
                z2().start()

        def s5():
            pl.when(end)(z1().wait_send)

            @pl.when(mid)
            def _():
                z2().wait_recv()
                for k in range(2):
                    add_into(b.h2.at[i, rlo + k], b.zb.at[i, k])
                z3().start()

        def s6():
            pl.when(mid)(z2().wait_send)

            @pl.when(end)
            def _():
                z3().wait_recv()
                add_into(b.h2.at[i, z], b.zb.at[i, 0])
            y1().start()

        def s7():
            pl.when(mid)(z3().wait_send)
            y1().wait_send()
            y1().wait_recv()
        return s1, s2, s3, s4, s5, s6, s7

    def out_copy(p, n, go):
        q = lax.rem(p, 16)
        layer = LAYERS - 1 - p // 16

        def one(dst):
            run(pltpu.make_async_copy(s.stage.at[n], dst, m_.out.at[n]), go)
        if not go:
            one(o.out.at[0])
            return

        @pl.when(q < 4)
        def _():
            one(o.down.at[layer, pl.ds(pl.multiple_of(jnp.minimum(q, 3) * 48, 48), 48)])

        @pl.when(jnp.logical_and(q >= 4, q < 12))
        def _():
            one(cols(o.gated.at[layer], jnp.clip(q - 4, 0, 7), 768))

        @pl.when(q == 12)
        def _():
            one(o.out.at[layer])

        @pl.when(q > 12)
        def _():
            one(cols(o.qkv.at[layer], jnp.clip(q - 13, 0, 2), 768))

    def write(p):
        n = lax.rem(p, 2)

        @pl.when(p >= 2)
        def _():
            out_copy(p, n, False)
        i = lax.rem(p, SLOTS)
        a = c_.h2[i, z].astype(F32)
        b = c_.yf[i].astype(F32)

        @pl.when(y == 0)
        def _():
            s.stage[n, :, :384] = a
            s.stage[n, :, 384:] = b

        @pl.when(y == 1)
        def _():
            s.stage[n, :, :384] = b
            s.stage[n, :, 384:] = a
        out_copy(p, n, True)


    vp = NP
    vc = rcopy(vp, 0, s.vall.at[1 - c], s.r0v.at[0], d_c)
    vsteps = steps(small, vp, 0, s.vall.at[c])
    VSTART = 27

    def pack_vectors():
        for l in range(LAYERS):
            v = jnp.concatenate([t_.gv[l], jnp.zeros((120, D), F32)], axis=0).T.astype(BF)
            for k in range(16):
                s.vall[k % 2, k // 4, (k // 2) % 2, l] = v[48 * k : 48 * k + 48]
        vc.start()


    top = LAYERS - 1
    first = pltpu.make_async_copy(cot, t_.cot, m_.vload)
    first.start()
    load_ff(top, 0, True)
    first.wait()
    t_.acc[...] = t_.cot[...].astype(F32)
    ff_task(top, 0)
    store_ff(top, 0, False)
    load(0, True)

    def body(r, carry):
        def at(k, f):
            p = r - LAG * k

            @pl.when(jnp.logical_and(p >= 0, p < NP))
            def _():
                f(jnp.clip(p, 0, NP - 1))

        def st(k):
            def f(p):
                steps(c_, p, lax.rem(p, SLOTS), s.own.at[lax.rem(p, LAG + 1)])[k - 1]()
                if k == 7:
                    write(p)
            return f
        even = lax.rem(r, 2) == 0

        @pl.when(jnp.logical_and(even, jnp.logical_and(r >= 2, r < 28)))
        def _():
            task(jnp.clip(r // 2, 1, 13), lambda l, j: store_ff(l, j, False), lambda l, i: store_att(l, i, False))
        for k in range(1, 8):
            pl.when(r == VSTART + LAG * k)(vsteps[k - 1])
        at(0, s0)
        for k in range(7, 0, -1):
            at(k, st(k))
        pl.when(r == VSTART)(pack_vectors)

        @pl.when(jnp.logical_and(jnp.logical_not(even), r < 26))
        def _():
            task(jnp.clip((r + 1) // 2, 1, 13), ff_task, att_task)
        return carry
    lax.fori_loop(0, NP + 7 * LAG, body, 0)

    for p in (NP - 2, NP - 1):
        c_copy(p, p % 2).wait_send()
        out_copy(p, p % 2, False)
    vc.wait_send()
    pltpu.make_async_copy(t_.cot, o.dx, m_.osem.at[7]).wait()
    va, vb = s.h2v[0, z].astype(F32), s.yfv[0].astype(F32)
    o.vec[0] = jnp.where(y == 0, va, vb)
    o.vec[1] = jnp.where(y == 0, vb, va)


def backward_all(cot, vec, kept, w):
    rows = cot.shape[0]
    hbm = pl.BlockSpec(memory_space=pltpu.HBM)
    vmem = pl.BlockSpec(memory_space=pltpu.VMEM)
    kept = [tuple(k[:8]) + (k[8].reshape(8, 2, 4, 48, rows),) + tuple(a.reshape(8, 2, 48, rows) for a in k[9:]) for k in kept]
    act = lambda c, t: jax.ShapeDtypeStruct((rows, c), t)
    out = [
        jax.ShapeDtypeStruct((LAYERS, 48, 3 * D), F32), jax.ShapeDtypeStruct((LAYERS, 48, D), F32),
        jax.ShapeDtypeStruct((LAYERS, 48, 2 * FF), F32), jax.ShapeDtypeStruct((LAYERS, 192, D), F32),
        jax.ShapeDtypeStruct((2, 48, 128), F32), act(D, BF),
    ]
    both = lambda c: jax.ShapeDtypeStruct((LAYERS, rows, c), BF)
    scratch_out = [both(D), both(FF), both(FF), both(D), both(D), both(D), both(D)]
    seqs, _, pad, _ = kept[0][7].shape
    v = pltpu.VMEM
    dma = pltpu.SemaphoreType.DMA
    mat = v((4, 2, 2, 48, D), BF)
    n = SLOTS
    scratch = [
        v((2, 2, 8, 48, rows), BF), v((2, rows, 768), BF), v((2, 4, 2, 2, 48, 384), BF), v((LAG + 1, 4, 2, 2, 48, 384), BF), v((2, 48, 768), F32),
        v((1, 4, 2, 2, 48, 128), BF), v((1, 4, 2, 48, 128), BF), v((1, 4, 48, 128), BF),
        v((1, 3, 48, 128), BF), v((1, 2, 48, 128), BF), v((1, 48, 128), BF), v((2, 4, 2, 2, 48, 128), BF),
        v((n, 4, 2, 2, 48, 384), BF), v((n, 4, 2, 48, 384), BF), v((n, 4, 48, 384), BF), v((n, 3, 48, 384), BF), v((n, 2, 48, 384), BF), v((n, 48, 384), BF),
        v((rows, D), F32), v((rows, D), F32), v((2, 2, 4, 48, D), BF), mat, mat, v((rows, 768), BF), v((rows, 768), BF), mat,
        v((rows, D), BF), v((rows, 768), BF), v((rows, 768), BF), v((rows, D), BF), v((3, rows, 256), BF),
        v((rows, 256), BF), v((rows, 256), BF), v((rows, 256), BF), v((seqs, 4, pad, pad), BF), mat, mat, mat,
        v((rows, 256), BF), v((rows, 256), BF), v((rows, 256), BF), v((LAYERS, 8, D), F32), v((rows, D), BF),
        dma((2, 2)), dma((2,)), dma((NPIECE, 7)), dma((NPIECE, 7)), dma((2,)), dma, dma((7,)), dma((7,)), dma((8,)),
    ]
    res = pl.pallas_call(
        backward_kernel, out_shape=out + scratch_out,
        in_specs=[hbm, vmem] + [hbm] * 25,
        out_specs=[hbm] * 4 + [vmem] + [hbm] * 8,
        scratch_shapes=scratch,
        compiler_params=pltpu.CompilerParams(collective_id=1, has_side_effects=True, vmem_limit_bytes=62 * 2**20), name="backward_reduce",
    )(cot, vec, *kept[0], *kept[1], w)
    return res[:4], res[4], res[5]


def forward_plain(seq_lengths, slopes, x, shards, vectors):
    mats = [lax.all_gather(w, "fsdp", axis=1, tiled=True) for w in shards]
    vec = lax.all_gather(jnp.stack(vectors, axis=1), "fsdp", axis=2, tiled=True).astype(F32)
    wq, wo, wg, wd = mats
    kept = []
    for l in range(LAYERS):
        q, k, v, att, pt, xt, at = attention_forward(l, seq_lengths, slopes, x, wq, vec)
        out_dtype = BF if l == LAYERS - 1 else F32
        r1, r2, ga, gb, ft, ht, x = ff_forward(l, att, x, wo, wg, wd, vec, out_dtype)
        kept.append((r1, r2, ga, gb, q, k, v, pt, ft, ht, at, xt))
    return mats, vec, x, kept


def backward_plain(dy, vec, kept, mats):
    wq, wo, wg, wd = mats

    def one(g, dim):
        part = lax.psum_scatter(g.astype(BF), "fsdp", scatter_dimension=dim, tiled=True)
        return lax.psum(part, "dp").astype(F32)
    sums, vecs = [None] * LAYERS, [None] * LAYERS
    for l in reversed(range(LAYERS)):
        r1, r2, ga, gb, q, k, v, pt, ft, ht, at, xt = kept[l]
        dm, dg, du, dr1, da, datt, gv = ff_backward(l, dy, r1, r2, ga, gb, wo, wg, wd, vec)
        dq, dk, dv, dy, gbias = attention_backward(l, datt, q, k, v, pt, wq, dr1, BF if l == 0 else F32)
        pairs = ((xt, jnp.concatenate([dq, dk, dv], axis=1)), (at, da), (ht, jnp.concatenate([dg, du], axis=1)), (ft, dm))
        sums[l] = [one(mm(a, b), 0) for a, b in pairs]
        vecs[l] = gv + gbias
    return [jnp.stack(m) for m in zip(*sums)], one(jnp.stack(vecs), 2), dy


def per_device(fast, inputs, lengths, cotangent, w_qkv, q_bias, v_bias, w_out, b_out, gain_one, shift_one, w_gated, w_down, b_down, gain_two, shift_two):
    shards = (w_qkv, w_out, w_gated, w_down)
    vectors = (q_bias, v_bias, b_out, gain_one, shift_one, b_down, gain_two, shift_two)
    seq_lengths = lengths.reshape(-1)
    slopes = jnp.array(slopes_list(HEADS), F32)
    x = inputs.reshape(-1, D)
    dy = cotangent.reshape(-1, D)
    if fast:
        w, vec, x, kept = forward_all(seq_lengths, slopes, x, shards, vectors)
        m, packed, dx = backward_all(dy, vec, kept, w)
        vs = packed[:, :, :8].transpose(0, 2, 1)
    else:
        mats, vec, x, kept = forward_plain(seq_lengths, slopes, x, shards, vectors)
        m, vs, dx = backward_plain(dy, vec, kept, mats)
    return (
        x.reshape(inputs.shape), dx.reshape(inputs.shape), m[0], vs[:, 0], vs[:, 1], m[1], vs[:, 2], vs[:, 3], vs[:, 4], m[2], m[3], vs[:, 5], vs[:, 6], vs[:, 7],
    )


def solution(mesh):
    placed = (
        P(None, ("dp", "fsdp"), None, None),
        P(None, ("dp", "fsdp")),
        P(None, ("dp", "fsdp"), None, None),
        P(None, "fsdp", None),
        P(None, "fsdp"),
        P(None, "fsdp"),
        P(None, "fsdp", None),
        P(None, "fsdp"),
        P(None, "fsdp"),
        P(None, "fsdp"),
        P(None, "fsdp", None),
        P(None, "fsdp", None),
        P(None, "fsdp"),
        P(None, "fsdp"),
        P(None, "fsdp"),
    )
    return jax.shard_map(
        functools.partial(per_device, dict(mesh.shape) == {"dp": 2, "fsdp": 16}),
        mesh=mesh,
        in_specs=placed,
        out_specs=(
            P(None, ("dp", "fsdp"), None, None),
            P(None, ("dp", "fsdp"), None, None),
            P(None, "fsdp", None),
            P(None, "fsdp"),
            P(None, "fsdp"),
            P(None, "fsdp", None),
            P(None, "fsdp"),
            P(None, "fsdp"),
            P(None, "fsdp"),
            P(None, "fsdp", None),
            P(None, "fsdp", None),
            P(None, "fsdp"),
            P(None, "fsdp"),
            P(None, "fsdp"),
        ),
        check_vma=False,
    )
```

```python
import functools
import math

import jax
import jax.numpy as jnp
from jax import lax
from jax.experimental import pallas as pl
from jax.experimental.pallas import tpu as pltpu
from jax.sharding import PartitionSpec as P

MESH = pl.DeviceIdType.MESH

BF = jnp.bfloat16
F32 = jnp.float32
D, HEADS, HEAD_DIM, FF, LAYERS = 768, 12, 64, 3072, 2
EPS = 1e-12
NEG = -1e30
NT = (((1,), (1,)), ((), ()))


def slopes_list(heads_count):
    nearest = 2 ** int(math.floor(math.log2(heads_count)))
    leading = [2.0 ** (-8.0 * (number + 1) / nearest) for number in range(nearest)]
    trailing = [2.0 ** (-8.0 * (number + 1) / (2 * nearest)) for number in range(2 * nearest)][0::2]
    return leading + trailing[: heads_count - nearest]


def mm(a, b):
    return jnp.dot(a, b, preferred_element_type=F32)


def mm_nt(a, b):
    return lax.dot_general(a, b, NT, preferred_element_type=F32)


def erf(x):
    return lax.erf(x)


def norm_parts(r):
    cent = r - jnp.mean(r, axis=-1, keepdims=True)
    rstd = lax.rsqrt(jnp.mean(cent * cent, axis=-1, keepdims=True) + EPS)
    return cent * rstd, rstd


def norm_back(dy, gain, n, rstd):
    dn = dy * gain
    return rstd * (dn - jnp.mean(dn, axis=-1, keepdims=True) - n * jnp.mean(dn * n, axis=-1, keepdims=True))


def halves(v, axis):
    first = lax.broadcasted_iota(jnp.int32, v.shape, axis) < HEAD_DIM
    zero = jnp.zeros_like(v)
    return jnp.where(first, v, zero), jnp.where(first, zero, v)


def attention_kernel(len_ref, slope_ref, x_ref, wq_ref, wk_ref, wv_ref, vec_ref, q_ref, k_ref, v_ref, att_ref, pt_ref, xt_ref, at_ref, xb_ref, dist_ref):
    i = pl.program_id(0)
    seqs, pad = pt_ref.shape[0], pt_ref.shape[-1]

    @pl.when(i == 0)
    def _():
        xb = x_ref[...].astype(BF)
        xb_ref[...] = xb
        xt_ref[...] = xb.T
        keys = lax.broadcasted_iota(jnp.int32, (pad, pad), 0)
        rows = lax.broadcasted_iota(jnp.int32, (pad, pad), 1)
        dist_ref[...] = jnp.abs(keys - rows).astype(F32)
    xb = xb_ref[...]
    q_ref[...] = (mm(xb, wq_ref[...]) + vec_ref[0:1, :]).astype(BF)
    k_ref[...] = mm(xb, wk_ref[...]).astype(BF)
    v_ref[...] = (mm(xb, wv_ref[...]) + vec_ref[1:2, :]).astype(BF)
    for s in range(seqs):
        rows = slice(s * pad, (s + 1) * pad)
        hidden = jnp.where(lax.broadcasted_iota(jnp.int32, (pad, 1), 0) < len_ref[s], 0.0, NEG)
        for pair in range(2):
            lanes = slice(128 * pair, 128 * pair + 128)
            q2 = q_ref[rows, lanes] * BF(HEAD_DIM ** -0.5)
            k0, k1 = halves(k_ref[rows, lanes], 1)
            v0, v1 = halves(v_ref[rows, lanes].T, 0)
            total = None
            for h, (kh, vh) in enumerate(((k0, v0), (k1, v1))):
                slope = slope_ref[4 * i + 2 * pair + h]
                sc = mm_nt(kh, q2) - slope * dist_ref[...] + hidden
                e = jnp.exp(sc - jnp.max(sc, axis=0, keepdims=True))
                p = (e * (1.0 / jnp.sum(e, axis=0, keepdims=True))).astype(BF)
                pt_ref[s, 2 * pair + h] = p
                part = mm(vh, p)
                total = part if total is None else total + part
            total = total.astype(BF)
            at_ref[lanes, rows] = total
            att_ref[rows, lanes] = total.T


def attention_forward(l, lengths, slopes, x, w_qkv, vec):
    rows = x.shape[0]
    seqs = lengths.shape[0]
    pad = rows // seqs
    col = lambda off: pl.BlockSpec((None, D, 256), lambda i: (l, 0, off + i))
    blk = pl.BlockSpec((rows, 256), lambda i: (0, i))
    smem = pl.BlockSpec(memory_space=pltpu.SMEM)
    act = jax.ShapeDtypeStruct((rows, D), BF)
    return pl.pallas_call(
        attention_kernel,
        grid=(3,),
        in_specs=[smem, smem, pl.BlockSpec((rows, D), lambda i: (0, 0)), col(0), col(3), col(6), pl.BlockSpec((None, 8, 256), lambda i: (l, 0, i))],
        out_specs=[blk, blk, blk, blk, pl.BlockSpec((seqs, 4, pad, pad), lambda i: (0, i, 0, 0)), pl.BlockSpec((D, rows), lambda i: (0, 0)), pl.BlockSpec((256, rows), lambda i: (i, 0))],
        out_shape=[act, act, act, act, jax.ShapeDtypeStruct((seqs, HEADS, pad, pad), BF), jax.ShapeDtypeStruct((D, rows), BF), jax.ShapeDtypeStruct((D, rows), BF)],
        scratch_shapes=[pltpu.VMEM((rows, D), BF), pltpu.VMEM((pad, pad), F32)],
        compiler_params=pltpu.CompilerParams(vmem_limit_bytes=56 * 2**20),
        name="attention_forward",
    )(lengths, slopes, x, w_qkv, w_qkv, w_qkv, vec)


def ff_kernel(att_ref, x_ref, wo_ref, wg_ref, wu_ref, wd_ref, vec_ref, r1_ref, r2_ref, ga_ref, gb_ref, ft_ref, ht_ref, out_ref, h_ref, hb_ref, acc_ref):
    j = pl.program_id(0)

    @pl.when(j == 0)
    def _():
        r1 = x_ref[...].astype(F32) + (mm(att_ref[...], wo_ref[...]) + vec_ref[2:3, :])
        r1_ref[...] = r1
        h = norm_parts(r1)[0] * vec_ref[3:4, :] + vec_ref[4:5, :]
        h_ref[...] = h
        hb = h.astype(BF)
        hb_ref[...] = hb
        ht_ref[...] = hb.T
        acc_ref[...] = jnp.zeros_like(acc_ref)
    hb = hb_ref[...]
    g = mm(hb, wg_ref[...])
    u = mm(hb, wu_ref[...])
    cdf = 0.5 + 0.5 * erf(g * math.sqrt(0.5))
    gelu = g * cdf
    slope = cdf + g * (jnp.exp(-0.5 * (g * g)) * (1.0 / math.sqrt(2.0 * math.pi)))
    ga_ref[...] = gelu.astype(BF)
    gb_ref[...] = (slope * u).astype(BF)
    f = (gelu * u).astype(BF)
    ft_ref[...] = f.T
    acc_ref[...] += mm(f, wd_ref[...])

    @pl.when(j == pl.num_programs(0) - 1)
    def _():
        r2 = h_ref[...] + (acc_ref[...] + vec_ref[5:6, :])
        r2_ref[...] = r2
        out_ref[...] = (norm_parts(r2)[0] * vec_ref[6:7, :] + vec_ref[7:8, :]).astype(out_ref.dtype)


def ff_forward(l, att, x, w_out, w_gated, w_down, vec, out_dtype):
    rows = x.shape[0]
    n = FF // 768
    whole = pl.BlockSpec((rows, D), lambda j: (0, 0))
    blk = pl.BlockSpec((rows, 768), lambda j: (0, j))
    return pl.pallas_call(
        ff_kernel,
        grid=(n,),
        in_specs=[whole, whole, pl.BlockSpec((None, D, D), lambda j: (l, 0, 0)),
                  pl.BlockSpec((None, D, 768), lambda j: (l, 0, j)), pl.BlockSpec((None, D, 768), lambda j: (l, 0, n + j)),
                  pl.BlockSpec((None, 768, D), lambda j: (l, j, 0)), pl.BlockSpec((None, 8, D), lambda j: (l, 0, 0))],
        out_specs=[whole, whole, blk, blk, pl.BlockSpec((768, rows), lambda j: (j, 0)), pl.BlockSpec((D, rows), lambda j: (0, 0)), whole],
        out_shape=[jax.ShapeDtypeStruct((rows, D), F32), jax.ShapeDtypeStruct((rows, D), F32),
                   jax.ShapeDtypeStruct((rows, FF), BF), jax.ShapeDtypeStruct((rows, FF), BF),
                   jax.ShapeDtypeStruct((FF, rows), BF), jax.ShapeDtypeStruct((D, rows), BF), jax.ShapeDtypeStruct((rows, D), out_dtype)],
        scratch_shapes=[pltpu.VMEM((rows, D), F32), pltpu.VMEM((rows, D), BF), pltpu.VMEM((rows, D), F32)],
        compiler_params=pltpu.CompilerParams(vmem_limit_bytes=56 * 2**20),
        name="ff_forward",
    )(att, x, w_out, w_gated, w_gated, w_down, vec)


def colsum(v):
    return jnp.sum(v, axis=0, keepdims=True)


def ff_back_kernel(dy_ref, r1_ref, r2_ref, ga_ref, gb_ref, wo_ref, wg_ref, wu_ref, wd_ref, vec_ref, dm_ref, dg_ref, du_ref, dr1_ref, da_ref, datt_ref, gv_ref, acc_ref):
    j = pl.program_id(0)

    @pl.when(j == 0)
    def _():
        dy = dy_ref[...].astype(F32)
        n, rstd = norm_parts(r2_ref[...])
        dr2 = norm_back(dy, vec_ref[6:7, :], n, rstd)
        acc_ref[...] = dr2
        dm = dr2.astype(BF)
        dm_ref[...] = dm
        gv_ref[5:6, :] = colsum(dm.astype(F32))
        gv_ref[6:7, :] = colsum(dy * n)
        gv_ref[7:8, :] = colsum(dy)
        gv_ref[0:2, :] = jnp.zeros((2, D), F32)
    df = mm_nt(dm_ref[...], wd_ref[...])
    dg = (df * gb_ref[...].astype(F32)).astype(BF)
    du = (df * ga_ref[...].astype(F32)).astype(BF)
    dg_ref[...] = dg
    du_ref[...] = du
    acc_ref[...] += mm_nt(dg, wg_ref[...]) + mm_nt(du, wu_ref[...])

    @pl.when(j == pl.num_programs(0) - 1)
    def _():
        dh = acc_ref[...]
        n, rstd = norm_parts(r1_ref[...])
        dr1 = norm_back(dh, vec_ref[3:4, :], n, rstd)
        dr1_ref[...] = dr1
        da = dr1.astype(BF)
        da_ref[...] = da
        gv_ref[2:3, :] = colsum(da.astype(F32))
        gv_ref[3:4, :] = colsum(dh * n)
        gv_ref[4:5, :] = colsum(dh)
        datt_ref[...] = mm_nt(da, wo_ref[...]).astype(BF)


def ff_backward(l, dy, r1, r2, ga, gb, w_out, w_gated, w_down, vec):
    rows = dy.shape[0]
    n = FF // 768
    whole = pl.BlockSpec((rows, D), lambda j: (0, 0))
    blk = pl.BlockSpec((rows, 768), lambda j: (0, j))
    act = lambda c, t: jax.ShapeDtypeStruct((rows, c), t)
    return pl.pallas_call(
        ff_back_kernel,
        grid=(n,),
        in_specs=[whole, whole, whole, blk, blk, pl.BlockSpec((None, D, D), lambda j: (l, 0, 0)),
                  pl.BlockSpec((None, D, 768), lambda j: (l, 0, j)), pl.BlockSpec((None, D, 768), lambda j: (l, 0, n + j)),
                  pl.BlockSpec((None, 768, D), lambda j: (l, j, 0)), pl.BlockSpec((None, 8, D), lambda j: (l, 0, 0))],
        out_specs=[whole, blk, blk, whole, whole, whole, pl.BlockSpec((8, D), lambda j: (0, 0))],
        out_shape=[act(D, BF), act(FF, BF), act(FF, BF), act(D, F32), act(D, BF), act(D, BF), jax.ShapeDtypeStruct((8, D), F32)],
        scratch_shapes=[pltpu.VMEM((rows, D), F32)],
        compiler_params=pltpu.CompilerParams(vmem_limit_bytes=56 * 2**20),
        name="ff_backward",
    )(dy, r1, r2, ga, gb, w_out, w_gated, w_gated, w_down, vec)


def attention_back_kernel(datt_ref, q_ref, k_ref, v_ref, pt_ref, wq_ref, wk_ref, wv_ref, dr1_ref, dq_ref, dk_ref, dv_ref, dx_ref, gb_ref, acc_ref):
    i = pl.program_id(0)
    seqs, pad = pt_ref.shape[0], pt_ref.shape[-1]
    scale = HEAD_DIM ** -0.5

    @pl.when(i == 0)
    def _():
        acc_ref[...] = dr1_ref[...]
    first = lax.broadcasted_iota(jnp.int32, (pad, 128), 1) < HEAD_DIM
    for s in range(seqs):
        rows = slice(s * pad, (s + 1) * pad)
        for pair in range(2):
            lanes = slice(128 * pair, 128 * pair + 128)
            q2 = q_ref[rows, lanes]
            d2 = datt_ref[rows, lanes]
            vs = halves(v_ref[rows, lanes], 1)
            ks = halves(k_ref[rows, lanes].T, 0)
            dv, dk, dq = [], [], None
            for h in range(2):
                pb = pt_ref[s, 2 * pair + h]
                p = pb.astype(F32)
                dp = mm_nt(vs[h], d2)
                ds = (p * (dp - jnp.sum(dp * p, axis=0, keepdims=True))).astype(BF)
                dv.append(mm(pb, d2))
                dk.append(mm(ds, q2))
                part = mm(ks[h], ds)
                dq = part if dq is None else dq + part
            dv_ref[rows, lanes] = jnp.where(first, dv[0], dv[1]).astype(BF)
            dk_ref[rows, lanes] = (jnp.where(first, dk[0], dk[1]) * scale).astype(BF)
            dq_ref[rows, lanes] = (dq * scale).astype(BF).T
    dq, dk, dv = dq_ref[...], dk_ref[...], dv_ref[...]
    gb_ref[0:1, :] = colsum(dq.astype(F32))
    gb_ref[1:2, :] = colsum(dv.astype(F32))
    gb_ref[2:8, :] = jnp.zeros((6, 256), F32)
    acc_ref[...] += mm_nt(dq, wq_ref[...]) + mm_nt(dk, wk_ref[...]) + mm_nt(dv, wv_ref[...])

    @pl.when(i == pl.num_programs(0) - 1)
    def _():
        dx_ref[...] = acc_ref[...].astype(dx_ref.dtype)


def attention_backward(l, datt, q, k, v, pt, w_qkv, dr1, out_dtype):
    rows = datt.shape[0]
    seqs, _, pad, _ = pt.shape
    col = lambda off: pl.BlockSpec((None, D, 256), lambda i: (l, 0, off + i))
    blk = pl.BlockSpec((rows, 256), lambda i: (0, i))
    whole = pl.BlockSpec((rows, D), lambda i: (0, 0))
    act = jax.ShapeDtypeStruct((rows, D), BF)
    return pl.pallas_call(
        attention_back_kernel,
        grid=(3,),
        in_specs=[blk, blk, blk, blk, pl.BlockSpec((seqs, 4, pad, pad), lambda i: (0, i, 0, 0)), col(0), col(3), col(6), whole],
        out_specs=[blk, blk, blk, whole, pl.BlockSpec((8, 256), lambda i: (0, i))],
        out_shape=[act, act, act, jax.ShapeDtypeStruct((rows, D), out_dtype), jax.ShapeDtypeStruct((8, D), F32)],
        scratch_shapes=[pltpu.VMEM((rows, D), F32)],
        compiler_params=pltpu.CompilerParams(vmem_limit_bytes=56 * 2**20),
        name="attention_backward",
    )(datt, q, k, v, pt, w_qkv, w_qkv, w_qkv, dr1)


def place():
    y = lax.axis_index("dp"); f = lax.axis_index("fsdp")
    z = f // 4; x = lax.rem(f // 2, 2); c = lax.rem(f, 2)
    return z, x, y, c

def dev(z, x, y, c):
    return (y, (z * 2 + x) * 2 + c)

PIECES = 8 * LAYERS
GLAG = 1


def along_z(p):
    return lax.rem(p, 5) == 1

KEPT = ("r1", "r2", "ga", "gb", "q", "k", "v", "pt", "ft", "ht", "at", "xt")


class Group:
    def __init__(self, names, refs):
        for name, ref in zip(names, refs):
            setattr(self, name, ref)


def taker(refs):
    refs = list(refs)

    def take(*names):
        g = Group(names, refs[: len(names)])
        del refs[: len(names)]
        return g
    return take


def run(cp, go):
    if go:
        cp.start()
    else:
        cp.wait()


def cols(ref, j, width):
    return ref.at[:, pl.ds(pl.multiple_of(j * width, width), width)]


def matrix_loads(w, p, k, dst, sem):
    return [pltpu.make_async_copy(w.at[p, :, :, :, h, k], dst.at[:, :, :, :, pl.ds(384 * h, 384)], sem) for h in range(2)]


def wait_all(dst, sem):
    pltpu.make_async_copy(dst, dst, sem).wait()


def forward_kernel(*refs):
    take = taker(refs)
    i_ = take("lens", "slopes", "x", "qkv", "out", "gated", "down", *["v%d" % i for i in range(8)])
    o_ = take("w", "v", "vec", "last")
    kept = [take(*KEPT) for _ in range(LAYERS)]
    t_ = take("x", "xb", "dist", "q", "k", "v", "att", "pt", "at", "xt", "wq", "wk", "wv", "wo", "wg", "wu", "wd", "h", "hb", "f", "ga", "gb", "ft", "res", "last", "vown", "vwide", "vec_in")
    m_ = take("local", "zsend", "fsend", "xysend", "rsend", "csend", "recv", "crecv", "vlocal", "vload", "load", "wload", "store")
    pad = t_.pt.shape[-1]
    seqs = t_.pt.shape[0]

    z, x, y, c = place()
    zp = z + 1 - 2 * lax.rem(z, 2)
    zm = 3 - z
    zf = lax.rem(z + 2, 4)
    mid = jnp.logical_and(z >= 1, z <= 2)
    end = jnp.logical_not(mid)
    d_zp, d_zm = dev(zp, x, y, c), dev(zm, x, y, c)
    d_x, d_y, d_c = dev(z, 1 - x, y, c), dev(z, x, 1 - y, c), dev(z, x, y, 1 - c)
    bar = pltpu.get_barrier_semaphore()
    for d in (d_zp, d_zm, d_x, d_y, d_c):
        pl.semaphore_signal(bar, 1, device_id=d, device_id_type=MESH)


    def local(p):
        u = lax.rem(p, 8)
        l = p // 8

        def put(h, k, src):
            pltpu.make_async_copy(src, o_.w.at[p, z, x, c, h, k], m_.local.at[p]).start()

        def part(ref, off):
            return ref.at[l, :, pl.ds(pl.multiple_of(off, 128), 384)]
        for h in range(2):
            @pl.when(u == 0)
            def _():
                put(h, 0, part(i_.qkv, 384 * h))
                put(h, 1, part(i_.qkv, 768 + 384 * h))

            @pl.when(u == 1)
            def _():
                put(h, 0, part(i_.qkv, 1536 + 384 * h))
                put(h, 1, part(i_.out, 384 * h))

            @pl.when(jnp.logical_and(u >= 2, u < 6))
            def _():
                j = jnp.clip(u - 2, 0, 3) * 768
                put(h, 0, part(i_.gated, j + 384 * h))
                put(h, 1, part(i_.gated, j + FF + 384 * h))

            @pl.when(u >= 6)
            def _():
                for k in range(2):
                    r = pl.multiple_of(jnp.clip(2 * (u - 6) + k, 0, 3) * 48, 48)
                    put(h, k, i_.down.at[l, pl.ds(r, 48), pl.ds(384 * h, 384)])

    def locals_from(p, carry):
        local(p)
        return carry
    local(0)
    t_.vwide[...] = jnp.zeros_like(t_.vwide)
    for n in range(8):
        row = getattr(i_, "v%d" % n)[...].astype(F32)
        for l in range(LAYERS):
            t_.vwide[l, n : n + 1, 0:48] = row[l : l + 1, :]
    t_.vown[...] = t_.vwide[...].astype(BF)
    vplace = pltpu.make_async_copy(t_.vown, o_.v.at[z, x, c], m_.vlocal.at[0])
    vplace.start()
    xload = pltpu.make_async_copy(i_.x, t_.last, m_.vlocal.at[1])
    xload.start()
    lax.fori_loop(1, PIECES, locals_from, 0)
    pl.semaphore_wait(bar, 5)


    def stages(b, s):
        def copy(zz, xx, hh, sem, d):
            u = b(zz, xx, c, hh)
            return pltpu.make_async_remote_copy(src_ref=u, dst_ref=u, send_sem=sem.at[s], recv_sem=m_.recv.at[s, (zz * 2 + xx) * 2 + hh], device_id=d, device_id_type=MESH)

        def zsend(zz, d, sem=m_.fsend):
            copy(zz, x, y, sem, d).start()

        def got(zz, xx, hh, d):
            copy(zz, xx, hh, m_.zsend, d).wait_recv()

        def plane(zz, cc=c):
            u = b(zz, slice(None), cc, slice(None))
            return pltpu.make_async_remote_copy(src_ref=u, dst_ref=u, send_sem=m_.csend.at[s], recv_sem=m_.crecv.at[s, zz], device_id=d_c, device_id_type=MESH)

        def spread(zz):
            copy(zz, x, y, m_.xysend, d_x).start()
            copy(zz, x, y, m_.xysend, d_y).start()

        def relay(zz, first_x):
            got(zz, 1 - x, y, d_x)
            got(zz, x, 1 - y, d_y)

            def through_y():
                copy(zz, 1 - x, y, m_.rsend, d_y).start()

            def through_x():
                copy(zz, x, 1 - y, m_.rsend, d_x).start()
            if first_x is True:
                through_y()
            elif first_x is False:
                through_x()
            else:
                pl.when(first_x)(through_y)
                pl.when(jnp.logical_not(first_x))(through_x)

        def diagonal(zz):
            got(zz, 1 - x, 1 - y, d_y)
            plane(zz).start()

        def st0():
            zsend(z, d_zp, m_.zsend)
            pl.when(mid)(lambda: zsend(z, d_zm, m_.zsend))
            copy(z, x, y, m_.xysend, d_x).start()

        def st1():
            got(zp, x, y, d_zp)

            @pl.when(mid)
            def _():
                zsend(zp, d_zm)
                got(zm, x, y, d_zm)
                zsend(zm, d_zp)
            spread(zp)
            got(z, 1 - x, y, d_x)
            copy(z, 1 - x, y, m_.xysend, d_y).start()

        def st2():
            got(zf, x, y, d_zp)
            pl.when(mid)(lambda: zsend(zf, d_zp))
            spread(zf)
            relay(zp, True)
            diagonal(z)

        def st3():
            pl.when(end)(lambda: got(zm, x, y, d_zp))
            spread(zm)
            relay(zf, False)
            diagonal(zp)

        def st4():
            relay(zm, lax.rem(s, 2) == 0)
            diagonal(zf)

        def st5():
            diagonal(zm)

        def st6():
            for zz in (z, zp, zf, zm):
                plane(zz, 1 - c).wait_recv()
        return st0, st1, st2, st3, st4, st5, st6

    def stages_z(b, s):
        def copy(zz, xx, hh, sem, d):
            u = b(zz, xx, c, hh)
            at = 0 if isinstance(hh, slice) else hh
            return pltpu.make_async_remote_copy(src_ref=u, dst_ref=u, send_sem=sem.at[s], recv_sem=m_.recv.at[s, (zz * 2 + xx) * 2 + at], device_id=d, device_id_type=MESH)
        both = slice(None)

        def zsend(zz, xx, d, sem=m_.fsend):
            copy(zz, xx, both, sem, d).start()

        def got(zz, xx, d):
            copy(zz, xx, both, m_.zsend, d).wait_recv()

        def plane(zz, cc=c):
            u = b(zz, both, cc, both)
            return pltpu.make_async_remote_copy(src_ref=u, dst_ref=u, send_sem=m_.csend.at[s], recv_sem=m_.crecv.at[s, zz], device_id=d_c, device_id_type=MESH)

        def own(xx):
            zsend(z, xx, d_zp, m_.zsend)
            pl.when(mid)(lambda: zsend(z, xx, d_zm, m_.zsend))

        def near(xx):
            got(zp, xx, d_zp)

            @pl.when(mid)
            def _():
                zsend(zp, xx, d_zm)
                got(zm, xx, d_zm)
                zsend(zm, xx, d_zp)

        def far(xx):
            got(zf, xx, d_zp)
            pl.when(mid)(lambda: zsend(zf, xx, d_zp))

        def farthest(xx):
            pl.when(end)(lambda: got(zm, xx, d_zp))

        def st0():
            own(x)
            copy(z, x, y, m_.xysend, d_x).start()

        def st1():
            near(x)
            copy(z, 1 - x, y, m_.xysend, d_x).wait_recv()
            copy(z, 1 - x, y, m_.xysend, d_y).start()

        def st2():
            far(x)
            copy(z, 1 - x, 1 - y, m_.xysend, d_y).wait_recv()
            own(1 - x)
            plane(z).start()

        def st3():
            farthest(x)
            near(1 - x)
            plane(zp).start()

        def st4():
            far(1 - x)
            plane(zf).start()

        def st5():
            farthest(1 - x)
            plane(zm).start()

        def st6():
            for zz in (z, zp, zf, zm):
                plane(zz, 1 - c).wait_recv()
        return st0, st1, st2, st3, st4, st5, st6

    def sent_z(s):
        wait_all(o_.w.at[0, 0, 0, 0], m_.xysend.at[s])
        wait_all(many_w(16), m_.csend.at[s])
        pl.when(end)(lambda: wait_all(o_.w.at[0, 0, 0], m_.zsend.at[s]))

        @pl.when(mid)
        def _():
            wait_all(many_w(8), m_.zsend.at[s])
            wait_all(o_.w.at[0, 0:3, :, 0], m_.fsend.at[s])

    def sent(b, s, many):
        wait_all(many(8), m_.xysend.at[s])
        wait_all(many(3), m_.rsend.at[s])
        wait_all(many(16), m_.csend.at[s])
        pl.when(end)(lambda: wait_all(many(1), m_.zsend.at[s]))

        @pl.when(mid)
        def _():
            wait_all(many(2), m_.zsend.at[s])
            wait_all(many(3), m_.fsend.at[s])

    def unit(p):
        return lambda zz, xx, cc, hh: o_.w.at[p, zz, xx, cc, hh]

    def vunit(zz, xx, cc, hh):
        return o_.v.at[zz, xx, cc, hh]

    def many_w(n):
        if n == 8:
            return o_.w.at[0, 0]
        if n == 16:
            return o_.w.at[0, :, :, 0]
        return o_.w.at[0:n, 0, 0, 0, 0]

    def many_v(n):
        if n == 8:
            return o_.v.at[0]
        if n == 16:
            return o_.v.at[:, :, 0]
        return o_.v.at[0:n, 0, 0, 0]


    def load_att(l):
        for cp in matrix_loads(o_.w, 8 * l, 0, t_.wq, m_.wload.at[0]) + matrix_loads(o_.w, 8 * l, 1, t_.wk, m_.wload.at[1]) + matrix_loads(o_.w, 8 * l + 1, 0, t_.wv, m_.wload.at[2]) + matrix_loads(o_.w, 8 * l + 1, 1, t_.wo, m_.wload.at[3]):
            cp.start()

    def load_gated(l, j):
        for cp in matrix_loads(o_.w, 8 * l + 2 + j, 0, t_.wg, m_.wload.at[4]) + matrix_loads(o_.w, 8 * l + 2 + j, 1, t_.wu, m_.wload.at[5]):
            cp.start()

    def load_down(l):
        for s in range(4):
            for h in range(2):
                pltpu.make_async_copy(o_.w.at[8 * l + 6 + s // 2, :, :, :, h, s % 2], t_.wd.at[:, :, :, s, :, pl.ds(384 * h, 384)], m_.wload.at[6]).start()

    def store(i, src, dst, go):
        run(pltpu.make_async_copy(src, dst, m_.store.at[i]), go)

    def per_layer(l, f):
        for n in range(LAYERS):
            @pl.when(l == n)
            def _():
                f(kept[n])

    def vrow(l, n):
        return o_.vec[l, n : n + 1, :]

    def store_att(kl, i, go):
        store(0, t_.q, cols(kl.q, i, 256), go)
        store(1, t_.k, cols(kl.k, i, 256), go)
        store(2, t_.v, cols(kl.v, i, 256), go)
        store(3, t_.pt, kl.pt.at[:, pl.ds(4 * i, 4)], go)
        store(4, t_.at, kl.at.at[pl.ds(pl.multiple_of(256 * i, 256), 256)], go)

        @pl.when(i == 0)
        def _():
            store(5, t_.xt, kl.xt, go)

    def att_task(l, i):
        @pl.when(i == 0)
        def _():
            wait_all(t_.wq, m_.wload.at[0])
            wait_all(t_.wk, m_.wload.at[1])
            wait_all(t_.wv, m_.wload.at[2])
            xb = t_.x[...].astype(BF)
            t_.xb[...] = xb
            t_.xt[...] = xb.T
        xb = t_.xb[...]
        lane = pl.multiple_of(256 * i, 256)
        at = pl.ds(lane, 256)
        t_.q[...] = (mm(xb, t_.wq[:, :, :, :, at].reshape(D, 256)) + o_.vec[l, 0:1, at]).astype(BF)
        t_.k[...] = mm(xb, t_.wk[:, :, :, :, at].reshape(D, 256)).astype(BF)
        t_.v[...] = (mm(xb, t_.wv[:, :, :, :, at].reshape(D, 256)) + o_.vec[l, 1:2, at]).astype(BF)
        for s in range(seqs):
            rows = slice(s * pad, (s + 1) * pad)
            hidden = jnp.where(lax.broadcasted_iota(jnp.int32, (pad, 1), 0) < i_.lens[s], 0.0, NEG)
            for pair in range(2):
                lanes = slice(128 * pair, 128 * pair + 128)
                q2 = t_.q[rows, lanes] * BF(HEAD_DIM ** -0.5)
                ks = halves(t_.k[rows, lanes], 1)
                vs = halves(t_.v[rows, lanes].T, 0)
                total = None
                for h in range(2):
                    slope = i_.slopes[4 * i + 2 * pair + h]
                    sc = mm_nt(ks[h], q2) - slope * t_.dist[...] + hidden
                    e = jnp.exp(sc - jnp.max(sc, axis=0, keepdims=True))
                    p = (e * (1.0 / jnp.sum(e, axis=0, keepdims=True))).astype(BF)
                    t_.pt[s, 2 * pair + h] = p
                    part = mm(vs[h], p)
                    total = part if total is None else total + part
                total = total.astype(BF)
                t_.at[lanes, rows] = total
                t_.att[rows, pl.ds(pl.multiple_of(lane + 128 * pair, 128), 128)] = total.T
        per_layer(l, lambda kl: store_att(kl, i, True))

    def store_ff(kl, j, go):
        store(6, t_.ga, cols(kl.ga, j, 768), go)
        store(7, t_.gb, cols(kl.gb, j, 768), go)
        store(8, t_.ft, kl.ft.at[pl.ds(pl.multiple_of(768 * j, 768), 768)], go)

        @pl.when(j == 0)
        def _():
            store(9, t_.res, kl.r1, go)
            store(10, t_.xt, kl.ht, go)

    def ff_task(l, j):
        @pl.when(j == 0)
        def _():
            wait_all(t_.wo, m_.wload.at[3])
            r1 = t_.x[...] + (mm(t_.att[...], t_.wo[...].reshape(D, D)) + vrow(l, 2))
            t_.res[...] = r1
            h = norm_parts(r1)[0] * vrow(l, 3) + vrow(l, 4)
            t_.h[...] = h
            hb = h.astype(BF)
            t_.hb[...] = hb
            t_.xt[...] = hb.T
        wait_all(t_.wg, m_.wload.at[4])
        wait_all(t_.wu, m_.wload.at[5])
        hb = t_.hb[...]
        g = mm(hb, t_.wg[...].reshape(D, 768))
        u = mm(hb, t_.wu[...].reshape(D, 768))
        cdf = 0.5 + 0.5 * erf(g * math.sqrt(0.5))
        gelu = g * cdf
        slope = cdf + g * (jnp.exp(-0.5 * (g * g)) * (1.0 / math.sqrt(2.0 * math.pi)))
        t_.ga[...] = gelu.astype(BF)
        t_.gb[...] = (slope * u).astype(BF)
        f = (gelu * u).astype(BF)
        t_.f[j] = f
        t_.ft[...] = f.T
        per_layer(l, lambda kl: store_ff(kl, j, True))

    def down_task(l):
        wait_all(t_.wd, m_.wload.at[6])
        total = t_.h[...] + vrow(l, 5)
        for j in range(4):
            total = total + mm(t_.f[j], t_.wd[j].reshape(768, D))
        t_.res[...] = total
        out = norm_parts(total)[0] * vrow(l, 6) + vrow(l, 7)
        t_.x[...] = out
        per_layer(l, lambda kl: store(9, t_.res, kl.r2, True))

        @pl.when(l == LAYERS - 1)
        def _():
            t_.last[...] = out.astype(BF)
            store(11, t_.last, o_.last, True)

    def task(t, att, ff, down):
        l = t // 8
        u = lax.rem(t, 8)
        pl.when(u < 3)(lambda: att(l, jnp.minimum(u, 2)))
        pl.when(jnp.logical_and(u >= 3, u < 7))(lambda: ff(l, jnp.clip(u - 3, 0, 3)))
        pl.when(u == 7)(lambda: down(l))

    def stored(t):
        task(t, lambda l, i: store_att(kept[0], i, False), lambda l, j: store_ff(kept[0], j, False), lambda l: store(9, t_.res, kept[0].r2, False))

    def fetch(t):
        def att(l, i):
            pl.when(i == 0)(lambda: load_att(l))
        task(t, att, load_gated, load_down)


    first_task = 7 * GLAG + 1
    last_round = first_task + 8 * LAYERS
    vst = stages(vunit, PIECES)

    def body(r, carry):
        def at(k):
            p = r - GLAG * k

            @pl.when(jnp.logical_and(p >= 0, p < PIECES))
            def _():
                q = jnp.clip(p, 0, PIECES - 1)
                if k == 0:
                    wait_all(o_.w.at[q, z, x, c], m_.local.at[q])
                pl.when(along_z(q))(lambda: stages_z(unit(q), q)[k]())
                pl.when(jnp.logical_not(along_z(q)))(lambda: stages(unit(q), q)[k]())
        for k in range(7):
            @pl.when(r == GLAG * k)
            def _():
                if k == 0:
                    vplace.wait()
                vst[k]()
        for k in (0, 6, 5, 4, 3, 2, 1):
            at(k)

        @pl.when(r == first_task - 1)
        def _():
            cp = pltpu.make_async_copy(o_.v, t_.vec_in, m_.vload)
            cp.start()
            xload.wait()
            t_.x[...] = t_.last[...].astype(F32)
            keys = lax.broadcasted_iota(jnp.int32, (pad, pad), 0)
            rows = lax.broadcasted_iota(jnp.int32, (pad, pad), 1)
            t_.dist[...] = jnp.abs(keys - rows).astype(F32)
            cp.wait()
            unpack_vectors()
        t = r - first_task

        @pl.when(t >= 1)
        def _():
            stored(jnp.clip(t - 1, 0, 8 * LAYERS - 1))

        @pl.when(t >= 0)
        def _():
            task(jnp.clip(t, 0, 8 * LAYERS - 1), att_task, ff_task, down_task)

        @pl.when(jnp.logical_and(t >= -1, t + 1 < 8 * LAYERS))
        def _():
            fetch(jnp.clip(t + 1, 0, 8 * LAYERS - 1))
        return carry

    def unpack_vectors():
        for l in range(LAYERS):
            parts = [t_.vec_in[b // 4, (b // 2) % 2, b % 2, l].astype(F32)[:, 0:48] for b in range(16)]
            o_.vec[l] = jnp.concatenate(parts, axis=1)
    lax.fori_loop(0, last_round, body, 0)
    stored(8 * LAYERS - 1)
    store(11, t_.last, o_.last, False)

    def finish(p, carry):
        pl.when(along_z(p))(lambda: sent_z(p))
        pl.when(jnp.logical_not(along_z(p)))(lambda: sent(unit(p), p, many_w))
        return carry
    lax.fori_loop(0, PIECES, finish, 0)
    sent(vunit, PIECES, many_v)


def forward_all(lengths, slopes, x, shards, vectors):
    rows = x.shape[0]
    seqs = lengths.shape[0]
    pad = rows // seqs
    hbm = pl.BlockSpec(memory_space=pltpu.HBM)
    vmem = pl.BlockSpec(memory_space=pltpu.VMEM)
    smem = pl.BlockSpec(memory_space=pltpu.SMEM)
    S = jax.ShapeDtypeStruct
    act = lambda n, t: S((rows, n), t)
    one = [act(D, F32), act(D, F32), act(FF, BF), act(FF, BF), act(D, BF), act(D, BF), act(D, BF), S((seqs, HEADS, pad, pad), BF), S((FF, rows), BF), S((D, rows), BF), S((D, rows), BF), S((D, rows), BF)]
    out = [S((PIECES, 4, 2, 2, 2, 2, 48, 384), BF), S((4, 2, 2, 2, 8, 128), BF), S((LAYERS, 8, D), F32), act(D, BF)] + one * LAYERS
    v = pltpu.VMEM
    dma = pltpu.SemaphoreType.DMA
    mat = v((4, 2, 2, 48, D), BF)
    n = PIECES + 1
    scratch = [
        v((rows, D), F32), v((rows, D), BF), v((pad, pad), F32), v((rows, 256), BF), v((rows, 256), BF), v((rows, 256), BF), v((rows, D), BF),
        v((seqs, 4, pad, pad), BF), v((256, rows), BF), v((D, rows), BF), mat, mat, mat, mat, mat, mat, v((4, 2, 2, 4, 48, D), BF),
        v((rows, D), F32), v((rows, D), BF), v((4, rows, 768), BF), v((rows, 768), BF), v((rows, 768), BF), v((768, rows), BF), v((rows, D), F32), v((rows, D), BF),
        v((2, 8, 128), BF), v((2, 8, 128), F32), v((4, 2, 2, 2, 8, 128), BF),
        dma((PIECES,)), dma((n,)), dma((n,)), dma((n,)), dma((n,)), dma((n,)), dma((n, 16)), dma((n, 4)), dma((2,)), dma, dma, dma((7,)), dma((12,)),
    ]
    res = pl.pallas_call(
        forward_kernel, out_shape=out,
        in_specs=[smem, smem, hbm] + [hbm] * 4 + [vmem] * 8,
        out_specs=[hbm, hbm, vmem, hbm] + [hbm] * (12 * LAYERS),
        scratch_shapes=scratch,
        compiler_params=pltpu.CompilerParams(collective_id=0, has_side_effects=True, vmem_limit_bytes=60 * 2**20), name="gather_forward",
    )(lengths, slopes, x, *shards, *vectors)
    return res[0], res[2], res[3], [res[4 + 12 * l : 16 + 12 * l] for l in range(LAYERS)]


NPIECE = 33
LAG = 2
SLOTS = 16


STEPS = (0, 1, 3, 5, 7, 9, 11, 13)
STEPS_Z = (0, 1, 4, 7, 9, 11, 12, 13)


def reduce_z(p):
    return lax.rem(p, 4) == 1


def piece_first_x(p):
    others = p - (p + 2) // 4
    return jnp.logical_or(reduce_z(p), lax.rem(others * 5, 8) < 5)


def add_into(dst, src):
    dst[...] = (dst[...].astype(F32) + src[...].astype(F32)).astype(BF)


GRADS = ("dm", "dg", "du", "da", "dq", "dk", "dv")


def backward_kernel(*refs):
    take = taker(refs)
    i_ = take("cot", "vec")
    cot, vec = i_.cot, i_.vec
    kept = [take(*KEPT) for _ in range(LAYERS)]
    w = take("w").w
    o = take("qkv", "out", "gated", "down", "vec", "dx")
    g = take(*GRADS)
    s = take("lbuf", "rbuf", "sbuf", "own", "stage", "r0v", "h1v", "h2v", "zav", "zbv", "yfv", "vall")
    c_ = take("r0", "h1", "h2", "za", "zb", "yf", "zza", "zzb")
    t_ = take("acc", "res", "wd", "wg", "wu", "ga", "gb", "wo", "dm", "dg", "du", "da", "datt", "q", "k", "v", "pt", "wq", "wk", "wv", "dq", "dk", "dv", "gv", "cot")
    m_ = take("lsem", "rsem", "send", "recv", "out", "vload", "fsem", "asem", "osem")
    pad = kept[0].pt.shape[-1]
    seqs = kept[0].pt.shape[0]

    z, x, y, c = place()
    zp = z + 1 - 2 * lax.rem(z, 2)
    zm = 3 - z
    mid = jnp.logical_and(z >= 1, z <= 2)
    end = jnp.logical_not(mid)
    d_zp, d_zm = dev(zp, x, y, c), dev(zm, x, y, c)
    d_x, d_y, d_c = dev(z, 1 - x, y, c), dev(z, x, 1 - y, c), dev(z, x, y, 1 - c)
    bar = pltpu.get_barrier_semaphore()
    for d in (d_zp, d_zm, d_x, d_y, d_c):
        pl.semaphore_signal(bar, 1, device_id=d, device_id_type=MESH)
    pl.semaphore_wait(bar, 5)
    NP = NPIECE - 1


    def load_ff(l, j, go):
        def one(i, src, dst):
            run(pltpu.make_async_copy(src, dst, m_.fsem.at[i]), go)
        if go:
            for n in range(4):
                for h in range(2):
                    one(0, w.at[8 * l + 6 + n // 2, j, :, :, h, n % 2], t_.wd.at[:, :, n, :, pl.ds(384 * h, 384)])
            for cp in matrix_loads(w, 8 * l + 2 + j, 0, t_.wg, m_.fsem.at[1]) + matrix_loads(w, 8 * l + 2 + j, 1, t_.wu, m_.fsem.at[2]):
                cp.start()
        else:
            wait_all(t_.wd, m_.fsem.at[0])
            wait_all(t_.wg, m_.fsem.at[1])
            wait_all(t_.wu, m_.fsem.at[2])

        def acts(kl):
            one(3, cols(kl.ga, j, 768), t_.ga)
            one(4, cols(kl.gb, j, 768), t_.gb)

            @pl.when(j == 0)
            def _():
                one(5, kl.r2, t_.res)

            @pl.when(j == 3)
            def _():
                one(5, kl.r1, t_.res)
        if go:
            for i in range(LAYERS):
                @pl.when(l == i)
                def _():
                    acts(kept[i])
        else:
            one(3, cols(kept[0].ga, j, 768), t_.ga)
            one(4, cols(kept[0].gb, j, 768), t_.gb)

            @pl.when(jnp.logical_or(j == 0, j == 3))
            def _():
                one(5, kept[0].r1, t_.res)

        @pl.when(j == 3)
        def _():
            if go:
                for cp in matrix_loads(w, 8 * l + 1, 1, t_.wo, m_.fsem.at[6]):
                    cp.start()
            else:
                wait_all(t_.wo, m_.fsem.at[6])

    def load_att(l, i, go):
        def one(n, src, dst):
            run(pltpu.make_async_copy(src, dst, m_.asem.at[n]), go)

        def acts(kl):
            one(0, cols(kl.q, i, 256), t_.q)
            one(1, cols(kl.k, i, 256), t_.k)
            one(2, cols(kl.v, i, 256), t_.v)
            one(3, kl.pt.at[:, pl.ds(4 * i, 4)], t_.pt)
        if go:
            for n in range(LAYERS):
                @pl.when(l == n)
                def _():
                    acts(kept[n])
        else:
            acts(kept[0])
        @pl.when(i == 0)
        def _():
            for n, dst in enumerate((t_.wq, t_.wk, t_.wv)):
                if go:
                    for cp in matrix_loads(w, 8 * l + n // 2, n % 2, dst, m_.asem.at[4 + n]):
                        cp.start()
                else:
                    wait_all(dst, m_.asem.at[4 + n])

    def ff_task(l, j):
        load_ff(l, j, False)

        @pl.when(j == 0)
        def _():
            dy = t_.acc[...]
            n, rstd = norm_parts(t_.res[...])
            dr2 = norm_back(dy, vec[l, 6:7, :], n, rstd)
            t_.acc[...] = dr2
            dm = dr2.astype(BF)
            t_.dm[...] = dm
            t_.gv[l, 5:6, :] = colsum(dm.astype(F32))
            t_.gv[l, 6:7, :] = colsum(dy * n)
            t_.gv[l, 7:8, :] = colsum(dy)
        df = mm_nt(t_.dm[...], t_.wd[...].reshape(768, D))
        dg = (df * t_.gb[...].astype(F32)).astype(BF)
        du = (df * t_.ga[...].astype(F32)).astype(BF)
        t_.dg[...] = dg
        t_.du[...] = du
        t_.acc[...] += mm_nt(dg, t_.wg[...].reshape(D, 768)) + mm_nt(du, t_.wu[...].reshape(D, 768))

        @pl.when(j == 3)
        def _():
            dh = t_.acc[...]
            n, rstd = norm_parts(t_.res[...])
            dr1 = norm_back(dh, vec[l, 3:4, :], n, rstd)
            t_.acc[...] = dr1
            da = dr1.astype(BF)
            t_.da[...] = da
            t_.gv[l, 2:3, :] = colsum(da.astype(F32))
            t_.gv[l, 3:4, :] = colsum(dh * n)
            t_.gv[l, 4:5, :] = colsum(dh)
            datt = mm_nt(da, t_.wo[...].reshape(D, D)).astype(BF)
            for i in range(3):
                t_.datt[i] = datt[:, 256 * i : 256 * i + 256]
        store_ff(l, j, True)

        @pl.when(j < 3)
        def _():
            load_ff(l, j + 1, True)

        @pl.when(j == 3)
        def _():
            load_att(l, 0, True)

    def store_ff(l, j, go):
        def one(i, src, dst):
            run(pltpu.make_async_copy(src, dst, m_.osem.at[i]), go)
        one(0, t_.dg, cols(g.dg.at[l], j, 768))
        one(1, t_.du, cols(g.du.at[l], j, 768))

        @pl.when(j == 0)
        def _():
            one(2, t_.dm, g.dm.at[l])

        @pl.when(j == 3)
        def _():
            one(3, t_.da, g.da.at[l])

    def att_task(l, i):
        load_att(l, i, False)
        scale = HEAD_DIM ** -0.5
        first = lax.broadcasted_iota(jnp.int32, (pad, 128), 1) < HEAD_DIM
        for sq in range(seqs):
            rows = slice(sq * pad, (sq + 1) * pad)
            for pair in range(2):
                lanes = slice(128 * pair, 128 * pair + 128)
                q2 = t_.q[rows, lanes]
                d2 = t_.datt[i, rows, lanes]
                vs = halves(t_.v[rows, lanes], 1)
                ks = halves(t_.k[rows, lanes].T, 0)
                dv, dk, dq = [], [], None
                for h in range(2):
                    pb = t_.pt[sq, 2 * pair + h]
                    p = pb.astype(F32)
                    dp = mm_nt(vs[h], d2)
                    ds = (p * (dp - jnp.sum(dp * p, axis=0, keepdims=True))).astype(BF)
                    dv.append(mm(pb, d2))
                    dk.append(mm(ds, q2))
                    part = mm(ks[h], ds)
                    dq = part if dq is None else dq + part
                t_.dv[rows, lanes] = jnp.where(first, dv[0], dv[1]).astype(BF)
                t_.dk[rows, lanes] = (jnp.where(first, dk[0], dk[1]) * scale).astype(BF)
                t_.dq[rows, lanes] = (dq * scale).astype(BF).T
        dq, dk, dv = t_.dq[...], t_.dk[...], t_.dv[...]
        at = pl.ds(pl.multiple_of(i * 256, 256), 256)
        t_.gv[l, 0:1, at] = colsum(dq.astype(F32))
        t_.gv[l, 1:2, at] = colsum(dv.astype(F32))
        t_.acc[...] += (
            mm_nt(dq, t_.wq[:, :, :, :, at].reshape(D, 256)) + mm_nt(dk, t_.wk[:, :, :, :, at].reshape(D, 256)) + mm_nt(dv, t_.wv[:, :, :, :, at].reshape(D, 256))
        )
        store_att(l, i, True)

        @pl.when(i < 2)
        def _():
            load_att(l, i + 1, True)

        @pl.when(jnp.logical_and(i == 2, l > 0))
        def _():
            load_ff(jnp.maximum(l - 1, 0), 0, True)

        @pl.when(jnp.logical_and(i == 2, l == 0))
        def _():
            t_.cot[...] = t_.acc[...].astype(BF)
            pltpu.make_async_copy(t_.cot, o.dx, m_.osem.at[7]).start()

    def store_att(l, i, go):
        def one(n, src, dst):
            run(pltpu.make_async_copy(src, dst, m_.osem.at[n]), go)
        one(4, t_.dq, cols(g.dq.at[l], i, 256))
        one(5, t_.dk, cols(g.dk.at[l], i, 256))
        one(6, t_.dv, cols(g.dv.at[l], i, 256))

    def task(t, ff, att):
        l = LAYERS - 1 - t // 7
        u = lax.rem(t, 7)

        @pl.when(u < 4)
        def _():
            ff(l, jnp.minimum(u, 3))

        @pl.when(u >= 4)
        def _():
            att(l, jnp.clip(u - 4, 0, 2))


    def load(p, go):
        q = lax.rem(p, 16)
        n = lax.rem(p, 2)
        layer = LAYERS - 1 - p // 16

        def left(ref, sub=None):
            for cc in range(2):
                src = ref.at[:, cc] if sub is None else ref.at[:, cc, sub]
                run(pltpu.make_async_copy(src, s.lbuf.at[n, cc], m_.lsem.at[n, cc]), go)

        def right(ref, col=None):
            src = ref.at[layer] if col is None else cols(ref.at[layer], jnp.clip(col, 0, 3), 768)
            run(pltpu.make_async_copy(src, s.rbuf.at[n], m_.rsem.at[n]), go)
        if not go:
            left(kept[0].ht)
            right(g.dm)
            return
        for l in range(LAYERS):
            here = layer == l
            kl = kept[l]

            @pl.when(jnp.logical_and(here, q < 4))
            def _():
                left(kl.ft, jnp.minimum(q, 3))

            @pl.when(jnp.logical_and(here, jnp.logical_and(q >= 4, q < 12)))
            def _():
                left(kl.ht)

            @pl.when(jnp.logical_and(here, q == 12))
            def _():
                left(kl.at)

            @pl.when(jnp.logical_and(here, q > 12))
            def _():
                left(kl.xt)

        @pl.when(q < 4)
        def _():
            right(g.dm)

        @pl.when(jnp.logical_and(q >= 4, q < 8))
        def _():
            right(g.dg, q - 4)

        @pl.when(jnp.logical_and(q >= 8, q < 12))
        def _():
            right(g.du, q - 8)
        for i, d in enumerate((g.da, g.dq, g.dk, g.dv)):
            @pl.when(q == 12 + i)
            def _():
                right(d)

    def rcopy(p, e, src, dst, d):
        return pltpu.make_async_remote_copy(src_ref=src, dst_ref=dst, send_sem=m_.send.at[p, e], recv_sem=m_.recv.at[p, e], device_id=d, device_id_type=MESH)

    def product(n, cc, dst):
        for i in range(4):
            v = mm(s.lbuf[n, cc, 2 * i : 2 * i + 2].reshape(96, 512), s.rbuf[n]).astype(BF)
            v = v.reshape(2, 48, 768)
            dst[i, :, 0] = v[:, :, :384]
            dst[i, :, 1] = v[:, :, 384:]

    def c_copy(p, n):
        return rcopy(p, 0, s.sbuf.at[n], c_.r0.at[lax.rem(p, SLOTS)], d_c)

    def s0(p):
        n = lax.rem(p, 2)
        load(p, False)

        @pl.when(p >= 2)
        def _():
            c_copy(jnp.maximum(p - 2, 0), n).wait_send()
        product(n, 1 - c, s.sbuf.at[n])
        c_copy(p, n).start()
        product(n, c, s.own.at[lax.rem(p, LAG + 1)])

        @pl.when(p + 1 < NP)
        def _():
            load(jnp.minimum(p + 1, NP - 1), True)
    small = Group(("r0", "h1", "h2", "za", "zb", "yf"), (s.r0v, s.h1v, s.h2v, s.zav, s.zbv, s.yfv))
    zlo = jnp.where(z == 1, 1, 0)
    elo = jnp.where(z == 0, 1, 0)
    mlo = jnp.where(z == 1, 2, 0)
    rlo = jnp.where(z == 1, 0, 2)

    def steps(b, p, i, my):
        fx = piece_first_x(p)
        fy = jnp.logical_not(fx)

        def hop1(go):
            a = rcopy(p, 1, b.r0.at[i, :, 1 - x], b.h1.at[i], d_x)
            if go == "start":
                pl.when(fx)(a.start)
                pl.when(fy)(rcopy(p, 1, b.r0.at[i, :, :, 1 - y], b.h1.at[i], d_y).start)
            elif go == "recv":
                a.wait_recv()
            else:
                a.wait_send()

        def hop2(go):
            a = rcopy(p, 2, b.h1.at[i, :, 1 - y], b.h2.at[i], d_y)
            if go == "start":
                pl.when(fx)(a.start)
                pl.when(fy)(rcopy(p, 2, b.h1.at[i, :, 1 - x], b.h2.at[i], d_x).start)
            elif go == "recv":
                a.wait_recv()
            else:
                a.wait_send()

        def z1():
            return rcopy(p, 3, b.h2.at[i, pl.ds(elo, 3)], b.za.at[i], d_zp)

        def z2():
            return rcopy(p, 4, b.h2.at[i, pl.ds(mlo, 2)], b.zb.at[i], d_zm)

        def z3():
            return rcopy(p, 5, b.h2.at[i, zp], b.zb.at[i, 0], d_zp)

        def y1():
            return rcopy(p, 6, b.h2.at[i, z], b.yf.at[i], d_y)

        def s1():
            rcopy(p, 0, b.r0.at[i], b.r0.at[i], d_c).wait_recv()
            for k in range(4):
                add_into(b.r0.at[i, k], my.at[k])
            hop1("start")

        def s2():
            hop1("recv")
            for k in range(4):
                @pl.when(fx)
                def _():
                    add_into(b.h1.at[i, k], b.r0.at[i, k, x])

                @pl.when(fy)
                def _():
                    add_into(b.h1.at[i, k], b.r0.at[i, k, :, y])
            hop2("start")

        def s3():
            hop1("send")
            hop2("recv")
            t = jnp.where(fx, y, x)
            for k in range(4):
                add_into(b.h2.at[i, k], b.h1.at[i, k, t])
            pl.when(end)(z1().start)

        def s4():
            hop2("send")

            @pl.when(mid)
            def _():
                z1().wait_recv()
                for k in range(3):
                    add_into(b.h2.at[i, zlo + k], b.za.at[i, k])
                z2().start()

        def s5():
            pl.when(end)(z1().wait_send)

            @pl.when(mid)
            def _():
                z2().wait_recv()
                for k in range(2):
                    add_into(b.h2.at[i, rlo + k], b.zb.at[i, k])
                z3().start()

        def s6():
            pl.when(mid)(z2().wait_send)

            @pl.when(end)
            def _():
                z3().wait_recv()
                add_into(b.h2.at[i, z], b.zb.at[i, 0])
            y1().start()

        def s7():
            pl.when(mid)(z3().wait_send)
            y1().wait_send()
            y1().wait_recv()
        return s1, s2, s3, s4, s5, s6, s7

    def steps_z(p, i, my):
        b = c_
        fx = piece_first_x(p)
        iz = lax.rem(p // 4, SLOTS // 4)

        def hop1():
            return rcopy(p, 1, b.r0.at[i, z, 1 - x], b.h1.at[i, 0], d_x)

        def hop2():
            return rcopy(p, 2, b.h1.at[i, 0, 1 - y], b.h2.at[i, z], d_y)

        def z1():
            return rcopy(p, 3, b.r0.at[i, pl.ds(elo, 3)], b.zza.at[iz], d_zp)

        def z2():
            return rcopy(p, 4, b.r0.at[i, pl.ds(mlo, 2)], b.zzb.at[iz], d_zm)

        def z3():
            return rcopy(p, 5, b.r0.at[i, zp], b.zzb.at[iz, 0], d_zp)

        def y1():
            return rcopy(p, 6, b.h2.at[i, z], b.yf.at[i], d_y)

        def s1():
            rcopy(p, 0, b.r0.at[i], b.r0.at[i], d_c).wait_recv()
            for k in range(4):
                add_into(b.r0.at[i, k], my.at[k])
            pl.when(end)(z1().start)

        def s2():
            @pl.when(mid)
            def _():
                z1().wait_recv()
                for k in range(3):
                    add_into(b.r0.at[i, zlo + k], b.zza.at[iz, k])
                z2().start()

        def s3():
            pl.when(end)(z1().wait_send)

            @pl.when(mid)
            def _():
                z2().wait_recv()
                for k in range(2):
                    add_into(b.r0.at[i, rlo + k], b.zzb.at[iz, k])
                z3().start()

        def s4():
            pl.when(mid)(z2().wait_send)

            @pl.when(end)
            def _():
                z3().wait_recv()
                add_into(b.r0.at[i, z], b.zzb.at[iz, 0])
            hop1().start()

        def s5():
            pl.when(mid)(z3().wait_send)
            hop1().wait_recv()
            add_into(b.h1.at[i, 0], b.r0.at[i, z, x])
            hop2().start()

        def s6():
            hop1().wait_send()
            hop2().wait_recv()
            add_into(b.h2.at[i, z], b.h1.at[i, 0, y])
            y1().start()

        def s7():
            hop2().wait_send()
            y1().wait_send()
            y1().wait_recv()
        return s1, s2, s3, s4, s5, s6, s7

    def out_copy(p, n, go):
        q = lax.rem(p, 16)
        layer = LAYERS - 1 - p // 16

        def one(dst):
            run(pltpu.make_async_copy(s.stage.at[n], dst, m_.out.at[n]), go)
        if not go:
            one(o.out.at[0])
            return

        @pl.when(q < 4)
        def _():
            one(o.down.at[layer, pl.ds(pl.multiple_of(jnp.minimum(q, 3) * 48, 48), 48)])

        @pl.when(jnp.logical_and(q >= 4, q < 12))
        def _():
            one(cols(o.gated.at[layer], jnp.clip(q - 4, 0, 7), 768))

        @pl.when(q == 12)
        def _():
            one(o.out.at[layer])

        @pl.when(q > 12)
        def _():
            one(cols(o.qkv.at[layer], jnp.clip(q - 13, 0, 2), 768))

    def write(p):
        n = lax.rem(p, 2)

        @pl.when(p >= 2)
        def _():
            out_copy(p, n, False)
        i = lax.rem(p, SLOTS)
        a = c_.h2[i, z].astype(F32)
        b = c_.yf[i].astype(F32)

        @pl.when(y == 0)
        def _():
            s.stage[n, :, :384] = a
            s.stage[n, :, 384:] = b

        @pl.when(y == 1)
        def _():
            s.stage[n, :, :384] = b
            s.stage[n, :, 384:] = a
        out_copy(p, n, True)


    vp = NP
    vc = rcopy(vp, 0, s.vall.at[1 - c], s.r0v.at[0], d_c)
    vsteps = steps(small, vp, 0, s.vall.at[c])
    VSTART = 27

    def pack_vectors():
        for l in range(LAYERS):
            v = jnp.concatenate([t_.gv[l], jnp.zeros((120, D), F32)], axis=0).T.astype(BF)
            for k in range(16):
                s.vall[k % 2, k // 4, (k // 2) % 2, l] = v[48 * k : 48 * k + 48]
        vc.start()


    top = LAYERS - 1
    first = pltpu.make_async_copy(cot, t_.cot, m_.vload)
    first.start()
    load_ff(top, 0, True)
    first.wait()
    t_.acc[...] = t_.cot[...].astype(F32)
    ff_task(top, 0)
    store_ff(top, 0, False)
    load(0, True)

    def body(r, carry):
        def at(k, off, f, kind=None):
            p = r - off[k]
            q = jnp.clip(p, 0, NP - 1)
            here = jnp.logical_and(p >= 0, p < NP)
            if kind is not None:
                here = jnp.logical_and(here, reduce_z(q) == kind)

            @pl.when(here)
            def _():
                f(q)

        def st(k, kind):
            def f(p):
                own = s.own.at[lax.rem(p, LAG + 1)]
                i = lax.rem(p, SLOTS)
                (steps_z(p, i, own) if kind else steps(c_, p, i, own))[k - 1]()
                if k == 7:
                    write(p)
            return f
        even = lax.rem(r, 2) == 0

        @pl.when(jnp.logical_and(even, jnp.logical_and(r >= 2, r < 28)))
        def _():
            task(jnp.clip(r // 2, 1, 13), lambda l, j: store_ff(l, j, False), lambda l, i: store_att(l, i, False))
        for k in range(1, 8):
            pl.when(r == VSTART + STEPS[k])(vsteps[k - 1])
        at(0, STEPS, s0)
        for k in range(7, 0, -1):
            at(k, STEPS_Z, st(k, True), True)
            at(k, STEPS, st(k, False), False)
        pl.when(r == VSTART)(pack_vectors)

        @pl.when(jnp.logical_and(jnp.logical_not(even), r < 26))
        def _():
            task(jnp.clip((r + 1) // 2, 1, 13), ff_task, att_task)
        return carry
    lax.fori_loop(0, NP + STEPS[7], body, 0)

    for p in (NP - 2, NP - 1):
        c_copy(p, p % 2).wait_send()
        out_copy(p, p % 2, False)
    vc.wait_send()
    pltpu.make_async_copy(t_.cot, o.dx, m_.osem.at[7]).wait()
    va, vb = s.h2v[0, z].astype(F32), s.yfv[0].astype(F32)
    o.vec[0] = jnp.where(y == 0, va, vb)
    o.vec[1] = jnp.where(y == 0, vb, va)


def backward_all(cot, vec, kept, w):
    rows = cot.shape[0]
    hbm = pl.BlockSpec(memory_space=pltpu.HBM)
    vmem = pl.BlockSpec(memory_space=pltpu.VMEM)
    kept = [tuple(k[:8]) + (k[8].reshape(8, 2, 4, 48, rows),) + tuple(a.reshape(8, 2, 48, rows) for a in k[9:]) for k in kept]
    act = lambda c, t: jax.ShapeDtypeStruct((rows, c), t)
    out = [
        jax.ShapeDtypeStruct((LAYERS, 48, 3 * D), F32), jax.ShapeDtypeStruct((LAYERS, 48, D), F32),
        jax.ShapeDtypeStruct((LAYERS, 48, 2 * FF), F32), jax.ShapeDtypeStruct((LAYERS, 192, D), F32),
        jax.ShapeDtypeStruct((2, 48, 128), F32), act(D, BF),
    ]
    both = lambda c: jax.ShapeDtypeStruct((LAYERS, rows, c), BF)
    scratch_out = [both(D), both(FF), both(FF), both(D), both(D), both(D), both(D)]
    seqs, _, pad, _ = kept[0][7].shape
    v = pltpu.VMEM
    dma = pltpu.SemaphoreType.DMA
    mat = v((4, 2, 2, 48, D), BF)
    n = SLOTS
    scratch = [
        v((2, 2, 8, 48, rows), BF), v((2, rows, 768), BF), v((2, 4, 2, 2, 48, 384), BF), v((LAG + 1, 4, 2, 2, 48, 384), BF), v((2, 48, 768), F32),
        v((1, 4, 2, 2, 48, 128), BF), v((1, 4, 2, 48, 128), BF), v((1, 4, 48, 128), BF),
        v((1, 3, 48, 128), BF), v((1, 2, 48, 128), BF), v((1, 48, 128), BF), v((2, 4, 2, 2, 48, 128), BF),
        v((n, 4, 2, 2, 48, 384), BF), v((n, 4, 2, 48, 384), BF), v((n, 4, 48, 384), BF), v((n, 3, 48, 384), BF), v((n, 2, 48, 384), BF), v((n, 48, 384), BF), v((n // 4, 3, 2, 2, 48, 384), BF), v((n // 4, 2, 2, 2, 48, 384), BF),
        v((rows, D), F32), v((rows, D), F32), v((2, 2, 4, 48, D), BF), mat, mat, v((rows, 768), BF), v((rows, 768), BF), mat,
        v((rows, D), BF), v((rows, 768), BF), v((rows, 768), BF), v((rows, D), BF), v((3, rows, 256), BF),
        v((rows, 256), BF), v((rows, 256), BF), v((rows, 256), BF), v((seqs, 4, pad, pad), BF), mat, mat, mat,
        v((rows, 256), BF), v((rows, 256), BF), v((rows, 256), BF), v((LAYERS, 8, D), F32), v((rows, D), BF),
        dma((2, 2)), dma((2,)), dma((NPIECE, 7)), dma((NPIECE, 7)), dma((2,)), dma, dma((7,)), dma((7,)), dma((8,)),
    ]
    res = pl.pallas_call(
        backward_kernel, out_shape=out + scratch_out,
        in_specs=[hbm, vmem] + [hbm] * 25,
        out_specs=[hbm] * 4 + [vmem] + [hbm] * 8,
        scratch_shapes=scratch,
        compiler_params=pltpu.CompilerParams(collective_id=1, has_side_effects=True, vmem_limit_bytes=62 * 2**20), name="backward_reduce",
    )(cot, vec, *kept[0], *kept[1], w)
    return res[:4], res[4], res[5]


def forward_plain(seq_lengths, slopes, x, shards, vectors):
    mats = [lax.all_gather(w, "fsdp", axis=1, tiled=True) for w in shards]
    vec = lax.all_gather(jnp.stack(vectors, axis=1), "fsdp", axis=2, tiled=True).astype(F32)
    wq, wo, wg, wd = mats
    kept = []
    for l in range(LAYERS):
        q, k, v, att, pt, xt, at = attention_forward(l, seq_lengths, slopes, x, wq, vec)
        out_dtype = BF if l == LAYERS - 1 else F32
        r1, r2, ga, gb, ft, ht, x = ff_forward(l, att, x, wo, wg, wd, vec, out_dtype)
        kept.append((r1, r2, ga, gb, q, k, v, pt, ft, ht, at, xt))
    return mats, vec, x, kept


def backward_plain(dy, vec, kept, mats):
    wq, wo, wg, wd = mats

    def one(g, dim):
        part = lax.psum_scatter(g.astype(BF), "fsdp", scatter_dimension=dim, tiled=True)
        return lax.psum(part, "dp").astype(F32)
    sums, vecs = [None] * LAYERS, [None] * LAYERS
    for l in reversed(range(LAYERS)):
        r1, r2, ga, gb, q, k, v, pt, ft, ht, at, xt = kept[l]
        dm, dg, du, dr1, da, datt, gv = ff_backward(l, dy, r1, r2, ga, gb, wo, wg, wd, vec)
        dq, dk, dv, dy, gbias = attention_backward(l, datt, q, k, v, pt, wq, dr1, BF if l == 0 else F32)
        pairs = ((xt, jnp.concatenate([dq, dk, dv], axis=1)), (at, da), (ht, jnp.concatenate([dg, du], axis=1)), (ft, dm))
        sums[l] = [one(mm(a, b), 0) for a, b in pairs]
        vecs[l] = gv + gbias
    return [jnp.stack(m) for m in zip(*sums)], one(jnp.stack(vecs), 2), dy


def per_device(fast, inputs, lengths, cotangent, w_qkv, q_bias, v_bias, w_out, b_out, gain_one, shift_one, w_gated, w_down, b_down, gain_two, shift_two):
    shards = (w_qkv, w_out, w_gated, w_down)
    vectors = (q_bias, v_bias, b_out, gain_one, shift_one, b_down, gain_two, shift_two)
    seq_lengths = lengths.reshape(-1)
    slopes = jnp.array(slopes_list(HEADS), F32)
    x = inputs.reshape(-1, D)
    dy = cotangent.reshape(-1, D)
    if fast:
        w, vec, x, kept = forward_all(seq_lengths, slopes, x, shards, vectors)
        m, packed, dx = backward_all(dy, vec, kept, w)
        vs = packed[:, :, :8].transpose(0, 2, 1)
    else:
        mats, vec, x, kept = forward_plain(seq_lengths, slopes, x, shards, vectors)
        m, vs, dx = backward_plain(dy, vec, kept, mats)
    return (
        x.reshape(inputs.shape), dx.reshape(inputs.shape), m[0], vs[:, 0], vs[:, 1], m[1], vs[:, 2], vs[:, 3], vs[:, 4], m[2], m[3], vs[:, 5], vs[:, 6], vs[:, 7],
    )


def solution(mesh):
    placed = (
        P(None, ("dp", "fsdp"), None, None),
        P(None, ("dp", "fsdp")),
        P(None, ("dp", "fsdp"), None, None),
        P(None, "fsdp", None),
        P(None, "fsdp"),
        P(None, "fsdp"),
        P(None, "fsdp", None),
        P(None, "fsdp"),
        P(None, "fsdp"),
        P(None, "fsdp"),
        P(None, "fsdp", None),
        P(None, "fsdp", None),
        P(None, "fsdp"),
        P(None, "fsdp"),
        P(None, "fsdp"),
    )
    return jax.shard_map(
        functools.partial(per_device, dict(mesh.shape) == {"dp": 2, "fsdp": 16}),
        mesh=mesh,
        in_specs=placed,
        out_specs=(
            P(None, ("dp", "fsdp"), None, None),
            P(None, ("dp", "fsdp"), None, None),
            P(None, "fsdp", None),
            P(None, "fsdp"),
            P(None, "fsdp"),
            P(None, "fsdp", None),
            P(None, "fsdp"),
            P(None, "fsdp"),
            P(None, "fsdp"),
            P(None, "fsdp", None),
            P(None, "fsdp", None),
            P(None, "fsdp"),
            P(None, "fsdp"),
            P(None, "fsdp"),
        ),
        check_vma=False,
    )
```

```python
import functools
import math

import jax
import jax.numpy as jnp
from jax import lax
from jax.experimental import pallas as pl
from jax.experimental.pallas import tpu as pltpu
from jax.sharding import PartitionSpec as P

MESH = pl.DeviceIdType.MESH

BF = jnp.bfloat16
F32 = jnp.float32
D, HEADS, HEAD_DIM, FF, LAYERS = 768, 12, 64, 3072, 2
EPS = 1e-12
NEG = -1e30
NT = (((1,), (1,)), ((), ()))


def slopes_list(heads_count):
    nearest = 2 ** int(math.floor(math.log2(heads_count)))
    leading = [2.0 ** (-8.0 * (number + 1) / nearest) for number in range(nearest)]
    trailing = [2.0 ** (-8.0 * (number + 1) / (2 * nearest)) for number in range(2 * nearest)][0::2]
    return leading + trailing[: heads_count - nearest]


def mm(a, b):
    return jnp.dot(a, b, preferred_element_type=F32)


def mm_nt(a, b):
    return lax.dot_general(a, b, NT, preferred_element_type=F32)


def erf(x):
    return lax.erf(x)


def norm_parts(r):
    cent = r - jnp.mean(r, axis=-1, keepdims=True)
    rstd = lax.rsqrt(jnp.mean(cent * cent, axis=-1, keepdims=True) + EPS)
    return cent * rstd, rstd


def norm_back(dy, gain, n, rstd):
    dn = dy * gain
    return rstd * (dn - jnp.mean(dn, axis=-1, keepdims=True) - n * jnp.mean(dn * n, axis=-1, keepdims=True))


def halves(v, axis):
    first = lax.broadcasted_iota(jnp.int32, v.shape, axis) < HEAD_DIM
    zero = jnp.zeros_like(v)
    return jnp.where(first, v, zero), jnp.where(first, zero, v)


def attention_kernel(len_ref, slope_ref, x_ref, wq_ref, wk_ref, wv_ref, vec_ref, q_ref, k_ref, v_ref, att_ref, pt_ref, xt_ref, at_ref, xb_ref, dist_ref):
    i = pl.program_id(0)
    seqs, pad = pt_ref.shape[0], pt_ref.shape[-1]

    @pl.when(i == 0)
    def _():
        xb = x_ref[...].astype(BF)
        xb_ref[...] = xb
        xt_ref[...] = xb.T
        keys = lax.broadcasted_iota(jnp.int32, (pad, pad), 0)
        rows = lax.broadcasted_iota(jnp.int32, (pad, pad), 1)
        dist_ref[...] = jnp.abs(keys - rows).astype(F32)
    xb = xb_ref[...]
    q_ref[...] = (mm(xb, wq_ref[...]) + vec_ref[0:1, :]).astype(BF)
    k_ref[...] = mm(xb, wk_ref[...]).astype(BF)
    v_ref[...] = (mm(xb, wv_ref[...]) + vec_ref[1:2, :]).astype(BF)
    for s in range(seqs):
        rows = slice(s * pad, (s + 1) * pad)
        hidden = jnp.where(lax.broadcasted_iota(jnp.int32, (pad, 1), 0) < len_ref[s], 0.0, NEG)
        for pair in range(2):
            lanes = slice(128 * pair, 128 * pair + 128)
            q2 = q_ref[rows, lanes] * BF(HEAD_DIM ** -0.5)
            k0, k1 = halves(k_ref[rows, lanes], 1)
            v0, v1 = halves(v_ref[rows, lanes].T, 0)
            total = None
            for h, (kh, vh) in enumerate(((k0, v0), (k1, v1))):
                slope = slope_ref[4 * i + 2 * pair + h]
                sc = mm_nt(kh, q2) - slope * dist_ref[...] + hidden
                e = jnp.exp(sc - jnp.max(sc, axis=0, keepdims=True))
                p = (e * (1.0 / jnp.sum(e, axis=0, keepdims=True))).astype(BF)
                pt_ref[s, 2 * pair + h] = p
                part = mm(vh, p)
                total = part if total is None else total + part
            total = total.astype(BF)
            at_ref[lanes, rows] = total
            att_ref[rows, lanes] = total.T


def attention_forward(l, lengths, slopes, x, w_qkv, vec):
    rows = x.shape[0]
    seqs = lengths.shape[0]
    pad = rows // seqs
    col = lambda off: pl.BlockSpec((None, D, 256), lambda i: (l, 0, off + i))
    blk = pl.BlockSpec((rows, 256), lambda i: (0, i))
    smem = pl.BlockSpec(memory_space=pltpu.SMEM)
    act = jax.ShapeDtypeStruct((rows, D), BF)
    return pl.pallas_call(
        attention_kernel,
        grid=(3,),
        in_specs=[smem, smem, pl.BlockSpec((rows, D), lambda i: (0, 0)), col(0), col(3), col(6), pl.BlockSpec((None, 8, 256), lambda i: (l, 0, i))],
        out_specs=[blk, blk, blk, blk, pl.BlockSpec((seqs, 4, pad, pad), lambda i: (0, i, 0, 0)), pl.BlockSpec((D, rows), lambda i: (0, 0)), pl.BlockSpec((256, rows), lambda i: (i, 0))],
        out_shape=[act, act, act, act, jax.ShapeDtypeStruct((seqs, HEADS, pad, pad), BF), jax.ShapeDtypeStruct((D, rows), BF), jax.ShapeDtypeStruct((D, rows), BF)],
        scratch_shapes=[pltpu.VMEM((rows, D), BF), pltpu.VMEM((pad, pad), F32)],
        compiler_params=pltpu.CompilerParams(vmem_limit_bytes=56 * 2**20),
        name="attention_forward",
    )(lengths, slopes, x, w_qkv, w_qkv, w_qkv, vec)


def ff_kernel(att_ref, x_ref, wo_ref, wg_ref, wu_ref, wd_ref, vec_ref, r1_ref, r2_ref, ga_ref, gb_ref, ft_ref, ht_ref, out_ref, h_ref, hb_ref, acc_ref):
    j = pl.program_id(0)

    @pl.when(j == 0)
    def _():
        r1 = x_ref[...].astype(F32) + (mm(att_ref[...], wo_ref[...]) + vec_ref[2:3, :])
        r1_ref[...] = r1
        h = norm_parts(r1)[0] * vec_ref[3:4, :] + vec_ref[4:5, :]
        h_ref[...] = h
        hb = h.astype(BF)
        hb_ref[...] = hb
        ht_ref[...] = hb.T
        acc_ref[...] = jnp.zeros_like(acc_ref)
    hb = hb_ref[...]
    g = mm(hb, wg_ref[...])
    u = mm(hb, wu_ref[...])
    cdf = 0.5 + 0.5 * erf(g * math.sqrt(0.5))
    gelu = g * cdf
    slope = cdf + g * (jnp.exp(-0.5 * (g * g)) * (1.0 / math.sqrt(2.0 * math.pi)))
    ga_ref[...] = gelu.astype(BF)
    gb_ref[...] = (slope * u).astype(BF)
    f = (gelu * u).astype(BF)
    ft_ref[...] = f.T
    acc_ref[...] += mm(f, wd_ref[...])

    @pl.when(j == pl.num_programs(0) - 1)
    def _():
        r2 = h_ref[...] + (acc_ref[...] + vec_ref[5:6, :])
        r2_ref[...] = r2
        out_ref[...] = (norm_parts(r2)[0] * vec_ref[6:7, :] + vec_ref[7:8, :]).astype(out_ref.dtype)


def ff_forward(l, att, x, w_out, w_gated, w_down, vec, out_dtype):
    rows = x.shape[0]
    n = FF // 768
    whole = pl.BlockSpec((rows, D), lambda j: (0, 0))
    blk = pl.BlockSpec((rows, 768), lambda j: (0, j))
    return pl.pallas_call(
        ff_kernel,
        grid=(n,),
        in_specs=[whole, whole, pl.BlockSpec((None, D, D), lambda j: (l, 0, 0)),
                  pl.BlockSpec((None, D, 768), lambda j: (l, 0, j)), pl.BlockSpec((None, D, 768), lambda j: (l, 0, n + j)),
                  pl.BlockSpec((None, 768, D), lambda j: (l, j, 0)), pl.BlockSpec((None, 8, D), lambda j: (l, 0, 0))],
        out_specs=[whole, whole, blk, blk, pl.BlockSpec((768, rows), lambda j: (j, 0)), pl.BlockSpec((D, rows), lambda j: (0, 0)), whole],
        out_shape=[jax.ShapeDtypeStruct((rows, D), F32), jax.ShapeDtypeStruct((rows, D), F32),
                   jax.ShapeDtypeStruct((rows, FF), BF), jax.ShapeDtypeStruct((rows, FF), BF),
                   jax.ShapeDtypeStruct((FF, rows), BF), jax.ShapeDtypeStruct((D, rows), BF), jax.ShapeDtypeStruct((rows, D), out_dtype)],
        scratch_shapes=[pltpu.VMEM((rows, D), F32), pltpu.VMEM((rows, D), BF), pltpu.VMEM((rows, D), F32)],
        compiler_params=pltpu.CompilerParams(vmem_limit_bytes=56 * 2**20),
        name="ff_forward",
    )(att, x, w_out, w_gated, w_gated, w_down, vec)


def colsum(v):
    return jnp.sum(v, axis=0, keepdims=True)


def ff_back_kernel(dy_ref, r1_ref, r2_ref, ga_ref, gb_ref, wo_ref, wg_ref, wu_ref, wd_ref, vec_ref, dm_ref, dg_ref, du_ref, dr1_ref, da_ref, datt_ref, gv_ref, acc_ref):
    j = pl.program_id(0)

    @pl.when(j == 0)
    def _():
        dy = dy_ref[...].astype(F32)
        n, rstd = norm_parts(r2_ref[...])
        dr2 = norm_back(dy, vec_ref[6:7, :], n, rstd)
        acc_ref[...] = dr2
        dm = dr2.astype(BF)
        dm_ref[...] = dm
        gv_ref[5:6, :] = colsum(dm.astype(F32))
        gv_ref[6:7, :] = colsum(dy * n)
        gv_ref[7:8, :] = colsum(dy)
        gv_ref[0:2, :] = jnp.zeros((2, D), F32)
    df = mm_nt(dm_ref[...], wd_ref[...])
    dg = (df * gb_ref[...].astype(F32)).astype(BF)
    du = (df * ga_ref[...].astype(F32)).astype(BF)
    dg_ref[...] = dg
    du_ref[...] = du
    acc_ref[...] += mm_nt(dg, wg_ref[...]) + mm_nt(du, wu_ref[...])

    @pl.when(j == pl.num_programs(0) - 1)
    def _():
        dh = acc_ref[...]
        n, rstd = norm_parts(r1_ref[...])
        dr1 = norm_back(dh, vec_ref[3:4, :], n, rstd)
        dr1_ref[...] = dr1
        da = dr1.astype(BF)
        da_ref[...] = da
        gv_ref[2:3, :] = colsum(da.astype(F32))
        gv_ref[3:4, :] = colsum(dh * n)
        gv_ref[4:5, :] = colsum(dh)
        datt_ref[...] = mm_nt(da, wo_ref[...]).astype(BF)


def ff_backward(l, dy, r1, r2, ga, gb, w_out, w_gated, w_down, vec):
    rows = dy.shape[0]
    n = FF // 768
    whole = pl.BlockSpec((rows, D), lambda j: (0, 0))
    blk = pl.BlockSpec((rows, 768), lambda j: (0, j))
    act = lambda c, t: jax.ShapeDtypeStruct((rows, c), t)
    return pl.pallas_call(
        ff_back_kernel,
        grid=(n,),
        in_specs=[whole, whole, whole, blk, blk, pl.BlockSpec((None, D, D), lambda j: (l, 0, 0)),
                  pl.BlockSpec((None, D, 768), lambda j: (l, 0, j)), pl.BlockSpec((None, D, 768), lambda j: (l, 0, n + j)),
                  pl.BlockSpec((None, 768, D), lambda j: (l, j, 0)), pl.BlockSpec((None, 8, D), lambda j: (l, 0, 0))],
        out_specs=[whole, blk, blk, whole, whole, whole, pl.BlockSpec((8, D), lambda j: (0, 0))],
        out_shape=[act(D, BF), act(FF, BF), act(FF, BF), act(D, F32), act(D, BF), act(D, BF), jax.ShapeDtypeStruct((8, D), F32)],
        scratch_shapes=[pltpu.VMEM((rows, D), F32)],
        compiler_params=pltpu.CompilerParams(vmem_limit_bytes=56 * 2**20),
        name="ff_backward",
    )(dy, r1, r2, ga, gb, w_out, w_gated, w_gated, w_down, vec)


def attention_back_kernel(datt_ref, q_ref, k_ref, v_ref, pt_ref, wq_ref, wk_ref, wv_ref, dr1_ref, dq_ref, dk_ref, dv_ref, dx_ref, gb_ref, acc_ref):
    i = pl.program_id(0)
    seqs, pad = pt_ref.shape[0], pt_ref.shape[-1]
    scale = HEAD_DIM ** -0.5

    @pl.when(i == 0)
    def _():
        acc_ref[...] = dr1_ref[...]
    first = lax.broadcasted_iota(jnp.int32, (pad, 128), 1) < HEAD_DIM
    for s in range(seqs):
        rows = slice(s * pad, (s + 1) * pad)
        for pair in range(2):
            lanes = slice(128 * pair, 128 * pair + 128)
            q2 = q_ref[rows, lanes]
            d2 = datt_ref[rows, lanes]
            vs = halves(v_ref[rows, lanes], 1)
            ks = halves(k_ref[rows, lanes].T, 0)
            dv, dk, dq = [], [], None
            for h in range(2):
                pb = pt_ref[s, 2 * pair + h]
                p = pb.astype(F32)
                dp = mm_nt(vs[h], d2)
                ds = (p * (dp - jnp.sum(dp * p, axis=0, keepdims=True))).astype(BF)
                dv.append(mm(pb, d2))
                dk.append(mm(ds, q2))
                part = mm(ks[h], ds)
                dq = part if dq is None else dq + part
            dv_ref[rows, lanes] = jnp.where(first, dv[0], dv[1]).astype(BF)
            dk_ref[rows, lanes] = (jnp.where(first, dk[0], dk[1]) * scale).astype(BF)
            dq_ref[rows, lanes] = (dq * scale).astype(BF).T
    dq, dk, dv = dq_ref[...], dk_ref[...], dv_ref[...]
    gb_ref[0:1, :] = colsum(dq.astype(F32))
    gb_ref[1:2, :] = colsum(dv.astype(F32))
    gb_ref[2:8, :] = jnp.zeros((6, 256), F32)
    acc_ref[...] += mm_nt(dq, wq_ref[...]) + mm_nt(dk, wk_ref[...]) + mm_nt(dv, wv_ref[...])

    @pl.when(i == pl.num_programs(0) - 1)
    def _():
        dx_ref[...] = acc_ref[...].astype(dx_ref.dtype)


def attention_backward(l, datt, q, k, v, pt, w_qkv, dr1, out_dtype):
    rows = datt.shape[0]
    seqs, _, pad, _ = pt.shape
    col = lambda off: pl.BlockSpec((None, D, 256), lambda i: (l, 0, off + i))
    blk = pl.BlockSpec((rows, 256), lambda i: (0, i))
    whole = pl.BlockSpec((rows, D), lambda i: (0, 0))
    act = jax.ShapeDtypeStruct((rows, D), BF)
    return pl.pallas_call(
        attention_back_kernel,
        grid=(3,),
        in_specs=[blk, blk, blk, blk, pl.BlockSpec((seqs, 4, pad, pad), lambda i: (0, i, 0, 0)), col(0), col(3), col(6), whole],
        out_specs=[blk, blk, blk, whole, pl.BlockSpec((8, 256), lambda i: (0, i))],
        out_shape=[act, act, act, jax.ShapeDtypeStruct((rows, D), out_dtype), jax.ShapeDtypeStruct((8, D), F32)],
        scratch_shapes=[pltpu.VMEM((rows, D), F32)],
        compiler_params=pltpu.CompilerParams(vmem_limit_bytes=56 * 2**20),
        name="attention_backward",
    )(datt, q, k, v, pt, w_qkv, w_qkv, w_qkv, dr1)


def place():
    y = lax.axis_index("dp"); f = lax.axis_index("fsdp")
    z = f // 4; x = lax.rem(f // 2, 2); c = lax.rem(f, 2)
    return z, x, y, c

def dev(z, x, y, c):
    return (y, (z * 2 + x) * 2 + c)

PIECES = 8 * LAYERS


def along_z(p):
    return lax.rem(p, 5) == 3

KEPT = ("r1", "r2", "ga", "gb", "q", "k", "v", "pt", "ft", "ht", "at", "xt")


class Group:
    def __init__(self, names, refs):
        for name, ref in zip(names, refs):
            setattr(self, name, ref)


def taker(refs):
    refs = list(refs)

    def take(*names):
        g = Group(names, refs[: len(names)])
        del refs[: len(names)]
        return g
    return take


def run(cp, go):
    if go:
        cp.start()
    else:
        cp.wait()


def cols(ref, j, width):
    return ref.at[:, pl.ds(pl.multiple_of(j * width, width), width)]


def matrix_loads(w, p, k, dst, sem):
    return [pltpu.make_async_copy(w.at[p, :, :, :, h, k], dst.at[:, :, :, :, pl.ds(384 * h, 384)], sem) for h in range(2)]


def wait_all(dst, sem):
    pltpu.make_async_copy(dst, dst, sem).wait()


def forward_kernel(*refs):
    take = taker(refs)
    i_ = take("lens", "slopes", "x", "qkv", "out", "gated", "down", *["v%d" % i for i in range(8)])
    o_ = take("w", "v", "vec", "last")
    kept = [take(*KEPT) for _ in range(LAYERS)]
    t_ = take("x", "xb", "dist", "q", "k", "v", "att", "pt", "at", "xt", "wq", "wk", "wv", "wo", "wg", "wu", "wd", "h", "hb", "f", "ga", "gb", "ft", "res", "last", "vown", "vwide", "vec_in")
    m_ = take("local", "zsend", "fsend", "xysend", "rsend", "csend", "recv", "crecv", "vlocal", "vload", "load", "wload", "store")
    pad = t_.pt.shape[-1]
    seqs = t_.pt.shape[0]

    z, x, y, c = place()
    zp = z + 1 - 2 * lax.rem(z, 2)
    zm = 3 - z
    zf = lax.rem(z + 2, 4)
    mid = jnp.logical_and(z >= 1, z <= 2)
    end = jnp.logical_not(mid)
    d_zp, d_zm = dev(zp, x, y, c), dev(zm, x, y, c)
    d_x, d_y, d_c = dev(z, 1 - x, y, c), dev(z, x, 1 - y, c), dev(z, x, y, 1 - c)
    bar = pltpu.get_barrier_semaphore()
    for d in (d_zp, d_zm, d_x, d_y, d_c):
        pl.semaphore_signal(bar, 1, device_id=d, device_id_type=MESH)


    def local(p):
        u = lax.rem(p, 8)
        l = p // 8

        def put(h, k, src):
            pltpu.make_async_copy(src, o_.w.at[p, z, x, c, h, k], m_.local.at[p]).start()

        def part(ref, off):
            return ref.at[l, :, pl.ds(pl.multiple_of(off, 128), 384)]
        for h in range(2):
            @pl.when(u == 0)
            def _():
                put(h, 0, part(i_.qkv, 384 * h))
                put(h, 1, part(i_.qkv, 768 + 384 * h))

            @pl.when(u == 1)
            def _():
                put(h, 0, part(i_.qkv, 1536 + 384 * h))
                put(h, 1, part(i_.out, 384 * h))

            @pl.when(jnp.logical_and(u >= 2, u < 6))
            def _():
                j = jnp.clip(u - 2, 0, 3) * 768
                put(h, 0, part(i_.gated, j + 384 * h))
                put(h, 1, part(i_.gated, j + FF + 384 * h))

            @pl.when(u >= 6)
            def _():
                for k in range(2):
                    r = pl.multiple_of(jnp.clip(2 * (u - 6) + k, 0, 3) * 48, 48)
                    put(h, k, i_.down.at[l, pl.ds(r, 48), pl.ds(384 * h, 384)])

    def locals_from(p, carry):
        local(p)
        return carry
    local(0)
    t_.vwide[...] = jnp.zeros_like(t_.vwide)
    for n in range(8):
        row = getattr(i_, "v%d" % n)[...].astype(F32)
        for l in range(LAYERS):
            t_.vwide[l, n : n + 1, 0:48] = row[l : l + 1, :]
    t_.vown[...] = t_.vwide[...].astype(BF)
    vplace = pltpu.make_async_copy(t_.vown, o_.v.at[z, x, c], m_.vlocal.at[0])
    vplace.start()
    xload = pltpu.make_async_copy(i_.x, t_.last, m_.vlocal.at[1])
    xload.start()
    lax.fori_loop(1, PIECES, locals_from, 0)
    pl.semaphore_wait(bar, 5)


    def stages(b, s):
        def copy(zz, xx, hh, sem, d):
            u = b(zz, xx, c, hh)
            return pltpu.make_async_remote_copy(src_ref=u, dst_ref=u, send_sem=sem.at[s], recv_sem=m_.recv.at[s, (zz * 2 + xx) * 2 + hh], device_id=d, device_id_type=MESH)

        def zsend(zz, d, sem=m_.fsend):
            copy(zz, x, y, sem, d).start()

        def got(zz, xx, hh, d):
            copy(zz, xx, hh, m_.zsend, d).wait_recv()

        def plane(zz, cc=c):
            u = b(zz, slice(None), cc, slice(None))
            return pltpu.make_async_remote_copy(src_ref=u, dst_ref=u, send_sem=m_.csend.at[s], recv_sem=m_.crecv.at[s, zz], device_id=d_c, device_id_type=MESH)

        def spread(zz):
            copy(zz, x, y, m_.xysend, d_x).start()
            copy(zz, x, y, m_.xysend, d_y).start()

        def relay(zz, first_x):
            got(zz, 1 - x, y, d_x)
            got(zz, x, 1 - y, d_y)

            def through_y():
                copy(zz, 1 - x, y, m_.rsend, d_y).start()

            def through_x():
                copy(zz, x, 1 - y, m_.rsend, d_x).start()
            if first_x is True:
                through_y()
            elif first_x is False:
                through_x()
            else:
                pl.when(first_x)(through_y)
                pl.when(jnp.logical_not(first_x))(through_x)

        def diagonal(zz):
            got(zz, 1 - x, 1 - y, d_y)
            plane(zz).start()

        def st0():
            zsend(z, d_zp, m_.zsend)
            pl.when(mid)(lambda: zsend(z, d_zm, m_.zsend))
            copy(z, x, y, m_.xysend, d_x).start()

        def st1():
            got(zp, x, y, d_zp)

            @pl.when(mid)
            def _():
                zsend(zp, d_zm)
                got(zm, x, y, d_zm)
                zsend(zm, d_zp)
            spread(zp)
            got(z, 1 - x, y, d_x)
            copy(z, 1 - x, y, m_.xysend, d_y).start()

        def st2():
            got(zf, x, y, d_zp)
            pl.when(mid)(lambda: zsend(zf, d_zp))
            spread(zf)
            relay(zp, True)
            diagonal(z)

        def st3():
            pl.when(end)(lambda: got(zm, x, y, d_zp))
            spread(zm)
            relay(zf, False)
            diagonal(zp)

        def st4():
            relay(zm, lax.rem(s, 2) == 0)
            diagonal(zf)

        def st5():
            diagonal(zm)

        def st6():
            for zz in (z, zp, zf, zm):
                plane(zz, 1 - c).wait_recv()
        return st0, st1, st2, st3, st4, st5, st6

    def stages_z(b, s):
        def copy(zz, xx, hh, sem, d):
            u = b(zz, xx, c, hh)
            at = 0 if isinstance(hh, slice) else hh
            return pltpu.make_async_remote_copy(src_ref=u, dst_ref=u, send_sem=sem.at[s], recv_sem=m_.recv.at[s, (zz * 2 + xx) * 2 + at], device_id=d, device_id_type=MESH)
        both = slice(None)

        def zsend(zz, xx, d, sem=m_.fsend):
            copy(zz, xx, both, sem, d).start()

        def got(zz, xx, d):
            copy(zz, xx, both, m_.zsend, d).wait_recv()

        def plane(zz, cc=c):
            u = b(zz, both, cc, both)
            return pltpu.make_async_remote_copy(src_ref=u, dst_ref=u, send_sem=m_.csend.at[s], recv_sem=m_.crecv.at[s, zz], device_id=d_c, device_id_type=MESH)

        def own(xx):
            zsend(z, xx, d_zp, m_.zsend)
            pl.when(mid)(lambda: zsend(z, xx, d_zm, m_.zsend))

        def near(xx):
            got(zp, xx, d_zp)

            @pl.when(mid)
            def _():
                zsend(zp, xx, d_zm)
                got(zm, xx, d_zm)
                zsend(zm, xx, d_zp)

        def far(xx):
            got(zf, xx, d_zp)
            pl.when(mid)(lambda: zsend(zf, xx, d_zp))

        def farthest(xx):
            pl.when(end)(lambda: got(zm, xx, d_zp))

        def st0():
            own(x)
            copy(z, x, y, m_.xysend, d_x).start()

        def st1():
            near(x)
            copy(z, 1 - x, y, m_.xysend, d_x).wait_recv()
            copy(z, 1 - x, y, m_.xysend, d_y).start()

        def st2():
            far(x)
            copy(z, 1 - x, 1 - y, m_.xysend, d_y).wait_recv()
            own(1 - x)
            plane(z).start()

        def st3():
            farthest(x)
            near(1 - x)
            plane(zp).start()

        def st4():
            far(1 - x)
            plane(zf).start()

        def st5():
            farthest(1 - x)
            plane(zm).start()

        def st6():
            for zz in (z, zp, zf, zm):
                plane(zz, 1 - c).wait_recv()
        return st0, st1, st2, st3, st4, st5, st6

    def sent_z(s):
        wait_all(o_.w.at[0, 0, 0, 0], m_.xysend.at[s])
        wait_all(many_w(16), m_.csend.at[s])
        pl.when(end)(lambda: wait_all(o_.w.at[0, 0, 0], m_.zsend.at[s]))

        @pl.when(mid)
        def _():
            wait_all(many_w(8), m_.zsend.at[s])
            wait_all(o_.w.at[0, 0:3, :, 0], m_.fsend.at[s])

    def sent(b, s, many):
        wait_all(many(8), m_.xysend.at[s])
        wait_all(many(3), m_.rsend.at[s])
        wait_all(many(16), m_.csend.at[s])
        pl.when(end)(lambda: wait_all(many(1), m_.zsend.at[s]))

        @pl.when(mid)
        def _():
            wait_all(many(2), m_.zsend.at[s])
            wait_all(many(3), m_.fsend.at[s])

    def unit(p):
        return lambda zz, xx, cc, hh: o_.w.at[p, zz, xx, cc, hh]

    def vunit(zz, xx, cc, hh):
        return o_.v.at[zz, xx, cc, hh]

    def many_w(n):
        if n == 8:
            return o_.w.at[0, 0]
        if n == 16:
            return o_.w.at[0, :, :, 0]
        return o_.w.at[0:n, 0, 0, 0, 0]

    def many_v(n):
        if n == 8:
            return o_.v.at[0]
        if n == 16:
            return o_.v.at[:, :, 0]
        return o_.v.at[0:n, 0, 0, 0]


    def load_att(l):
        for cp in matrix_loads(o_.w, 8 * l, 0, t_.wq, m_.wload.at[0]) + matrix_loads(o_.w, 8 * l, 1, t_.wk, m_.wload.at[1]) + matrix_loads(o_.w, 8 * l + 1, 0, t_.wv, m_.wload.at[2]) + matrix_loads(o_.w, 8 * l + 1, 1, t_.wo, m_.wload.at[3]):
            cp.start()

    def load_gated(l, j):
        for cp in matrix_loads(o_.w, 8 * l + 2 + j, 0, t_.wg, m_.wload.at[4]) + matrix_loads(o_.w, 8 * l + 2 + j, 1, t_.wu, m_.wload.at[5]):
            cp.start()

    def load_down(l):
        for s in range(4):
            for h in range(2):
                pltpu.make_async_copy(o_.w.at[8 * l + 6 + s // 2, :, :, :, h, s % 2], t_.wd.at[:, :, :, s, :, pl.ds(384 * h, 384)], m_.wload.at[6]).start()

    def store(i, src, dst, go):
        run(pltpu.make_async_copy(src, dst, m_.store.at[i]), go)

    def per_layer(l, f):
        for n in range(LAYERS):
            @pl.when(l == n)
            def _():
                f(kept[n])

    def vrow(l, n):
        return o_.vec[l, n : n + 1, :]

    def store_att(kl, i, go):
        store(0, t_.q, cols(kl.q, i, 256), go)
        store(1, t_.k, cols(kl.k, i, 256), go)
        store(2, t_.v, cols(kl.v, i, 256), go)
        store(3, t_.pt, kl.pt.at[:, pl.ds(4 * i, 4)], go)
        store(4, t_.at, kl.at.at[pl.ds(pl.multiple_of(256 * i, 256), 256)], go)

        @pl.when(i == 0)
        def _():
            store(5, t_.xt, kl.xt, go)

    def att_task(l, i):
        @pl.when(i == 0)
        def _():
            wait_all(t_.wq, m_.wload.at[0])
            wait_all(t_.wk, m_.wload.at[1])
            wait_all(t_.wv, m_.wload.at[2])
            xb = t_.x[...].astype(BF)
            t_.xb[...] = xb
            t_.xt[...] = xb.T
        xb = t_.xb[...]
        lane = pl.multiple_of(256 * i, 256)
        at = pl.ds(lane, 256)
        t_.q[...] = (mm(xb, t_.wq[:, :, :, :, at].reshape(D, 256)) + o_.vec[l, 0:1, at]).astype(BF)
        t_.k[...] = mm(xb, t_.wk[:, :, :, :, at].reshape(D, 256)).astype(BF)
        t_.v[...] = (mm(xb, t_.wv[:, :, :, :, at].reshape(D, 256)) + o_.vec[l, 1:2, at]).astype(BF)
        for s in range(seqs):
            rows = slice(s * pad, (s + 1) * pad)
            hidden = jnp.where(lax.broadcasted_iota(jnp.int32, (pad, 1), 0) < i_.lens[s], 0.0, NEG)
            for pair in range(2):
                lanes = slice(128 * pair, 128 * pair + 128)
                q2 = t_.q[rows, lanes] * BF(HEAD_DIM ** -0.5)
                ks = halves(t_.k[rows, lanes], 1)
                vs = halves(t_.v[rows, lanes].T, 0)
                total = None
                for h in range(2):
                    slope = i_.slopes[4 * i + 2 * pair + h]
                    sc = mm_nt(ks[h], q2) - slope * t_.dist[...] + hidden
                    e = jnp.exp(sc - jnp.max(sc, axis=0, keepdims=True))
                    p = (e * (1.0 / jnp.sum(e, axis=0, keepdims=True))).astype(BF)
                    t_.pt[s, 2 * pair + h] = p
                    part = mm(vs[h], p)
                    total = part if total is None else total + part
                total = total.astype(BF)
                t_.at[lanes, rows] = total
                t_.att[rows, pl.ds(pl.multiple_of(lane + 128 * pair, 128), 128)] = total.T
        per_layer(l, lambda kl: store_att(kl, i, True))

    def store_ff(kl, j, go):
        store(6, t_.ga, cols(kl.ga, j, 768), go)
        store(7, t_.gb, cols(kl.gb, j, 768), go)
        store(8, t_.ft, kl.ft.at[pl.ds(pl.multiple_of(768 * j, 768), 768)], go)

        @pl.when(j == 0)
        def _():
            store(9, t_.res, kl.r1, go)
            store(10, t_.xt, kl.ht, go)

    def ff_task(l, j):
        @pl.when(j == 0)
        def _():
            wait_all(t_.wo, m_.wload.at[3])
            r1 = t_.x[...] + (mm(t_.att[...], t_.wo[...].reshape(D, D)) + vrow(l, 2))
            t_.res[...] = r1
            h = norm_parts(r1)[0] * vrow(l, 3) + vrow(l, 4)
            t_.h[...] = h
            hb = h.astype(BF)
            t_.hb[...] = hb
            t_.xt[...] = hb.T
        wait_all(t_.wg, m_.wload.at[4])
        wait_all(t_.wu, m_.wload.at[5])
        hb = t_.hb[...]
        g = mm(hb, t_.wg[...].reshape(D, 768))
        u = mm(hb, t_.wu[...].reshape(D, 768))
        cdf = 0.5 + 0.5 * erf(g * math.sqrt(0.5))
        gelu = g * cdf
        slope = cdf + g * (jnp.exp(-0.5 * (g * g)) * (1.0 / math.sqrt(2.0 * math.pi)))
        t_.ga[...] = gelu.astype(BF)
        t_.gb[...] = (slope * u).astype(BF)
        f = (gelu * u).astype(BF)
        t_.f[j] = f
        t_.ft[...] = f.T
        per_layer(l, lambda kl: store_ff(kl, j, True))

    def down_task(l):
        wait_all(t_.wd, m_.wload.at[6])
        total = t_.h[...] + vrow(l, 5)
        for j in range(4):
            total = total + mm(t_.f[j], t_.wd[j].reshape(768, D))
        t_.res[...] = total
        out = norm_parts(total)[0] * vrow(l, 6) + vrow(l, 7)
        t_.x[...] = out
        per_layer(l, lambda kl: store(9, t_.res, kl.r2, True))

        @pl.when(l == LAYERS - 1)
        def _():
            t_.last[...] = out.astype(BF)
            store(11, t_.last, o_.last, True)

    def task(t, att, ff, down):
        l = t // 8
        u = lax.rem(t, 8)
        pl.when(u < 3)(lambda: att(l, jnp.minimum(u, 2)))
        pl.when(jnp.logical_and(u >= 3, u < 7))(lambda: ff(l, jnp.clip(u - 3, 0, 3)))
        pl.when(u == 7)(lambda: down(l))

    def stored(t):
        task(t, lambda l, i: store_att(kept[0], i, False), lambda l, j: store_ff(kept[0], j, False), lambda l: store(9, t_.res, kept[0].r2, False))

    def fetch(t):
        def att(l, i):
            pl.when(i == 0)(lambda: load_att(l))
        task(t, att, load_gated, load_down)


    vst = stages(vunit, PIECES)

    def begun(r):
        return jnp.clip(jnp.where(r <= 15, r - 7, r - 6), 0, 8 * LAYERS)

    def first(p):
        wait_all(o_.w.at[p, z, x, c], m_.local.at[p])
        pl.when(along_z(p))(stages_z(unit(p), p)[0])
        pl.when(jnp.logical_not(along_z(p)))(stages(unit(p), p)[0])

    def body(r, carry):
        def at(k):
            p = r - k

            @pl.when(jnp.logical_and(p >= 0, p < PIECES))
            def _():
                q = jnp.clip(p, 0, PIECES - 1)
                pl.when(along_z(q))(lambda: stages_z(unit(q), q)[k]())
                pl.when(jnp.logical_not(along_z(q)))(lambda: stages(unit(q), q)[k]())

        @pl.when(r < PIECES)
        def _():
            first(jnp.minimum(r, PIECES - 1))
        for k in range(1, 7):
            pl.when(r == k)(vst[k])
        at(6)
        low, high = begun(r), begun(r + 1)

        @pl.when(high > low)
        def _():
            fetch(jnp.minimum(low, 8 * LAYERS - 1))
        for k in (1, 2, 3, 4, 5):
            at(k)

        @pl.when(r == 6)
        def _():
            cp = pltpu.make_async_copy(o_.v, t_.vec_in, m_.vload)
            cp.start()
            xload.wait()
            t_.x[...] = t_.last[...].astype(F32)
            keys = lax.broadcasted_iota(jnp.int32, (pad, pad), 0)
            rows = lax.broadcasted_iota(jnp.int32, (pad, pad), 1)
            t_.dist[...] = jnp.abs(keys - rows).astype(F32)
            cp.wait()
            unpack_vectors()

        def one(t, carry):
            @pl.when(t >= 1)
            def _():
                stored(jnp.maximum(t - 1, 0))
            task(t, att_task, ff_task, down_task)
            return carry
        lax.fori_loop(low, high, one, 0)
        return carry

    def unpack_vectors():
        for l in range(LAYERS):
            parts = [t_.vec_in[b // 4, (b // 2) % 2, b % 2, l].astype(F32)[:, 0:48] for b in range(16)]
            o_.vec[l] = jnp.concatenate(parts, axis=1)
    vplace.wait()
    vst[0]()
    lax.fori_loop(0, PIECES + 6, body, 0)
    stored(8 * LAYERS - 1)
    store(11, t_.last, o_.last, False)

    def finish(p, carry):
        pl.when(along_z(p))(lambda: sent_z(p))
        pl.when(jnp.logical_not(along_z(p)))(lambda: sent(unit(p), p, many_w))
        return carry
    lax.fori_loop(0, PIECES, finish, 0)
    sent(vunit, PIECES, many_v)


def forward_all(lengths, slopes, x, shards, vectors):
    rows = x.shape[0]
    seqs = lengths.shape[0]
    pad = rows // seqs
    hbm = pl.BlockSpec(memory_space=pltpu.HBM)
    vmem = pl.BlockSpec(memory_space=pltpu.VMEM)
    smem = pl.BlockSpec(memory_space=pltpu.SMEM)
    S = jax.ShapeDtypeStruct
    act = lambda n, t: S((rows, n), t)
    one = [act(D, F32), act(D, F32), act(FF, BF), act(FF, BF), act(D, BF), act(D, BF), act(D, BF), S((seqs, HEADS, pad, pad), BF), S((FF, rows), BF), S((D, rows), BF), S((D, rows), BF), S((D, rows), BF)]
    out = [S((PIECES, 4, 2, 2, 2, 2, 48, 384), BF), S((4, 2, 2, 2, 8, 128), BF), S((LAYERS, 8, D), F32), act(D, BF)] + one * LAYERS
    v = pltpu.VMEM
    dma = pltpu.SemaphoreType.DMA
    mat = v((4, 2, 2, 48, D), BF)
    n = PIECES + 1
    scratch = [
        v((rows, D), F32), v((rows, D), BF), v((pad, pad), F32), v((rows, 256), BF), v((rows, 256), BF), v((rows, 256), BF), v((rows, D), BF),
        v((seqs, 4, pad, pad), BF), v((256, rows), BF), v((D, rows), BF), mat, mat, mat, mat, mat, mat, v((4, 2, 2, 4, 48, D), BF),
        v((rows, D), F32), v((rows, D), BF), v((4, rows, 768), BF), v((rows, 768), BF), v((rows, 768), BF), v((768, rows), BF), v((rows, D), F32), v((rows, D), BF),
        v((2, 8, 128), BF), v((2, 8, 128), F32), v((4, 2, 2, 2, 8, 128), BF),
        dma((PIECES,)), dma((n,)), dma((n,)), dma((n,)), dma((n,)), dma((n,)), dma((n, 16)), dma((n, 4)), dma((2,)), dma, dma, dma((7,)), dma((12,)),
    ]
    res = pl.pallas_call(
        forward_kernel, out_shape=out,
        in_specs=[smem, smem, hbm] + [hbm] * 4 + [vmem] * 8,
        out_specs=[hbm, hbm, vmem, hbm] + [hbm] * (12 * LAYERS),
        scratch_shapes=scratch,
        compiler_params=pltpu.CompilerParams(collective_id=0, has_side_effects=True, vmem_limit_bytes=60 * 2**20), name="gather_forward",
    )(lengths, slopes, x, *shards, *vectors)
    return res[0], res[2], res[3], [res[4 + 12 * l : 16 + 12 * l] for l in range(LAYERS)]


NPIECE = 33
LAG = 2
SLOTS = 16


STEPS = (0, 1, 4, 6, 8, 10, 12, 14)
STEPS_Z = (0, 1, 4, 7, 9, 11, 12, 13)


def reduce_z(p):
    return lax.rem(p, 4) == 1


def piece_first_x(p):
    others = p - (p + 2) // 4
    return jnp.logical_or(reduce_z(p), lax.rem(others * 5, 8) < 5)


def add_into(dst, src):
    dst[...] = (dst[...].astype(F32) + src[...].astype(F32)).astype(BF)


GRADS = ("dg", "du", "dq", "dk", "dv")


def backward_kernel(*refs):
    take = taker(refs)
    i_ = take("cot", "vec")
    cot, vec = i_.cot, i_.vec
    kept = [take(*KEPT) for _ in range(LAYERS)]
    w = take("w").w
    o = take("qkv", "out", "gated", "down", "vec", "dx")
    g = take(*GRADS)
    s = take("lbuf", "rbuf", "sbuf", "own", "stage", "r0v", "h1v", "h2v", "zav", "zbv", "yfv", "vall")
    c_ = take("r0", "h1", "h2", "za", "zb", "yf", "zza", "zzb")
    t_ = take("acc", "res", "wd", "wg", "wu", "ga", "gb", "wo", "dm", "dg", "du", "da", "datt", "q", "k", "v", "pt", "wq", "wk", "wv", "dq", "dk", "dv", "gv", "cot")
    m_ = take("lsem", "rsem", "send", "recv", "out", "vload", "fsem", "asem", "osem")
    pad = kept[0].pt.shape[-1]
    seqs = kept[0].pt.shape[0]

    z, x, y, c = place()
    zp = z + 1 - 2 * lax.rem(z, 2)
    zm = 3 - z
    mid = jnp.logical_and(z >= 1, z <= 2)
    end = jnp.logical_not(mid)
    d_zp, d_zm = dev(zp, x, y, c), dev(zm, x, y, c)
    d_x, d_y, d_c = dev(z, 1 - x, y, c), dev(z, x, 1 - y, c), dev(z, x, y, 1 - c)
    bar = pltpu.get_barrier_semaphore()
    for d in (d_zp, d_zm, d_x, d_y, d_c):
        pl.semaphore_signal(bar, 1, device_id=d, device_id_type=MESH)
    NP = NPIECE - 1


    def load_ff(l, j, go):
        def one(i, src, dst):
            run(pltpu.make_async_copy(src, dst, m_.fsem.at[i]), go)
        def acts(kl):
            @pl.when(j == 0)
            def _():
                one(5, kl.r2, t_.res)

            @pl.when(j == 3)
            def _():
                one(5, kl.r1, t_.res)
            one(3, cols(kl.ga, j, 768), t_.ga)
            one(4, cols(kl.gb, j, 768), t_.gb)
        if go:
            for i in range(LAYERS):
                @pl.when(l == i)
                def _():
                    acts(kept[i])
        else:
            one(3, cols(kept[0].ga, j, 768), t_.ga)
            one(4, cols(kept[0].gb, j, 768), t_.gb)

            @pl.when(j == 3)
            def _():
                one(5, kept[0].r1, t_.res)

        if go:
            for n in range(4):
                for h in range(2):
                    one(0, w.at[8 * l + 6 + n // 2, j, :, :, h, n % 2], t_.wd.at[:, :, n, :, pl.ds(384 * h, 384)])
            for cp in matrix_loads(w, 8 * l + 2 + j, 0, t_.wg, m_.fsem.at[1]) + matrix_loads(w, 8 * l + 2 + j, 1, t_.wu, m_.fsem.at[2]):
                cp.start()
        else:
            wait_all(t_.wd, m_.fsem.at[0])
            wait_all(t_.wg, m_.fsem.at[1])
            wait_all(t_.wu, m_.fsem.at[2])

        @pl.when(j == 3)
        def _():
            if go:
                for cp in matrix_loads(w, 8 * l + 1, 1, t_.wo, m_.fsem.at[6]):
                    cp.start()
            else:
                wait_all(t_.wo, m_.fsem.at[6])

    def load_att(l, i, go):
        def one(n, src, dst):
            run(pltpu.make_async_copy(src, dst, m_.asem.at[n]), go)

        def acts(kl):
            one(0, cols(kl.q, i, 256), t_.q)
            one(1, cols(kl.k, i, 256), t_.k)
            one(2, cols(kl.v, i, 256), t_.v)
            one(3, kl.pt.at[:, pl.ds(4 * i, 4)], t_.pt)
        if go:
            for n in range(LAYERS):
                @pl.when(l == n)
                def _():
                    acts(kept[n])
        else:
            acts(kept[0])
        @pl.when(i == 0)
        def _():
            for n, dst in enumerate((t_.wq, t_.wk, t_.wv)):
                if go:
                    for cp in matrix_loads(w, 8 * l + n // 2, n % 2, dst, m_.asem.at[4 + n]):
                        cp.start()
                else:
                    wait_all(dst, m_.asem.at[4 + n])

    def norm_two(l):
        pltpu.make_async_copy(kept[0].r2, t_.res, m_.fsem.at[5]).wait()
        dy = t_.acc[...]
        n, rstd = norm_parts(t_.res[...])
        dr2 = norm_back(dy, vec[l, 6:7, :], n, rstd)
        t_.acc[...] = dr2
        dm = dr2.astype(BF)
        t_.dm[...] = dm
        t_.gv[l, 5:6, :] = colsum(dm.astype(F32))
        t_.gv[l, 6:7, :] = colsum(dy * n)
        t_.gv[l, 7:8, :] = colsum(dy)

    def ff_task(l, j):
        load_ff(l, j, False)

        @pl.when(jnp.logical_and(j == 0, l < LAYERS - 1))
        def _():
            norm_two(l)
        df = mm_nt(t_.dm[...], t_.wd[...].reshape(768, D))
        dg = (df * t_.gb[...].astype(F32)).astype(BF)
        du = (df * t_.ga[...].astype(F32)).astype(BF)
        t_.dg[...] = dg
        t_.du[...] = du
        t_.acc[...] += mm_nt(dg, t_.wg[...].reshape(D, 768)) + mm_nt(du, t_.wu[...].reshape(D, 768))

        @pl.when(j == 3)
        def _():
            dh = t_.acc[...]
            n, rstd = norm_parts(t_.res[...])
            dr1 = norm_back(dh, vec[l, 3:4, :], n, rstd)
            t_.acc[...] = dr1
            da = dr1.astype(BF)
            t_.da[...] = da
            t_.gv[l, 2:3, :] = colsum(da.astype(F32))
            t_.gv[l, 3:4, :] = colsum(dh * n)
            t_.gv[l, 4:5, :] = colsum(dh)
            datt = mm_nt(da, t_.wo[...].reshape(D, D)).astype(BF)
            for i in range(3):
                t_.datt[i] = datt[:, 256 * i : 256 * i + 256]
        store_ff(l, j, True)

        @pl.when(j < 3)
        def _():
            load_ff(l, j + 1, True)

        @pl.when(j == 3)
        def _():
            load_att(l, 0, True)

    def store_ff(l, j, go):
        def one(i, src, dst):
            run(pltpu.make_async_copy(src, dst, m_.osem.at[i]), go)
        one(0, t_.dg, cols(g.dg.at[l], j, 768))
        one(1, t_.du, cols(g.du.at[l], j, 768))

    def att_task(l, i):
        load_att(l, i, False)
        scale = HEAD_DIM ** -0.5
        first = lax.broadcasted_iota(jnp.int32, (pad, 128), 1) < HEAD_DIM
        for sq in range(seqs):
            rows = slice(sq * pad, (sq + 1) * pad)
            for pair in range(2):
                lanes = slice(128 * pair, 128 * pair + 128)
                q2 = t_.q[rows, lanes]
                d2 = t_.datt[i, rows, lanes]
                vs = halves(t_.v[rows, lanes], 1)
                ks = halves(t_.k[rows, lanes].T, 0)
                dv, dk, dq = [], [], None
                for h in range(2):
                    pb = t_.pt[sq, 2 * pair + h]
                    p = pb.astype(F32)
                    dp = mm_nt(vs[h], d2)
                    ds = (p * (dp - jnp.sum(dp * p, axis=0, keepdims=True))).astype(BF)
                    dv.append(mm(pb, d2))
                    dk.append(mm(ds, q2))
                    part = mm(ks[h], ds)
                    dq = part if dq is None else dq + part
                t_.dv[rows, lanes] = jnp.where(first, dv[0], dv[1]).astype(BF)
                t_.dk[rows, lanes] = (jnp.where(first, dk[0], dk[1]) * scale).astype(BF)
                t_.dq[rows, lanes] = (dq * scale).astype(BF).T
        dq, dk, dv = t_.dq[...], t_.dk[...], t_.dv[...]
        at = pl.ds(pl.multiple_of(i * 256, 256), 256)
        t_.gv[l, 0:1, at] = colsum(dq.astype(F32))
        t_.gv[l, 1:2, at] = colsum(dv.astype(F32))
        t_.acc[...] += (
            mm_nt(dq, t_.wq[:, :, :, :, at].reshape(D, 256)) + mm_nt(dk, t_.wk[:, :, :, :, at].reshape(D, 256)) + mm_nt(dv, t_.wv[:, :, :, :, at].reshape(D, 256))
        )
        store_att(l, i, True)

        @pl.when(i < 2)
        def _():
            load_att(l, i + 1, True)

        @pl.when(jnp.logical_and(i == 2, l > 0))
        def _():
            load_ff(jnp.maximum(l - 1, 0), 0, True)

        @pl.when(jnp.logical_and(i == 2, l == 0))
        def _():
            t_.cot[...] = t_.acc[...].astype(BF)
            pltpu.make_async_copy(t_.cot, o.dx, m_.osem.at[7]).start()

    def store_att(l, i, go):
        def one(n, src, dst):
            run(pltpu.make_async_copy(src, dst, m_.osem.at[n]), go)
        one(4, t_.dq, cols(g.dq.at[l], i, 256))
        one(5, t_.dk, cols(g.dk.at[l], i, 256))
        one(6, t_.dv, cols(g.dv.at[l], i, 256))

    def task(t, ff, att):
        l = LAYERS - 1 - t // 7
        u = lax.rem(t, 7)

        @pl.when(u < 4)
        def _():
            ff(l, jnp.minimum(u, 3))

        @pl.when(u >= 4)
        def _():
            att(l, jnp.clip(u - 4, 0, 2))


    def load(p, go):
        q = lax.rem(p, 16)
        n = lax.rem(p, 2)
        layer = LAYERS - 1 - p // 16

        def left(ref, sub=None):
            for k in range(2):
                cc = c if k else 1 - c
                src = ref.at[:, cc] if sub is None else ref.at[:, cc, sub]
                run(pltpu.make_async_copy(src, s.lbuf.at[n, k], m_.lsem.at[n, k]), go)

        def right(ref, col=None):
            src = ref if col is None else cols(ref.at[layer], jnp.clip(col, 0, 3), 768)
            run(pltpu.make_async_copy(src, s.rbuf.at[n], m_.rsem.at[n]), go)
        if not go:
            left(kept[0].ht)
            right(t_.dm)
            return
        for l in range(LAYERS):
            here = layer == l
            kl = kept[l]

            @pl.when(jnp.logical_and(here, q < 4))
            def _():
                left(kl.ft, jnp.minimum(q, 3))

            @pl.when(jnp.logical_and(here, jnp.logical_and(q >= 4, q < 12)))
            def _():
                left(kl.ht)

            @pl.when(jnp.logical_and(here, q == 12))
            def _():
                left(kl.at)

            @pl.when(jnp.logical_and(here, q > 12))
            def _():
                left(kl.xt)

        @pl.when(q < 4)
        def _():
            right(t_.dm)

        @pl.when(jnp.logical_and(q >= 4, q < 8))
        def _():
            right(g.dg, q - 4)

        @pl.when(jnp.logical_and(q >= 8, q < 12))
        def _():
            right(g.du, q - 8)
        for i, d in enumerate((t_.da, g.dq.at[layer], g.dk.at[layer], g.dv.at[layer])):
            @pl.when(q == 12 + i)
            def _():
                right(d)

    def rcopy(p, e, src, dst, d):
        return pltpu.make_async_remote_copy(src_ref=src, dst_ref=dst, send_sem=m_.send.at[p, e], recv_sem=m_.recv.at[p, e], device_id=d, device_id_type=MESH)

    def product(n, theirs, mine):
        v = mm(s.lbuf[n].reshape(768, -1), s.rbuf[n]).astype(BF).reshape(2, 4, 2, 48, 768)
        for k, dst in enumerate((theirs, mine)):
            dst[:, :, 0] = v[k, :, :, :, :384]
            dst[:, :, 1] = v[k, :, :, :, 384:]

    def c_copy(p, n):
        return rcopy(p, 0, s.sbuf.at[n], c_.r0.at[lax.rem(p, SLOTS)], d_c)

    def s0(p):
        n = lax.rem(p, 2)
        load(p, False)

        @pl.when(p >= 2)
        def _():
            c_copy(jnp.maximum(p - 2, 0), n).wait_send()
        product(n, s.sbuf.at[n], s.own.at[lax.rem(p, LAG + 1)])
        c_copy(p, n).start()

        @pl.when(p + 1 < NP)
        def _():
            load(jnp.minimum(p + 1, NP - 1), True)
    small = Group(("r0", "h1", "h2", "za", "zb", "yf"), (s.r0v, s.h1v, s.h2v, s.zav, s.zbv, s.yfv))
    zlo = jnp.where(z == 1, 1, 0)
    elo = jnp.where(z == 0, 1, 0)
    mlo = jnp.where(z == 1, 2, 0)
    rlo = jnp.where(z == 1, 0, 2)

    def steps(b, p, i, my):
        fx = piece_first_x(p)
        fy = jnp.logical_not(fx)

        def hop1(go):
            a = rcopy(p, 1, b.r0.at[i, :, 1 - x], b.h1.at[i], d_x)
            if go == "start":
                pl.when(fx)(a.start)
                pl.when(fy)(rcopy(p, 1, b.r0.at[i, :, :, 1 - y], b.h1.at[i], d_y).start)
            elif go == "recv":
                a.wait_recv()
            else:
                a.wait_send()

        def hop2(go):
            a = rcopy(p, 2, b.h1.at[i, :, 1 - y], b.h2.at[i], d_y)
            if go == "start":
                pl.when(fx)(a.start)
                pl.when(fy)(rcopy(p, 2, b.h1.at[i, :, 1 - x], b.h2.at[i], d_x).start)
            elif go == "recv":
                a.wait_recv()
            else:
                a.wait_send()

        def z1():
            return rcopy(p, 3, b.h2.at[i, pl.ds(elo, 3)], b.za.at[i], d_zp)

        def z2():
            return rcopy(p, 4, b.h2.at[i, pl.ds(mlo, 2)], b.zb.at[i], d_zm)

        def z3():
            return rcopy(p, 5, b.h2.at[i, zp], b.zb.at[i, 0], d_zp)

        def y1():
            return rcopy(p, 6, b.h2.at[i, z], b.yf.at[i], d_y)

        def s1():
            rcopy(p, 0, b.r0.at[i], b.r0.at[i], d_c).wait_recv()
            for k in range(4):
                add_into(b.r0.at[i, k], my.at[k])
            hop1("start")

        def s2():
            hop1("recv")
            for k in range(4):
                @pl.when(fx)
                def _():
                    add_into(b.h1.at[i, k], b.r0.at[i, k, x])

                @pl.when(fy)
                def _():
                    add_into(b.h1.at[i, k], b.r0.at[i, k, :, y])
            hop2("start")

        def s3():
            hop1("send")
            hop2("recv")
            t = jnp.where(fx, y, x)
            for k in range(4):
                add_into(b.h2.at[i, k], b.h1.at[i, k, t])
            pl.when(end)(z1().start)

        def s4():
            hop2("send")

            @pl.when(mid)
            def _():
                z1().wait_recv()
                for k in range(3):
                    add_into(b.h2.at[i, zlo + k], b.za.at[i, k])
                z2().start()

        def s5():
            pl.when(end)(z1().wait_send)

            @pl.when(mid)
            def _():
                z2().wait_recv()
                for k in range(2):
                    add_into(b.h2.at[i, rlo + k], b.zb.at[i, k])
                z3().start()

        def s6():
            pl.when(mid)(z2().wait_send)

            @pl.when(end)
            def _():
                z3().wait_recv()
                add_into(b.h2.at[i, z], b.zb.at[i, 0])
            y1().start()

        def s7():
            pl.when(mid)(z3().wait_send)
            y1().wait_send()
            y1().wait_recv()
        return s1, s2, s3, s4, s5, s6, s7

    def steps_z(p, i, my):
        b = c_
        fx = piece_first_x(p)
        iz = lax.rem(p // 4, SLOTS // 4)

        def hop1():
            return rcopy(p, 1, b.r0.at[i, z, 1 - x], b.h1.at[i, 0], d_x)

        def hop2():
            return rcopy(p, 2, b.h1.at[i, 0, 1 - y], b.h2.at[i, z], d_y)

        def z1():
            return rcopy(p, 3, b.r0.at[i, pl.ds(elo, 3)], b.zza.at[iz], d_zp)

        def z2():
            return rcopy(p, 4, b.r0.at[i, pl.ds(mlo, 2)], b.zzb.at[iz], d_zm)

        def z3():
            return rcopy(p, 5, b.r0.at[i, zp], b.zzb.at[iz, 0], d_zp)

        def y1():
            return rcopy(p, 6, b.h2.at[i, z], b.yf.at[i], d_y)

        def s1():
            rcopy(p, 0, b.r0.at[i], b.r0.at[i], d_c).wait_recv()
            for k in range(4):
                add_into(b.r0.at[i, k], my.at[k])
            pl.when(end)(z1().start)

        def s2():
            @pl.when(mid)
            def _():
                z1().wait_recv()
                for k in range(3):
                    add_into(b.r0.at[i, zlo + k], b.zza.at[iz, k])
                z2().start()

        def s3():
            pl.when(end)(z1().wait_send)

            @pl.when(mid)
            def _():
                z2().wait_recv()
                for k in range(2):
                    add_into(b.r0.at[i, rlo + k], b.zzb.at[iz, k])
                z3().start()

        def s4():
            pl.when(mid)(z2().wait_send)

            @pl.when(end)
            def _():
                z3().wait_recv()
                add_into(b.r0.at[i, z], b.zzb.at[iz, 0])
            hop1().start()

        def s5():
            pl.when(mid)(z3().wait_send)
            hop1().wait_recv()
            add_into(b.h1.at[i, 0], b.r0.at[i, z, x])
            hop2().start()

        def s6():
            hop1().wait_send()
            hop2().wait_recv()
            add_into(b.h2.at[i, z], b.h1.at[i, 0, y])
            y1().start()

        def s7():
            hop2().wait_send()
            y1().wait_send()
            y1().wait_recv()
        return s1, s2, s3, s4, s5, s6, s7

    def out_copy(p, n, go):
        q = lax.rem(p, 16)
        layer = LAYERS - 1 - p // 16

        def one(dst):
            run(pltpu.make_async_copy(s.stage.at[n], dst, m_.out.at[n]), go)
        if not go:
            one(o.out.at[0])
            return

        @pl.when(q < 4)
        def _():
            one(o.down.at[layer, pl.ds(pl.multiple_of(jnp.minimum(q, 3) * 48, 48), 48)])

        @pl.when(jnp.logical_and(q >= 4, q < 12))
        def _():
            one(cols(o.gated.at[layer], jnp.clip(q - 4, 0, 7), 768))

        @pl.when(q == 12)
        def _():
            one(o.out.at[layer])

        @pl.when(q > 12)
        def _():
            one(cols(o.qkv.at[layer], jnp.clip(q - 13, 0, 2), 768))

    def write(p):
        n = lax.rem(p, 2)

        @pl.when(p >= 2)
        def _():
            out_copy(p, n, False)
        i = lax.rem(p, SLOTS)
        a = c_.h2[i, z].astype(F32)
        b = c_.yf[i].astype(F32)

        @pl.when(y == 0)
        def _():
            s.stage[n, :, :384] = a
            s.stage[n, :, 384:] = b

        @pl.when(y == 1)
        def _():
            s.stage[n, :, :384] = b
            s.stage[n, :, 384:] = a
        out_copy(p, n, True)


    vp = NP
    vc = rcopy(vp, 0, s.vall.at[1 - c], s.r0v.at[0], d_c)
    vsteps = steps(small, vp, 0, s.vall.at[c])
    VSTART = 27

    def pack_vectors():
        for l in range(LAYERS):
            v = jnp.concatenate([t_.gv[l], jnp.zeros((120, D), F32)], axis=0).T.astype(BF)
            for k in range(16):
                s.vall[k % 2, k // 4, (k // 2) % 2, l] = v[48 * k : 48 * k + 48]
        vc.start()


    top = LAYERS - 1
    first = pltpu.make_async_copy(cot, t_.cot, m_.vload)
    first.start()
    load_ff(top, 0, True)
    first.wait()
    t_.acc[...] = t_.cot[...].astype(F32)
    norm_two(top)
    load(0, True)
    pl.semaphore_wait(bar, 5)

    def body(r, carry):
        def at(k, off, f, kind=None):
            p = r - off[k]
            q = jnp.clip(p, 0, NP - 1)
            here = jnp.logical_and(p >= 0, p < NP)
            if kind is not None:
                here = jnp.logical_and(here, reduce_z(q) == kind)

            @pl.when(here)
            def _():
                f(q)

        def st(k, kind):
            def f(p):
                own = s.own.at[lax.rem(p, LAG + 1)]
                i = lax.rem(p, SLOTS)
                (steps_z(p, i, own) if kind else steps(c_, p, i, own))[k - 1]()
                if k == 7:
                    write(p)
            return f
        even = lax.rem(r, 2) == 0

        @pl.when(jnp.logical_or(r == 1, jnp.logical_and(even, jnp.logical_and(r >= 2, r < 28))))
        def _():
            task(jnp.clip(r // 2, 0, 13), lambda l, j: store_ff(l, j, False), lambda l, i: store_att(l, i, False))
        for k in range(1, 8):
            pl.when(r == VSTART + STEPS[k])(vsteps[k - 1])
        at(0, STEPS, s0)
        for k in range(7, 0, -1):
            at(k, STEPS_Z, st(k, True), True)
            at(k, STEPS, st(k, False), False)
        pl.when(r == VSTART)(pack_vectors)

        @pl.when(jnp.logical_or(r == 0, jnp.logical_and(jnp.logical_not(even), r < 26)))
        def _():
            task(jnp.clip((r + 1) // 2, 0, 13), ff_task, att_task)
        return carry
    lax.fori_loop(0, NP + max(STEPS[7], STEPS_Z[7]), body, 0)

    for p in (NP - 2, NP - 1):
        c_copy(p, p % 2).wait_send()
        out_copy(p, p % 2, False)
    vc.wait_send()
    pltpu.make_async_copy(t_.cot, o.dx, m_.osem.at[7]).wait()
    va, vb = s.h2v[0, z].astype(F32), s.yfv[0].astype(F32)
    o.vec[0] = jnp.where(y == 0, va, vb)
    o.vec[1] = jnp.where(y == 0, vb, va)


def backward_all(cot, vec, kept, w):
    rows = cot.shape[0]
    hbm = pl.BlockSpec(memory_space=pltpu.HBM)
    vmem = pl.BlockSpec(memory_space=pltpu.VMEM)
    kept = [tuple(k[:8]) + (k[8].reshape(8, 2, 4, 48, rows),) + tuple(a.reshape(8, 2, 48, rows) for a in k[9:]) for k in kept]
    act = lambda c, t: jax.ShapeDtypeStruct((rows, c), t)
    out = [
        jax.ShapeDtypeStruct((LAYERS, 48, 3 * D), F32), jax.ShapeDtypeStruct((LAYERS, 48, D), F32),
        jax.ShapeDtypeStruct((LAYERS, 48, 2 * FF), F32), jax.ShapeDtypeStruct((LAYERS, 192, D), F32),
        jax.ShapeDtypeStruct((2, 48, 128), F32), act(D, BF),
    ]
    both = lambda c: jax.ShapeDtypeStruct((LAYERS, rows, c), BF)
    scratch_out = [both(FF), both(FF), both(D), both(D), both(D)]
    seqs, _, pad, _ = kept[0][7].shape
    v = pltpu.VMEM
    dma = pltpu.SemaphoreType.DMA
    mat = v((4, 2, 2, 48, D), BF)
    n = SLOTS
    scratch = [
        v((2, 2, 8, 48, rows), BF), v((2, rows, 768), BF), v((2, 4, 2, 2, 48, 384), BF), v((LAG + 1, 4, 2, 2, 48, 384), BF), v((2, 48, 768), F32),
        v((1, 4, 2, 2, 48, 128), BF), v((1, 4, 2, 48, 128), BF), v((1, 4, 48, 128), BF),
        v((1, 3, 48, 128), BF), v((1, 2, 48, 128), BF), v((1, 48, 128), BF), v((2, 4, 2, 2, 48, 128), BF),
        v((n, 4, 2, 2, 48, 384), BF), v((n, 4, 2, 48, 384), BF), v((n, 4, 48, 384), BF), v((n, 3, 48, 384), BF), v((n, 2, 48, 384), BF), v((n, 48, 384), BF), v((n // 4, 3, 2, 2, 48, 384), BF), v((n // 4, 2, 2, 2, 48, 384), BF),
        v((rows, D), F32), v((rows, D), F32), v((2, 2, 4, 48, D), BF), mat, mat, v((rows, 768), BF), v((rows, 768), BF), mat,
        v((rows, D), BF), v((rows, 768), BF), v((rows, 768), BF), v((rows, D), BF), v((3, rows, 256), BF),
        v((rows, 256), BF), v((rows, 256), BF), v((rows, 256), BF), v((seqs, 4, pad, pad), BF), mat, mat, mat,
        v((rows, 256), BF), v((rows, 256), BF), v((rows, 256), BF), v((LAYERS, 8, D), F32), v((rows, D), BF),
        dma((2, 2)), dma((2,)), dma((NPIECE, 7)), dma((NPIECE, 7)), dma((2,)), dma, dma((7,)), dma((7,)), dma((8,)),
    ]
    res = pl.pallas_call(
        backward_kernel, out_shape=out + scratch_out,
        in_specs=[hbm, vmem] + [hbm] * 25,
        out_specs=[hbm] * 4 + [vmem] + [hbm] * 6,
        scratch_shapes=scratch,
        compiler_params=pltpu.CompilerParams(collective_id=1, has_side_effects=True, vmem_limit_bytes=62 * 2**20), name="backward_reduce",
    )(cot, vec, *kept[0], *kept[1], w)
    return res[:4], res[4], res[5]


def forward_plain(seq_lengths, slopes, x, shards, vectors):
    mats = [lax.all_gather(w, "fsdp", axis=1, tiled=True) for w in shards]
    vec = lax.all_gather(jnp.stack(vectors, axis=1), "fsdp", axis=2, tiled=True).astype(F32)
    wq, wo, wg, wd = mats
    kept = []
    for l in range(LAYERS):
        q, k, v, att, pt, xt, at = attention_forward(l, seq_lengths, slopes, x, wq, vec)
        out_dtype = BF if l == LAYERS - 1 else F32
        r1, r2, ga, gb, ft, ht, x = ff_forward(l, att, x, wo, wg, wd, vec, out_dtype)
        kept.append((r1, r2, ga, gb, q, k, v, pt, ft, ht, at, xt))
    return mats, vec, x, kept


def backward_plain(dy, vec, kept, mats):
    wq, wo, wg, wd = mats

    def one(g, dim):
        part = lax.psum_scatter(g.astype(BF), "fsdp", scatter_dimension=dim, tiled=True)
        return lax.psum(part, "dp").astype(F32)
    sums, vecs = [None] * LAYERS, [None] * LAYERS
    for l in reversed(range(LAYERS)):
        r1, r2, ga, gb, q, k, v, pt, ft, ht, at, xt = kept[l]
        dm, dg, du, dr1, da, datt, gv = ff_backward(l, dy, r1, r2, ga, gb, wo, wg, wd, vec)
        dq, dk, dv, dy, gbias = attention_backward(l, datt, q, k, v, pt, wq, dr1, BF if l == 0 else F32)
        pairs = ((xt, jnp.concatenate([dq, dk, dv], axis=1)), (at, da), (ht, jnp.concatenate([dg, du], axis=1)), (ft, dm))
        sums[l] = [one(mm(a, b), 0) for a, b in pairs]
        vecs[l] = gv + gbias
    return [jnp.stack(m) for m in zip(*sums)], one(jnp.stack(vecs), 2), dy


def per_device(fast, inputs, lengths, cotangent, w_qkv, q_bias, v_bias, w_out, b_out, gain_one, shift_one, w_gated, w_down, b_down, gain_two, shift_two):
    shards = (w_qkv, w_out, w_gated, w_down)
    vectors = (q_bias, v_bias, b_out, gain_one, shift_one, b_down, gain_two, shift_two)
    seq_lengths = lengths.reshape(-1)
    slopes = jnp.array(slopes_list(HEADS), F32)
    x = inputs.reshape(-1, D)
    dy = cotangent.reshape(-1, D)
    if fast:
        w, vec, x, kept = forward_all(seq_lengths, slopes, x, shards, vectors)
        m, packed, dx = backward_all(dy, vec, kept, w)
        vs = packed[:, :, :8].transpose(0, 2, 1)
    else:
        mats, vec, x, kept = forward_plain(seq_lengths, slopes, x, shards, vectors)
        m, vs, dx = backward_plain(dy, vec, kept, mats)
    return (
        x.reshape(inputs.shape), dx.reshape(inputs.shape), m[0], vs[:, 0], vs[:, 1], m[1], vs[:, 2], vs[:, 3], vs[:, 4], m[2], m[3], vs[:, 5], vs[:, 6], vs[:, 7],
    )


def solution(mesh):
    placed = (
        P(None, ("dp", "fsdp"), None, None),
        P(None, ("dp", "fsdp")),
        P(None, ("dp", "fsdp"), None, None),
        P(None, "fsdp", None),
        P(None, "fsdp"),
        P(None, "fsdp"),
        P(None, "fsdp", None),
        P(None, "fsdp"),
        P(None, "fsdp"),
        P(None, "fsdp"),
        P(None, "fsdp", None),
        P(None, "fsdp", None),
        P(None, "fsdp"),
        P(None, "fsdp"),
        P(None, "fsdp"),
    )
    return jax.shard_map(
        functools.partial(per_device, dict(mesh.shape) == {"dp": 2, "fsdp": 16}),
        mesh=mesh,
        in_specs=placed,
        out_specs=(
            P(None, ("dp", "fsdp"), None, None),
            P(None, ("dp", "fsdp"), None, None),
            P(None, "fsdp", None),
            P(None, "fsdp"),
            P(None, "fsdp"),
            P(None, "fsdp", None),
            P(None, "fsdp"),
            P(None, "fsdp"),
            P(None, "fsdp"),
            P(None, "fsdp", None),
            P(None, "fsdp", None),
            P(None, "fsdp"),
            P(None, "fsdp"),
            P(None, "fsdp"),
        ),
        check_vma=False,
    )
```

```python
import functools
import math

import jax
import jax.numpy as jnp
from jax import lax
from jax.experimental import pallas as pl
from jax.experimental.pallas import tpu as pltpu
from jax.sharding import PartitionSpec as P

MESH = pl.DeviceIdType.MESH

BF = jnp.bfloat16
F32 = jnp.float32
D, HEADS, HEAD_DIM, FF, LAYERS = 768, 12, 64, 3072, 2
EPS = 1e-12
NEG = -1e30
NT = (((1,), (1,)), ((), ()))


def slopes_list(heads_count):
    nearest = 2 ** int(math.floor(math.log2(heads_count)))
    leading = [2.0 ** (-8.0 * (number + 1) / nearest) for number in range(nearest)]
    trailing = [2.0 ** (-8.0 * (number + 1) / (2 * nearest)) for number in range(2 * nearest)][0::2]
    return leading + trailing[: heads_count - nearest]


def mm(a, b):
    return jnp.dot(a, b, preferred_element_type=F32)


def mm_nt(a, b):
    return lax.dot_general(a, b, NT, preferred_element_type=F32)


def erf(x):
    return lax.erf(x)


def norm_parts(r):
    cent = r - jnp.mean(r, axis=-1, keepdims=True)
    rstd = lax.rsqrt(jnp.mean(cent * cent, axis=-1, keepdims=True) + EPS)
    return cent * rstd, rstd


def norm_back(dy, gain, n, rstd):
    dn = dy * gain
    return rstd * (dn - jnp.mean(dn, axis=-1, keepdims=True) - n * jnp.mean(dn * n, axis=-1, keepdims=True))


def halves(v, axis):
    first = lax.broadcasted_iota(jnp.int32, v.shape, axis) < HEAD_DIM
    zero = jnp.zeros_like(v)
    return jnp.where(first, v, zero), jnp.where(first, zero, v)


def attention_kernel(len_ref, slope_ref, x_ref, wq_ref, wk_ref, wv_ref, vec_ref, q_ref, k_ref, v_ref, att_ref, pt_ref, xt_ref, at_ref, xb_ref, dist_ref):
    i = pl.program_id(0)
    seqs, pad = pt_ref.shape[0], pt_ref.shape[-1]

    @pl.when(i == 0)
    def _():
        xb = x_ref[...].astype(BF)
        xb_ref[...] = xb
        xt_ref[...] = xb.T
        keys = lax.broadcasted_iota(jnp.int32, (pad, pad), 0)
        rows = lax.broadcasted_iota(jnp.int32, (pad, pad), 1)
        dist_ref[...] = jnp.abs(keys - rows).astype(F32)
    xb = xb_ref[...]
    q_ref[...] = (mm(xb, wq_ref[...]) + vec_ref[0:1, :]).astype(BF)
    k_ref[...] = mm(xb, wk_ref[...]).astype(BF)
    v_ref[...] = (mm(xb, wv_ref[...]) + vec_ref[1:2, :]).astype(BF)
    for s in range(seqs):
        rows = slice(s * pad, (s + 1) * pad)
        hidden = jnp.where(lax.broadcasted_iota(jnp.int32, (pad, 1), 0) < len_ref[s], 0.0, NEG)
        for pair in range(2):
            lanes = slice(128 * pair, 128 * pair + 128)
            q2 = q_ref[rows, lanes] * BF(HEAD_DIM ** -0.5)
            k0, k1 = halves(k_ref[rows, lanes], 1)
            v0, v1 = halves(v_ref[rows, lanes].T, 0)
            total = None
            for h, (kh, vh) in enumerate(((k0, v0), (k1, v1))):
                slope = slope_ref[4 * i + 2 * pair + h]
                sc = mm_nt(kh, q2) - slope * dist_ref[...] + hidden
                e = jnp.exp(sc - jnp.max(sc, axis=0, keepdims=True))
                p = (e * (1.0 / jnp.sum(e, axis=0, keepdims=True))).astype(BF)
                pt_ref[s, 2 * pair + h] = p
                part = mm(vh, p)
                total = part if total is None else total + part
            total = total.astype(BF)
            at_ref[lanes, rows] = total
            att_ref[rows, lanes] = total.T


def attention_forward(l, lengths, slopes, x, w_qkv, vec):
    rows = x.shape[0]
    seqs = lengths.shape[0]
    pad = rows // seqs
    col = lambda off: pl.BlockSpec((None, D, 256), lambda i: (l, 0, off + i))
    blk = pl.BlockSpec((rows, 256), lambda i: (0, i))
    smem = pl.BlockSpec(memory_space=pltpu.SMEM)
    act = jax.ShapeDtypeStruct((rows, D), BF)
    return pl.pallas_call(
        attention_kernel,
        grid=(3,),
        in_specs=[smem, smem, pl.BlockSpec((rows, D), lambda i: (0, 0)), col(0), col(3), col(6), pl.BlockSpec((None, 8, 256), lambda i: (l, 0, i))],
        out_specs=[blk, blk, blk, blk, pl.BlockSpec((seqs, 4, pad, pad), lambda i: (0, i, 0, 0)), pl.BlockSpec((D, rows), lambda i: (0, 0)), pl.BlockSpec((256, rows), lambda i: (i, 0))],
        out_shape=[act, act, act, act, jax.ShapeDtypeStruct((seqs, HEADS, pad, pad), BF), jax.ShapeDtypeStruct((D, rows), BF), jax.ShapeDtypeStruct((D, rows), BF)],
        scratch_shapes=[pltpu.VMEM((rows, D), BF), pltpu.VMEM((pad, pad), F32)],
        compiler_params=pltpu.CompilerParams(vmem_limit_bytes=56 * 2**20),
        name="attention_forward",
    )(lengths, slopes, x, w_qkv, w_qkv, w_qkv, vec)


def ff_kernel(att_ref, x_ref, wo_ref, wg_ref, wu_ref, wd_ref, vec_ref, r1_ref, r2_ref, ga_ref, gb_ref, ft_ref, ht_ref, out_ref, h_ref, hb_ref, acc_ref):
    j = pl.program_id(0)

    @pl.when(j == 0)
    def _():
        r1 = x_ref[...].astype(F32) + (mm(att_ref[...], wo_ref[...]) + vec_ref[2:3, :])
        r1_ref[...] = r1
        h = norm_parts(r1)[0] * vec_ref[3:4, :] + vec_ref[4:5, :]
        h_ref[...] = h
        hb = h.astype(BF)
        hb_ref[...] = hb
        ht_ref[...] = hb.T
        acc_ref[...] = jnp.zeros_like(acc_ref)
    hb = hb_ref[...]
    g = mm(hb, wg_ref[...])
    u = mm(hb, wu_ref[...])
    cdf = 0.5 + 0.5 * erf(g * math.sqrt(0.5))
    gelu = g * cdf
    slope = cdf + g * (jnp.exp(-0.5 * (g * g)) * (1.0 / math.sqrt(2.0 * math.pi)))
    ga_ref[...] = gelu.astype(BF)
    gb_ref[...] = (slope * u).astype(BF)
    f = (gelu * u).astype(BF)
    ft_ref[...] = f.T
    acc_ref[...] += mm(f, wd_ref[...])

    @pl.when(j == pl.num_programs(0) - 1)
    def _():
        r2 = h_ref[...] + (acc_ref[...] + vec_ref[5:6, :])
        r2_ref[...] = r2
        out_ref[...] = (norm_parts(r2)[0] * vec_ref[6:7, :] + vec_ref[7:8, :]).astype(out_ref.dtype)


def ff_forward(l, att, x, w_out, w_gated, w_down, vec, out_dtype):
    rows = x.shape[0]
    n = FF // 768
    whole = pl.BlockSpec((rows, D), lambda j: (0, 0))
    blk = pl.BlockSpec((rows, 768), lambda j: (0, j))
    return pl.pallas_call(
        ff_kernel,
        grid=(n,),
        in_specs=[whole, whole, pl.BlockSpec((None, D, D), lambda j: (l, 0, 0)),
                  pl.BlockSpec((None, D, 768), lambda j: (l, 0, j)), pl.BlockSpec((None, D, 768), lambda j: (l, 0, n + j)),
                  pl.BlockSpec((None, 768, D), lambda j: (l, j, 0)), pl.BlockSpec((None, 8, D), lambda j: (l, 0, 0))],
        out_specs=[whole, whole, blk, blk, pl.BlockSpec((768, rows), lambda j: (j, 0)), pl.BlockSpec((D, rows), lambda j: (0, 0)), whole],
        out_shape=[jax.ShapeDtypeStruct((rows, D), F32), jax.ShapeDtypeStruct((rows, D), F32),
                   jax.ShapeDtypeStruct((rows, FF), BF), jax.ShapeDtypeStruct((rows, FF), BF),
                   jax.ShapeDtypeStruct((FF, rows), BF), jax.ShapeDtypeStruct((D, rows), BF), jax.ShapeDtypeStruct((rows, D), out_dtype)],
        scratch_shapes=[pltpu.VMEM((rows, D), F32), pltpu.VMEM((rows, D), BF), pltpu.VMEM((rows, D), F32)],
        compiler_params=pltpu.CompilerParams(vmem_limit_bytes=56 * 2**20),
        name="ff_forward",
    )(att, x, w_out, w_gated, w_gated, w_down, vec)


def colsum(v):
    return jnp.sum(v, axis=0, keepdims=True)


def ff_back_kernel(dy_ref, r1_ref, r2_ref, ga_ref, gb_ref, wo_ref, wg_ref, wu_ref, wd_ref, vec_ref, dm_ref, dg_ref, du_ref, dr1_ref, da_ref, datt_ref, gv_ref, acc_ref):
    j = pl.program_id(0)

    @pl.when(j == 0)
    def _():
        dy = dy_ref[...].astype(F32)
        n, rstd = norm_parts(r2_ref[...])
        dr2 = norm_back(dy, vec_ref[6:7, :], n, rstd)
        acc_ref[...] = dr2
        dm = dr2.astype(BF)
        dm_ref[...] = dm
        gv_ref[5:6, :] = colsum(dm.astype(F32))
        gv_ref[6:7, :] = colsum(dy * n)
        gv_ref[7:8, :] = colsum(dy)
        gv_ref[0:2, :] = jnp.zeros((2, D), F32)
    df = mm_nt(dm_ref[...], wd_ref[...])
    dg = (df * gb_ref[...].astype(F32)).astype(BF)
    du = (df * ga_ref[...].astype(F32)).astype(BF)
    dg_ref[...] = dg
    du_ref[...] = du
    acc_ref[...] += mm_nt(dg, wg_ref[...]) + mm_nt(du, wu_ref[...])

    @pl.when(j == pl.num_programs(0) - 1)
    def _():
        dh = acc_ref[...]
        n, rstd = norm_parts(r1_ref[...])
        dr1 = norm_back(dh, vec_ref[3:4, :], n, rstd)
        dr1_ref[...] = dr1
        da = dr1.astype(BF)
        da_ref[...] = da
        gv_ref[2:3, :] = colsum(da.astype(F32))
        gv_ref[3:4, :] = colsum(dh * n)
        gv_ref[4:5, :] = colsum(dh)
        datt_ref[...] = mm_nt(da, wo_ref[...]).astype(BF)


def ff_backward(l, dy, r1, r2, ga, gb, w_out, w_gated, w_down, vec):
    rows = dy.shape[0]
    n = FF // 768
    whole = pl.BlockSpec((rows, D), lambda j: (0, 0))
    blk = pl.BlockSpec((rows, 768), lambda j: (0, j))
    act = lambda c, t: jax.ShapeDtypeStruct((rows, c), t)
    return pl.pallas_call(
        ff_back_kernel,
        grid=(n,),
        in_specs=[whole, whole, whole, blk, blk, pl.BlockSpec((None, D, D), lambda j: (l, 0, 0)),
                  pl.BlockSpec((None, D, 768), lambda j: (l, 0, j)), pl.BlockSpec((None, D, 768), lambda j: (l, 0, n + j)),
                  pl.BlockSpec((None, 768, D), lambda j: (l, j, 0)), pl.BlockSpec((None, 8, D), lambda j: (l, 0, 0))],
        out_specs=[whole, blk, blk, whole, whole, whole, pl.BlockSpec((8, D), lambda j: (0, 0))],
        out_shape=[act(D, BF), act(FF, BF), act(FF, BF), act(D, F32), act(D, BF), act(D, BF), jax.ShapeDtypeStruct((8, D), F32)],
        scratch_shapes=[pltpu.VMEM((rows, D), F32)],
        compiler_params=pltpu.CompilerParams(vmem_limit_bytes=56 * 2**20),
        name="ff_backward",
    )(dy, r1, r2, ga, gb, w_out, w_gated, w_gated, w_down, vec)


def attention_back_kernel(datt_ref, q_ref, k_ref, v_ref, pt_ref, wq_ref, wk_ref, wv_ref, dr1_ref, dq_ref, dk_ref, dv_ref, dx_ref, gb_ref, acc_ref):
    i = pl.program_id(0)
    seqs, pad = pt_ref.shape[0], pt_ref.shape[-1]
    scale = HEAD_DIM ** -0.5

    @pl.when(i == 0)
    def _():
        acc_ref[...] = dr1_ref[...]
    first = lax.broadcasted_iota(jnp.int32, (pad, 128), 1) < HEAD_DIM
    for s in range(seqs):
        rows = slice(s * pad, (s + 1) * pad)
        for pair in range(2):
            lanes = slice(128 * pair, 128 * pair + 128)
            q2 = q_ref[rows, lanes]
            d2 = datt_ref[rows, lanes]
            vs = halves(v_ref[rows, lanes], 1)
            ks = halves(k_ref[rows, lanes].T, 0)
            dv, dk, dq = [], [], None
            for h in range(2):
                pb = pt_ref[s, 2 * pair + h]
                p = pb.astype(F32)
                dp = mm_nt(vs[h], d2)
                ds = (p * (dp - jnp.sum(dp * p, axis=0, keepdims=True))).astype(BF)
                dv.append(mm(pb, d2))
                dk.append(mm(ds, q2))
                part = mm(ks[h], ds)
                dq = part if dq is None else dq + part
            dv_ref[rows, lanes] = jnp.where(first, dv[0], dv[1]).astype(BF)
            dk_ref[rows, lanes] = (jnp.where(first, dk[0], dk[1]) * scale).astype(BF)
            dq_ref[rows, lanes] = (dq * scale).astype(BF).T
    dq, dk, dv = dq_ref[...], dk_ref[...], dv_ref[...]
    gb_ref[0:1, :] = colsum(dq.astype(F32))
    gb_ref[1:2, :] = colsum(dv.astype(F32))
    gb_ref[2:8, :] = jnp.zeros((6, 256), F32)
    acc_ref[...] += mm_nt(dq, wq_ref[...]) + mm_nt(dk, wk_ref[...]) + mm_nt(dv, wv_ref[...])

    @pl.when(i == pl.num_programs(0) - 1)
    def _():
        dx_ref[...] = acc_ref[...].astype(dx_ref.dtype)


def attention_backward(l, datt, q, k, v, pt, w_qkv, dr1, out_dtype):
    rows = datt.shape[0]
    seqs, _, pad, _ = pt.shape
    col = lambda off: pl.BlockSpec((None, D, 256), lambda i: (l, 0, off + i))
    blk = pl.BlockSpec((rows, 256), lambda i: (0, i))
    whole = pl.BlockSpec((rows, D), lambda i: (0, 0))
    act = jax.ShapeDtypeStruct((rows, D), BF)
    return pl.pallas_call(
        attention_back_kernel,
        grid=(3,),
        in_specs=[blk, blk, blk, blk, pl.BlockSpec((seqs, 4, pad, pad), lambda i: (0, i, 0, 0)), col(0), col(3), col(6), whole],
        out_specs=[blk, blk, blk, whole, pl.BlockSpec((8, 256), lambda i: (0, i))],
        out_shape=[act, act, act, jax.ShapeDtypeStruct((rows, D), out_dtype), jax.ShapeDtypeStruct((8, D), F32)],
        scratch_shapes=[pltpu.VMEM((rows, D), F32)],
        compiler_params=pltpu.CompilerParams(vmem_limit_bytes=56 * 2**20),
        name="attention_backward",
    )(datt, q, k, v, pt, w_qkv, w_qkv, w_qkv, dr1)


def place():
    y = lax.axis_index("dp"); f = lax.axis_index("fsdp")
    z = f // 4; x = lax.rem(f // 2, 2); c = lax.rem(f, 2)
    return z, x, y, c

def dev(z, x, y, c):
    return (y, (z * 2 + x) * 2 + c)

PIECES = 8 * LAYERS
EARLY = 3


def along_z(p):
    return lax.rem(p, 5) == 3

KEPT = ("r1", "r2", "ga", "gb", "q", "k", "v", "pt", "ft", "ht", "at", "xt")


class Group:
    def __init__(self, names, refs):
        for name, ref in zip(names, refs):
            setattr(self, name, ref)


def taker(refs):
    refs = list(refs)

    def take(*names):
        g = Group(names, refs[: len(names)])
        del refs[: len(names)]
        return g
    return take


def run(cp, go):
    if go:
        cp.start()
    else:
        cp.wait()


def cols(ref, j, width):
    return ref.at[:, pl.ds(pl.multiple_of(j * width, width), width)]


def matrix_loads(w, p, k, dst, sem):
    return [pltpu.make_async_copy(w.at[p, :, :, :, h, k], dst.at[:, :, :, :, pl.ds(384 * h, 384)], sem) for h in range(2)]


def wait_all(dst, sem):
    pltpu.make_async_copy(dst, dst, sem).wait()


def forward_kernel(*refs):
    take = taker(refs)
    i_ = take("lens", "slopes", "x", "qkv", "out", "gated", "down", *["v%d" % i for i in range(8)])
    o_ = take("w", "v", "vec", "last")
    kept = [take(*KEPT) for _ in range(LAYERS)]
    t_ = take("x", "xb", "dist", "q", "k", "v", "att", "pt", "at", "xt", "wq", "wk", "wv", "wo", "wg", "wu", "wd", "h", "hb", "f", "ga", "gb", "ft", "res", "last", "vown", "vwide", "vec_in")
    m_ = take("local", "zsend", "fsend", "xysend", "rsend", "csend", "recv", "crecv", "vlocal", "vload", "load", "wload", "store")
    pad = t_.pt.shape[-1]
    seqs = t_.pt.shape[0]

    z, x, y, c = place()
    zp = z + 1 - 2 * lax.rem(z, 2)
    zm = 3 - z
    zf = lax.rem(z + 2, 4)
    mid = jnp.logical_and(z >= 1, z <= 2)
    end = jnp.logical_not(mid)
    d_zp, d_zm = dev(zp, x, y, c), dev(zm, x, y, c)
    d_x, d_y, d_c = dev(z, 1 - x, y, c), dev(z, x, 1 - y, c), dev(z, x, y, 1 - c)
    bar = pltpu.get_barrier_semaphore()
    for d in (d_zp, d_zm, d_x, d_y, d_c):
        pl.semaphore_signal(bar, 1, device_id=d, device_id_type=MESH)


    def local(p):
        u = lax.rem(p, 8)
        l = p // 8

        def put(h, k, src):
            pltpu.make_async_copy(src, o_.w.at[p, z, x, c, h, k], m_.local.at[p]).start()

        def part(ref, off):
            return ref.at[l, :, pl.ds(pl.multiple_of(off, 128), 384)]
        for h in range(2):
            @pl.when(u == 0)
            def _():
                put(h, 0, part(i_.qkv, 384 * h))
                put(h, 1, part(i_.qkv, 768 + 384 * h))

            @pl.when(u == 1)
            def _():
                put(h, 0, part(i_.qkv, 1536 + 384 * h))
                put(h, 1, part(i_.out, 384 * h))

            @pl.when(jnp.logical_and(u >= 2, u < 6))
            def _():
                j = jnp.clip(u - 2, 0, 3) * 768
                put(h, 0, part(i_.gated, j + 384 * h))
                put(h, 1, part(i_.gated, j + FF + 384 * h))

            @pl.when(u >= 6)
            def _():
                for k in range(2):
                    r = pl.multiple_of(jnp.clip(2 * (u - 6) + k, 0, 3) * 48, 48)
                    put(h, k, i_.down.at[l, pl.ds(r, 48), pl.ds(384 * h, 384)])

    for p in range(EARLY):
        local(p)
    t_.vwide[...] = jnp.zeros_like(t_.vwide)
    for n in range(8):
        row = getattr(i_, "v%d" % n)[...].astype(F32)
        for l in range(LAYERS):
            t_.vwide[l, n : n + 1, 0:48] = row[l : l + 1, :]
    t_.vown[...] = t_.vwide[...].astype(BF)
    vplace = pltpu.make_async_copy(t_.vown, o_.v.at[z, x, c], m_.vlocal.at[0])
    vplace.start()
    xload = pltpu.make_async_copy(i_.x, t_.last, m_.vlocal.at[1])
    xload.start()
    pl.semaphore_wait(bar, 5)


    def stages(b, s):
        def copy(zz, xx, hh, sem, d):
            u = b(zz, xx, c, hh)
            return pltpu.make_async_remote_copy(src_ref=u, dst_ref=u, send_sem=sem.at[s], recv_sem=m_.recv.at[s, (zz * 2 + xx) * 2 + hh], device_id=d, device_id_type=MESH)

        def zsend(zz, d, sem=m_.fsend):
            copy(zz, x, y, sem, d).start()

        def got(zz, xx, hh, d):
            copy(zz, xx, hh, m_.zsend, d).wait_recv()

        def plane(zz, cc=c):
            u = b(zz, slice(None), cc, slice(None))
            return pltpu.make_async_remote_copy(src_ref=u, dst_ref=u, send_sem=m_.csend.at[s], recv_sem=m_.crecv.at[s, zz], device_id=d_c, device_id_type=MESH)

        def spread(zz):
            copy(zz, x, y, m_.xysend, d_x).start()
            copy(zz, x, y, m_.xysend, d_y).start()

        def relay(zz, first_x):
            got(zz, 1 - x, y, d_x)
            got(zz, x, 1 - y, d_y)

            def through_y():
                copy(zz, 1 - x, y, m_.rsend, d_y).start()

            def through_x():
                copy(zz, x, 1 - y, m_.rsend, d_x).start()
            if first_x is True:
                through_y()
            elif first_x is False:
                through_x()
            else:
                pl.when(first_x)(through_y)
                pl.when(jnp.logical_not(first_x))(through_x)

        def diagonal(zz):
            got(zz, 1 - x, 1 - y, d_y)
            plane(zz).start()

        def st0():
            zsend(z, d_zp, m_.zsend)
            pl.when(mid)(lambda: zsend(z, d_zm, m_.zsend))
            copy(z, x, y, m_.xysend, d_x).start()

        def st1():
            got(zp, x, y, d_zp)

            @pl.when(mid)
            def _():
                zsend(zp, d_zm)
                got(zm, x, y, d_zm)
                zsend(zm, d_zp)
            spread(zp)
            got(z, 1 - x, y, d_x)
            copy(z, 1 - x, y, m_.xysend, d_y).start()

        def st2():
            got(zf, x, y, d_zp)
            pl.when(mid)(lambda: zsend(zf, d_zp))
            spread(zf)
            relay(zp, True)
            diagonal(z)

        def st3():
            pl.when(end)(lambda: got(zm, x, y, d_zp))
            spread(zm)
            relay(zf, False)
            diagonal(zp)

        def st4():
            relay(zm, lax.rem(s, 2) == 0)
            diagonal(zf)

        def st5():
            diagonal(zm)

        def st6():
            for zz in (z, zp, zf, zm):
                plane(zz, 1 - c).wait_recv()
        return st0, st1, st2, st3, st4, st5, st6

    def stages_z(b, s):
        def copy(zz, xx, hh, sem, d):
            u = b(zz, xx, c, hh)
            at = 0 if isinstance(hh, slice) else hh
            return pltpu.make_async_remote_copy(src_ref=u, dst_ref=u, send_sem=sem.at[s], recv_sem=m_.recv.at[s, (zz * 2 + xx) * 2 + at], device_id=d, device_id_type=MESH)
        both = slice(None)

        def zsend(zz, xx, d, sem=m_.fsend):
            copy(zz, xx, both, sem, d).start()

        def got(zz, xx, d):
            copy(zz, xx, both, m_.zsend, d).wait_recv()

        def plane(zz, cc=c):
            u = b(zz, both, cc, both)
            return pltpu.make_async_remote_copy(src_ref=u, dst_ref=u, send_sem=m_.csend.at[s], recv_sem=m_.crecv.at[s, zz], device_id=d_c, device_id_type=MESH)

        def own(xx):
            zsend(z, xx, d_zp, m_.zsend)
            pl.when(mid)(lambda: zsend(z, xx, d_zm, m_.zsend))

        def near(xx):
            got(zp, xx, d_zp)

            @pl.when(mid)
            def _():
                zsend(zp, xx, d_zm)
                got(zm, xx, d_zm)
                zsend(zm, xx, d_zp)

        def far(xx):
            got(zf, xx, d_zp)
            pl.when(mid)(lambda: zsend(zf, xx, d_zp))

        def farthest(xx):
            pl.when(end)(lambda: got(zm, xx, d_zp))

        def st0():
            own(x)
            copy(z, x, y, m_.xysend, d_x).start()

        def st1():
            near(x)
            copy(z, 1 - x, y, m_.xysend, d_x).wait_recv()
            copy(z, 1 - x, y, m_.xysend, d_y).start()

        def st2():
            far(x)
            copy(z, 1 - x, 1 - y, m_.xysend, d_y).wait_recv()
            own(1 - x)
            plane(z).start()

        def st3():
            farthest(x)
            near(1 - x)
            plane(zp).start()

        def st4():
            far(1 - x)
            plane(zf).start()

        def st5():
            farthest(1 - x)
            plane(zm).start()

        def st6():
            for zz in (z, zp, zf, zm):
                plane(zz, 1 - c).wait_recv()
        return st0, st1, st2, st3, st4, st5, st6

    def sent_z(s):
        wait_all(o_.w.at[0, 0, 0, 0], m_.xysend.at[s])
        wait_all(many_w(16), m_.csend.at[s])
        pl.when(end)(lambda: wait_all(o_.w.at[0, 0, 0], m_.zsend.at[s]))

        @pl.when(mid)
        def _():
            wait_all(many_w(8), m_.zsend.at[s])
            wait_all(o_.w.at[0, 0:3, :, 0], m_.fsend.at[s])

    def sent(b, s, many):
        wait_all(many(8), m_.xysend.at[s])
        wait_all(many(3), m_.rsend.at[s])
        wait_all(many(16), m_.csend.at[s])
        pl.when(end)(lambda: wait_all(many(1), m_.zsend.at[s]))

        @pl.when(mid)
        def _():
            wait_all(many(2), m_.zsend.at[s])
            wait_all(many(3), m_.fsend.at[s])

    def unit(p):
        return lambda zz, xx, cc, hh: o_.w.at[p, zz, xx, cc, hh]

    def vunit(zz, xx, cc, hh):
        return o_.v.at[zz, xx, cc, hh]

    def many_w(n):
        if n == 8:
            return o_.w.at[0, 0]
        if n == 16:
            return o_.w.at[0, :, :, 0]
        return o_.w.at[0:n, 0, 0, 0, 0]

    def many_v(n):
        if n == 8:
            return o_.v.at[0]
        if n == 16:
            return o_.v.at[:, :, 0]
        return o_.v.at[0:n, 0, 0, 0]


    def load_att(l):
        for cp in matrix_loads(o_.w, 8 * l, 0, t_.wq, m_.wload.at[0]) + matrix_loads(o_.w, 8 * l, 1, t_.wk, m_.wload.at[1]) + matrix_loads(o_.w, 8 * l + 1, 0, t_.wv, m_.wload.at[2]) + matrix_loads(o_.w, 8 * l + 1, 1, t_.wo, m_.wload.at[3]):
            cp.start()

    def load_gated(l, j):
        for cp in matrix_loads(o_.w, 8 * l + 2 + j, 0, t_.wg, m_.wload.at[4]) + matrix_loads(o_.w, 8 * l + 2 + j, 1, t_.wu, m_.wload.at[5]):
            cp.start()

    def load_down(l, part):
        for s in (2 * part, 2 * part + 1):
            for h in range(2):
                pltpu.make_async_copy(o_.w.at[8 * l + 6 + s // 2, :, :, :, h, s % 2], t_.wd.at[:, :, :, s, :, pl.ds(384 * h, 384)], m_.wload.at[6]).start()

    def store(i, src, dst, go):
        run(pltpu.make_async_copy(src, dst, m_.store.at[i]), go)

    def per_layer(l, f):
        for n in range(LAYERS):
            @pl.when(l == n)
            def _():
                f(kept[n])

    def vrow(l, n):
        return o_.vec[l, n : n + 1, :]

    def store_att(kl, i, go):
        store(0, t_.q, cols(kl.q, i, 256), go)
        store(1, t_.k, cols(kl.k, i, 256), go)
        store(2, t_.v, cols(kl.v, i, 256), go)
        store(3, t_.pt, kl.pt.at[:, pl.ds(4 * i, 4)], go)
        store(4, t_.at, kl.at.at[pl.ds(pl.multiple_of(256 * i, 256), 256)], go)

        @pl.when(i == 0)
        def _():
            store(5, t_.xt, kl.xt, go)

    def att_task(l, i):
        @pl.when(i == 0)
        def _():
            wait_all(t_.wq, m_.wload.at[0])
            wait_all(t_.wk, m_.wload.at[1])
            wait_all(t_.wv, m_.wload.at[2])
            xb = t_.x[...].astype(BF)
            t_.xb[...] = xb
            t_.xt[...] = xb.T
        xb = t_.xb[...]
        lane = pl.multiple_of(256 * i, 256)
        at = pl.ds(lane, 256)
        t_.q[...] = (mm(xb, t_.wq[:, :, :, :, at].reshape(D, 256)) + o_.vec[l, 0:1, at]).astype(BF)
        t_.k[...] = mm(xb, t_.wk[:, :, :, :, at].reshape(D, 256)).astype(BF)
        t_.v[...] = (mm(xb, t_.wv[:, :, :, :, at].reshape(D, 256)) + o_.vec[l, 1:2, at]).astype(BF)
        for s in range(seqs):
            rows = slice(s * pad, (s + 1) * pad)
            hidden = jnp.where(lax.broadcasted_iota(jnp.int32, (pad, 1), 0) < i_.lens[s], 0.0, NEG)
            for pair in range(2):
                lanes = slice(128 * pair, 128 * pair + 128)
                q2 = t_.q[rows, lanes] * BF(HEAD_DIM ** -0.5)
                ks = halves(t_.k[rows, lanes], 1)
                vs = halves(t_.v[rows, lanes].T, 0)
                total = None
                for h in range(2):
                    slope = i_.slopes[4 * i + 2 * pair + h]
                    sc = mm_nt(ks[h], q2) - slope * t_.dist[...] + hidden
                    e = jnp.exp(sc - jnp.max(sc, axis=0, keepdims=True))
                    p = (e * (1.0 / jnp.sum(e, axis=0, keepdims=True))).astype(BF)
                    t_.pt[s, 2 * pair + h] = p
                    part = mm(vs[h], p)
                    total = part if total is None else total + part
                total = total.astype(BF)
                t_.at[lanes, rows] = total
                t_.att[rows, pl.ds(pl.multiple_of(lane + 128 * pair, 128), 128)] = total.T
        per_layer(l, lambda kl: store_att(kl, i, True))

    def store_ff(kl, j, go):
        store(6, t_.ga, cols(kl.ga, j, 768), go)
        store(7, t_.gb, cols(kl.gb, j, 768), go)
        store(8, t_.ft, kl.ft.at[pl.ds(pl.multiple_of(768 * j, 768), 768)], go)

        @pl.when(j == 0)
        def _():
            store(9, t_.res, kl.r1, go)
            store(10, t_.xt, kl.ht, go)

    def ff_task(l, j):
        @pl.when(j == 0)
        def _():
            wait_all(t_.wo, m_.wload.at[3])
            r1 = t_.x[...] + (mm(t_.att[...], t_.wo[...].reshape(D, D)) + vrow(l, 2))
            t_.res[...] = r1
            h = norm_parts(r1)[0] * vrow(l, 3) + vrow(l, 4)
            t_.h[...] = h
            hb = h.astype(BF)
            t_.hb[...] = hb
            t_.xt[...] = hb.T
        wait_all(t_.wg, m_.wload.at[4])
        wait_all(t_.wu, m_.wload.at[5])
        hb = t_.hb[...]
        g = mm(hb, t_.wg[...].reshape(D, 768))
        u = mm(hb, t_.wu[...].reshape(D, 768))
        cdf = 0.5 + 0.5 * erf(g * math.sqrt(0.5))
        gelu = g * cdf
        slope = cdf + g * (jnp.exp(-0.5 * (g * g)) * (1.0 / math.sqrt(2.0 * math.pi)))
        t_.ga[...] = gelu.astype(BF)
        t_.gb[...] = (slope * u).astype(BF)
        f = (gelu * u).astype(BF)
        t_.f[j] = f
        t_.ft[...] = f.T
        per_layer(l, lambda kl: store_ff(kl, j, True))

    def down_task(l):
        wait_all(t_.wd, m_.wload.at[6])
        total = t_.h[...] + vrow(l, 5)
        for j in range(4):
            total = total + mm(t_.f[j], t_.wd[j].reshape(768, D))
        t_.res[...] = total
        out = norm_parts(total)[0] * vrow(l, 6) + vrow(l, 7)
        t_.x[...] = out
        per_layer(l, lambda kl: store(9, t_.res, kl.r2, True))

        @pl.when(l == LAYERS - 1)
        def _():
            t_.last[...] = out.astype(BF)
            store(11, t_.last, o_.last, True)

    def task(t, att, ff, down):
        l = t // 8
        u = lax.rem(t, 8)
        pl.when(u < 3)(lambda: att(l, jnp.minimum(u, 2)))
        pl.when(jnp.logical_and(u >= 3, u < 7))(lambda: ff(l, jnp.clip(u - 3, 0, 3)))
        pl.when(u == 7)(lambda: down(l))

    def stored(t):
        task(t, lambda l, i: store_att(kept[0], i, False), lambda l, j: store_ff(kept[0], j, False), lambda l: store(9, t_.res, kept[0].r2, False))

    def fetch(t):
        def att(l, i):
            pl.when(i == 0)(lambda: load_att(l))

        def ff(l, j):
            load_gated(l, j)
            pl.when(j == 3)(lambda: load_down(l, 0))
        task(t, att, ff, lambda l: load_down(l, 1))


    vst = stages(vunit, PIECES)

    def begun(r):
        return jnp.clip(jnp.where(r <= 15, r - 7, r - 6), 0, 8 * LAYERS)

    def first(p):
        wait_all(o_.w.at[p, z, x, c], m_.local.at[p])
        pl.when(along_z(p))(stages_z(unit(p), p)[0])
        pl.when(jnp.logical_not(along_z(p)))(stages(unit(p), p)[0])

    def body(r, carry):
        def at(k):
            p = r - k

            @pl.when(jnp.logical_and(p >= 0, p < PIECES))
            def _():
                q = jnp.clip(p, 0, PIECES - 1)
                pl.when(along_z(q))(lambda: stages_z(unit(q), q)[k]())
                pl.when(jnp.logical_not(along_z(q)))(lambda: stages(unit(q), q)[k]())

        @pl.when(r + EARLY < PIECES)
        def _():
            local(jnp.minimum(r + EARLY, PIECES - 1))

        @pl.when(r < PIECES)
        def _():
            first(jnp.minimum(r, PIECES - 1))
        for k in range(1, 7):
            pl.when(r == k)(vst[k])
        at(6)
        low, high = begun(r), begun(r + 1)

        @pl.when(high > low)
        def _():
            fetch(jnp.minimum(low, 8 * LAYERS - 1))
        for k in (1, 2, 3, 4, 5):
            at(k)

        @pl.when(r == 6)
        def _():
            cp = pltpu.make_async_copy(o_.v, t_.vec_in, m_.vload)
            cp.start()
            xload.wait()
            t_.x[...] = t_.last[...].astype(F32)
            keys = lax.broadcasted_iota(jnp.int32, (pad, pad), 0)
            rows = lax.broadcasted_iota(jnp.int32, (pad, pad), 1)
            t_.dist[...] = jnp.abs(keys - rows).astype(F32)
            cp.wait()
            unpack_vectors()

        def one(t, carry):
            @pl.when(t >= 1)
            def _():
                stored(jnp.maximum(t - 1, 0))
            task(t, att_task, ff_task, down_task)
            return carry
        lax.fori_loop(low, high, one, 0)
        return carry

    def unpack_vectors():
        for l in range(LAYERS):
            parts = [t_.vec_in[b // 4, (b // 2) % 2, b % 2, l].astype(F32)[:, 0:48] for b in range(16)]
            o_.vec[l] = jnp.concatenate(parts, axis=1)
    vplace.wait()
    vst[0]()
    lax.fori_loop(0, PIECES + 6, body, 0)
    stored(8 * LAYERS - 1)
    store(11, t_.last, o_.last, False)

    def finish(p, carry):
        pl.when(along_z(p))(lambda: sent_z(p))
        pl.when(jnp.logical_not(along_z(p)))(lambda: sent(unit(p), p, many_w))
        return carry
    lax.fori_loop(0, PIECES, finish, 0)
    sent(vunit, PIECES, many_v)


def forward_all(lengths, slopes, x, shards, vectors):
    rows = x.shape[0]
    seqs = lengths.shape[0]
    pad = rows // seqs
    hbm = pl.BlockSpec(memory_space=pltpu.HBM)
    vmem = pl.BlockSpec(memory_space=pltpu.VMEM)
    smem = pl.BlockSpec(memory_space=pltpu.SMEM)
    S = jax.ShapeDtypeStruct
    act = lambda n, t: S((rows, n), t)
    one = [act(D, F32), act(D, F32), act(FF, BF), act(FF, BF), act(D, BF), act(D, BF), act(D, BF), S((seqs, HEADS, pad, pad), BF), S((FF, rows), BF), S((D, rows), BF), S((D, rows), BF), S((D, rows), BF)]
    out = [S((PIECES, 4, 2, 2, 2, 2, 48, 384), BF), S((4, 2, 2, 2, 8, 128), BF), S((LAYERS, 8, D), F32), act(D, BF)] + one * LAYERS
    v = pltpu.VMEM
    dma = pltpu.SemaphoreType.DMA
    mat = v((4, 2, 2, 48, D), BF)
    n = PIECES + 1
    scratch = [
        v((rows, D), F32), v((rows, D), BF), v((pad, pad), F32), v((rows, 256), BF), v((rows, 256), BF), v((rows, 256), BF), v((rows, D), BF),
        v((seqs, 4, pad, pad), BF), v((256, rows), BF), v((D, rows), BF), mat, mat, mat, mat, mat, mat, v((4, 2, 2, 4, 48, D), BF),
        v((rows, D), F32), v((rows, D), BF), v((4, rows, 768), BF), v((rows, 768), BF), v((rows, 768), BF), v((768, rows), BF), v((rows, D), F32), v((rows, D), BF),
        v((2, 8, 128), BF), v((2, 8, 128), F32), v((4, 2, 2, 2, 8, 128), BF),
        dma((PIECES,)), dma((n,)), dma((n,)), dma((n,)), dma((n,)), dma((n,)), dma((n, 16)), dma((n, 4)), dma((2,)), dma, dma, dma((7,)), dma((12,)),
    ]
    res = pl.pallas_call(
        forward_kernel, out_shape=out,
        in_specs=[smem, smem, hbm] + [hbm] * 4 + [vmem] * 8,
        out_specs=[hbm, hbm, vmem, hbm] + [hbm] * (12 * LAYERS),
        scratch_shapes=scratch,
        compiler_params=pltpu.CompilerParams(collective_id=0, has_side_effects=True, vmem_limit_bytes=60 * 2**20), name="gather_forward",
    )(lengths, slopes, x, *shards, *vectors)
    return res[0], res[2], res[3], [res[4 + 12 * l : 16 + 12 * l] for l in range(LAYERS)]


NPIECE = 33
LAG = 2
SLOTS = 16


STEPS = (0, 1, 4, 6, 8, 10, 12, 14)
STEPS_Z = (0, 1, 4, 7, 9, 11, 12, 13)


def reduce_z(p):
    return lax.rem(p, 4) == 1


def piece_first_x(p):
    others = p - (p + 2) // 4
    return jnp.logical_or(reduce_z(p), lax.rem(others * 5, 8) < 5)


def add_into(dst, src):
    dst[...] = dst[...] + src[...]


GRADS = ("dg", "du", "dq", "dk", "dv")


def backward_kernel(*refs):
    take = taker(refs)
    i_ = take("cot", "vec")
    cot, vec = i_.cot, i_.vec
    kept = [take(*KEPT) for _ in range(LAYERS)]
    w = take("w").w
    o = take("qkv", "out", "gated", "down", "vec", "dx")
    g = take(*GRADS)
    s = take("lbuf", "rbuf", "sbuf", "own", "stage", "r0v", "h1v", "h2v", "zav", "zbv", "yfv", "vall")
    c_ = take("r0", "h1", "h2", "za", "zb", "yf", "zza", "zzb")
    t_ = take("acc", "res", "wd", "wg", "wu", "ga", "gb", "wo", "dm", "dg", "du", "da", "datt", "q", "k", "v", "pt", "wq", "wk", "wv", "dq", "dk", "dv", "gv", "cot")
    m_ = take("lsem", "rsem", "send", "recv", "out", "vload", "fsem", "asem", "osem")
    pad = kept[0].pt.shape[-1]
    seqs = kept[0].pt.shape[0]

    z, x, y, c = place()
    zp = z + 1 - 2 * lax.rem(z, 2)
    zm = 3 - z
    mid = jnp.logical_and(z >= 1, z <= 2)
    end = jnp.logical_not(mid)
    d_zp, d_zm = dev(zp, x, y, c), dev(zm, x, y, c)
    d_x, d_y, d_c = dev(z, 1 - x, y, c), dev(z, x, 1 - y, c), dev(z, x, y, 1 - c)
    bar = pltpu.get_barrier_semaphore()
    for d in (d_zp, d_zm, d_x, d_y, d_c):
        pl.semaphore_signal(bar, 1, device_id=d, device_id_type=MESH)
    NP = NPIECE - 1


    def load_ff(l, j, go):
        def one(i, src, dst):
            run(pltpu.make_async_copy(src, dst, m_.fsem.at[i]), go)
        def acts(kl):
            @pl.when(j == 0)
            def _():
                one(5, kl.r2, t_.res)

            @pl.when(j == 3)
            def _():
                one(5, kl.r1, t_.res)
            one(3, cols(kl.ga, j, 768), t_.ga)
            one(4, cols(kl.gb, j, 768), t_.gb)
        if go:
            for i in range(LAYERS):
                @pl.when(l == i)
                def _():
                    acts(kept[i])
        else:
            one(3, cols(kept[0].ga, j, 768), t_.ga)
            one(4, cols(kept[0].gb, j, 768), t_.gb)

            @pl.when(j == 3)
            def _():
                one(5, kept[0].r1, t_.res)

        if go:
            for n in range(4):
                for h in range(2):
                    one(0, w.at[8 * l + 6 + n // 2, j, :, :, h, n % 2], t_.wd.at[:, :, n, :, pl.ds(384 * h, 384)])
            for cp in matrix_loads(w, 8 * l + 2 + j, 0, t_.wg, m_.fsem.at[1]) + matrix_loads(w, 8 * l + 2 + j, 1, t_.wu, m_.fsem.at[2]):
                cp.start()
        else:
            wait_all(t_.wd, m_.fsem.at[0])
            wait_all(t_.wg, m_.fsem.at[1])
            wait_all(t_.wu, m_.fsem.at[2])

        @pl.when(j == 3)
        def _():
            if go:
                for cp in matrix_loads(w, 8 * l + 1, 1, t_.wo, m_.fsem.at[6]):
                    cp.start()
            else:
                wait_all(t_.wo, m_.fsem.at[6])

    def load_att(l, i, go):
        def one(n, src, dst):
            run(pltpu.make_async_copy(src, dst, m_.asem.at[n]), go)

        def acts(kl):
            one(0, cols(kl.q, i, 256), t_.q)
            one(1, cols(kl.k, i, 256), t_.k)
            one(2, cols(kl.v, i, 256), t_.v)
            one(3, kl.pt.at[:, pl.ds(4 * i, 4)], t_.pt)
        if go:
            for n in range(LAYERS):
                @pl.when(l == n)
                def _():
                    acts(kept[n])
        else:
            acts(kept[0])
        @pl.when(i == 0)
        def _():
            for n, dst in enumerate((t_.wq, t_.wk, t_.wv)):
                if go:
                    for cp in matrix_loads(w, 8 * l + n // 2, n % 2, dst, m_.asem.at[4 + n]):
                        cp.start()
                else:
                    wait_all(dst, m_.asem.at[4 + n])

    def norm_two(l):
        pltpu.make_async_copy(kept[0].r2, t_.res, m_.fsem.at[5]).wait()
        dy = t_.acc[...]
        n, rstd = norm_parts(t_.res[...])
        dr2 = norm_back(dy, vec[l, 6:7, :], n, rstd)
        t_.acc[...] = dr2
        dm = dr2.astype(BF)
        t_.dm[...] = dm
        t_.gv[l, 5:6, :] = colsum(dm.astype(F32))
        t_.gv[l, 6:7, :] = colsum(dy * n)
        t_.gv[l, 7:8, :] = colsum(dy)

    def ff_task(l, j):
        load_ff(l, j, False)

        @pl.when(jnp.logical_and(j == 0, l < LAYERS - 1))
        def _():
            norm_two(l)
        df = mm_nt(t_.dm[...], t_.wd[...].reshape(768, D))
        dg = (df * t_.gb[...].astype(F32)).astype(BF)
        du = (df * t_.ga[...].astype(F32)).astype(BF)
        t_.dg[...] = dg
        t_.du[...] = du
        t_.acc[...] += mm_nt(dg, t_.wg[...].reshape(D, 768)) + mm_nt(du, t_.wu[...].reshape(D, 768))

        @pl.when(j == 3)
        def _():
            dh = t_.acc[...]
            n, rstd = norm_parts(t_.res[...])
            dr1 = norm_back(dh, vec[l, 3:4, :], n, rstd)
            t_.acc[...] = dr1
            da = dr1.astype(BF)
            t_.da[...] = da
            t_.gv[l, 2:3, :] = colsum(da.astype(F32))
            t_.gv[l, 3:4, :] = colsum(dh * n)
            t_.gv[l, 4:5, :] = colsum(dh)
            datt = mm_nt(da, t_.wo[...].reshape(D, D)).astype(BF)
            for i in range(3):
                t_.datt[i] = datt[:, 256 * i : 256 * i + 256]
        store_ff(l, j, True)

        @pl.when(j < 3)
        def _():
            load_ff(l, j + 1, True)

        @pl.when(j == 3)
        def _():
            load_att(l, 0, True)

    def store_ff(l, j, go):
        def one(i, src, dst):
            run(pltpu.make_async_copy(src, dst, m_.osem.at[i]), go)
        one(0, t_.dg, cols(g.dg.at[l], j, 768))
        one(1, t_.du, cols(g.du.at[l], j, 768))

    def att_task(l, i):
        load_att(l, i, False)
        scale = HEAD_DIM ** -0.5
        first = lax.broadcasted_iota(jnp.int32, (pad, 128), 1) < HEAD_DIM
        for sq in range(seqs):
            rows = slice(sq * pad, (sq + 1) * pad)
            for pair in range(2):
                lanes = slice(128 * pair, 128 * pair + 128)
                q2 = t_.q[rows, lanes]
                d2 = t_.datt[i, rows, lanes]
                vs = halves(t_.v[rows, lanes], 1)
                ks = halves(t_.k[rows, lanes].T, 0)
                dv, dk, dq = [], [], None
                for h in range(2):
                    pb = t_.pt[sq, 2 * pair + h]
                    p = pb.astype(F32)
                    dp = mm_nt(vs[h], d2)
                    ds = (p * (dp - jnp.sum(dp * p, axis=0, keepdims=True))).astype(BF)
                    dv.append(mm(pb, d2))
                    dk.append(mm(ds, q2))
                    part = mm(ks[h], ds)
                    dq = part if dq is None else dq + part
                t_.dv[rows, lanes] = jnp.where(first, dv[0], dv[1]).astype(BF)
                t_.dk[rows, lanes] = (jnp.where(first, dk[0], dk[1]) * scale).astype(BF)
                t_.dq[rows, lanes] = (dq * scale).astype(BF).T
        dq, dk, dv = t_.dq[...], t_.dk[...], t_.dv[...]
        at = pl.ds(pl.multiple_of(i * 256, 256), 256)
        t_.gv[l, 0:1, at] = colsum(dq.astype(F32))
        t_.gv[l, 1:2, at] = colsum(dv.astype(F32))
        t_.acc[...] += (
            mm_nt(dq, t_.wq[:, :, :, :, at].reshape(D, 256)) + mm_nt(dk, t_.wk[:, :, :, :, at].reshape(D, 256)) + mm_nt(dv, t_.wv[:, :, :, :, at].reshape(D, 256))
        )
        store_att(l, i, True)

        @pl.when(i < 2)
        def _():
            load_att(l, i + 1, True)

        @pl.when(jnp.logical_and(i == 2, l > 0))
        def _():
            load_ff(jnp.maximum(l - 1, 0), 0, True)

        @pl.when(jnp.logical_and(i == 2, l == 0))
        def _():
            t_.cot[...] = t_.acc[...].astype(BF)
            pltpu.make_async_copy(t_.cot, o.dx, m_.osem.at[7]).start()

    def store_att(l, i, go):
        def one(n, src, dst):
            run(pltpu.make_async_copy(src, dst, m_.osem.at[n]), go)
        one(4, t_.dq, cols(g.dq.at[l], i, 256))
        one(5, t_.dk, cols(g.dk.at[l], i, 256))
        one(6, t_.dv, cols(g.dv.at[l], i, 256))

    def task(t, ff, att):
        l = LAYERS - 1 - t // 7
        u = lax.rem(t, 7)

        @pl.when(u < 4)
        def _():
            ff(l, jnp.minimum(u, 3))

        @pl.when(u >= 4)
        def _():
            att(l, jnp.clip(u - 4, 0, 2))


    def load(p, go):
        q = lax.rem(p, 16)
        n = lax.rem(p, 2)
        layer = LAYERS - 1 - p // 16

        def left(ref, sub=None):
            for k in range(2):
                cc = c if k else 1 - c
                src = ref.at[:, cc] if sub is None else ref.at[:, cc, sub]
                run(pltpu.make_async_copy(src, s.lbuf.at[n, k], m_.lsem.at[n, k]), go)

        def right(ref, col=None):
            src = ref if col is None else cols(ref.at[layer], jnp.clip(col, 0, 3), 768)
            run(pltpu.make_async_copy(src, s.rbuf.at[n], m_.rsem.at[n]), go)
        if not go:
            left(kept[0].ht)
            right(t_.dm)
            return
        for l in range(LAYERS):
            here = layer == l
            kl = kept[l]

            @pl.when(jnp.logical_and(here, q < 4))
            def _():
                left(kl.ft, jnp.minimum(q, 3))

            @pl.when(jnp.logical_and(here, jnp.logical_and(q >= 4, q < 12)))
            def _():
                left(kl.ht)

            @pl.when(jnp.logical_and(here, q == 12))
            def _():
                left(kl.at)

            @pl.when(jnp.logical_and(here, q > 12))
            def _():
                left(kl.xt)

        @pl.when(q < 4)
        def _():
            right(t_.dm)

        @pl.when(jnp.logical_and(q >= 4, q < 8))
        def _():
            right(g.dg, q - 4)

        @pl.when(jnp.logical_and(q >= 8, q < 12))
        def _():
            right(g.du, q - 8)
        for i, d in enumerate((t_.da, g.dq.at[layer], g.dk.at[layer], g.dv.at[layer])):
            @pl.when(q == 12 + i)
            def _():
                right(d)

    def rcopy(p, e, src, dst, d):
        return pltpu.make_async_remote_copy(src_ref=src, dst_ref=dst, send_sem=m_.send.at[p, e], recv_sem=m_.recv.at[p, e], device_id=d, device_id_type=MESH)

    def product(n, theirs, mine):
        v = mm(s.lbuf[n].reshape(768, -1), s.rbuf[n]).astype(BF).reshape(2, 4, 2, 48, 768)
        for k, dst in enumerate((theirs, mine)):
            dst[:, :, 0] = v[k, :, :, :, :384]
            dst[:, :, 1] = v[k, :, :, :, 384:]

    def c_copy(p, n):
        return rcopy(p, 0, s.sbuf.at[n], c_.r0.at[lax.rem(p, SLOTS)], d_c)

    def s0(p):
        n = lax.rem(p, 2)
        load(p, False)

        @pl.when(p >= 2)
        def _():
            c_copy(jnp.maximum(p - 2, 0), n).wait_send()
        product(n, s.sbuf.at[n], s.own.at[lax.rem(p, LAG + 1)])
        c_copy(p, n).start()

        @pl.when(p + 1 < NP)
        def _():
            load(jnp.minimum(p + 1, NP - 1), True)
    small = Group(("r0", "h1", "h2", "za", "zb", "yf"), (s.r0v, s.h1v, s.h2v, s.zav, s.zbv, s.yfv))
    zlo = jnp.where(z == 1, 1, 0)
    elo = jnp.where(z == 0, 1, 0)
    mlo = jnp.where(z == 1, 2, 0)
    rlo = jnp.where(z == 1, 0, 2)

    def steps(b, p, i, my):
        fx = piece_first_x(p)
        fy = jnp.logical_not(fx)

        def hop1(go):
            a = rcopy(p, 1, b.r0.at[i, :, 1 - x], b.h1.at[i], d_x)
            if go == "start":
                pl.when(fx)(a.start)
                pl.when(fy)(rcopy(p, 1, b.r0.at[i, :, :, 1 - y], b.h1.at[i], d_y).start)
            elif go == "recv":
                a.wait_recv()
            else:
                a.wait_send()

        def hop2(go):
            a = rcopy(p, 2, b.h1.at[i, :, 1 - y], b.h2.at[i], d_y)
            if go == "start":
                pl.when(fx)(a.start)
                pl.when(fy)(rcopy(p, 2, b.h1.at[i, :, 1 - x], b.h2.at[i], d_x).start)
            elif go == "recv":
                a.wait_recv()
            else:
                a.wait_send()

        def z1():
            return rcopy(p, 3, b.h2.at[i, pl.ds(elo, 3)], b.za.at[i], d_zp)

        def z2():
            return rcopy(p, 4, b.h2.at[i, pl.ds(mlo, 2)], b.zb.at[i], d_zm)

        def z3():
            return rcopy(p, 5, b.h2.at[i, zp], b.zb.at[i, 0], d_zp)

        def y1():
            return rcopy(p, 6, b.h2.at[i, z], b.yf.at[i], d_y)

        def s1():
            rcopy(p, 0, b.r0.at[i], b.r0.at[i], d_c).wait_recv()
            for k in range(4):
                add_into(b.r0.at[i, k], my.at[k])
            hop1("start")

        def s2():
            hop1("recv")
            for k in range(4):
                @pl.when(fx)
                def _():
                    add_into(b.h1.at[i, k], b.r0.at[i, k, x])

                @pl.when(fy)
                def _():
                    add_into(b.h1.at[i, k], b.r0.at[i, k, :, y])
            hop2("start")

        def s3():
            hop1("send")
            hop2("recv")
            t = jnp.where(fx, y, x)
            for k in range(4):
                add_into(b.h2.at[i, k], b.h1.at[i, k, t])
            pl.when(end)(z1().start)

        def s4():
            hop2("send")

            @pl.when(mid)
            def _():
                z1().wait_recv()
                for k in range(3):
                    add_into(b.h2.at[i, zlo + k], b.za.at[i, k])
                z2().start()

        def s5():
            pl.when(end)(z1().wait_send)

            @pl.when(mid)
            def _():
                z2().wait_recv()
                for k in range(2):
                    add_into(b.h2.at[i, rlo + k], b.zb.at[i, k])
                z3().start()

        def s6():
            pl.when(mid)(z2().wait_send)

            @pl.when(end)
            def _():
                z3().wait_recv()
                add_into(b.h2.at[i, z], b.zb.at[i, 0])
            y1().start()

        def s7():
            pl.when(mid)(z3().wait_send)
            y1().wait_send()
            y1().wait_recv()
        return s1, s2, s3, s4, s5, s6, s7

    def steps_z(p, i, my):
        b = c_
        fx = piece_first_x(p)
        iz = lax.rem(p // 4, SLOTS // 4)

        def hop1():
            return rcopy(p, 1, b.r0.at[i, z, 1 - x], b.h1.at[i, 0], d_x)

        def hop2():
            return rcopy(p, 2, b.h1.at[i, 0, 1 - y], b.h2.at[i, z], d_y)

        def z1():
            return rcopy(p, 3, b.r0.at[i, pl.ds(elo, 3)], b.zza.at[iz], d_zp)

        def z2():
            return rcopy(p, 4, b.r0.at[i, pl.ds(mlo, 2)], b.zzb.at[iz], d_zm)

        def z3():
            return rcopy(p, 5, b.r0.at[i, zp], b.zzb.at[iz, 0], d_zp)

        def y1():
            return rcopy(p, 6, b.h2.at[i, z], b.yf.at[i], d_y)

        def s1():
            rcopy(p, 0, b.r0.at[i], b.r0.at[i], d_c).wait_recv()
            for k in range(4):
                add_into(b.r0.at[i, k], my.at[k])
            pl.when(end)(z1().start)

        def s2():
            @pl.when(mid)
            def _():
                z1().wait_recv()
                for k in range(3):
                    add_into(b.r0.at[i, zlo + k], b.zza.at[iz, k])
                z2().start()

        def s3():
            pl.when(end)(z1().wait_send)

            @pl.when(mid)
            def _():
                z2().wait_recv()
                for k in range(2):
                    add_into(b.r0.at[i, rlo + k], b.zzb.at[iz, k])
                z3().start()

        def s4():
            pl.when(mid)(z2().wait_send)

            @pl.when(end)
            def _():
                z3().wait_recv()
                add_into(b.r0.at[i, z], b.zzb.at[iz, 0])
            hop1().start()

        def s5():
            pl.when(mid)(z3().wait_send)
            hop1().wait_recv()
            add_into(b.h1.at[i, 0], b.r0.at[i, z, x])
            hop2().start()

        def s6():
            hop1().wait_send()
            hop2().wait_recv()
            add_into(b.h2.at[i, z], b.h1.at[i, 0, y])
            y1().start()

        def s7():
            hop2().wait_send()
            y1().wait_send()
            y1().wait_recv()
        return s1, s2, s3, s4, s5, s6, s7

    def out_copy(p, n, go):
        q = lax.rem(p, 16)
        layer = LAYERS - 1 - p // 16

        def one(dst):
            run(pltpu.make_async_copy(s.stage.at[n], dst, m_.out.at[n]), go)
        if not go:
            one(o.out.at[0])
            return

        @pl.when(q < 4)
        def _():
            one(o.down.at[layer, pl.ds(pl.multiple_of(jnp.minimum(q, 3) * 48, 48), 48)])

        @pl.when(jnp.logical_and(q >= 4, q < 12))
        def _():
            one(cols(o.gated.at[layer], jnp.clip(q - 4, 0, 7), 768))

        @pl.when(q == 12)
        def _():
            one(o.out.at[layer])

        @pl.when(q > 12)
        def _():
            one(cols(o.qkv.at[layer], jnp.clip(q - 13, 0, 2), 768))

    def write(p):
        n = lax.rem(p, 2)

        @pl.when(p >= 2)
        def _():
            out_copy(p, n, False)
        i = lax.rem(p, SLOTS)
        a = c_.h2[i, z]
        b = c_.yf[i]

        @pl.when(y == 0)
        def _():
            s.stage[n, :, :384] = a
            s.stage[n, :, 384:] = b

        @pl.when(y == 1)
        def _():
            s.stage[n, :, :384] = b
            s.stage[n, :, 384:] = a
        out_copy(p, n, True)


    vp = NP
    vc = rcopy(vp, 0, s.vall.at[1 - c], s.r0v.at[0], d_c)
    vsteps = steps(small, vp, 0, s.vall.at[c])
    VSTART = 27

    def pack_vectors():
        for l in range(LAYERS):
            v = jnp.concatenate([t_.gv[l], jnp.zeros((120, D), F32)], axis=0).T.astype(BF)
            for k in range(16):
                s.vall[k % 2, k // 4, (k // 2) % 2, l] = v[48 * k : 48 * k + 48]
        vc.start()


    top = LAYERS - 1
    first = pltpu.make_async_copy(cot, t_.cot, m_.vload)
    first.start()
    load_ff(top, 0, True)
    first.wait()
    t_.acc[...] = t_.cot[...].astype(F32)
    norm_two(top)
    load(0, True)
    pl.semaphore_wait(bar, 5)

    def task_of(r):
        t = jnp.where(jnp.logical_and(lax.rem(r, 2) == 1, r >= 7), (r + 1) // 2, -1)
        for n, at in enumerate((1, 2, 4, 5)):
            t = jnp.where(r == at, n, t)
        return jnp.where(t <= 13, t, -1)

    def body(r, carry):
        def at(k, off, f, kind=None):
            p = r - off[k]
            q = jnp.clip(p, 0, NP - 1)
            here = jnp.logical_and(p >= 0, p < NP)
            if kind is not None:
                here = jnp.logical_and(here, reduce_z(q) == kind)

            @pl.when(here)
            def _():
                f(q)

        def st(k, kind):
            def f(p):
                own = s.own.at[lax.rem(p, LAG + 1)]
                i = lax.rem(p, SLOTS)
                (steps_z(p, i, own) if kind else steps(c_, p, i, own))[k - 1]()
                if k == 7:
                    write(p)
            return f

        now, before = task_of(r), task_of(r - 1)

        @pl.when(before >= 0)
        def _():
            task(jnp.clip(before, 0, 13), lambda l, j: store_ff(l, j, False), lambda l, i: store_att(l, i, False))
        for k in range(1, 8):
            pl.when(r == VSTART + STEPS[k])(vsteps[k - 1])
        at(0, STEPS, s0)
        for k in range(7, 0, -1):
            at(k, STEPS_Z, st(k, True), True)
            at(k, STEPS, st(k, False), False)
        pl.when(r == VSTART)(pack_vectors)

        @pl.when(now >= 0)
        def _():
            task(jnp.clip(now, 0, 13), ff_task, att_task)
        return carry
    lax.fori_loop(0, NP + max(STEPS[7], STEPS_Z[7]), body, 0)

    for p in (NP - 2, NP - 1):
        c_copy(p, p % 2).wait_send()
        out_copy(p, p % 2, False)
    vc.wait_send()
    pltpu.make_async_copy(t_.cot, o.dx, m_.osem.at[7]).wait()
    va, vb = s.h2v[0, z].astype(F32), s.yfv[0].astype(F32)
    o.vec[0] = jnp.where(y == 0, va, vb)
    o.vec[1] = jnp.where(y == 0, vb, va)


def backward_all(cot, vec, kept, w):
    rows = cot.shape[0]
    hbm = pl.BlockSpec(memory_space=pltpu.HBM)
    vmem = pl.BlockSpec(memory_space=pltpu.VMEM)
    kept = [tuple(k[:8]) + (k[8].reshape(8, 2, 4, 48, rows),) + tuple(a.reshape(8, 2, 48, rows) for a in k[9:]) for k in kept]
    act = lambda c, t: jax.ShapeDtypeStruct((rows, c), t)
    out = [
        jax.ShapeDtypeStruct((LAYERS, 48, 3 * D), BF), jax.ShapeDtypeStruct((LAYERS, 48, D), BF),
        jax.ShapeDtypeStruct((LAYERS, 48, 2 * FF), BF), jax.ShapeDtypeStruct((LAYERS, 192, D), BF),
        jax.ShapeDtypeStruct((2, 48, 128), F32), act(D, BF),
    ]
    both = lambda c: jax.ShapeDtypeStruct((LAYERS, rows, c), BF)
    scratch_out = [both(FF), both(FF), both(D), both(D), both(D)]
    seqs, _, pad, _ = kept[0][7].shape
    v = pltpu.VMEM
    dma = pltpu.SemaphoreType.DMA
    mat = v((4, 2, 2, 48, D), BF)
    n = SLOTS
    scratch = [
        v((2, 2, 8, 48, rows), BF), v((2, rows, 768), BF), v((2, 4, 2, 2, 48, 384), BF), v((LAG + 1, 4, 2, 2, 48, 384), BF), v((2, 48, 768), BF),
        v((1, 4, 2, 2, 48, 128), BF), v((1, 4, 2, 48, 128), BF), v((1, 4, 48, 128), BF),
        v((1, 3, 48, 128), BF), v((1, 2, 48, 128), BF), v((1, 48, 128), BF), v((2, 4, 2, 2, 48, 128), BF),
        v((n, 4, 2, 2, 48, 384), BF), v((n, 4, 2, 48, 384), BF), v((n, 4, 48, 384), BF), v((n, 3, 48, 384), BF), v((n, 2, 48, 384), BF), v((n, 48, 384), BF), v((n // 4, 3, 2, 2, 48, 384), BF), v((n // 4, 2, 2, 2, 48, 384), BF),
        v((rows, D), F32), v((rows, D), F32), v((2, 2, 4, 48, D), BF), mat, mat, v((rows, 768), BF), v((rows, 768), BF), mat,
        v((rows, D), BF), v((rows, 768), BF), v((rows, 768), BF), v((rows, D), BF), v((3, rows, 256), BF),
        v((rows, 256), BF), v((rows, 256), BF), v((rows, 256), BF), v((seqs, 4, pad, pad), BF), mat, mat, mat,
        v((rows, 256), BF), v((rows, 256), BF), v((rows, 256), BF), v((LAYERS, 8, D), F32), v((rows, D), BF),
        dma((2, 2)), dma((2,)), dma((NPIECE, 7)), dma((NPIECE, 7)), dma((2,)), dma, dma((7,)), dma((7,)), dma((8,)),
    ]
    res = pl.pallas_call(
        backward_kernel, out_shape=out + scratch_out,
        in_specs=[hbm, vmem] + [hbm] * 25,
        out_specs=[hbm] * 4 + [vmem] + [hbm] * 6,
        scratch_shapes=scratch,
        compiler_params=pltpu.CompilerParams(collective_id=1, has_side_effects=True, vmem_limit_bytes=62 * 2**20), name="backward_reduce",
    )(cot, vec, *kept[0], *kept[1], w)
    return res[:4], res[4], res[5]


def finish_kernel(qkv, out, gated, down, vec, last, dx, *outs):
    for src, dst in zip((qkv, out, gated, down, last, dx), outs[:6]):
        dst[...] = src[...].astype(dst.dtype)

    @pl.when(pl.program_id(0) == 0)
    def _():
        for l in range(LAYERS):
            rows = vec[l].T
            for n in range(8):
                outs[6 + n][l : l + 1, :] = rows[n : n + 1, :]


def finish_all(mats, vec, last, dx):
    rows = last.shape[0]
    half = pl.BlockSpec((rows // 2, D), lambda i: (i, 0))
    blocks = [pl.BlockSpec((1,) + m.shape[1:], lambda i: (i, 0, 0)) for m in mats]
    vecs = pl.BlockSpec((LAYERS, 48), lambda i: (0, 0))
    S = jax.ShapeDtypeStruct
    return pl.pallas_call(
        finish_kernel,
        grid=(LAYERS,),
        in_specs=blocks + [pl.BlockSpec(vec.shape, lambda i: (0, 0, 0)), half, half],
        out_specs=blocks + [half, half] + [vecs] * 8,
        out_shape=[S(m.shape, F32) for m in mats] + [S(last.shape, BF), S(dx.shape, BF)] + [S((LAYERS, 48), F32)] * 8,
        name="finish",
    )(*mats, vec, last, dx)


def forward_plain(seq_lengths, slopes, x, shards, vectors):
    mats = [lax.all_gather(w, "fsdp", axis=1, tiled=True) for w in shards]
    vec = lax.all_gather(jnp.stack(vectors, axis=1), "fsdp", axis=2, tiled=True).astype(F32)
    wq, wo, wg, wd = mats
    kept = []
    for l in range(LAYERS):
        q, k, v, att, pt, xt, at = attention_forward(l, seq_lengths, slopes, x, wq, vec)
        out_dtype = BF if l == LAYERS - 1 else F32
        r1, r2, ga, gb, ft, ht, x = ff_forward(l, att, x, wo, wg, wd, vec, out_dtype)
        kept.append((r1, r2, ga, gb, q, k, v, pt, ft, ht, at, xt))
    return mats, vec, x, kept


def backward_plain(dy, vec, kept, mats):
    wq, wo, wg, wd = mats

    def one(g, dim):
        part = lax.psum_scatter(g.astype(BF), "fsdp", scatter_dimension=dim, tiled=True)
        return lax.psum(part, "dp").astype(F32)
    sums, vecs = [None] * LAYERS, [None] * LAYERS
    for l in reversed(range(LAYERS)):
        r1, r2, ga, gb, q, k, v, pt, ft, ht, at, xt = kept[l]
        dm, dg, du, dr1, da, datt, gv = ff_backward(l, dy, r1, r2, ga, gb, wo, wg, wd, vec)
        dq, dk, dv, dy, gbias = attention_backward(l, datt, q, k, v, pt, wq, dr1, BF if l == 0 else F32)
        pairs = ((xt, jnp.concatenate([dq, dk, dv], axis=1)), (at, da), (ht, jnp.concatenate([dg, du], axis=1)), (ft, dm))
        sums[l] = [one(mm(a, b), 0) for a, b in pairs]
        vecs[l] = gv + gbias
    return [jnp.stack(m) for m in zip(*sums)], one(jnp.stack(vecs), 2), dy


def per_device(fast, inputs, lengths, cotangent, w_qkv, q_bias, v_bias, w_out, b_out, gain_one, shift_one, w_gated, w_down, b_down, gain_two, shift_two):
    shards = (w_qkv, w_out, w_gated, w_down)
    vectors = (q_bias, v_bias, b_out, gain_one, shift_one, b_down, gain_two, shift_two)
    seq_lengths = lengths.reshape(-1)
    slopes = jnp.array(slopes_list(HEADS), F32)
    x = inputs.reshape(-1, D)
    dy = cotangent.reshape(-1, D)
    if fast:
        w, vec, x, kept = forward_all(seq_lengths, slopes, x, shards, vectors)
        m, packed, dx = backward_all(dy, vec, kept, w)
        *m, x, dx, v0, v1, v2, v3, v4, v5, v6, v7 = finish_all(m, packed, x, dx)
    else:
        mats, vec, x, kept = forward_plain(seq_lengths, slopes, x, shards, vectors)
        m, vs, dx = backward_plain(dy, vec, kept, mats)
        v0, v1, v2, v3, v4, v5, v6, v7 = (vs[:, n] for n in range(8))
    return (
        x.reshape(inputs.shape), dx.reshape(inputs.shape), m[0], v0, v1, m[1], v2, v3, v4, m[2], m[3], v5, v6, v7,
    )


def solution(mesh):
    placed = (
        P(None, ("dp", "fsdp"), None, None),
        P(None, ("dp", "fsdp")),
        P(None, ("dp", "fsdp"), None, None),
        P(None, "fsdp", None),
        P(None, "fsdp"),
        P(None, "fsdp"),
        P(None, "fsdp", None),
        P(None, "fsdp"),
        P(None, "fsdp"),
        P(None, "fsdp"),
        P(None, "fsdp", None),
        P(None, "fsdp", None),
        P(None, "fsdp"),
        P(None, "fsdp"),
        P(None, "fsdp"),
    )
    return jax.shard_map(
        functools.partial(per_device, dict(mesh.shape) == {"dp": 2, "fsdp": 16}),
        mesh=mesh,
        in_specs=placed,
        out_specs=(
            P(None, ("dp", "fsdp"), None, None),
            P(None, ("dp", "fsdp"), None, None),
            P(None, "fsdp", None),
            P(None, "fsdp"),
            P(None, "fsdp"),
            P(None, "fsdp", None),
            P(None, "fsdp"),
            P(None, "fsdp"),
            P(None, "fsdp"),
            P(None, "fsdp", None),
            P(None, "fsdp", None),
            P(None, "fsdp"),
            P(None, "fsdp"),
            P(None, "fsdp"),
        ),
        check_vma=False,
    )
```

```python
import functools
import math

import jax
import jax.numpy as jnp
from jax import lax
from jax.experimental import pallas as pl
from jax.experimental.pallas import tpu as pltpu
from jax.sharding import PartitionSpec as P

MESH = pl.DeviceIdType.MESH

BF = jnp.bfloat16
F32 = jnp.float32
D, HEADS, HEAD_DIM, FF, LAYERS = 768, 12, 64, 3072, 2
EPS = 1e-12
NEG = -1e30
NT = (((1,), (1,)), ((), ()))


def slopes_list(heads_count):
    nearest = 2 ** int(math.floor(math.log2(heads_count)))
    leading = [2.0 ** (-8.0 * (number + 1) / nearest) for number in range(nearest)]
    trailing = [2.0 ** (-8.0 * (number + 1) / (2 * nearest)) for number in range(2 * nearest)][0::2]
    return leading + trailing[: heads_count - nearest]


def mm(a, b):
    return jnp.dot(a, b, preferred_element_type=F32)


def mm_nt(a, b):
    return lax.dot_general(a, b, NT, preferred_element_type=F32)


def erf(x):
    return lax.erf(x)


def norm_parts(r):
    cent = r - jnp.mean(r, axis=-1, keepdims=True)
    rstd = lax.rsqrt(jnp.mean(cent * cent, axis=-1, keepdims=True) + EPS)
    return cent * rstd, rstd


def norm_back(dy, gain, n, rstd):
    dn = dy * gain
    return rstd * (dn - jnp.mean(dn, axis=-1, keepdims=True) - n * jnp.mean(dn * n, axis=-1, keepdims=True))


def halves(v, axis):
    first = lax.broadcasted_iota(jnp.int32, v.shape, axis) < HEAD_DIM
    zero = jnp.zeros_like(v)
    return jnp.where(first, v, zero), jnp.where(first, zero, v)


def attention_kernel(len_ref, slope_ref, x_ref, wq_ref, wk_ref, wv_ref, vec_ref, q_ref, k_ref, v_ref, att_ref, pt_ref, xt_ref, at_ref, xb_ref, dist_ref):
    i = pl.program_id(0)
    seqs, pad = pt_ref.shape[0], pt_ref.shape[-1]

    @pl.when(i == 0)
    def _():
        xb = x_ref[...].astype(BF)
        xb_ref[...] = xb
        xt_ref[...] = xb.T
        keys = lax.broadcasted_iota(jnp.int32, (pad, pad), 0)
        rows = lax.broadcasted_iota(jnp.int32, (pad, pad), 1)
        dist_ref[...] = jnp.abs(keys - rows).astype(F32)
    xb = xb_ref[...]
    q_ref[...] = (mm(xb, wq_ref[...]) + vec_ref[0:1, :]).astype(BF)
    k_ref[...] = mm(xb, wk_ref[...]).astype(BF)
    v_ref[...] = (mm(xb, wv_ref[...]) + vec_ref[1:2, :]).astype(BF)
    for s in range(seqs):
        rows = slice(s * pad, (s + 1) * pad)
        hidden = jnp.where(lax.broadcasted_iota(jnp.int32, (pad, 1), 0) < len_ref[s], 0.0, NEG)
        for pair in range(2):
            lanes = slice(128 * pair, 128 * pair + 128)
            q2 = q_ref[rows, lanes] * BF(HEAD_DIM ** -0.5)
            k0, k1 = halves(k_ref[rows, lanes], 1)
            v0, v1 = halves(v_ref[rows, lanes].T, 0)
            total = None
            for h, (kh, vh) in enumerate(((k0, v0), (k1, v1))):
                slope = slope_ref[4 * i + 2 * pair + h]
                sc = mm_nt(kh, q2) - slope * dist_ref[...] + hidden
                e = jnp.exp(sc - jnp.max(sc, axis=0, keepdims=True))
                p = (e * (1.0 / jnp.sum(e, axis=0, keepdims=True))).astype(BF)
                pt_ref[s, 2 * pair + h] = p
                part = mm(vh, p)
                total = part if total is None else total + part
            total = total.astype(BF)
            at_ref[lanes, rows] = total
            att_ref[rows, lanes] = total.T


def attention_forward(l, lengths, slopes, x, w_qkv, vec):
    rows = x.shape[0]
    seqs = lengths.shape[0]
    pad = rows // seqs
    col = lambda off: pl.BlockSpec((None, D, 256), lambda i: (l, 0, off + i))
    blk = pl.BlockSpec((rows, 256), lambda i: (0, i))
    smem = pl.BlockSpec(memory_space=pltpu.SMEM)
    act = jax.ShapeDtypeStruct((rows, D), BF)
    return pl.pallas_call(
        attention_kernel,
        grid=(3,),
        in_specs=[smem, smem, pl.BlockSpec((rows, D), lambda i: (0, 0)), col(0), col(3), col(6), pl.BlockSpec((None, 8, 256), lambda i: (l, 0, i))],
        out_specs=[blk, blk, blk, blk, pl.BlockSpec((seqs, 4, pad, pad), lambda i: (0, i, 0, 0)), pl.BlockSpec((D, rows), lambda i: (0, 0)), pl.BlockSpec((256, rows), lambda i: (i, 0))],
        out_shape=[act, act, act, act, jax.ShapeDtypeStruct((seqs, HEADS, pad, pad), BF), jax.ShapeDtypeStruct((D, rows), BF), jax.ShapeDtypeStruct((D, rows), BF)],
        scratch_shapes=[pltpu.VMEM((rows, D), BF), pltpu.VMEM((pad, pad), F32)],
        compiler_params=pltpu.CompilerParams(vmem_limit_bytes=56 * 2**20),
        name="attention_forward",
    )(lengths, slopes, x, w_qkv, w_qkv, w_qkv, vec)


def ff_kernel(att_ref, x_ref, wo_ref, wg_ref, wu_ref, wd_ref, vec_ref, r1_ref, r2_ref, ga_ref, gb_ref, ft_ref, ht_ref, out_ref, h_ref, hb_ref, acc_ref):
    j = pl.program_id(0)

    @pl.when(j == 0)
    def _():
        r1 = x_ref[...].astype(F32) + (mm(att_ref[...], wo_ref[...]) + vec_ref[2:3, :])
        r1_ref[...] = r1
        h = norm_parts(r1)[0] * vec_ref[3:4, :] + vec_ref[4:5, :]
        h_ref[...] = h
        hb = h.astype(BF)
        hb_ref[...] = hb
        ht_ref[...] = hb.T
        acc_ref[...] = jnp.zeros_like(acc_ref)
    hb = hb_ref[...]
    g = mm(hb, wg_ref[...])
    u = mm(hb, wu_ref[...])
    cdf = 0.5 + 0.5 * erf(g * math.sqrt(0.5))
    gelu = g * cdf
    slope = cdf + g * (jnp.exp(-0.5 * (g * g)) * (1.0 / math.sqrt(2.0 * math.pi)))
    ga_ref[...] = gelu.astype(BF)
    gb_ref[...] = (slope * u).astype(BF)
    f = (gelu * u).astype(BF)
    ft_ref[...] = f.T
    acc_ref[...] += mm(f, wd_ref[...])

    @pl.when(j == pl.num_programs(0) - 1)
    def _():
        r2 = h_ref[...] + (acc_ref[...] + vec_ref[5:6, :])
        r2_ref[...] = r2
        out_ref[...] = (norm_parts(r2)[0] * vec_ref[6:7, :] + vec_ref[7:8, :]).astype(out_ref.dtype)


def ff_forward(l, att, x, w_out, w_gated, w_down, vec, out_dtype):
    rows = x.shape[0]
    n = FF // 768
    whole = pl.BlockSpec((rows, D), lambda j: (0, 0))
    blk = pl.BlockSpec((rows, 768), lambda j: (0, j))
    return pl.pallas_call(
        ff_kernel,
        grid=(n,),
        in_specs=[whole, whole, pl.BlockSpec((None, D, D), lambda j: (l, 0, 0)),
                  pl.BlockSpec((None, D, 768), lambda j: (l, 0, j)), pl.BlockSpec((None, D, 768), lambda j: (l, 0, n + j)),
                  pl.BlockSpec((None, 768, D), lambda j: (l, j, 0)), pl.BlockSpec((None, 8, D), lambda j: (l, 0, 0))],
        out_specs=[whole, whole, blk, blk, pl.BlockSpec((768, rows), lambda j: (j, 0)), pl.BlockSpec((D, rows), lambda j: (0, 0)), whole],
        out_shape=[jax.ShapeDtypeStruct((rows, D), F32), jax.ShapeDtypeStruct((rows, D), F32),
                   jax.ShapeDtypeStruct((rows, FF), BF), jax.ShapeDtypeStruct((rows, FF), BF),
                   jax.ShapeDtypeStruct((FF, rows), BF), jax.ShapeDtypeStruct((D, rows), BF), jax.ShapeDtypeStruct((rows, D), out_dtype)],
        scratch_shapes=[pltpu.VMEM((rows, D), F32), pltpu.VMEM((rows, D), BF), pltpu.VMEM((rows, D), F32)],
        compiler_params=pltpu.CompilerParams(vmem_limit_bytes=56 * 2**20),
        name="ff_forward",
    )(att, x, w_out, w_gated, w_gated, w_down, vec)


def colsum(v):
    return jnp.sum(v, axis=0, keepdims=True)


def ff_back_kernel(dy_ref, r1_ref, r2_ref, ga_ref, gb_ref, wo_ref, wg_ref, wu_ref, wd_ref, vec_ref, dm_ref, dg_ref, du_ref, dr1_ref, da_ref, datt_ref, gv_ref, acc_ref):
    j = pl.program_id(0)

    @pl.when(j == 0)
    def _():
        dy = dy_ref[...].astype(F32)
        n, rstd = norm_parts(r2_ref[...])
        dr2 = norm_back(dy, vec_ref[6:7, :], n, rstd)
        acc_ref[...] = dr2
        dm = dr2.astype(BF)
        dm_ref[...] = dm
        gv_ref[5:6, :] = colsum(dm.astype(F32))
        gv_ref[6:7, :] = colsum(dy * n)
        gv_ref[7:8, :] = colsum(dy)
        gv_ref[0:2, :] = jnp.zeros((2, D), F32)
    df = mm_nt(dm_ref[...], wd_ref[...])
    dg = (df * gb_ref[...].astype(F32)).astype(BF)
    du = (df * ga_ref[...].astype(F32)).astype(BF)
    dg_ref[...] = dg
    du_ref[...] = du
    acc_ref[...] += mm_nt(dg, wg_ref[...]) + mm_nt(du, wu_ref[...])

    @pl.when(j == pl.num_programs(0) - 1)
    def _():
        dh = acc_ref[...]
        n, rstd = norm_parts(r1_ref[...])
        dr1 = norm_back(dh, vec_ref[3:4, :], n, rstd)
        dr1_ref[...] = dr1
        da = dr1.astype(BF)
        da_ref[...] = da
        gv_ref[2:3, :] = colsum(da.astype(F32))
        gv_ref[3:4, :] = colsum(dh * n)
        gv_ref[4:5, :] = colsum(dh)
        datt_ref[...] = mm_nt(da, wo_ref[...]).astype(BF)


def ff_backward(l, dy, r1, r2, ga, gb, w_out, w_gated, w_down, vec):
    rows = dy.shape[0]
    n = FF // 768
    whole = pl.BlockSpec((rows, D), lambda j: (0, 0))
    blk = pl.BlockSpec((rows, 768), lambda j: (0, j))
    act = lambda c, t: jax.ShapeDtypeStruct((rows, c), t)
    return pl.pallas_call(
        ff_back_kernel,
        grid=(n,),
        in_specs=[whole, whole, whole, blk, blk, pl.BlockSpec((None, D, D), lambda j: (l, 0, 0)),
                  pl.BlockSpec((None, D, 768), lambda j: (l, 0, j)), pl.BlockSpec((None, D, 768), lambda j: (l, 0, n + j)),
                  pl.BlockSpec((None, 768, D), lambda j: (l, j, 0)), pl.BlockSpec((None, 8, D), lambda j: (l, 0, 0))],
        out_specs=[whole, blk, blk, whole, whole, whole, pl.BlockSpec((8, D), lambda j: (0, 0))],
        out_shape=[act(D, BF), act(FF, BF), act(FF, BF), act(D, F32), act(D, BF), act(D, BF), jax.ShapeDtypeStruct((8, D), F32)],
        scratch_shapes=[pltpu.VMEM((rows, D), F32)],
        compiler_params=pltpu.CompilerParams(vmem_limit_bytes=56 * 2**20),
        name="ff_backward",
    )(dy, r1, r2, ga, gb, w_out, w_gated, w_gated, w_down, vec)


def attention_back_kernel(datt_ref, q_ref, k_ref, v_ref, pt_ref, wq_ref, wk_ref, wv_ref, dr1_ref, dq_ref, dk_ref, dv_ref, dx_ref, gb_ref, acc_ref):
    i = pl.program_id(0)
    seqs, pad = pt_ref.shape[0], pt_ref.shape[-1]
    scale = HEAD_DIM ** -0.5

    @pl.when(i == 0)
    def _():
        acc_ref[...] = dr1_ref[...]
    first = lax.broadcasted_iota(jnp.int32, (pad, 128), 1) < HEAD_DIM
    for s in range(seqs):
        rows = slice(s * pad, (s + 1) * pad)
        for pair in range(2):
            lanes = slice(128 * pair, 128 * pair + 128)
            q2 = q_ref[rows, lanes]
            d2 = datt_ref[rows, lanes]
            vs = halves(v_ref[rows, lanes], 1)
            ks = halves(k_ref[rows, lanes].T, 0)
            dv, dk, dq = [], [], None
            for h in range(2):
                pb = pt_ref[s, 2 * pair + h]
                p = pb.astype(F32)
                dp = mm_nt(vs[h], d2)
                ds = (p * (dp - jnp.sum(dp * p, axis=0, keepdims=True))).astype(BF)
                dv.append(mm(pb, d2))
                dk.append(mm(ds, q2))
                part = mm(ks[h], ds)
                dq = part if dq is None else dq + part
            dv_ref[rows, lanes] = jnp.where(first, dv[0], dv[1]).astype(BF)
            dk_ref[rows, lanes] = (jnp.where(first, dk[0], dk[1]) * scale).astype(BF)
            dq_ref[rows, lanes] = (dq * scale).astype(BF).T
    dq, dk, dv = dq_ref[...], dk_ref[...], dv_ref[...]
    gb_ref[0:1, :] = colsum(dq.astype(F32))
    gb_ref[1:2, :] = colsum(dv.astype(F32))
    gb_ref[2:8, :] = jnp.zeros((6, 256), F32)
    acc_ref[...] += mm_nt(dq, wq_ref[...]) + mm_nt(dk, wk_ref[...]) + mm_nt(dv, wv_ref[...])

    @pl.when(i == pl.num_programs(0) - 1)
    def _():
        dx_ref[...] = acc_ref[...].astype(dx_ref.dtype)


def attention_backward(l, datt, q, k, v, pt, w_qkv, dr1, out_dtype):
    rows = datt.shape[0]
    seqs, _, pad, _ = pt.shape
    col = lambda off: pl.BlockSpec((None, D, 256), lambda i: (l, 0, off + i))
    blk = pl.BlockSpec((rows, 256), lambda i: (0, i))
    whole = pl.BlockSpec((rows, D), lambda i: (0, 0))
    act = jax.ShapeDtypeStruct((rows, D), BF)
    return pl.pallas_call(
        attention_back_kernel,
        grid=(3,),
        in_specs=[blk, blk, blk, blk, pl.BlockSpec((seqs, 4, pad, pad), lambda i: (0, i, 0, 0)), col(0), col(3), col(6), whole],
        out_specs=[blk, blk, blk, whole, pl.BlockSpec((8, 256), lambda i: (0, i))],
        out_shape=[act, act, act, jax.ShapeDtypeStruct((rows, D), out_dtype), jax.ShapeDtypeStruct((8, D), F32)],
        scratch_shapes=[pltpu.VMEM((rows, D), F32)],
        compiler_params=pltpu.CompilerParams(vmem_limit_bytes=56 * 2**20),
        name="attention_backward",
    )(datt, q, k, v, pt, w_qkv, w_qkv, w_qkv, dr1)


def place():
    y = lax.axis_index("dp"); f = lax.axis_index("fsdp")
    z = f // 4; x = lax.rem(f // 2, 2); c = lax.rem(f, 2)
    return z, x, y, c

def dev(z, x, y, c):
    return (y, (z * 2 + x) * 2 + c)

PIECES = 8 * LAYERS
EARLY = 3


def along_z(p):
    return lax.rem(p, 5) == 3

KEPT = ("r1", "r2", "ga", "gb", "q", "k", "v", "pt", "ft", "ht", "at", "xt")


class Group:
    def __init__(self, names, refs):
        for name, ref in zip(names, refs):
            setattr(self, name, ref)


def taker(refs):
    refs = list(refs)

    def take(*names):
        g = Group(names, refs[: len(names)])
        del refs[: len(names)]
        return g
    return take


def run(cp, go):
    if go:
        cp.start()
    else:
        cp.wait()


def cols(ref, j, width):
    return ref.at[:, pl.ds(pl.multiple_of(j * width, width), width)]


def matrix_loads(w, p, k, dst, sem):
    return [pltpu.make_async_copy(w.at[p, :, :, :, h, k], dst.at[:, :, :, :, pl.ds(384 * h, 384)], sem) for h in range(2)]


def wait_all(dst, sem):
    pltpu.make_async_copy(dst, dst, sem).wait()


def forward_kernel(*refs):
    take = taker(refs)
    i_ = take("lens", "slopes", "x", "qkv", "out", "gated", "down", *["v%d" % i for i in range(8)])
    o_ = take("w", "v", "vec", "last")
    kept = [take(*KEPT) for _ in range(LAYERS)]
    t_ = take("x", "xb", "dist", "q", "k", "v", "att", "pt", "at", "xt", "wq", "wk", "wv", "wo", "wg", "wu", "wd", "h", "hb", "f", "ga", "gb", "ft", "res", "last", "vown", "vwide", "vec_in")
    m_ = take("local", "zsend", "fsend", "xysend", "rsend", "csend", "recv", "crecv", "vlocal", "vload", "load", "wload", "store")
    pad = t_.pt.shape[-1]
    seqs = t_.pt.shape[0]

    z, x, y, c = place()
    zp = z + 1 - 2 * lax.rem(z, 2)
    zm = 3 - z
    zf = lax.rem(z + 2, 4)
    mid = jnp.logical_and(z >= 1, z <= 2)
    end = jnp.logical_not(mid)
    d_zp, d_zm = dev(zp, x, y, c), dev(zm, x, y, c)
    d_x, d_y, d_c = dev(z, 1 - x, y, c), dev(z, x, 1 - y, c), dev(z, x, y, 1 - c)
    bar = pltpu.get_barrier_semaphore()
    for d in (d_zp, d_zm, d_x, d_y, d_c):
        pl.semaphore_signal(bar, 1, device_id=d, device_id_type=MESH)


    def local(p):
        u = lax.rem(p, 8)
        l = p // 8

        def put(h, k, src):
            pltpu.make_async_copy(src, o_.w.at[p, z, x, c, h, k], m_.local.at[p]).start()

        def part(ref, off):
            return ref.at[l, :, pl.ds(pl.multiple_of(off, 128), 384)]
        for h in range(2):
            @pl.when(u == 0)
            def _():
                put(h, 0, part(i_.qkv, 384 * h))
                put(h, 1, part(i_.qkv, 768 + 384 * h))

            @pl.when(u == 1)
            def _():
                put(h, 0, part(i_.qkv, 1536 + 384 * h))
                put(h, 1, part(i_.out, 384 * h))

            @pl.when(jnp.logical_and(u >= 2, u < 6))
            def _():
                j = jnp.clip(u - 2, 0, 3) * 768
                put(h, 0, part(i_.gated, j + 384 * h))
                put(h, 1, part(i_.gated, j + FF + 384 * h))

            @pl.when(u >= 6)
            def _():
                for k in range(2):
                    r = pl.multiple_of(jnp.clip(2 * (u - 6) + k, 0, 3) * 48, 48)
                    put(h, k, i_.down.at[l, pl.ds(r, 48), pl.ds(384 * h, 384)])

    for p in range(EARLY):
        local(p)
    t_.vwide[...] = jnp.zeros_like(t_.vwide)
    for n in range(8):
        row = getattr(i_, "v%d" % n)[...].astype(F32)
        for l in range(LAYERS):
            t_.vwide[l, n : n + 1, 0:48] = row[l : l + 1, :]
    t_.vown[...] = t_.vwide[...].astype(BF)
    vplace = pltpu.make_async_copy(t_.vown, o_.v.at[z, x, c], m_.vlocal.at[0])
    vplace.start()
    xload = pltpu.make_async_copy(i_.x, t_.last, m_.vlocal.at[1])
    xload.start()
    pl.semaphore_wait(bar, 5)


    def stages(b, s):
        def copy(zz, xx, hh, sem, d):
            u = b(zz, xx, c, hh)
            return pltpu.make_async_remote_copy(src_ref=u, dst_ref=u, send_sem=sem.at[s], recv_sem=m_.recv.at[s, (zz * 2 + xx) * 2 + hh], device_id=d, device_id_type=MESH)

        def zsend(zz, d, sem=m_.fsend):
            copy(zz, x, y, sem, d).start()

        def got(zz, xx, hh, d):
            copy(zz, xx, hh, m_.zsend, d).wait_recv()

        def plane(zz, cc=c):
            u = b(zz, slice(None), cc, slice(None))
            return pltpu.make_async_remote_copy(src_ref=u, dst_ref=u, send_sem=m_.csend.at[s], recv_sem=m_.crecv.at[s, zz], device_id=d_c, device_id_type=MESH)

        def spread(zz):
            copy(zz, x, y, m_.xysend, d_x).start()
            copy(zz, x, y, m_.xysend, d_y).start()

        def relay(zz, first_x):
            got(zz, 1 - x, y, d_x)
            got(zz, x, 1 - y, d_y)

            def through_y():
                copy(zz, 1 - x, y, m_.rsend, d_y).start()

            def through_x():
                copy(zz, x, 1 - y, m_.rsend, d_x).start()
            if first_x is True:
                through_y()
            elif first_x is False:
                through_x()
            else:
                pl.when(first_x)(through_y)
                pl.when(jnp.logical_not(first_x))(through_x)

        def diagonal(zz):
            got(zz, 1 - x, 1 - y, d_y)
            plane(zz).start()

        def st0():
            zsend(z, d_zp, m_.zsend)
            pl.when(mid)(lambda: zsend(z, d_zm, m_.zsend))
            copy(z, x, y, m_.xysend, d_x).start()

        def st1():
            got(zp, x, y, d_zp)

            @pl.when(mid)
            def _():
                zsend(zp, d_zm)
                got(zm, x, y, d_zm)
                zsend(zm, d_zp)
            spread(zp)
            got(z, 1 - x, y, d_x)
            copy(z, 1 - x, y, m_.xysend, d_y).start()

        def st2():
            got(zf, x, y, d_zp)
            pl.when(mid)(lambda: zsend(zf, d_zp))
            spread(zf)
            relay(zp, True)
            diagonal(z)

        def st3():
            pl.when(end)(lambda: got(zm, x, y, d_zp))
            spread(zm)
            relay(zf, False)
            diagonal(zp)

        def st4():
            relay(zm, lax.rem(s, 2) == 0)
            diagonal(zf)

        def st5():
            diagonal(zm)

        def st6():
            for zz in (z, zp, zf, zm):
                plane(zz, 1 - c).wait_recv()
        return st0, st1, st2, st3, st4, st5, st6

    def stages_z(b, s):
        def copy(zz, xx, hh, sem, d):
            u = b(zz, xx, c, hh)
            at = 0 if isinstance(hh, slice) else hh
            return pltpu.make_async_remote_copy(src_ref=u, dst_ref=u, send_sem=sem.at[s], recv_sem=m_.recv.at[s, (zz * 2 + xx) * 2 + at], device_id=d, device_id_type=MESH)
        both = slice(None)

        def zsend(zz, xx, d, sem=m_.fsend):
            copy(zz, xx, both, sem, d).start()

        def got(zz, xx, d):
            copy(zz, xx, both, m_.zsend, d).wait_recv()

        def plane(zz, cc=c):
            u = b(zz, both, cc, both)
            return pltpu.make_async_remote_copy(src_ref=u, dst_ref=u, send_sem=m_.csend.at[s], recv_sem=m_.crecv.at[s, zz], device_id=d_c, device_id_type=MESH)

        def own(xx):
            zsend(z, xx, d_zp, m_.zsend)
            pl.when(mid)(lambda: zsend(z, xx, d_zm, m_.zsend))

        def near(xx):
            got(zp, xx, d_zp)

            @pl.when(mid)
            def _():
                zsend(zp, xx, d_zm)
                got(zm, xx, d_zm)
                zsend(zm, xx, d_zp)

        def far(xx):
            got(zf, xx, d_zp)
            pl.when(mid)(lambda: zsend(zf, xx, d_zp))

        def farthest(xx):
            pl.when(end)(lambda: got(zm, xx, d_zp))

        def st0():
            own(x)
            copy(z, x, y, m_.xysend, d_x).start()

        def st1():
            near(x)
            copy(z, 1 - x, y, m_.xysend, d_x).wait_recv()
            copy(z, 1 - x, y, m_.xysend, d_y).start()

        def st2():
            far(x)
            copy(z, 1 - x, 1 - y, m_.xysend, d_y).wait_recv()
            own(1 - x)
            plane(z).start()

        def st3():
            farthest(x)
            near(1 - x)
            plane(zp).start()

        def st4():
            far(1 - x)
            plane(zf).start()

        def st5():
            farthest(1 - x)
            plane(zm).start()

        def st6():
            for zz in (z, zp, zf, zm):
                plane(zz, 1 - c).wait_recv()
        return st0, st1, st2, st3, st4, st5, st6

    def sent_z(s):
        wait_all(o_.w.at[0, 0, 0, 0], m_.xysend.at[s])
        wait_all(many_w(16), m_.csend.at[s])
        pl.when(end)(lambda: wait_all(o_.w.at[0, 0, 0], m_.zsend.at[s]))

        @pl.when(mid)
        def _():
            wait_all(many_w(8), m_.zsend.at[s])
            wait_all(o_.w.at[0, 0:3, :, 0], m_.fsend.at[s])

    def sent(b, s, many):
        wait_all(many(8), m_.xysend.at[s])
        wait_all(many(3), m_.rsend.at[s])
        wait_all(many(16), m_.csend.at[s])
        pl.when(end)(lambda: wait_all(many(1), m_.zsend.at[s]))

        @pl.when(mid)
        def _():
            wait_all(many(2), m_.zsend.at[s])
            wait_all(many(3), m_.fsend.at[s])

    def unit(p):
        return lambda zz, xx, cc, hh: o_.w.at[p, zz, xx, cc, hh]

    def vunit(zz, xx, cc, hh):
        return o_.v.at[zz, xx, cc, hh]

    def many_w(n):
        if n == 8:
            return o_.w.at[0, 0]
        if n == 16:
            return o_.w.at[0, :, :, 0]
        return o_.w.at[0:n, 0, 0, 0, 0]

    def many_v(n):
        if n == 8:
            return o_.v.at[0]
        if n == 16:
            return o_.v.at[:, :, 0]
        return o_.v.at[0:n, 0, 0, 0]


    def load_att(l):
        for cp in matrix_loads(o_.w, 8 * l, 0, t_.wq, m_.wload.at[0]) + matrix_loads(o_.w, 8 * l, 1, t_.wk, m_.wload.at[1]) + matrix_loads(o_.w, 8 * l + 1, 0, t_.wv, m_.wload.at[2]) + matrix_loads(o_.w, 8 * l + 1, 1, t_.wo, m_.wload.at[3]):
            cp.start()

    def load_gated(l, j):
        for cp in matrix_loads(o_.w, 8 * l + 2 + j, 0, t_.wg, m_.wload.at[4]) + matrix_loads(o_.w, 8 * l + 2 + j, 1, t_.wu, m_.wload.at[5]):
            cp.start()

    def load_down(l, part):
        for s in (2 * part, 2 * part + 1):
            for h in range(2):
                pltpu.make_async_copy(o_.w.at[8 * l + 6 + s // 2, :, :, :, h, s % 2], t_.wd.at[:, :, :, s, :, pl.ds(384 * h, 384)], m_.wload.at[6]).start()

    def store(i, src, dst, go):
        run(pltpu.make_async_copy(src, dst, m_.store.at[i]), go)

    def per_layer(l, f):
        for n in range(LAYERS):
            @pl.when(l == n)
            def _():
                f(kept[n])

    def vrow(l, n):
        return o_.vec[l, n : n + 1, :]

    def store_att(kl, i, go):
        store(0, t_.q, cols(kl.q, i, 256), go)
        store(1, t_.k, cols(kl.k, i, 256), go)
        store(2, t_.v, cols(kl.v, i, 256), go)
        store(3, t_.pt, kl.pt.at[:, pl.ds(4 * i, 4)], go)
        store(4, t_.at, kl.at.at[pl.ds(pl.multiple_of(256 * i, 256), 256)], go)

        @pl.when(i == 0)
        def _():
            store(5, t_.xt, kl.xt, go)

    def att_task(l, i):
        @pl.when(i == 0)
        def _():
            wait_all(t_.wq, m_.wload.at[0])
            wait_all(t_.wk, m_.wload.at[1])
            wait_all(t_.wv, m_.wload.at[2])
            xb = t_.x[...].astype(BF)
            t_.xb[...] = xb
            t_.xt[...] = xb.T
        xb = t_.xb[...]
        lane = pl.multiple_of(256 * i, 256)
        at = pl.ds(lane, 256)
        t_.q[...] = (mm(xb, t_.wq[:, :, :, :, at].reshape(D, 256)) + o_.vec[l, 0:1, at]).astype(BF)
        t_.k[...] = mm(xb, t_.wk[:, :, :, :, at].reshape(D, 256)).astype(BF)
        t_.v[...] = (mm(xb, t_.wv[:, :, :, :, at].reshape(D, 256)) + o_.vec[l, 1:2, at]).astype(BF)
        for s in range(seqs):
            rows = slice(s * pad, (s + 1) * pad)
            hidden = jnp.where(lax.broadcasted_iota(jnp.int32, (pad, 1), 0) < i_.lens[s], 0.0, NEG)
            for pair in range(2):
                lanes = slice(128 * pair, 128 * pair + 128)
                q2 = t_.q[rows, lanes] * BF(HEAD_DIM ** -0.5)
                ks = halves(t_.k[rows, lanes], 1)
                vs = halves(t_.v[rows, lanes].T, 0)
                total = None
                for h in range(2):
                    slope = i_.slopes[4 * i + 2 * pair + h]
                    sc = mm_nt(ks[h], q2) - slope * t_.dist[...] + hidden
                    e = jnp.exp(sc - jnp.max(sc, axis=0, keepdims=True))
                    p = (e * (1.0 / jnp.sum(e, axis=0, keepdims=True))).astype(BF)
                    t_.pt[s, 2 * pair + h] = p
                    part = mm(vs[h], p)
                    total = part if total is None else total + part
                total = total.astype(BF)
                t_.at[lanes, rows] = total
                t_.att[rows, pl.ds(pl.multiple_of(lane + 128 * pair, 128), 128)] = total.T
        per_layer(l, lambda kl: store_att(kl, i, True))

    def store_ff(kl, j, go):
        store(6, t_.ga, cols(kl.ga, j, 768), go)
        store(7, t_.gb, cols(kl.gb, j, 768), go)
        store(8, t_.ft, kl.ft.at[pl.ds(pl.multiple_of(768 * j, 768), 768)], go)

        @pl.when(j == 0)
        def _():
            store(9, t_.res, kl.r1, go)
            store(10, t_.xt, kl.ht, go)

    def ff_task(l, j):
        @pl.when(j == 0)
        def _():
            wait_all(t_.wo, m_.wload.at[3])
            r1 = t_.x[...] + (mm(t_.att[...], t_.wo[...].reshape(D, D)) + vrow(l, 2))
            t_.res[...] = r1
            h = norm_parts(r1)[0] * vrow(l, 3) + vrow(l, 4)
            t_.h[...] = h
            hb = h.astype(BF)
            t_.hb[...] = hb
            t_.xt[...] = hb.T
        wait_all(t_.wg, m_.wload.at[4])
        wait_all(t_.wu, m_.wload.at[5])
        hb = t_.hb[...]
        g = mm(hb, t_.wg[...].reshape(D, 768))
        u = mm(hb, t_.wu[...].reshape(D, 768))
        cdf = 0.5 + 0.5 * erf(g * math.sqrt(0.5))
        gelu = g * cdf
        slope = cdf + g * (jnp.exp(-0.5 * (g * g)) * (1.0 / math.sqrt(2.0 * math.pi)))
        t_.ga[...] = gelu.astype(BF)
        t_.gb[...] = (slope * u).astype(BF)
        f = (gelu * u).astype(BF)
        t_.f[j] = f
        t_.ft[...] = f.T
        per_layer(l, lambda kl: store_ff(kl, j, True))

    def down_task(l):
        wait_all(t_.wd, m_.wload.at[6])
        total = t_.h[...] + vrow(l, 5)
        for j in range(4):
            total = total + mm(t_.f[j], t_.wd[j].reshape(768, D))
        t_.res[...] = total
        out = norm_parts(total)[0] * vrow(l, 6) + vrow(l, 7)
        t_.x[...] = out
        per_layer(l, lambda kl: store(9, t_.res, kl.r2, True))

        @pl.when(l == LAYERS - 1)
        def _():
            t_.last[...] = out.astype(BF)
            store(11, t_.last, o_.last, True)

    def task(t, att, ff, down):
        l = t // 8
        u = lax.rem(t, 8)
        pl.when(u < 3)(lambda: att(l, jnp.minimum(u, 2)))
        pl.when(jnp.logical_and(u >= 3, u < 7))(lambda: ff(l, jnp.clip(u - 3, 0, 3)))
        pl.when(u == 7)(lambda: down(l))

    def stored(t):
        task(t, lambda l, i: store_att(kept[0], i, False), lambda l, j: store_ff(kept[0], j, False), lambda l: store(9, t_.res, kept[0].r2, False))

    def fetch(t):
        def att(l, i):
            pl.when(i == 0)(lambda: load_att(l))

        def ff(l, j):
            load_gated(l, j)
            pl.when(j == 3)(lambda: load_down(l, 0))
        task(t, att, ff, lambda l: load_down(l, 1))


    vst = stages(vunit, PIECES)

    def begun(r):
        return jnp.clip(jnp.where(r <= 15, r - 7, r - 6), 0, 8 * LAYERS)

    def first(p):
        wait_all(o_.w.at[p, z, x, c], m_.local.at[p])
        pl.when(along_z(p))(stages_z(unit(p), p)[0])
        pl.when(jnp.logical_not(along_z(p)))(stages(unit(p), p)[0])

    def body(r, carry):
        def at(k):
            p = r - k

            @pl.when(jnp.logical_and(p >= 0, p < PIECES))
            def _():
                q = jnp.clip(p, 0, PIECES - 1)
                pl.when(along_z(q))(lambda: stages_z(unit(q), q)[k]())
                pl.when(jnp.logical_not(along_z(q)))(lambda: stages(unit(q), q)[k]())

        @pl.when(r + EARLY < PIECES)
        def _():
            local(jnp.minimum(r + EARLY, PIECES - 1))

        @pl.when(r < PIECES)
        def _():
            first(jnp.minimum(r, PIECES - 1))
        for k in range(1, 7):
            pl.when(r == k)(vst[k])
        at(6)
        low, high = begun(r), begun(r + 1)

        @pl.when(high > low)
        def _():
            fetch(jnp.minimum(low, 8 * LAYERS - 1))
        for k in (1, 2, 3, 4, 5):
            at(k)

        @pl.when(r == 6)
        def _():
            cp = pltpu.make_async_copy(o_.v, t_.vec_in, m_.vload)
            cp.start()
            xload.wait()
            t_.x[...] = t_.last[...].astype(F32)
            keys = lax.broadcasted_iota(jnp.int32, (pad, pad), 0)
            rows = lax.broadcasted_iota(jnp.int32, (pad, pad), 1)
            t_.dist[...] = jnp.abs(keys - rows).astype(F32)
            cp.wait()
            unpack_vectors()

        def one(t, carry):
            @pl.when(t >= 1)
            def _():
                stored(jnp.maximum(t - 1, 0))
            task(t, att_task, ff_task, down_task)
            return carry
        lax.fori_loop(low, high, one, 0)
        return carry

    def unpack_vectors():
        for l in range(LAYERS):
            parts = [t_.vec_in[b // 4, (b // 2) % 2, b % 2, l].astype(F32)[:, 0:48] for b in range(16)]
            o_.vec[l] = jnp.concatenate(parts, axis=1)
    vplace.wait()
    vst[0]()
    lax.fori_loop(0, PIECES + 6, body, 0)
    stored(8 * LAYERS - 1)
    store(11, t_.last, o_.last, False)

    def finish(p, carry):
        pl.when(along_z(p))(lambda: sent_z(p))
        pl.when(jnp.logical_not(along_z(p)))(lambda: sent(unit(p), p, many_w))
        return carry
    lax.fori_loop(0, PIECES, finish, 0)
    sent(vunit, PIECES, many_v)


def forward_all(lengths, slopes, x, shards, vectors):
    rows = x.shape[0]
    seqs = lengths.shape[0]
    pad = rows // seqs
    hbm = pl.BlockSpec(memory_space=pltpu.HBM)
    vmem = pl.BlockSpec(memory_space=pltpu.VMEM)
    smem = pl.BlockSpec(memory_space=pltpu.SMEM)
    S = jax.ShapeDtypeStruct
    act = lambda n, t: S((rows, n), t)
    one = [act(D, F32), act(D, F32), act(FF, BF), act(FF, BF), act(D, BF), act(D, BF), act(D, BF), S((seqs, HEADS, pad, pad), BF), S((FF, rows), BF), S((D, rows), BF), S((D, rows), BF), S((D, rows), BF)]
    out = [S((PIECES, 4, 2, 2, 2, 2, 48, 384), BF), S((4, 2, 2, 2, 8, 128), BF), S((LAYERS, 8, D), F32), act(D, BF)] + one * LAYERS
    v = pltpu.VMEM
    dma = pltpu.SemaphoreType.DMA
    mat = v((4, 2, 2, 48, D), BF)
    n = PIECES + 1
    scratch = [
        v((rows, D), F32), v((rows, D), BF), v((pad, pad), F32), v((rows, 256), BF), v((rows, 256), BF), v((rows, 256), BF), v((rows, D), BF),
        v((seqs, 4, pad, pad), BF), v((256, rows), BF), v((D, rows), BF), mat, mat, mat, mat, mat, mat, v((4, 2, 2, 4, 48, D), BF),
        v((rows, D), F32), v((rows, D), BF), v((4, rows, 768), BF), v((rows, 768), BF), v((rows, 768), BF), v((768, rows), BF), v((rows, D), F32), v((rows, D), BF),
        v((2, 8, 128), BF), v((2, 8, 128), F32), v((4, 2, 2, 2, 8, 128), BF),
        dma((PIECES,)), dma((n,)), dma((n,)), dma((n,)), dma((n,)), dma((n,)), dma((n, 16)), dma((n, 4)), dma((2,)), dma, dma, dma((7,)), dma((12,)),
    ]
    res = pl.pallas_call(
        forward_kernel, out_shape=out,
        in_specs=[smem, smem, hbm] + [hbm] * 4 + [vmem] * 8,
        out_specs=[hbm, hbm, vmem, hbm] + [hbm] * (12 * LAYERS),
        scratch_shapes=scratch,
        compiler_params=pltpu.CompilerParams(collective_id=0, has_side_effects=True, vmem_limit_bytes=60 * 2**20), name="gather_forward",
    )(lengths, slopes, x, *shards, *vectors)
    return res[0], res[2], res[3], [res[4 + 12 * l : 16 + 12 * l] for l in range(LAYERS)]


NPIECE = 33
LAG = 2
SLOTS = 16


STEPS = (0, 1, 4, 6, 8, 10, 12, 14)
STEPS_Z = (0, 1, 4, 7, 9, 11, 12, 13)


def reduce_z(p):
    return lax.rem(p, 4) == 1


def piece_first_x(p):
    others = p - (p + 2) // 4
    return jnp.logical_or(reduce_z(p), lax.rem(others * 5, 8) < 5)


def add_into(dst, src):
    dst[...] = dst[...] + src[...]


GRADS = ("dg", "du", "dq", "dk", "dv")


def backward_kernel(*refs):
    take = taker(refs)
    i_ = take("cot", "vec")
    cot, vec = i_.cot, i_.vec
    kept = [take(*KEPT) for _ in range(LAYERS)]
    w = take("w").w
    o = take("qkv", "out", "gated", "down", "vec", "dx")
    g = take(*GRADS)
    s = take("lbuf", "rbuf", "sbuf", "own", "stage", "r0v", "h1v", "h2v", "zav", "zbv", "yfv", "vall")
    c_ = take("r0", "h1", "h2", "za", "zb", "yf", "zza", "zzb")
    t_ = take("acc", "res", "wd", "wg", "wu", "ga", "gb", "wo", "dm", "dg", "du", "da", "datt", "q", "k", "v", "pt", "wq", "wk", "wv", "dq", "dk", "dv", "gv", "cot")
    m_ = take("lsem", "rsem", "send", "recv", "out", "vload", "fsem", "asem", "osem")
    pad = kept[0].pt.shape[-1]
    seqs = kept[0].pt.shape[0]

    z, x, y, c = place()
    zp = z + 1 - 2 * lax.rem(z, 2)
    zm = 3 - z
    mid = jnp.logical_and(z >= 1, z <= 2)
    end = jnp.logical_not(mid)
    d_zp, d_zm = dev(zp, x, y, c), dev(zm, x, y, c)
    d_x, d_y, d_c = dev(z, 1 - x, y, c), dev(z, x, 1 - y, c), dev(z, x, y, 1 - c)
    bar = pltpu.get_barrier_semaphore()
    for d in (d_zp, d_zm, d_x, d_y, d_c):
        pl.semaphore_signal(bar, 1, device_id=d, device_id_type=MESH)
    NP = NPIECE - 1


    def per_layer(l, f):
        for n in range(LAYERS):
            @pl.when(l == n)
            def _():
                f(kept[n])

    def load_ff_a(l, j, go):
        def one(i, src, dst):
            run(pltpu.make_async_copy(src, dst, m_.fsem.at[i]), go)

        def acts(kl):
            one(3, cols(kl.ga, j, 768), t_.ga)
            one(4, cols(kl.gb, j, 768), t_.gb)
        if go:
            pl.when(j == 0)(lambda: per_layer(l, lambda kl: one(5, kl.r2, t_.res)))
            for n in range(4):
                for h in range(2):
                    one(0, w.at[8 * l + 6 + n // 2, j, :, :, h, n % 2], t_.wd.at[:, :, n, :, pl.ds(384 * h, 384)])
            per_layer(l, acts)
        else:
            wait_all(t_.wd, m_.fsem.at[0])
            acts(kept[0])

    def load_ff_b(l, j, go):
        def one(i, src, dst):
            run(pltpu.make_async_copy(src, dst, m_.fsem.at[i]), go)
        for n, (k, dst) in enumerate(((0, t_.wg), (1, t_.wu))):
            if go:
                for cp in matrix_loads(w, 8 * l + 2 + j, k, dst, m_.fsem.at[1 + n]):
                    cp.start()
            else:
                wait_all(dst, m_.fsem.at[1 + n])

        @pl.when(j == 3)
        def _():
            if go:
                per_layer(l, lambda kl: one(5, kl.r1, t_.res))
                for cp in matrix_loads(w, 8 * l + 1, 1, t_.wo, m_.fsem.at[6]):
                    cp.start()
            else:
                one(5, kept[0].r1, t_.res)
                wait_all(t_.wo, m_.fsem.at[6])

    def load_att(l, i, go):
        def one(n, src, dst):
            run(pltpu.make_async_copy(src, dst, m_.asem.at[n]), go)

        def acts(kl):
            one(0, cols(kl.q, i, 256), t_.q)
            one(1, cols(kl.k, i, 256), t_.k)
            one(2, cols(kl.v, i, 256), t_.v)
            one(3, kl.pt.at[:, pl.ds(4 * i, 4)], t_.pt)
        if go:
            for n in range(LAYERS):
                @pl.when(l == n)
                def _():
                    acts(kept[n])
        else:
            acts(kept[0])
        @pl.when(i == 0)
        def _():
            for n, dst in enumerate((t_.wq, t_.wk, t_.wv)):
                if go:
                    for cp in matrix_loads(w, 8 * l + n // 2, n % 2, dst, m_.asem.at[4 + n]):
                        cp.start()
                else:
                    wait_all(dst, m_.asem.at[4 + n])

    def norm_two(l):
        pltpu.make_async_copy(kept[0].r2, t_.res, m_.fsem.at[5]).wait()
        dy = t_.acc[...]
        n, rstd = norm_parts(t_.res[...])
        dr2 = norm_back(dy, vec[l, 6:7, :], n, rstd)
        t_.acc[...] = dr2
        dm = dr2.astype(BF)
        t_.dm[...] = dm
        t_.gv[l, 5:6, :] = colsum(dm.astype(F32))
        t_.gv[l, 6:7, :] = colsum(dy * n)
        t_.gv[l, 7:8, :] = colsum(dy)

    def ff_a(l, j):
        load_ff_a(l, j, False)

        @pl.when(jnp.logical_and(j == 0, l < LAYERS - 1))
        def _():
            norm_two(l)
        df = mm_nt(t_.dm[...], t_.wd[...].reshape(768, D))
        t_.dg[...] = (df * t_.gb[...].astype(F32)).astype(BF)
        t_.du[...] = (df * t_.ga[...].astype(F32)).astype(BF)
        store_ff(l, j, True)

        @pl.when(j < 3)
        def _():
            load_ff_a(l, j + 1, True)

    def ff_b(l, j):
        load_ff_b(l, j, False)
        t_.acc[...] += mm_nt(t_.dg[...], t_.wg[...].reshape(D, 768)) + mm_nt(t_.du[...], t_.wu[...].reshape(D, 768))

        @pl.when(j < 3)
        def _():
            load_ff_b(l, j + 1, True)

        @pl.when(j == 3)
        def _():
            load_att(l, 0, True)
            dh = t_.acc[...]
            n, rstd = norm_parts(t_.res[...])
            dr1 = norm_back(dh, vec[l, 3:4, :], n, rstd)
            t_.acc[...] = dr1
            da = dr1.astype(BF)
            t_.da[...] = da
            t_.gv[l, 2:3, :] = colsum(da.astype(F32))
            t_.gv[l, 3:4, :] = colsum(dh * n)
            t_.gv[l, 4:5, :] = colsum(dh)
            datt = mm_nt(da, t_.wo[...].reshape(D, D)).astype(BF)
            for i in range(3):
                t_.datt[i] = datt[:, 256 * i : 256 * i + 256]

    def store_ff(l, j, go):
        def one(i, src, dst):
            run(pltpu.make_async_copy(src, dst, m_.osem.at[i]), go)
        one(0, t_.dg, cols(g.dg.at[l], j, 768))
        one(1, t_.du, cols(g.du.at[l], j, 768))

    def att_a(l, i):
        load_att(l, i, False)
        scale = HEAD_DIM ** -0.5
        first = lax.broadcasted_iota(jnp.int32, (pad, 128), 1) < HEAD_DIM
        for sq in range(seqs):
            rows = slice(sq * pad, (sq + 1) * pad)
            for pair in range(2):
                lanes = slice(128 * pair, 128 * pair + 128)
                q2 = t_.q[rows, lanes]
                d2 = t_.datt[i, rows, lanes]
                vs = halves(t_.v[rows, lanes], 1)
                ks = halves(t_.k[rows, lanes].T, 0)
                dv, dk, dq = [], [], None
                for h in range(2):
                    pb = t_.pt[sq, 2 * pair + h]
                    p = pb.astype(F32)
                    dp = mm_nt(vs[h], d2)
                    ds = (p * (dp - jnp.sum(dp * p, axis=0, keepdims=True))).astype(BF)
                    dv.append(mm(pb, d2))
                    dk.append(mm(ds, q2))
                    part = mm(ks[h], ds)
                    dq = part if dq is None else dq + part
                t_.dv[rows, lanes] = jnp.where(first, dv[0], dv[1]).astype(BF)
                t_.dk[rows, lanes] = (jnp.where(first, dk[0], dk[1]) * scale).astype(BF)
                t_.dq[rows, lanes] = (dq * scale).astype(BF).T
        dq, dk, dv = t_.dq[...], t_.dk[...], t_.dv[...]
        at = pl.ds(pl.multiple_of(i * 256, 256), 256)
        t_.gv[l, 0:1, at] = colsum(dq.astype(F32))
        t_.gv[l, 1:2, at] = colsum(dv.astype(F32))
        store_att(l, i, True)

        @pl.when(i < 2)
        def _():
            load_att(l, i + 1, True)

    def att_b(l, i):
        at = pl.ds(pl.multiple_of(i * 256, 256), 256)
        t_.acc[...] += (
            mm_nt(t_.dq[...], t_.wq[:, :, :, :, at].reshape(D, 256)) + mm_nt(t_.dk[...], t_.wk[:, :, :, :, at].reshape(D, 256)) + mm_nt(t_.dv[...], t_.wv[:, :, :, :, at].reshape(D, 256))
        )

        @pl.when(jnp.logical_and(i == 2, l > 0))
        def _():
            load_ff_a(jnp.maximum(l - 1, 0), 0, True)
            load_ff_b(jnp.maximum(l - 1, 0), 0, True)

        @pl.when(jnp.logical_and(i == 2, l == 0))
        def _():
            t_.cot[...] = t_.acc[...].astype(BF)
            pltpu.make_async_copy(t_.cot, o.dx, m_.osem.at[7]).start()

    def store_att(l, i, go):
        def one(n, src, dst):
            run(pltpu.make_async_copy(src, dst, m_.osem.at[n]), go)
        one(4, t_.dq, cols(g.dq.at[l], i, 256))
        one(5, t_.dk, cols(g.dk.at[l], i, 256))
        one(6, t_.dv, cols(g.dv.at[l], i, 256))

    def task(t, ff, att):
        l = LAYERS - 1 - t // 7
        u = lax.rem(t, 7)

        @pl.when(u < 4)
        def _():
            ff(l, jnp.minimum(u, 3))

        @pl.when(u >= 4)
        def _():
            att(l, jnp.clip(u - 4, 0, 2))


    def load(p, go):
        q = lax.rem(p, 16)
        n = lax.rem(p, 2)
        layer = LAYERS - 1 - p // 16

        def left(ref, sub=None):
            for k in range(2):
                cc = c if k else 1 - c
                src = ref.at[:, cc] if sub is None else ref.at[:, cc, sub]
                run(pltpu.make_async_copy(src, s.lbuf.at[n, k], m_.lsem.at[n, k]), go)

        def right(ref, col=None):
            src = ref if col is None else cols(ref.at[layer], jnp.clip(col, 0, 3), 768)
            run(pltpu.make_async_copy(src, s.rbuf.at[n], m_.rsem.at[n]), go)
        if not go:
            left(kept[0].ht)
            right(t_.dm)
            return
        for l in range(LAYERS):
            here = layer == l
            kl = kept[l]

            @pl.when(jnp.logical_and(here, q < 4))
            def _():
                left(kl.ft, jnp.minimum(q, 3))

            @pl.when(jnp.logical_and(here, jnp.logical_and(q >= 4, q < 12)))
            def _():
                left(kl.ht)

            @pl.when(jnp.logical_and(here, q == 12))
            def _():
                left(kl.at)

            @pl.when(jnp.logical_and(here, q > 12))
            def _():
                left(kl.xt)

        @pl.when(q < 4)
        def _():
            right(t_.dm)

        @pl.when(jnp.logical_and(q >= 4, q < 8))
        def _():
            right(g.dg, q - 4)

        @pl.when(jnp.logical_and(q >= 8, q < 12))
        def _():
            right(g.du, q - 8)
        for i, d in enumerate((t_.da, g.dq.at[layer], g.dk.at[layer], g.dv.at[layer])):
            @pl.when(q == 12 + i)
            def _():
                right(d)

    def rcopy(p, e, src, dst, d):
        return pltpu.make_async_remote_copy(src_ref=src, dst_ref=dst, send_sem=m_.send.at[p, e], recv_sem=m_.recv.at[p, e], device_id=d, device_id_type=MESH)

    def product(n, theirs, mine):
        v = mm(s.lbuf[n].reshape(768, -1), s.rbuf[n]).astype(BF).reshape(2, 4, 2, 48, 768)
        for k, dst in enumerate((theirs, mine)):
            dst[:, :, 0] = v[k, :, :, :, :384]
            dst[:, :, 1] = v[k, :, :, :, 384:]

    def c_copy(p, n):
        return rcopy(p, 0, s.sbuf.at[n], c_.r0.at[lax.rem(p, SLOTS)], d_c)

    def s0(p):
        n = lax.rem(p, 2)
        load(p, False)

        @pl.when(p >= 2)
        def _():
            c_copy(jnp.maximum(p - 2, 0), n).wait_send()
        product(n, s.sbuf.at[n], s.own.at[lax.rem(p, LAG + 1)])
        c_copy(p, n).start()

        @pl.when(p + 1 < NP)
        def _():
            load(jnp.minimum(p + 1, NP - 1), True)
    small = Group(("r0", "h1", "h2", "za", "zb", "yf"), (s.r0v, s.h1v, s.h2v, s.zav, s.zbv, s.yfv))
    zlo = jnp.where(z == 1, 1, 0)
    elo = jnp.where(z == 0, 1, 0)
    mlo = jnp.where(z == 1, 2, 0)
    rlo = jnp.where(z == 1, 0, 2)

    def steps(b, p, i, my):
        fx = piece_first_x(p)
        fy = jnp.logical_not(fx)

        def hop1(go):
            a = rcopy(p, 1, b.r0.at[i, :, 1 - x], b.h1.at[i], d_x)
            if go == "start":
                pl.when(fx)(a.start)
                pl.when(fy)(rcopy(p, 1, b.r0.at[i, :, :, 1 - y], b.h1.at[i], d_y).start)
            elif go == "recv":
                a.wait_recv()
            else:
                a.wait_send()

        def hop2(go):
            a = rcopy(p, 2, b.h1.at[i, :, 1 - y], b.h2.at[i], d_y)
            if go == "start":
                pl.when(fx)(a.start)
                pl.when(fy)(rcopy(p, 2, b.h1.at[i, :, 1 - x], b.h2.at[i], d_x).start)
            elif go == "recv":
                a.wait_recv()
            else:
                a.wait_send()

        def z1():
            return rcopy(p, 3, b.h2.at[i, pl.ds(elo, 3)], b.za.at[i], d_zp)

        def z2():
            return rcopy(p, 4, b.h2.at[i, pl.ds(mlo, 2)], b.zb.at[i], d_zm)

        def z3():
            return rcopy(p, 5, b.h2.at[i, zp], b.zb.at[i, 0], d_zp)

        def y1():
            return rcopy(p, 6, b.h2.at[i, z], b.yf.at[i], d_y)

        def s1():
            rcopy(p, 0, b.r0.at[i], b.r0.at[i], d_c).wait_recv()
            for k in range(4):
                add_into(b.r0.at[i, k], my.at[k])
            hop1("start")

        def s2():
            hop1("recv")
            for k in range(4):
                @pl.when(fx)
                def _():
                    add_into(b.h1.at[i, k], b.r0.at[i, k, x])

                @pl.when(fy)
                def _():
                    add_into(b.h1.at[i, k], b.r0.at[i, k, :, y])
            hop2("start")

        def s3():
            hop1("send")
            hop2("recv")
            t = jnp.where(fx, y, x)
            for k in range(4):
                add_into(b.h2.at[i, k], b.h1.at[i, k, t])
            pl.when(end)(z1().start)

        def s4():
            hop2("send")

            @pl.when(mid)
            def _():
                z1().wait_recv()
                for k in range(3):
                    add_into(b.h2.at[i, zlo + k], b.za.at[i, k])
                z2().start()

        def s5():
            pl.when(end)(z1().wait_send)

            @pl.when(mid)
            def _():
                z2().wait_recv()
                for k in range(2):
                    add_into(b.h2.at[i, rlo + k], b.zb.at[i, k])
                z3().start()

        def s6():
            pl.when(mid)(z2().wait_send)

            @pl.when(end)
            def _():
                z3().wait_recv()
                add_into(b.h2.at[i, z], b.zb.at[i, 0])
            y1().start()

        def s7():
            pl.when(mid)(z3().wait_send)
            y1().wait_send()
            y1().wait_recv()
        return s1, s2, s3, s4, s5, s6, s7

    def steps_z(p, i, my):
        b = c_
        fx = piece_first_x(p)
        iz = lax.rem(p // 4, SLOTS // 4)

        def hop1():
            return rcopy(p, 1, b.r0.at[i, z, 1 - x], b.h1.at[i, 0], d_x)

        def hop2():
            return rcopy(p, 2, b.h1.at[i, 0, 1 - y], b.h2.at[i, z], d_y)

        def z1():
            return rcopy(p, 3, b.r0.at[i, pl.ds(elo, 3)], b.zza.at[iz], d_zp)

        def z2():
            return rcopy(p, 4, b.r0.at[i, pl.ds(mlo, 2)], b.zzb.at[iz], d_zm)

        def z3():
            return rcopy(p, 5, b.r0.at[i, zp], b.zzb.at[iz, 0], d_zp)

        def y1():
            return rcopy(p, 6, b.h2.at[i, z], b.yf.at[i], d_y)

        def s1():
            rcopy(p, 0, b.r0.at[i], b.r0.at[i], d_c).wait_recv()
            for k in range(4):
                add_into(b.r0.at[i, k], my.at[k])
            pl.when(end)(z1().start)

        def s2():
            @pl.when(mid)
            def _():
                z1().wait_recv()
                for k in range(3):
                    add_into(b.r0.at[i, zlo + k], b.zza.at[iz, k])
                z2().start()

        def s3():
            pl.when(end)(z1().wait_send)

            @pl.when(mid)
            def _():
                z2().wait_recv()
                for k in range(2):
                    add_into(b.r0.at[i, rlo + k], b.zzb.at[iz, k])
                z3().start()

        def s4():
            pl.when(mid)(z2().wait_send)

            @pl.when(end)
            def _():
                z3().wait_recv()
                add_into(b.r0.at[i, z], b.zzb.at[iz, 0])
            hop1().start()

        def s5():
            pl.when(mid)(z3().wait_send)
            hop1().wait_recv()
            add_into(b.h1.at[i, 0], b.r0.at[i, z, x])
            hop2().start()

        def s6():
            hop1().wait_send()
            hop2().wait_recv()
            add_into(b.h2.at[i, z], b.h1.at[i, 0, y])
            y1().start()

        def s7():
            hop2().wait_send()
            y1().wait_send()
            y1().wait_recv()
        return s1, s2, s3, s4, s5, s6, s7

    def out_copy(p, n, go):
        q = lax.rem(p, 16)
        layer = LAYERS - 1 - p // 16

        def one(dst):
            run(pltpu.make_async_copy(s.stage.at[n], dst, m_.out.at[n]), go)
        if not go:
            one(o.out.at[0])
            return

        @pl.when(q < 4)
        def _():
            one(o.down.at[layer, pl.ds(pl.multiple_of(jnp.minimum(q, 3) * 48, 48), 48)])

        @pl.when(jnp.logical_and(q >= 4, q < 12))
        def _():
            one(cols(o.gated.at[layer], jnp.clip(q - 4, 0, 7), 768))

        @pl.when(q == 12)
        def _():
            one(o.out.at[layer])

        @pl.when(q > 12)
        def _():
            one(cols(o.qkv.at[layer], jnp.clip(q - 13, 0, 2), 768))

    def write(p):
        n = lax.rem(p, 2)

        @pl.when(p >= 2)
        def _():
            out_copy(p, n, False)
        i = lax.rem(p, SLOTS)
        a = c_.h2[i, z]
        b = c_.yf[i]

        @pl.when(y == 0)
        def _():
            s.stage[n, :, :384] = a
            s.stage[n, :, 384:] = b

        @pl.when(y == 1)
        def _():
            s.stage[n, :, :384] = b
            s.stage[n, :, 384:] = a
        out_copy(p, n, True)


    vp = NP
    vc = rcopy(vp, 0, s.vall.at[1 - c], s.r0v.at[0], d_c)
    vsteps = steps(small, vp, 0, s.vall.at[c])
    VSTART = 28

    def pack_vectors():
        for l in range(LAYERS):
            v = jnp.concatenate([t_.gv[l], jnp.zeros((120, D), F32)], axis=0).T.astype(BF)
            for k in range(16):
                s.vall[k % 2, k // 4, (k // 2) % 2, l] = v[48 * k : 48 * k + 48]
        vc.start()


    top = LAYERS - 1
    first = pltpu.make_async_copy(cot, t_.cot, m_.vload)
    first.start()
    load_ff_a(top, 0, True)
    load_ff_b(top, 0, True)
    first.wait()
    t_.acc[...] = t_.cot[...].astype(F32)
    norm_two(top)
    load(0, True)
    pl.semaphore_wait(bar, 5)

    def task_of(r):
        t = jnp.where(jnp.logical_and(lax.rem(r, 2) == 1, r >= 7), (r + 1) // 2, -1)
        for n, at in enumerate((1, 2, 4, 5)):
            t = jnp.where(r == at, n, t)
        return jnp.where(t <= 13, t, -1)

    def body(r, carry):
        def at(k, off, f, kind=None):
            p = r - off[k]
            q = jnp.clip(p, 0, NP - 1)
            here = jnp.logical_and(p >= 0, p < NP)
            if kind is not None:
                here = jnp.logical_and(here, reduce_z(q) == kind)

            @pl.when(here)
            def _():
                f(q)

        def st(k, kind):
            def f(p):
                own = s.own.at[lax.rem(p, LAG + 1)]
                i = lax.rem(p, SLOTS)
                (steps_z(p, i, own) if kind else steps(c_, p, i, own))[k - 1]()
                if k == 7:
                    write(p)
            return f

        now, before = task_of(r), task_of(r - 1)

        @pl.when(before >= 0)
        def _():
            task(jnp.clip(before, 0, 13), lambda l, j: store_ff(l, j, False), lambda l, i: store_att(l, i, False))
        for k in range(1, 8):
            pl.when(r == VSTART + STEPS[k])(vsteps[k - 1])
        at(0, STEPS, s0)
        for k in range(7, 0, -1):
            at(k, STEPS_Z, st(k, True), True)
            at(k, STEPS, st(k, False), False)
        pl.when(r == VSTART)(pack_vectors)

        @pl.when(before >= 0)
        def _():
            task(jnp.clip(before, 0, 13), ff_b, att_b)

        @pl.when(now >= 0)
        def _():
            task(jnp.clip(now, 0, 13), ff_a, att_a)
        return carry
    lax.fori_loop(0, NP + max(STEPS[7], STEPS_Z[7]), body, 0)

    for p in (NP - 2, NP - 1):
        c_copy(p, p % 2).wait_send()
        out_copy(p, p % 2, False)
    vc.wait_send()
    pltpu.make_async_copy(t_.cot, o.dx, m_.osem.at[7]).wait()
    va, vb = s.h2v[0, z].astype(F32), s.yfv[0].astype(F32)
    o.vec[0] = jnp.where(y == 0, va, vb)
    o.vec[1] = jnp.where(y == 0, vb, va)


def backward_all(cot, vec, kept, w):
    rows = cot.shape[0]
    hbm = pl.BlockSpec(memory_space=pltpu.HBM)
    vmem = pl.BlockSpec(memory_space=pltpu.VMEM)
    kept = [tuple(k[:8]) + (k[8].reshape(8, 2, 4, 48, rows),) + tuple(a.reshape(8, 2, 48, rows) for a in k[9:]) for k in kept]
    act = lambda c, t: jax.ShapeDtypeStruct((rows, c), t)
    out = [
        jax.ShapeDtypeStruct((LAYERS, 48, 3 * D), BF), jax.ShapeDtypeStruct((LAYERS, 48, D), BF),
        jax.ShapeDtypeStruct((LAYERS, 48, 2 * FF), BF), jax.ShapeDtypeStruct((LAYERS, 192, D), BF),
        jax.ShapeDtypeStruct((2, 48, 128), F32), act(D, BF),
    ]
    both = lambda c: jax.ShapeDtypeStruct((LAYERS, rows, c), BF)
    scratch_out = [both(FF), both(FF), both(D), both(D), both(D)]
    seqs, _, pad, _ = kept[0][7].shape
    v = pltpu.VMEM
    dma = pltpu.SemaphoreType.DMA
    mat = v((4, 2, 2, 48, D), BF)
    n = SLOTS
    scratch = [
        v((2, 2, 8, 48, rows), BF), v((2, rows, 768), BF), v((2, 4, 2, 2, 48, 384), BF), v((LAG + 1, 4, 2, 2, 48, 384), BF), v((2, 48, 768), BF),
        v((1, 4, 2, 2, 48, 128), BF), v((1, 4, 2, 48, 128), BF), v((1, 4, 48, 128), BF),
        v((1, 3, 48, 128), BF), v((1, 2, 48, 128), BF), v((1, 48, 128), BF), v((2, 4, 2, 2, 48, 128), BF),
        v((n, 4, 2, 2, 48, 384), BF), v((n, 4, 2, 48, 384), BF), v((n, 4, 48, 384), BF), v((n, 3, 48, 384), BF), v((n, 2, 48, 384), BF), v((n, 48, 384), BF), v((n // 4, 3, 2, 2, 48, 384), BF), v((n // 4, 2, 2, 2, 48, 384), BF),
        v((rows, D), F32), v((rows, D), F32), v((2, 2, 4, 48, D), BF), mat, mat, v((rows, 768), BF), v((rows, 768), BF), mat,
        v((rows, D), BF), v((rows, 768), BF), v((rows, 768), BF), v((rows, D), BF), v((3, rows, 256), BF),
        v((rows, 256), BF), v((rows, 256), BF), v((rows, 256), BF), v((seqs, 4, pad, pad), BF), mat, mat, mat,
        v((rows, 256), BF), v((rows, 256), BF), v((rows, 256), BF), v((LAYERS, 8, D), F32), v((rows, D), BF),
        dma((2, 2)), dma((2,)), dma((NPIECE, 7)), dma((NPIECE, 7)), dma((2,)), dma, dma((7,)), dma((7,)), dma((8,)),
    ]
    res = pl.pallas_call(
        backward_kernel, out_shape=out + scratch_out,
        in_specs=[hbm, vmem] + [hbm] * 25,
        out_specs=[hbm] * 4 + [vmem] + [hbm] * 6,
        scratch_shapes=scratch,
        compiler_params=pltpu.CompilerParams(collective_id=1, has_side_effects=True, vmem_limit_bytes=62 * 2**20), name="backward_reduce",
    )(cot, vec, *kept[0], *kept[1], w)
    return res[:4], res[4], res[5]


def finish_kernel(qkv, out, gated, down, vec, last, dx, *outs):
    for src, dst in zip((qkv, out, gated, down, last, dx), outs[:6]):
        dst[...] = src[...].astype(dst.dtype)

    @pl.when(pl.program_id(0) == 0)
    def _():
        for l in range(LAYERS):
            rows = vec[l].T
            for n in range(8):
                outs[6 + n][l : l + 1, :] = rows[n : n + 1, :]


def finish_all(mats, vec, last, dx):
    rows = last.shape[0]
    half = pl.BlockSpec((rows // 2, D), lambda i: (i, 0))
    blocks = [pl.BlockSpec((1,) + m.shape[1:], lambda i: (i, 0, 0)) for m in mats]
    vecs = pl.BlockSpec((LAYERS, 48), lambda i: (0, 0))
    S = jax.ShapeDtypeStruct
    return pl.pallas_call(
        finish_kernel,
        grid=(LAYERS,),
        in_specs=blocks + [pl.BlockSpec(vec.shape, lambda i: (0, 0, 0)), half, half],
        out_specs=blocks + [half, half] + [vecs] * 8,
        out_shape=[S(m.shape, F32) for m in mats] + [S(last.shape, BF), S(dx.shape, BF)] + [S((LAYERS, 48), F32)] * 8,
        name="finish",
    )(*mats, vec, last, dx)


def forward_plain(seq_lengths, slopes, x, shards, vectors):
    mats = [lax.all_gather(w, "fsdp", axis=1, tiled=True) for w in shards]
    vec = lax.all_gather(jnp.stack(vectors, axis=1), "fsdp", axis=2, tiled=True).astype(F32)
    wq, wo, wg, wd = mats
    kept = []
    for l in range(LAYERS):
        q, k, v, att, pt, xt, at = attention_forward(l, seq_lengths, slopes, x, wq, vec)
        out_dtype = BF if l == LAYERS - 1 else F32
        r1, r2, ga, gb, ft, ht, x = ff_forward(l, att, x, wo, wg, wd, vec, out_dtype)
        kept.append((r1, r2, ga, gb, q, k, v, pt, ft, ht, at, xt))
    return mats, vec, x, kept


def backward_plain(dy, vec, kept, mats):
    wq, wo, wg, wd = mats

    def one(g, dim):
        part = lax.psum_scatter(g.astype(BF), "fsdp", scatter_dimension=dim, tiled=True)
        return lax.psum(part, "dp").astype(F32)
    sums, vecs = [None] * LAYERS, [None] * LAYERS
    for l in reversed(range(LAYERS)):
        r1, r2, ga, gb, q, k, v, pt, ft, ht, at, xt = kept[l]
        dm, dg, du, dr1, da, datt, gv = ff_backward(l, dy, r1, r2, ga, gb, wo, wg, wd, vec)
        dq, dk, dv, dy, gbias = attention_backward(l, datt, q, k, v, pt, wq, dr1, BF if l == 0 else F32)
        pairs = ((xt, jnp.concatenate([dq, dk, dv], axis=1)), (at, da), (ht, jnp.concatenate([dg, du], axis=1)), (ft, dm))
        sums[l] = [one(mm(a, b), 0) for a, b in pairs]
        vecs[l] = gv + gbias
    return [jnp.stack(m) for m in zip(*sums)], one(jnp.stack(vecs), 2), dy


def per_device(fast, inputs, lengths, cotangent, w_qkv, q_bias, v_bias, w_out, b_out, gain_one, shift_one, w_gated, w_down, b_down, gain_two, shift_two):
    shards = (w_qkv, w_out, w_gated, w_down)
    vectors = (q_bias, v_bias, b_out, gain_one, shift_one, b_down, gain_two, shift_two)
    seq_lengths = lengths.reshape(-1)
    slopes = jnp.array(slopes_list(HEADS), F32)
    x = inputs.reshape(-1, D)
    dy = cotangent.reshape(-1, D)
    if fast:
        w, vec, x, kept = forward_all(seq_lengths, slopes, x, shards, vectors)
        m, packed, dx = backward_all(dy, vec, kept, w)
        *m, x, dx, v0, v1, v2, v3, v4, v5, v6, v7 = finish_all(m, packed, x, dx)
    else:
        mats, vec, x, kept = forward_plain(seq_lengths, slopes, x, shards, vectors)
        m, vs, dx = backward_plain(dy, vec, kept, mats)
        v0, v1, v2, v3, v4, v5, v6, v7 = (vs[:, n] for n in range(8))
    return (
        x.reshape(inputs.shape), dx.reshape(inputs.shape), m[0], v0, v1, m[1], v2, v3, v4, m[2], m[3], v5, v6, v7,
    )


def solution(mesh):
    placed = (
        P(None, ("dp", "fsdp"), None, None),
        P(None, ("dp", "fsdp")),
        P(None, ("dp", "fsdp"), None, None),
        P(None, "fsdp", None),
        P(None, "fsdp"),
        P(None, "fsdp"),
        P(None, "fsdp", None),
        P(None, "fsdp"),
        P(None, "fsdp"),
        P(None, "fsdp"),
        P(None, "fsdp", None),
        P(None, "fsdp", None),
        P(None, "fsdp"),
        P(None, "fsdp"),
        P(None, "fsdp"),
    )
    return jax.shard_map(
        functools.partial(per_device, dict(mesh.shape) == {"dp": 2, "fsdp": 16}),
        mesh=mesh,
        in_specs=placed,
        out_specs=(
            P(None, ("dp", "fsdp"), None, None),
            P(None, ("dp", "fsdp"), None, None),
            P(None, "fsdp", None),
            P(None, "fsdp"),
            P(None, "fsdp"),
            P(None, "fsdp", None),
            P(None, "fsdp"),
            P(None, "fsdp"),
            P(None, "fsdp"),
            P(None, "fsdp", None),
            P(None, "fsdp", None),
            P(None, "fsdp"),
            P(None, "fsdp"),
            P(None, "fsdp"),
        ),
        check_vma=False,
    )
```

```python
import functools
import math

import jax
import jax.numpy as jnp
from jax import lax
from jax.experimental import pallas as pl
from jax.experimental.pallas import tpu as pltpu
from jax.sharding import PartitionSpec as P

MESH = pl.DeviceIdType.MESH

BF = jnp.bfloat16
F32 = jnp.float32
D, HEADS, HEAD_DIM, FF, LAYERS = 768, 12, 64, 3072, 2
EPS = 1e-12
NEG = -1e30
NT = (((1,), (1,)), ((), ()))


def slopes_list(heads_count):
    nearest = 2 ** int(math.floor(math.log2(heads_count)))
    leading = [2.0 ** (-8.0 * (number + 1) / nearest) for number in range(nearest)]
    trailing = [2.0 ** (-8.0 * (number + 1) / (2 * nearest)) for number in range(2 * nearest)][0::2]
    return leading + trailing[: heads_count - nearest]


def mm(a, b):
    return jnp.dot(a, b, preferred_element_type=F32)


def mm_nt(a, b):
    return lax.dot_general(a, b, NT, preferred_element_type=F32)


def erf(x):
    return lax.erf(x)


def norm_parts(r):
    cent = r - jnp.mean(r, axis=-1, keepdims=True)
    rstd = lax.rsqrt(jnp.mean(cent * cent, axis=-1, keepdims=True) + EPS)
    return cent * rstd, rstd


def norm_back(dy, gain, n, rstd):
    dn = dy * gain
    return rstd * (dn - jnp.mean(dn, axis=-1, keepdims=True) - n * jnp.mean(dn * n, axis=-1, keepdims=True))


def halves(v, axis):
    first = lax.broadcasted_iota(jnp.int32, v.shape, axis) < HEAD_DIM
    zero = jnp.zeros_like(v)
    return jnp.where(first, v, zero), jnp.where(first, zero, v)


def attention_kernel(len_ref, slope_ref, x_ref, wq_ref, wk_ref, wv_ref, vec_ref, q_ref, k_ref, v_ref, att_ref, pt_ref, xt_ref, at_ref, xb_ref, dist_ref):
    i = pl.program_id(0)
    seqs, pad = pt_ref.shape[0], pt_ref.shape[-1]

    @pl.when(i == 0)
    def _():
        xb = x_ref[...].astype(BF)
        xb_ref[...] = xb
        xt_ref[...] = xb.T
        keys = lax.broadcasted_iota(jnp.int32, (pad, pad), 0)
        rows = lax.broadcasted_iota(jnp.int32, (pad, pad), 1)
        dist_ref[...] = jnp.abs(keys - rows).astype(F32)
    xb = xb_ref[...]
    q_ref[...] = (mm(xb, wq_ref[...]) + vec_ref[0:1, :]).astype(BF)
    k_ref[...] = mm(xb, wk_ref[...]).astype(BF)
    v_ref[...] = (mm(xb, wv_ref[...]) + vec_ref[1:2, :]).astype(BF)
    for s in range(seqs):
        rows = slice(s * pad, (s + 1) * pad)
        hidden = jnp.where(lax.broadcasted_iota(jnp.int32, (pad, 1), 0) < len_ref[s], 0.0, NEG)
        for pair in range(2):
            lanes = slice(128 * pair, 128 * pair + 128)
            q2 = q_ref[rows, lanes] * BF(HEAD_DIM ** -0.5)
            k0, k1 = halves(k_ref[rows, lanes], 1)
            v0, v1 = halves(v_ref[rows, lanes].T, 0)
            total = None
            for h, (kh, vh) in enumerate(((k0, v0), (k1, v1))):
                slope = slope_ref[4 * i + 2 * pair + h]
                sc = mm_nt(kh, q2) - slope * dist_ref[...] + hidden
                e = jnp.exp(sc - jnp.max(sc, axis=0, keepdims=True))
                p = (e * (1.0 / jnp.sum(e, axis=0, keepdims=True))).astype(BF)
                pt_ref[s, 2 * pair + h] = p
                part = mm(vh, p)
                total = part if total is None else total + part
            total = total.astype(BF)
            at_ref[lanes, rows] = total
            att_ref[rows, lanes] = total.T


def attention_forward(l, lengths, slopes, x, w_qkv, vec):
    rows = x.shape[0]
    seqs = lengths.shape[0]
    pad = rows // seqs
    col = lambda off: pl.BlockSpec((None, D, 256), lambda i: (l, 0, off + i))
    blk = pl.BlockSpec((rows, 256), lambda i: (0, i))
    smem = pl.BlockSpec(memory_space=pltpu.SMEM)
    act = jax.ShapeDtypeStruct((rows, D), BF)
    return pl.pallas_call(
        attention_kernel,
        grid=(3,),
        in_specs=[smem, smem, pl.BlockSpec((rows, D), lambda i: (0, 0)), col(0), col(3), col(6), pl.BlockSpec((None, 8, 256), lambda i: (l, 0, i))],
        out_specs=[blk, blk, blk, blk, pl.BlockSpec((seqs, 4, pad, pad), lambda i: (0, i, 0, 0)), pl.BlockSpec((D, rows), lambda i: (0, 0)), pl.BlockSpec((256, rows), lambda i: (i, 0))],
        out_shape=[act, act, act, act, jax.ShapeDtypeStruct((seqs, HEADS, pad, pad), BF), jax.ShapeDtypeStruct((D, rows), BF), jax.ShapeDtypeStruct((D, rows), BF)],
        scratch_shapes=[pltpu.VMEM((rows, D), BF), pltpu.VMEM((pad, pad), F32)],
        compiler_params=pltpu.CompilerParams(vmem_limit_bytes=56 * 2**20),
        name="attention_forward",
    )(lengths, slopes, x, w_qkv, w_qkv, w_qkv, vec)


def ff_kernel(att_ref, x_ref, wo_ref, wg_ref, wu_ref, wd_ref, vec_ref, r1_ref, r2_ref, ga_ref, gb_ref, ft_ref, ht_ref, out_ref, h_ref, hb_ref, acc_ref):
    j = pl.program_id(0)

    @pl.when(j == 0)
    def _():
        r1 = x_ref[...].astype(F32) + (mm(att_ref[...], wo_ref[...]) + vec_ref[2:3, :])
        r1_ref[...] = r1
        h = norm_parts(r1)[0] * vec_ref[3:4, :] + vec_ref[4:5, :]
        h_ref[...] = h
        hb = h.astype(BF)
        hb_ref[...] = hb
        ht_ref[...] = hb.T
        acc_ref[...] = jnp.zeros_like(acc_ref)
    hb = hb_ref[...]
    g = mm(hb, wg_ref[...])
    u = mm(hb, wu_ref[...])
    cdf = 0.5 + 0.5 * erf(g * math.sqrt(0.5))
    gelu = g * cdf
    slope = cdf + g * (jnp.exp(-0.5 * (g * g)) * (1.0 / math.sqrt(2.0 * math.pi)))
    ga_ref[...] = gelu.astype(BF)
    gb_ref[...] = (slope * u).astype(BF)
    f = (gelu * u).astype(BF)
    ft_ref[...] = f.T
    acc_ref[...] += mm(f, wd_ref[...])

    @pl.when(j == pl.num_programs(0) - 1)
    def _():
        r2 = h_ref[...] + (acc_ref[...] + vec_ref[5:6, :])
        r2_ref[...] = r2
        out_ref[...] = (norm_parts(r2)[0] * vec_ref[6:7, :] + vec_ref[7:8, :]).astype(out_ref.dtype)


def ff_forward(l, att, x, w_out, w_gated, w_down, vec, out_dtype):
    rows = x.shape[0]
    n = FF // 768
    whole = pl.BlockSpec((rows, D), lambda j: (0, 0))
    blk = pl.BlockSpec((rows, 768), lambda j: (0, j))
    return pl.pallas_call(
        ff_kernel,
        grid=(n,),
        in_specs=[whole, whole, pl.BlockSpec((None, D, D), lambda j: (l, 0, 0)),
                  pl.BlockSpec((None, D, 768), lambda j: (l, 0, j)), pl.BlockSpec((None, D, 768), lambda j: (l, 0, n + j)),
                  pl.BlockSpec((None, 768, D), lambda j: (l, j, 0)), pl.BlockSpec((None, 8, D), lambda j: (l, 0, 0))],
        out_specs=[whole, whole, blk, blk, pl.BlockSpec((768, rows), lambda j: (j, 0)), pl.BlockSpec((D, rows), lambda j: (0, 0)), whole],
        out_shape=[jax.ShapeDtypeStruct((rows, D), F32), jax.ShapeDtypeStruct((rows, D), F32),
                   jax.ShapeDtypeStruct((rows, FF), BF), jax.ShapeDtypeStruct((rows, FF), BF),
                   jax.ShapeDtypeStruct((FF, rows), BF), jax.ShapeDtypeStruct((D, rows), BF), jax.ShapeDtypeStruct((rows, D), out_dtype)],
        scratch_shapes=[pltpu.VMEM((rows, D), F32), pltpu.VMEM((rows, D), BF), pltpu.VMEM((rows, D), F32)],
        compiler_params=pltpu.CompilerParams(vmem_limit_bytes=56 * 2**20),
        name="ff_forward",
    )(att, x, w_out, w_gated, w_gated, w_down, vec)


def colsum(v):
    return jnp.sum(v, axis=0, keepdims=True)


def ff_back_kernel(dy_ref, r1_ref, r2_ref, ga_ref, gb_ref, wo_ref, wg_ref, wu_ref, wd_ref, vec_ref, dm_ref, dg_ref, du_ref, dr1_ref, da_ref, datt_ref, gv_ref, acc_ref):
    j = pl.program_id(0)

    @pl.when(j == 0)
    def _():
        dy = dy_ref[...].astype(F32)
        n, rstd = norm_parts(r2_ref[...])
        dr2 = norm_back(dy, vec_ref[6:7, :], n, rstd)
        acc_ref[...] = dr2
        dm = dr2.astype(BF)
        dm_ref[...] = dm
        gv_ref[5:6, :] = colsum(dm.astype(F32))
        gv_ref[6:7, :] = colsum(dy * n)
        gv_ref[7:8, :] = colsum(dy)
        gv_ref[0:2, :] = jnp.zeros((2, D), F32)
    df = mm_nt(dm_ref[...], wd_ref[...])
    dg = (df * gb_ref[...].astype(F32)).astype(BF)
    du = (df * ga_ref[...].astype(F32)).astype(BF)
    dg_ref[...] = dg
    du_ref[...] = du
    acc_ref[...] += mm_nt(dg, wg_ref[...]) + mm_nt(du, wu_ref[...])

    @pl.when(j == pl.num_programs(0) - 1)
    def _():
        dh = acc_ref[...]
        n, rstd = norm_parts(r1_ref[...])
        dr1 = norm_back(dh, vec_ref[3:4, :], n, rstd)
        dr1_ref[...] = dr1
        da = dr1.astype(BF)
        da_ref[...] = da
        gv_ref[2:3, :] = colsum(da.astype(F32))
        gv_ref[3:4, :] = colsum(dh * n)
        gv_ref[4:5, :] = colsum(dh)
        datt_ref[...] = mm_nt(da, wo_ref[...]).astype(BF)


def ff_backward(l, dy, r1, r2, ga, gb, w_out, w_gated, w_down, vec):
    rows = dy.shape[0]
    n = FF // 768
    whole = pl.BlockSpec((rows, D), lambda j: (0, 0))
    blk = pl.BlockSpec((rows, 768), lambda j: (0, j))
    act = lambda c, t: jax.ShapeDtypeStruct((rows, c), t)
    return pl.pallas_call(
        ff_back_kernel,
        grid=(n,),
        in_specs=[whole, whole, whole, blk, blk, pl.BlockSpec((None, D, D), lambda j: (l, 0, 0)),
                  pl.BlockSpec((None, D, 768), lambda j: (l, 0, j)), pl.BlockSpec((None, D, 768), lambda j: (l, 0, n + j)),
                  pl.BlockSpec((None, 768, D), lambda j: (l, j, 0)), pl.BlockSpec((None, 8, D), lambda j: (l, 0, 0))],
        out_specs=[whole, blk, blk, whole, whole, whole, pl.BlockSpec((8, D), lambda j: (0, 0))],
        out_shape=[act(D, BF), act(FF, BF), act(FF, BF), act(D, F32), act(D, BF), act(D, BF), jax.ShapeDtypeStruct((8, D), F32)],
        scratch_shapes=[pltpu.VMEM((rows, D), F32)],
        compiler_params=pltpu.CompilerParams(vmem_limit_bytes=56 * 2**20),
        name="ff_backward",
    )(dy, r1, r2, ga, gb, w_out, w_gated, w_gated, w_down, vec)


def attention_back_kernel(datt_ref, q_ref, k_ref, v_ref, pt_ref, wq_ref, wk_ref, wv_ref, dr1_ref, dq_ref, dk_ref, dv_ref, dx_ref, gb_ref, acc_ref):
    i = pl.program_id(0)
    seqs, pad = pt_ref.shape[0], pt_ref.shape[-1]
    scale = HEAD_DIM ** -0.5

    @pl.when(i == 0)
    def _():
        acc_ref[...] = dr1_ref[...]
    first = lax.broadcasted_iota(jnp.int32, (pad, 128), 1) < HEAD_DIM
    for s in range(seqs):
        rows = slice(s * pad, (s + 1) * pad)
        for pair in range(2):
            lanes = slice(128 * pair, 128 * pair + 128)
            q2 = q_ref[rows, lanes]
            d2 = datt_ref[rows, lanes]
            vs = halves(v_ref[rows, lanes], 1)
            ks = halves(k_ref[rows, lanes].T, 0)
            dv, dk, dq = [], [], None
            for h in range(2):
                pb = pt_ref[s, 2 * pair + h]
                p = pb.astype(F32)
                dp = mm_nt(vs[h], d2)
                ds = (p * (dp - jnp.sum(dp * p, axis=0, keepdims=True))).astype(BF)
                dv.append(mm(pb, d2))
                dk.append(mm(ds, q2))
                part = mm(ks[h], ds)
                dq = part if dq is None else dq + part
            dv_ref[rows, lanes] = jnp.where(first, dv[0], dv[1]).astype(BF)
            dk_ref[rows, lanes] = (jnp.where(first, dk[0], dk[1]) * scale).astype(BF)
            dq_ref[rows, lanes] = (dq * scale).astype(BF).T
    dq, dk, dv = dq_ref[...], dk_ref[...], dv_ref[...]
    gb_ref[0:1, :] = colsum(dq.astype(F32))
    gb_ref[1:2, :] = colsum(dv.astype(F32))
    gb_ref[2:8, :] = jnp.zeros((6, 256), F32)
    acc_ref[...] += mm_nt(dq, wq_ref[...]) + mm_nt(dk, wk_ref[...]) + mm_nt(dv, wv_ref[...])

    @pl.when(i == pl.num_programs(0) - 1)
    def _():
        dx_ref[...] = acc_ref[...].astype(dx_ref.dtype)


def attention_backward(l, datt, q, k, v, pt, w_qkv, dr1, out_dtype):
    rows = datt.shape[0]
    seqs, _, pad, _ = pt.shape
    col = lambda off: pl.BlockSpec((None, D, 256), lambda i: (l, 0, off + i))
    blk = pl.BlockSpec((rows, 256), lambda i: (0, i))
    whole = pl.BlockSpec((rows, D), lambda i: (0, 0))
    act = jax.ShapeDtypeStruct((rows, D), BF)
    return pl.pallas_call(
        attention_back_kernel,
        grid=(3,),
        in_specs=[blk, blk, blk, blk, pl.BlockSpec((seqs, 4, pad, pad), lambda i: (0, i, 0, 0)), col(0), col(3), col(6), whole],
        out_specs=[blk, blk, blk, whole, pl.BlockSpec((8, 256), lambda i: (0, i))],
        out_shape=[act, act, act, jax.ShapeDtypeStruct((rows, D), out_dtype), jax.ShapeDtypeStruct((8, D), F32)],
        scratch_shapes=[pltpu.VMEM((rows, D), F32)],
        compiler_params=pltpu.CompilerParams(vmem_limit_bytes=56 * 2**20),
        name="attention_backward",
    )(datt, q, k, v, pt, w_qkv, w_qkv, w_qkv, dr1)


def place():
    y = lax.axis_index("dp"); f = lax.axis_index("fsdp")
    z = f // 4; x = lax.rem(f // 2, 2); c = lax.rem(f, 2)
    return z, x, y, c

def dev(z, x, y, c):
    return (y, (z * 2 + x) * 2 + c)

PIECES = 8 * LAYERS
EARLY = 3


def along_z(p):
    return lax.rem(p, 5) == 3

KEPT = ("r1", "r2", "ga", "gb", "q", "k", "v", "pt", "ft", "ht", "at", "xt")


class Group:
    def __init__(self, names, refs):
        for name, ref in zip(names, refs):
            setattr(self, name, ref)


def taker(refs):
    refs = list(refs)

    def take(*names):
        g = Group(names, refs[: len(names)])
        del refs[: len(names)]
        return g
    return take


def run(cp, go):
    if go:
        cp.start()
    else:
        cp.wait()


def cols(ref, j, width):
    return ref.at[:, pl.ds(pl.multiple_of(j * width, width), width)]


def matrix_loads(w, p, k, dst, sem):
    return [pltpu.make_async_copy(w.at[p, :, :, :, h, k], dst.at[:, :, :, :, pl.ds(384 * h, 384)], sem) for h in range(2)]


def wait_all(dst, sem):
    pltpu.make_async_copy(dst, dst, sem).wait()


def forward_kernel(*refs):
    take = taker(refs)
    i_ = take("lens", "slopes", "x", "qkv", "out", "gated", "down", *["v%d" % i for i in range(8)])
    o_ = take("w", "v", "vec", "last")
    kept = [take(*KEPT) for _ in range(LAYERS)]
    t_ = take("x", "xb", "dist", "q", "k", "v", "att", "pt", "at", "xt", "wq", "wk", "wv", "wo", "wg", "wu", "wd", "h", "hb", "f", "ga", "gb", "ft", "res", "last", "vown", "vwide", "vec_in")
    m_ = take("local", "zsend", "fsend", "xysend", "rsend", "csend", "recv", "crecv", "vlocal", "vload", "load", "wload", "store")
    pad = t_.pt.shape[-1]
    seqs = t_.pt.shape[0]

    z, x, y, c = place()
    zp = z + 1 - 2 * lax.rem(z, 2)
    zm = 3 - z
    zf = lax.rem(z + 2, 4)
    mid = jnp.logical_and(z >= 1, z <= 2)
    end = jnp.logical_not(mid)
    d_zp, d_zm = dev(zp, x, y, c), dev(zm, x, y, c)
    d_x, d_y, d_c = dev(z, 1 - x, y, c), dev(z, x, 1 - y, c), dev(z, x, y, 1 - c)
    bar = pltpu.get_barrier_semaphore()
    for d in (d_zp, d_zm, d_x, d_y, d_c):
        pl.semaphore_signal(bar, 1, device_id=d, device_id_type=MESH)


    def local(p):
        u = lax.rem(p, 8)
        l = p // 8

        def put(h, k, src):
            pltpu.make_async_copy(src, o_.w.at[p, z, x, c, h, k], m_.local.at[p]).start()

        def part(ref, off):
            return ref.at[l, :, pl.ds(pl.multiple_of(off, 128), 384)]
        for h in range(2):
            @pl.when(u == 0)
            def _():
                put(h, 0, part(i_.qkv, 384 * h))
                put(h, 1, part(i_.qkv, 768 + 384 * h))

            @pl.when(u == 1)
            def _():
                put(h, 0, part(i_.qkv, 1536 + 384 * h))
                put(h, 1, part(i_.out, 384 * h))

            @pl.when(jnp.logical_and(u >= 2, u < 6))
            def _():
                j = jnp.clip(u - 2, 0, 3) * 768
                put(h, 0, part(i_.gated, j + 384 * h))
                put(h, 1, part(i_.gated, j + FF + 384 * h))

            @pl.when(u >= 6)
            def _():
                for k in range(2):
                    r = pl.multiple_of(jnp.clip(2 * (u - 6) + k, 0, 3) * 48, 48)
                    put(h, k, i_.down.at[l, pl.ds(r, 48), pl.ds(384 * h, 384)])

    for p in range(EARLY):
        local(p)
    t_.vwide[...] = jnp.zeros_like(t_.vwide)
    for n in range(8):
        row = getattr(i_, "v%d" % n)[...].astype(F32)
        for l in range(LAYERS):
            t_.vwide[l, n : n + 1, 0:48] = row[l : l + 1, :]
    t_.vown[...] = t_.vwide[...].astype(BF)
    vplace = pltpu.make_async_copy(t_.vown, o_.v.at[z, x, c], m_.vlocal.at[0])
    vplace.start()
    xload = pltpu.make_async_copy(i_.x, t_.last, m_.vlocal.at[1])
    xload.start()
    pl.semaphore_wait(bar, 5)


    def stages(b, s):
        def copy(zz, xx, hh, sem, d):
            u = b(zz, xx, c, hh)
            return pltpu.make_async_remote_copy(src_ref=u, dst_ref=u, send_sem=sem.at[s], recv_sem=m_.recv.at[s, (zz * 2 + xx) * 2 + hh], device_id=d, device_id_type=MESH)

        def zsend(zz, d, sem=m_.fsend):
            copy(zz, x, y, sem, d).start()

        def got(zz, xx, hh, d):
            copy(zz, xx, hh, m_.zsend, d).wait_recv()

        def plane(zz, cc=c):
            u = b(zz, slice(None), cc, slice(None))
            return pltpu.make_async_remote_copy(src_ref=u, dst_ref=u, send_sem=m_.csend.at[s], recv_sem=m_.crecv.at[s, zz], device_id=d_c, device_id_type=MESH)

        def spread(zz):
            copy(zz, x, y, m_.xysend, d_x).start()
            copy(zz, x, y, m_.xysend, d_y).start()

        def relay(zz, first_x):
            got(zz, 1 - x, y, d_x)
            got(zz, x, 1 - y, d_y)

            def through_y():
                copy(zz, 1 - x, y, m_.rsend, d_y).start()

            def through_x():
                copy(zz, x, 1 - y, m_.rsend, d_x).start()
            if first_x is True:
                through_y()
            elif first_x is False:
                through_x()
            else:
                pl.when(first_x)(through_y)
                pl.when(jnp.logical_not(first_x))(through_x)

        def diagonal(zz):
            got(zz, 1 - x, 1 - y, d_y)
            plane(zz).start()

        def st0():
            zsend(z, d_zp, m_.zsend)
            pl.when(mid)(lambda: zsend(z, d_zm, m_.zsend))
            copy(z, x, y, m_.xysend, d_x).start()

        def st1():
            got(zp, x, y, d_zp)

            @pl.when(mid)
            def _():
                zsend(zp, d_zm)
                got(zm, x, y, d_zm)
                zsend(zm, d_zp)
            spread(zp)
            got(z, 1 - x, y, d_x)
            copy(z, 1 - x, y, m_.xysend, d_y).start()

        def st2():
            got(zf, x, y, d_zp)
            pl.when(mid)(lambda: zsend(zf, d_zp))
            spread(zf)
            relay(zp, True)
            diagonal(z)

        def st3():
            pl.when(end)(lambda: got(zm, x, y, d_zp))
            spread(zm)
            relay(zf, False)
            diagonal(zp)

        def st4():
            relay(zm, lax.rem(s, 2) == 0)
            diagonal(zf)

        def st5():
            diagonal(zm)

        def st6():
            for zz in (z, zp, zf, zm):
                plane(zz, 1 - c).wait_recv()
        return st0, st1, st2, st3, st4, st5, st6

    def stages_z(b, s):
        def copy(zz, xx, hh, sem, d):
            u = b(zz, xx, c, hh)
            at = 0 if isinstance(hh, slice) else hh
            return pltpu.make_async_remote_copy(src_ref=u, dst_ref=u, send_sem=sem.at[s], recv_sem=m_.recv.at[s, (zz * 2 + xx) * 2 + at], device_id=d, device_id_type=MESH)
        both = slice(None)

        def zsend(zz, xx, d, sem=m_.fsend):
            copy(zz, xx, both, sem, d).start()

        def got(zz, xx, d):
            copy(zz, xx, both, m_.zsend, d).wait_recv()

        def plane(zz, cc=c):
            u = b(zz, both, cc, both)
            return pltpu.make_async_remote_copy(src_ref=u, dst_ref=u, send_sem=m_.csend.at[s], recv_sem=m_.crecv.at[s, zz], device_id=d_c, device_id_type=MESH)

        def own(xx):
            zsend(z, xx, d_zp, m_.zsend)
            pl.when(mid)(lambda: zsend(z, xx, d_zm, m_.zsend))

        def near(xx):
            got(zp, xx, d_zp)

            @pl.when(mid)
            def _():
                zsend(zp, xx, d_zm)
                got(zm, xx, d_zm)
                zsend(zm, xx, d_zp)

        def far(xx):
            got(zf, xx, d_zp)
            pl.when(mid)(lambda: zsend(zf, xx, d_zp))

        def farthest(xx):
            pl.when(end)(lambda: got(zm, xx, d_zp))

        def st0():
            own(x)
            copy(z, x, y, m_.xysend, d_x).start()

        def st1():
            near(x)
            copy(z, 1 - x, y, m_.xysend, d_x).wait_recv()
            copy(z, 1 - x, y, m_.xysend, d_y).start()

        def st2():
            far(x)
            copy(z, 1 - x, 1 - y, m_.xysend, d_y).wait_recv()
            own(1 - x)
            plane(z).start()

        def st3():
            farthest(x)
            near(1 - x)
            plane(zp).start()

        def st4():
            far(1 - x)
            plane(zf).start()

        def st5():
            farthest(1 - x)
            plane(zm).start()

        def st6():
            for zz in (z, zp, zf, zm):
                plane(zz, 1 - c).wait_recv()
        return st0, st1, st2, st3, st4, st5, st6

    def sent_z(s):
        wait_all(o_.w.at[0, 0, 0, 0], m_.xysend.at[s])
        wait_all(many_w(16), m_.csend.at[s])
        pl.when(end)(lambda: wait_all(o_.w.at[0, 0, 0], m_.zsend.at[s]))

        @pl.when(mid)
        def _():
            wait_all(many_w(8), m_.zsend.at[s])
            wait_all(o_.w.at[0, 0:3, :, 0], m_.fsend.at[s])

    def sent(b, s, many):
        wait_all(many(8), m_.xysend.at[s])
        wait_all(many(3), m_.rsend.at[s])
        wait_all(many(16), m_.csend.at[s])
        pl.when(end)(lambda: wait_all(many(1), m_.zsend.at[s]))

        @pl.when(mid)
        def _():
            wait_all(many(2), m_.zsend.at[s])
            wait_all(many(3), m_.fsend.at[s])

    def unit(p):
        return lambda zz, xx, cc, hh: o_.w.at[p, zz, xx, cc, hh]

    def vunit(zz, xx, cc, hh):
        return o_.v.at[zz, xx, cc, hh]

    def many_w(n):
        if n == 8:
            return o_.w.at[0, 0]
        if n == 16:
            return o_.w.at[0, :, :, 0]
        return o_.w.at[0:n, 0, 0, 0, 0]

    def many_v(n):
        if n == 8:
            return o_.v.at[0]
        if n == 16:
            return o_.v.at[:, :, 0]
        return o_.v.at[0:n, 0, 0, 0]


    def load_att(l):
        for cp in matrix_loads(o_.w, 8 * l, 0, t_.wq, m_.wload.at[0]) + matrix_loads(o_.w, 8 * l, 1, t_.wk, m_.wload.at[1]) + matrix_loads(o_.w, 8 * l + 1, 0, t_.wv, m_.wload.at[2]) + matrix_loads(o_.w, 8 * l + 1, 1, t_.wo, m_.wload.at[3]):
            cp.start()

    def load_gated(l, j):
        for cp in matrix_loads(o_.w, 8 * l + 2 + j, 0, t_.wg, m_.wload.at[4]) + matrix_loads(o_.w, 8 * l + 2 + j, 1, t_.wu, m_.wload.at[5]):
            cp.start()

    def load_down(l, part):
        for s in (2 * part, 2 * part + 1):
            for h in range(2):
                pltpu.make_async_copy(o_.w.at[8 * l + 6 + s // 2, :, :, :, h, s % 2], t_.wd.at[:, :, :, s, :, pl.ds(384 * h, 384)], m_.wload.at[6]).start()

    def store(i, src, dst, go):
        run(pltpu.make_async_copy(src, dst, m_.store.at[i]), go)

    def per_layer(l, f):
        for n in range(LAYERS):
            @pl.when(l == n)
            def _():
                f(kept[n])

    def vrow(l, n):
        return o_.vec[l, n : n + 1, :]

    def store_att(kl, i, go):
        store(0, t_.q, cols(kl.q, i, 256), go)
        store(1, t_.k, cols(kl.k, i, 256), go)
        store(2, t_.v, cols(kl.v, i, 256), go)
        store(3, t_.pt, kl.pt.at[:, pl.ds(4 * i, 4)], go)
        store(4, t_.at, kl.at.at[pl.ds(pl.multiple_of(256 * i, 256), 256)], go)

        @pl.when(i == 0)
        def _():
            store(5, t_.xt, kl.xt, go)

    def att_task(l, i):
        @pl.when(i == 0)
        def _():
            wait_all(t_.wq, m_.wload.at[0])
            wait_all(t_.wk, m_.wload.at[1])
            wait_all(t_.wv, m_.wload.at[2])
            xb = t_.x[...].astype(BF)
            t_.xb[...] = xb
            t_.xt[...] = xb.T
        xb = t_.xb[...]
        lane = pl.multiple_of(256 * i, 256)
        at = pl.ds(lane, 256)
        t_.q[...] = (mm(xb, t_.wq[:, :, :, :, at].reshape(D, 256)) + o_.vec[l, 0:1, at]).astype(BF)
        t_.k[...] = mm(xb, t_.wk[:, :, :, :, at].reshape(D, 256)).astype(BF)
        t_.v[...] = (mm(xb, t_.wv[:, :, :, :, at].reshape(D, 256)) + o_.vec[l, 1:2, at]).astype(BF)
        for s in range(seqs):
            rows = slice(s * pad, (s + 1) * pad)
            hidden = jnp.where(lax.broadcasted_iota(jnp.int32, (pad, 1), 0) < i_.lens[s], 0.0, NEG)
            for pair in range(2):
                lanes = slice(128 * pair, 128 * pair + 128)
                q2 = t_.q[rows, lanes] * BF(HEAD_DIM ** -0.5)
                ks = halves(t_.k[rows, lanes], 1)
                vs = halves(t_.v[rows, lanes].T, 0)
                total = None
                for h in range(2):
                    slope = i_.slopes[4 * i + 2 * pair + h]
                    sc = mm_nt(ks[h], q2) - slope * t_.dist[...] + hidden
                    e = jnp.exp(sc - jnp.max(sc, axis=0, keepdims=True))
                    p = (e * (1.0 / jnp.sum(e, axis=0, keepdims=True))).astype(BF)
                    t_.pt[s, 2 * pair + h] = p
                    part = mm(vs[h], p)
                    total = part if total is None else total + part
                total = total.astype(BF)
                t_.at[lanes, rows] = total
                t_.att[rows, pl.ds(pl.multiple_of(lane + 128 * pair, 128), 128)] = total.T
        per_layer(l, lambda kl: store_att(kl, i, True))

    def store_ff(kl, j, go):
        store(6, t_.ga, cols(kl.ga, j, 768), go)
        store(7, t_.gb, cols(kl.gb, j, 768), go)
        store(8, t_.ft, kl.ft.at[pl.ds(pl.multiple_of(768 * j, 768), 768)], go)

        @pl.when(j == 0)
        def _():
            store(9, t_.res, kl.r1, go)
            store(10, t_.xt, kl.ht, go)

    def ff_task(l, j):
        @pl.when(j == 0)
        def _():
            wait_all(t_.wo, m_.wload.at[3])
            r1 = t_.x[...] + (mm(t_.att[...], t_.wo[...].reshape(D, D)) + vrow(l, 2))
            t_.res[...] = r1
            h = norm_parts(r1)[0] * vrow(l, 3) + vrow(l, 4)
            t_.h[...] = h
            hb = h.astype(BF)
            t_.hb[...] = hb
            t_.xt[...] = hb.T
        wait_all(t_.wg, m_.wload.at[4])
        wait_all(t_.wu, m_.wload.at[5])
        hb = t_.hb[...]
        g = mm(hb, t_.wg[...].reshape(D, 768))
        u = mm(hb, t_.wu[...].reshape(D, 768))
        cdf = 0.5 + 0.5 * erf(g * math.sqrt(0.5))
        gelu = g * cdf
        slope = cdf + g * (jnp.exp(-0.5 * (g * g)) * (1.0 / math.sqrt(2.0 * math.pi)))
        t_.ga[...] = gelu.astype(BF)
        t_.gb[...] = (slope * u).astype(BF)
        f = (gelu * u).astype(BF)
        t_.f[j] = f
        t_.ft[...] = f.T
        per_layer(l, lambda kl: store_ff(kl, j, True))

    def down_task(l):
        wait_all(t_.wd, m_.wload.at[6])
        total = t_.h[...] + vrow(l, 5)
        for j in range(4):
            total = total + mm(t_.f[j], t_.wd[j].reshape(768, D))
        t_.res[...] = total
        out = norm_parts(total)[0] * vrow(l, 6) + vrow(l, 7)
        t_.x[...] = out
        per_layer(l, lambda kl: store(9, t_.res, kl.r2, True))

        @pl.when(l == LAYERS - 1)
        def _():
            t_.last[...] = out.astype(BF)
            store(11, t_.last, o_.last, True)

    def task(t, att, ff, down):
        l = t // 8
        u = lax.rem(t, 8)
        pl.when(u < 3)(lambda: att(l, jnp.minimum(u, 2)))
        pl.when(jnp.logical_and(u >= 3, u < 7))(lambda: ff(l, jnp.clip(u - 3, 0, 3)))
        pl.when(u == 7)(lambda: down(l))

    def stored(t):
        task(t, lambda l, i: store_att(kept[0], i, False), lambda l, j: store_ff(kept[0], j, False), lambda l: store(9, t_.res, kept[0].r2, False))

    def fetch(t):
        def att(l, i):
            pl.when(i == 0)(lambda: load_att(l))

        def ff(l, j):
            load_gated(l, j)
            pl.when(j == 3)(lambda: load_down(l, 0))
        task(t, att, ff, lambda l: load_down(l, 1))


    vst = stages(vunit, PIECES)

    def begun(r):
        return jnp.clip(jnp.where(r <= 16, r - 7, r - 6), 0, 8 * LAYERS)

    def first(p):
        wait_all(o_.w.at[p, z, x, c], m_.local.at[p])
        pl.when(along_z(p))(stages_z(unit(p), p)[0])
        pl.when(jnp.logical_not(along_z(p)))(stages(unit(p), p)[0])

    def body(r, carry):
        def at(k):
            p = r - k

            @pl.when(jnp.logical_and(p >= 0, p < PIECES))
            def _():
                q = jnp.clip(p, 0, PIECES - 1)
                pl.when(along_z(q))(lambda: stages_z(unit(q), q)[k]())
                pl.when(jnp.logical_not(along_z(q)))(lambda: stages(unit(q), q)[k]())

        @pl.when(r + EARLY < PIECES)
        def _():
            local(jnp.minimum(r + EARLY, PIECES - 1))

        @pl.when(r < PIECES)
        def _():
            first(jnp.minimum(r, PIECES - 1))
        for k in range(1, 7):
            pl.when(r == k)(vst[k])
        at(6)
        low, high = begun(r), begun(r + 1)

        @pl.when(high > low)
        def _():
            fetch(jnp.minimum(low, 8 * LAYERS - 1))
        for k in (1, 2, 3, 4, 5):
            at(k)

        @pl.when(r == 6)
        def _():
            cp = pltpu.make_async_copy(o_.v, t_.vec_in, m_.vload)
            cp.start()
            xload.wait()
            t_.x[...] = t_.last[...].astype(F32)
            keys = lax.broadcasted_iota(jnp.int32, (pad, pad), 0)
            rows = lax.broadcasted_iota(jnp.int32, (pad, pad), 1)
            t_.dist[...] = jnp.abs(keys - rows).astype(F32)
            cp.wait()
            unpack_vectors()

        def one(t, carry):
            @pl.when(t >= 1)
            def _():
                stored(jnp.maximum(t - 1, 0))
            task(t, att_task, ff_task, down_task)
            return carry
        lax.fori_loop(low, high, one, 0)
        return carry

    def unpack_vectors():
        for l in range(LAYERS):
            parts = [t_.vec_in[b // 4, (b // 2) % 2, b % 2, l].astype(F32)[:, 0:48] for b in range(16)]
            o_.vec[l] = jnp.concatenate(parts, axis=1)
    vplace.wait()
    vst[0]()
    lax.fori_loop(0, PIECES + 6, body, 0)
    stored(8 * LAYERS - 1)
    store(11, t_.last, o_.last, False)

    def finish(p, carry):
        pl.when(along_z(p))(lambda: sent_z(p))
        pl.when(jnp.logical_not(along_z(p)))(lambda: sent(unit(p), p, many_w))
        return carry
    lax.fori_loop(0, PIECES, finish, 0)
    sent(vunit, PIECES, many_v)


def forward_all(lengths, slopes, x, shards, vectors):
    rows = x.shape[0]
    seqs = lengths.shape[0]
    pad = rows // seqs
    hbm = pl.BlockSpec(memory_space=pltpu.HBM)
    vmem = pl.BlockSpec(memory_space=pltpu.VMEM)
    smem = pl.BlockSpec(memory_space=pltpu.SMEM)
    S = jax.ShapeDtypeStruct
    act = lambda n, t: S((rows, n), t)
    one = [act(D, F32), act(D, F32), act(FF, BF), act(FF, BF), act(D, BF), act(D, BF), act(D, BF), S((seqs, HEADS, pad, pad), BF), S((FF, rows), BF), S((D, rows), BF), S((D, rows), BF), S((D, rows), BF)]
    out = [S((PIECES, 4, 2, 2, 2, 2, 48, 384), BF), S((4, 2, 2, 2, 8, 128), BF), S((LAYERS, 8, D), F32), act(D, BF)] + one * LAYERS
    v = pltpu.VMEM
    dma = pltpu.SemaphoreType.DMA
    mat = v((4, 2, 2, 48, D), BF)
    n = PIECES + 1
    scratch = [
        v((rows, D), F32), v((rows, D), BF), v((pad, pad), F32), v((rows, 256), BF), v((rows, 256), BF), v((rows, 256), BF), v((rows, D), BF),
        v((seqs, 4, pad, pad), BF), v((256, rows), BF), v((D, rows), BF), mat, mat, mat, mat, mat, mat, v((4, 2, 2, 4, 48, D), BF),
        v((rows, D), F32), v((rows, D), BF), v((4, rows, 768), BF), v((rows, 768), BF), v((rows, 768), BF), v((768, rows), BF), v((rows, D), F32), v((rows, D), BF),
        v((2, 8, 128), BF), v((2, 8, 128), F32), v((4, 2, 2, 2, 8, 128), BF),
        dma((PIECES,)), dma((n,)), dma((n,)), dma((n,)), dma((n,)), dma((n,)), dma((n, 16)), dma((n, 4)), dma((2,)), dma, dma, dma((7,)), dma((12,)),
    ]
    res = pl.pallas_call(
        forward_kernel, out_shape=out,
        in_specs=[smem, smem, hbm] + [hbm] * 4 + [vmem] * 8,
        out_specs=[hbm, hbm, vmem, hbm] + [hbm] * (12 * LAYERS),
        scratch_shapes=scratch,
        compiler_params=pltpu.CompilerParams(collective_id=0, has_side_effects=True, vmem_limit_bytes=60 * 2**20), name="gather_forward",
    )(lengths, slopes, x, *shards, *vectors)
    return res[0], res[2], res[3], [res[4 + 12 * l : 16 + 12 * l] for l in range(LAYERS)]


NPIECE = 33
LAG = 2
SLOTS = 16


STEPS = (0, 1, 4, 6, 8, 10, 12, 14)
STEPS_Z = (0, 1, 4, 7, 9, 11, 12, 13)


def reduce_z(p):
    return lax.rem(p, 4) == 1


def piece_first_x(p):
    others = p - (p + 2) // 4
    return jnp.logical_or(reduce_z(p), lax.rem(others * 5, 8) < 5)


def add_into(dst, src):
    dst[...] = dst[...] + src[...]


GRADS = ("dg", "du", "dq", "dk", "dv")


def backward_kernel(*refs):
    take = taker(refs)
    i_ = take("cot", "vec")
    cot, vec = i_.cot, i_.vec
    kept = [take(*KEPT) for _ in range(LAYERS)]
    w = take("w").w
    o = take("qkv", "out", "gated", "down", "vec", "dx")
    g = take(*GRADS)
    s = take("lbuf", "rbuf", "sbuf", "own", "stage", "r0v", "h1v", "h2v", "zav", "zbv", "yfv", "vall")
    c_ = take("r0", "h1", "h2", "za", "zb", "yf", "zza", "zzb")
    t_ = take("acc", "res", "wd", "wg", "wu", "ga", "gb", "wo", "dm", "dg", "du", "da", "datt", "q", "k", "v", "pt", "wq", "wk", "wv", "dq", "dk", "dv", "gv", "cot")
    m_ = take("lsem", "rsem", "send", "recv", "out", "vload", "fsem", "asem", "osem")
    pad = kept[0].pt.shape[-1]
    seqs = kept[0].pt.shape[0]

    z, x, y, c = place()
    zp = z + 1 - 2 * lax.rem(z, 2)
    zm = 3 - z
    mid = jnp.logical_and(z >= 1, z <= 2)
    end = jnp.logical_not(mid)
    d_zp, d_zm = dev(zp, x, y, c), dev(zm, x, y, c)
    d_x, d_y, d_c = dev(z, 1 - x, y, c), dev(z, x, 1 - y, c), dev(z, x, y, 1 - c)
    bar = pltpu.get_barrier_semaphore()
    for d in (d_zp, d_zm, d_x, d_y, d_c):
        pl.semaphore_signal(bar, 1, device_id=d, device_id_type=MESH)
    NP = NPIECE - 1


    def per_layer(l, f):
        for n in range(LAYERS):
            @pl.when(l == n)
            def _():
                f(kept[n])

    def load_ff_a(l, j, go):
        def one(i, src, dst):
            run(pltpu.make_async_copy(src, dst, m_.fsem.at[i]), go)

        def acts(kl):
            one(3, cols(kl.ga, j, 768), t_.ga)
            one(4, cols(kl.gb, j, 768), t_.gb)
        if go:
            pl.when(j == 0)(lambda: per_layer(l, lambda kl: one(5, kl.r2, t_.res)))
            for n in range(4):
                for h in range(2):
                    one(0, w.at[8 * l + 6 + n // 2, j, :, :, h, n % 2], t_.wd.at[:, :, n, :, pl.ds(384 * h, 384)])
            per_layer(l, acts)
        else:
            wait_all(t_.wd, m_.fsem.at[0])
            acts(kept[0])

    def load_ff_b(l, j, go):
        def one(i, src, dst):
            run(pltpu.make_async_copy(src, dst, m_.fsem.at[i]), go)
        for n, (k, dst) in enumerate(((0, t_.wg), (1, t_.wu))):
            if go:
                for cp in matrix_loads(w, 8 * l + 2 + j, k, dst, m_.fsem.at[1 + n]):
                    cp.start()
            else:
                wait_all(dst, m_.fsem.at[1 + n])

        @pl.when(j == 3)
        def _():
            if go:
                per_layer(l, lambda kl: one(5, kl.r1, t_.res))
                for cp in matrix_loads(w, 8 * l + 1, 1, t_.wo, m_.fsem.at[6]):
                    cp.start()
            else:
                one(5, kept[0].r1, t_.res)
                wait_all(t_.wo, m_.fsem.at[6])

    def load_att(l, i, go):
        def one(n, src, dst):
            run(pltpu.make_async_copy(src, dst, m_.asem.at[n]), go)

        def acts(kl):
            one(0, cols(kl.q, i, 256), t_.q)
            one(1, cols(kl.k, i, 256), t_.k)
            one(2, cols(kl.v, i, 256), t_.v)
            one(3, kl.pt.at[:, pl.ds(4 * i, 4)], t_.pt)
        if go:
            for n in range(LAYERS):
                @pl.when(l == n)
                def _():
                    acts(kept[n])
        else:
            acts(kept[0])
        @pl.when(i == 0)
        def _():
            for n, dst in enumerate((t_.wq, t_.wk, t_.wv)):
                if go:
                    for cp in matrix_loads(w, 8 * l + n // 2, n % 2, dst, m_.asem.at[4 + n]):
                        cp.start()
                else:
                    wait_all(dst, m_.asem.at[4 + n])

    def norm_two(l):
        pltpu.make_async_copy(kept[0].r2, t_.res, m_.fsem.at[5]).wait()
        dy = t_.acc[...]
        n, rstd = norm_parts(t_.res[...])
        dr2 = norm_back(dy, vec[l, 6:7, :], n, rstd)
        t_.acc[...] = dr2
        dm = dr2.astype(BF)
        t_.dm[...] = dm
        t_.gv[l, 5:6, :] = colsum(dm.astype(F32))
        t_.gv[l, 6:7, :] = colsum(dy * n)
        t_.gv[l, 7:8, :] = colsum(dy)

    def ff_a(l, j):
        load_ff_a(l, j, False)

        @pl.when(jnp.logical_and(j == 0, l < LAYERS - 1))
        def _():
            norm_two(l)
        df = mm_nt(t_.dm[...], t_.wd[...].reshape(768, D))
        t_.dg[...] = (df * t_.gb[...].astype(F32)).astype(BF)
        t_.du[...] = (df * t_.ga[...].astype(F32)).astype(BF)
        store_ff(l, j, True)

        @pl.when(j < 3)
        def _():
            load_ff_a(l, j + 1, True)

    def ff_b(l, j):
        load_ff_b(l, j, False)
        t_.acc[...] += mm_nt(t_.dg[...], t_.wg[...].reshape(D, 768)) + mm_nt(t_.du[...], t_.wu[...].reshape(D, 768))

        @pl.when(j < 3)
        def _():
            load_ff_b(l, j + 1, True)

        @pl.when(j == 3)
        def _():
            load_att(l, 0, True)
            dh = t_.acc[...]
            n, rstd = norm_parts(t_.res[...])
            dr1 = norm_back(dh, vec[l, 3:4, :], n, rstd)
            t_.acc[...] = dr1
            da = dr1.astype(BF)
            t_.da[...] = da
            t_.gv[l, 2:3, :] = colsum(da.astype(F32))
            t_.gv[l, 3:4, :] = colsum(dh * n)
            t_.gv[l, 4:5, :] = colsum(dh)
            datt = mm_nt(da, t_.wo[...].reshape(D, D)).astype(BF)
            for i in range(3):
                t_.datt[i] = datt[:, 256 * i : 256 * i + 256]

    def store_ff(l, j, go):
        def one(i, src, dst):
            run(pltpu.make_async_copy(src, dst, m_.osem.at[i]), go)
        one(0, t_.dg, cols(g.dg.at[l], j, 768))
        one(1, t_.du, cols(g.du.at[l], j, 768))

    def att_a(l, i):
        load_att(l, i, False)
        scale = HEAD_DIM ** -0.5
        first = lax.broadcasted_iota(jnp.int32, (pad, 128), 1) < HEAD_DIM
        for sq in range(seqs):
            rows = slice(sq * pad, (sq + 1) * pad)
            for pair in range(2):
                lanes = slice(128 * pair, 128 * pair + 128)
                q2 = t_.q[rows, lanes]
                d2 = t_.datt[i, rows, lanes]
                vs = halves(t_.v[rows, lanes], 1)
                ks = halves(t_.k[rows, lanes].T, 0)
                dv, dk, dq = [], [], None
                for h in range(2):
                    pb = t_.pt[sq, 2 * pair + h]
                    p = pb.astype(F32)
                    dp = mm_nt(vs[h], d2)
                    ds = (p * (dp - jnp.sum(dp * p, axis=0, keepdims=True))).astype(BF)
                    dv.append(mm(pb, d2))
                    dk.append(mm(ds, q2))
                    part = mm(ks[h], ds)
                    dq = part if dq is None else dq + part
                t_.dv[rows, lanes] = jnp.where(first, dv[0], dv[1]).astype(BF)
                t_.dk[rows, lanes] = (jnp.where(first, dk[0], dk[1]) * scale).astype(BF)
                t_.dq[rows, lanes] = (dq * scale).astype(BF).T
        dq, dk, dv = t_.dq[...], t_.dk[...], t_.dv[...]
        at = pl.ds(pl.multiple_of(i * 256, 256), 256)
        t_.gv[l, 0:1, at] = colsum(dq.astype(F32))
        t_.gv[l, 1:2, at] = colsum(dv.astype(F32))
        store_att(l, i, True)

        @pl.when(i < 2)
        def _():
            load_att(l, i + 1, True)

    def att_b(l, i):
        at = pl.ds(pl.multiple_of(i * 256, 256), 256)
        t_.acc[...] += (
            mm_nt(t_.dq[...], t_.wq[:, :, :, :, at].reshape(D, 256)) + mm_nt(t_.dk[...], t_.wk[:, :, :, :, at].reshape(D, 256)) + mm_nt(t_.dv[...], t_.wv[:, :, :, :, at].reshape(D, 256))
        )

        @pl.when(jnp.logical_and(i == 2, l > 0))
        def _():
            load_ff_a(jnp.maximum(l - 1, 0), 0, True)
            load_ff_b(jnp.maximum(l - 1, 0), 0, True)

        @pl.when(jnp.logical_and(i == 2, l == 0))
        def _():
            t_.cot[...] = t_.acc[...].astype(BF)
            pltpu.make_async_copy(t_.cot, o.dx, m_.osem.at[7]).start()

    def store_att(l, i, go):
        def one(n, src, dst):
            run(pltpu.make_async_copy(src, dst, m_.osem.at[n]), go)
        one(4, t_.dq, cols(g.dq.at[l], i, 256))
        one(5, t_.dk, cols(g.dk.at[l], i, 256))
        one(6, t_.dv, cols(g.dv.at[l], i, 256))

    def task(t, ff, att):
        l = LAYERS - 1 - t // 7
        u = lax.rem(t, 7)

        @pl.when(u < 4)
        def _():
            ff(l, jnp.minimum(u, 3))

        @pl.when(u >= 4)
        def _():
            att(l, jnp.clip(u - 4, 0, 2))


    def load(p, go):
        q = lax.rem(p, 16)
        n = lax.rem(p, 2)
        layer = LAYERS - 1 - p // 16

        def left(ref, sub=None):
            for k in range(2):
                cc = c if k else 1 - c
                src = ref.at[:, cc] if sub is None else ref.at[:, cc, sub]
                run(pltpu.make_async_copy(src, s.lbuf.at[n, k], m_.lsem.at[n, k]), go)

        def right(ref, col=None):
            src = ref if col is None else cols(ref.at[layer], jnp.clip(col, 0, 3), 768)
            run(pltpu.make_async_copy(src, s.rbuf.at[n], m_.rsem.at[n]), go)
        if not go:
            left(kept[0].ht)
            right(t_.dm)
            return
        for l in range(LAYERS):
            here = layer == l
            kl = kept[l]

            @pl.when(jnp.logical_and(here, q < 4))
            def _():
                left(kl.ft, jnp.minimum(q, 3))

            @pl.when(jnp.logical_and(here, jnp.logical_and(q >= 4, q < 12)))
            def _():
                left(kl.ht)

            @pl.when(jnp.logical_and(here, q == 12))
            def _():
                left(kl.at)

            @pl.when(jnp.logical_and(here, q > 12))
            def _():
                left(kl.xt)

        @pl.when(q < 4)
        def _():
            right(t_.dm)

        @pl.when(jnp.logical_and(q >= 4, q < 8))
        def _():
            right(g.dg, q - 4)

        @pl.when(jnp.logical_and(q >= 8, q < 12))
        def _():
            right(g.du, q - 8)
        for i, d in enumerate((t_.da, g.dq.at[layer], g.dk.at[layer], g.dv.at[layer])):
            @pl.when(q == 12 + i)
            def _():
                right(d)

    def rcopy(p, e, src, dst, d):
        return pltpu.make_async_remote_copy(src_ref=src, dst_ref=dst, send_sem=m_.send.at[p, e], recv_sem=m_.recv.at[p, e], device_id=d, device_id_type=MESH)

    def product(n, theirs, mine):
        v = mm(s.lbuf[n].reshape(768, -1), s.rbuf[n]).astype(BF).reshape(2, 4, 2, 48, 768)
        for k, dst in enumerate((theirs, mine)):
            dst[:, :, 0] = v[k, :, :, :, :384]
            dst[:, :, 1] = v[k, :, :, :, 384:]

    def c_copy(p, n):
        return rcopy(p, 0, s.sbuf.at[n], c_.r0.at[lax.rem(p, SLOTS)], d_c)

    def s0(p):
        n = lax.rem(p, 2)
        load(p, False)

        @pl.when(p >= 2)
        def _():
            c_copy(jnp.maximum(p - 2, 0), n).wait_send()
        product(n, s.sbuf.at[n], s.own.at[lax.rem(p, LAG + 1)])
        c_copy(p, n).start()

        @pl.when(p + 1 < NP)
        def _():
            load(jnp.minimum(p + 1, NP - 1), True)
    small = Group(("r0", "h1", "h2", "za", "zb", "yf"), (s.r0v, s.h1v, s.h2v, s.zav, s.zbv, s.yfv))
    zlo = jnp.where(z == 1, 1, 0)
    elo = jnp.where(z == 0, 1, 0)
    mlo = jnp.where(z == 1, 2, 0)
    rlo = jnp.where(z == 1, 0, 2)

    def steps(b, p, i, my):
        fx = piece_first_x(p)
        fy = jnp.logical_not(fx)

        def hop1(go):
            a = rcopy(p, 1, b.r0.at[i, :, 1 - x], b.h1.at[i], d_x)
            if go == "start":
                pl.when(fx)(a.start)
                pl.when(fy)(rcopy(p, 1, b.r0.at[i, :, :, 1 - y], b.h1.at[i], d_y).start)
            elif go == "recv":
                a.wait_recv()
            else:
                a.wait_send()

        def hop2(go):
            a = rcopy(p, 2, b.h1.at[i, :, 1 - y], b.h2.at[i], d_y)
            if go == "start":
                pl.when(fx)(a.start)
                pl.when(fy)(rcopy(p, 2, b.h1.at[i, :, 1 - x], b.h2.at[i], d_x).start)
            elif go == "recv":
                a.wait_recv()
            else:
                a.wait_send()

        def z1():
            return rcopy(p, 3, b.h2.at[i, pl.ds(elo, 3)], b.za.at[i], d_zp)

        def z2():
            return rcopy(p, 4, b.h2.at[i, pl.ds(mlo, 2)], b.zb.at[i], d_zm)

        def z3():
            return rcopy(p, 5, b.h2.at[i, zp], b.zb.at[i, 0], d_zp)

        def y1():
            return rcopy(p, 6, b.h2.at[i, z], b.yf.at[i], d_y)

        def s1():
            rcopy(p, 0, b.r0.at[i], b.r0.at[i], d_c).wait_recv()
            for k in range(4):
                add_into(b.r0.at[i, k], my.at[k])
            hop1("start")

        def s2():
            hop1("recv")
            for k in range(4):
                @pl.when(fx)
                def _():
                    add_into(b.h1.at[i, k], b.r0.at[i, k, x])

                @pl.when(fy)
                def _():
                    add_into(b.h1.at[i, k], b.r0.at[i, k, :, y])
            hop2("start")

        def s3():
            hop1("send")
            hop2("recv")
            t = jnp.where(fx, y, x)
            for k in range(4):
                add_into(b.h2.at[i, k], b.h1.at[i, k, t])
            pl.when(end)(z1().start)

        def s4():
            hop2("send")

            @pl.when(mid)
            def _():
                z1().wait_recv()
                for k in range(3):
                    add_into(b.h2.at[i, zlo + k], b.za.at[i, k])
                z2().start()

        def s5():
            pl.when(end)(z1().wait_send)

            @pl.when(mid)
            def _():
                z2().wait_recv()
                for k in range(2):
                    add_into(b.h2.at[i, rlo + k], b.zb.at[i, k])
                z3().start()

        def s6():
            pl.when(mid)(z2().wait_send)

            @pl.when(end)
            def _():
                z3().wait_recv()
                add_into(b.h2.at[i, z], b.zb.at[i, 0])
            y1().start()

        def s7():
            pl.when(mid)(z3().wait_send)
            y1().wait_send()
            y1().wait_recv()
        return s1, s2, s3, s4, s5, s6, s7

    def steps_z(p, i, my):
        b = c_
        fx = piece_first_x(p)
        iz = lax.rem(p // 4, SLOTS // 4)

        def hop1():
            return rcopy(p, 1, b.r0.at[i, z, 1 - x], b.h1.at[i, 0], d_x)

        def hop2():
            return rcopy(p, 2, b.h1.at[i, 0, 1 - y], b.h2.at[i, z], d_y)

        def z1():
            return rcopy(p, 3, b.r0.at[i, pl.ds(elo, 3)], b.zza.at[iz], d_zp)

        def z2():
            return rcopy(p, 4, b.r0.at[i, pl.ds(mlo, 2)], b.zzb.at[iz], d_zm)

        def z3():
            return rcopy(p, 5, b.r0.at[i, zp], b.zzb.at[iz, 0], d_zp)

        def y1():
            return rcopy(p, 6, b.h2.at[i, z], b.yf.at[i], d_y)

        def s1():
            rcopy(p, 0, b.r0.at[i], b.r0.at[i], d_c).wait_recv()
            for k in range(4):
                add_into(b.r0.at[i, k], my.at[k])
            pl.when(end)(z1().start)

        def s2():
            @pl.when(mid)
            def _():
                z1().wait_recv()
                for k in range(3):
                    add_into(b.r0.at[i, zlo + k], b.zza.at[iz, k])
                z2().start()

        def s3():
            pl.when(end)(z1().wait_send)

            @pl.when(mid)
            def _():
                z2().wait_recv()
                for k in range(2):
                    add_into(b.r0.at[i, rlo + k], b.zzb.at[iz, k])
                z3().start()

        def s4():
            pl.when(mid)(z2().wait_send)

            @pl.when(end)
            def _():
                z3().wait_recv()
                add_into(b.r0.at[i, z], b.zzb.at[iz, 0])
            hop1().start()

        def s5():
            pl.when(mid)(z3().wait_send)
            hop1().wait_recv()
            add_into(b.h1.at[i, 0], b.r0.at[i, z, x])
            hop2().start()

        def s6():
            hop1().wait_send()
            hop2().wait_recv()
            add_into(b.h2.at[i, z], b.h1.at[i, 0, y])
            y1().start()

        def s7():
            hop2().wait_send()
            y1().wait_send()
            y1().wait_recv()
        return s1, s2, s3, s4, s5, s6, s7

    def out_copy(p, n, go):
        q = lax.rem(p, 16)
        layer = LAYERS - 1 - p // 16

        def one(dst):
            run(pltpu.make_async_copy(s.stage.at[n], dst, m_.out.at[n]), go)
        if not go:
            one(o.out.at[0])
            return

        @pl.when(q < 4)
        def _():
            one(o.down.at[layer, pl.ds(pl.multiple_of(jnp.minimum(q, 3) * 48, 48), 48)])

        @pl.when(jnp.logical_and(q >= 4, q < 12))
        def _():
            one(cols(o.gated.at[layer], jnp.clip(q - 4, 0, 7), 768))

        @pl.when(q == 12)
        def _():
            one(o.out.at[layer])

        @pl.when(q > 12)
        def _():
            one(cols(o.qkv.at[layer], jnp.clip(q - 13, 0, 2), 768))

    def write(p):
        n = lax.rem(p, 2)

        @pl.when(p >= 2)
        def _():
            out_copy(p, n, False)
        i = lax.rem(p, SLOTS)
        a = c_.h2[i, z]
        b = c_.yf[i]

        @pl.when(y == 0)
        def _():
            s.stage[n, :, :384] = a
            s.stage[n, :, 384:] = b

        @pl.when(y == 1)
        def _():
            s.stage[n, :, :384] = b
            s.stage[n, :, 384:] = a
        out_copy(p, n, True)


    vp = NP
    vc = rcopy(vp, 0, s.vall.at[1 - c], s.r0v.at[0], d_c)
    vsteps = steps(small, vp, 0, s.vall.at[c])
    VSTART = 28

    def pack_vectors():
        for l in range(LAYERS):
            v = jnp.concatenate([t_.gv[l], jnp.zeros((120, D), F32)], axis=0).T.astype(BF)
            for k in range(16):
                s.vall[k % 2, k // 4, (k // 2) % 2, l] = v[48 * k : 48 * k + 48]
        vc.start()


    top = LAYERS - 1
    first = pltpu.make_async_copy(cot, t_.cot, m_.vload)
    first.start()
    load_ff_a(top, 0, True)
    load_ff_b(top, 0, True)
    first.wait()
    t_.acc[...] = t_.cot[...].astype(F32)
    norm_two(top)
    load(0, True)
    pl.semaphore_wait(bar, 5)

    def task_of(r):
        t = jnp.where(jnp.logical_and(lax.rem(r, 2) == 1, r >= 7), (r + 1) // 2, -1)
        for n, at in enumerate((1, 2, 4, 5)):
            t = jnp.where(r == at, n, t)
        return jnp.where(t <= 13, t, -1)

    def body(r, carry):
        def at(k, off, f, kind=None):
            p = r - off[k]
            q = jnp.clip(p, 0, NP - 1)
            here = jnp.logical_and(p >= 0, p < NP)
            if kind is not None:
                here = jnp.logical_and(here, reduce_z(q) == kind)

            @pl.when(here)
            def _():
                f(q)

        def st(k, kind):
            def f(p):
                own = s.own.at[lax.rem(p, LAG + 1)]
                i = lax.rem(p, SLOTS)
                (steps_z(p, i, own) if kind else steps(c_, p, i, own))[k - 1]()
                if k == 7:
                    write(p)
            return f

        now, before = task_of(r), task_of(r - 1)

        @pl.when(before >= 0)
        def _():
            task(jnp.clip(before, 0, 13), lambda l, j: store_ff(l, j, False), lambda l, i: store_att(l, i, False))
        for k in range(1, 8):
            pl.when(r == VSTART + STEPS[k])(vsteps[k - 1])
        at(0, STEPS, s0)
        for k in range(7, 0, -1):
            at(k, STEPS_Z, st(k, True), True)
            at(k, STEPS, st(k, False), False)
        pl.when(r == VSTART)(pack_vectors)

        @pl.when(before >= 0)
        def _():
            task(jnp.clip(before, 0, 13), ff_b, att_b)

        @pl.when(now >= 0)
        def _():
            task(jnp.clip(now, 0, 13), ff_a, att_a)
        return carry
    lax.fori_loop(0, NP + max(STEPS[7], STEPS_Z[7]), body, 0)

    for p in (NP - 2, NP - 1):
        c_copy(p, p % 2).wait_send()
        out_copy(p, p % 2, False)
    vc.wait_send()
    pltpu.make_async_copy(t_.cot, o.dx, m_.osem.at[7]).wait()
    va, vb = s.h2v[0, z].astype(F32), s.yfv[0].astype(F32)
    o.vec[0] = jnp.where(y == 0, va, vb)
    o.vec[1] = jnp.where(y == 0, vb, va)


def backward_all(cot, vec, kept, w):
    rows = cot.shape[0]
    hbm = pl.BlockSpec(memory_space=pltpu.HBM)
    vmem = pl.BlockSpec(memory_space=pltpu.VMEM)
    kept = [tuple(k[:8]) + (k[8].reshape(8, 2, 4, 48, rows),) + tuple(a.reshape(8, 2, 48, rows) for a in k[9:]) for k in kept]
    act = lambda c, t: jax.ShapeDtypeStruct((rows, c), t)
    out = [
        jax.ShapeDtypeStruct((LAYERS, 48, 3 * D), BF), jax.ShapeDtypeStruct((LAYERS, 48, D), BF),
        jax.ShapeDtypeStruct((LAYERS, 48, 2 * FF), BF), jax.ShapeDtypeStruct((LAYERS, 192, D), BF),
        jax.ShapeDtypeStruct((2, 48, 128), F32), act(D, BF),
    ]
    both = lambda c: jax.ShapeDtypeStruct((LAYERS, rows, c), BF)
    scratch_out = [both(FF), both(FF), both(D), both(D), both(D)]
    seqs, _, pad, _ = kept[0][7].shape
    v = pltpu.VMEM
    dma = pltpu.SemaphoreType.DMA
    mat = v((4, 2, 2, 48, D), BF)
    n = SLOTS
    scratch = [
        v((2, 2, 8, 48, rows), BF), v((2, rows, 768), BF), v((2, 4, 2, 2, 48, 384), BF), v((LAG + 1, 4, 2, 2, 48, 384), BF), v((2, 48, 768), BF),
        v((1, 4, 2, 2, 48, 128), BF), v((1, 4, 2, 48, 128), BF), v((1, 4, 48, 128), BF),
        v((1, 3, 48, 128), BF), v((1, 2, 48, 128), BF), v((1, 48, 128), BF), v((2, 4, 2, 2, 48, 128), BF),
        v((n, 4, 2, 2, 48, 384), BF), v((n, 4, 2, 48, 384), BF), v((n, 4, 48, 384), BF), v((n, 3, 48, 384), BF), v((n, 2, 48, 384), BF), v((n, 48, 384), BF), v((n // 4, 3, 2, 2, 48, 384), BF), v((n // 4, 2, 2, 2, 48, 384), BF),
        v((rows, D), F32), v((rows, D), F32), v((2, 2, 4, 48, D), BF), mat, mat, v((rows, 768), BF), v((rows, 768), BF), mat,
        v((rows, D), BF), v((rows, 768), BF), v((rows, 768), BF), v((rows, D), BF), v((3, rows, 256), BF),
        v((rows, 256), BF), v((rows, 256), BF), v((rows, 256), BF), v((seqs, 4, pad, pad), BF), mat, mat, mat,
        v((rows, 256), BF), v((rows, 256), BF), v((rows, 256), BF), v((LAYERS, 8, D), F32), v((rows, D), BF),
        dma((2, 2)), dma((2,)), dma((NPIECE, 7)), dma((NPIECE, 7)), dma((2,)), dma, dma((7,)), dma((7,)), dma((8,)),
    ]
    res = pl.pallas_call(
        backward_kernel, out_shape=out + scratch_out,
        in_specs=[hbm, vmem] + [hbm] * 25,
        out_specs=[hbm] * 4 + [vmem] + [hbm] * 6,
        scratch_shapes=scratch,
        compiler_params=pltpu.CompilerParams(collective_id=1, has_side_effects=True, vmem_limit_bytes=62 * 2**20), name="backward_reduce",
    )(cot, vec, *kept[0], *kept[1], w)
    return res[:4], res[4], res[5]


def finish_kernel(qkv, out, gated, down, vec, last, dx, *outs):
    for src, dst in zip((qkv, out, gated, down, last, dx), outs[:6]):
        dst[...] = src[...].astype(dst.dtype)

    @pl.when(pl.program_id(0) == 0)
    def _():
        for l in range(LAYERS):
            rows = vec[l].T
            for n in range(8):
                outs[6 + n][l : l + 1, :] = rows[n : n + 1, :]


def finish_all(mats, vec, last, dx):
    rows = last.shape[0]
    half = pl.BlockSpec((rows // 2, D), lambda i: (i, 0))
    blocks = [pl.BlockSpec((1,) + m.shape[1:], lambda i: (i, 0, 0)) for m in mats]
    vecs = pl.BlockSpec((LAYERS, 48), lambda i: (0, 0))
    S = jax.ShapeDtypeStruct
    return pl.pallas_call(
        finish_kernel,
        grid=(LAYERS,),
        in_specs=blocks + [pl.BlockSpec(vec.shape, lambda i: (0, 0, 0)), half, half],
        out_specs=blocks + [half, half] + [vecs] * 8,
        out_shape=[S(m.shape, F32) for m in mats] + [S(last.shape, BF), S(dx.shape, BF)] + [S((LAYERS, 48), F32)] * 8,
        name="finish",
    )(*mats, vec, last, dx)


def forward_plain(seq_lengths, slopes, x, shards, vectors):
    mats = [lax.all_gather(w, "fsdp", axis=1, tiled=True) for w in shards]
    vec = lax.all_gather(jnp.stack(vectors, axis=1), "fsdp", axis=2, tiled=True).astype(F32)
    wq, wo, wg, wd = mats
    kept = []
    for l in range(LAYERS):
        q, k, v, att, pt, xt, at = attention_forward(l, seq_lengths, slopes, x, wq, vec)
        out_dtype = BF if l == LAYERS - 1 else F32
        r1, r2, ga, gb, ft, ht, x = ff_forward(l, att, x, wo, wg, wd, vec, out_dtype)
        kept.append((r1, r2, ga, gb, q, k, v, pt, ft, ht, at, xt))
    return mats, vec, x, kept


def backward_plain(dy, vec, kept, mats):
    wq, wo, wg, wd = mats

    def one(g, dim):
        part = lax.psum_scatter(g.astype(BF), "fsdp", scatter_dimension=dim, tiled=True)
        return lax.psum(part, "dp").astype(F32)
    sums, vecs = [None] * LAYERS, [None] * LAYERS
    for l in reversed(range(LAYERS)):
        r1, r2, ga, gb, q, k, v, pt, ft, ht, at, xt = kept[l]
        dm, dg, du, dr1, da, datt, gv = ff_backward(l, dy, r1, r2, ga, gb, wo, wg, wd, vec)
        dq, dk, dv, dy, gbias = attention_backward(l, datt, q, k, v, pt, wq, dr1, BF if l == 0 else F32)
        pairs = ((xt, jnp.concatenate([dq, dk, dv], axis=1)), (at, da), (ht, jnp.concatenate([dg, du], axis=1)), (ft, dm))
        sums[l] = [one(mm(a, b), 0) for a, b in pairs]
        vecs[l] = gv + gbias
    return [jnp.stack(m) for m in zip(*sums)], one(jnp.stack(vecs), 2), dy


def per_device(fast, inputs, lengths, cotangent, w_qkv, q_bias, v_bias, w_out, b_out, gain_one, shift_one, w_gated, w_down, b_down, gain_two, shift_two):
    shards = (w_qkv, w_out, w_gated, w_down)
    vectors = (q_bias, v_bias, b_out, gain_one, shift_one, b_down, gain_two, shift_two)
    seq_lengths = lengths.reshape(-1)
    slopes = jnp.array(slopes_list(HEADS), F32)
    x = inputs.reshape(-1, D)
    dy = cotangent.reshape(-1, D)
    if fast:
        w, vec, x, kept = forward_all(seq_lengths, slopes, x, shards, vectors)
        m, packed, dx = backward_all(dy, vec, kept, w)
        *m, x, dx, v0, v1, v2, v3, v4, v5, v6, v7 = finish_all(m, packed, x, dx)
    else:
        mats, vec, x, kept = forward_plain(seq_lengths, slopes, x, shards, vectors)
        m, vs, dx = backward_plain(dy, vec, kept, mats)
        v0, v1, v2, v3, v4, v5, v6, v7 = (vs[:, n] for n in range(8))
    return (
        x.reshape(inputs.shape), dx.reshape(inputs.shape), m[0], v0, v1, m[1], v2, v3, v4, m[2], m[3], v5, v6, v7,
    )


def solution(mesh):
    placed = (
        P(None, ("dp", "fsdp"), None, None),
        P(None, ("dp", "fsdp")),
        P(None, ("dp", "fsdp"), None, None),
        P(None, "fsdp", None),
        P(None, "fsdp"),
        P(None, "fsdp"),
        P(None, "fsdp", None),
        P(None, "fsdp"),
        P(None, "fsdp"),
        P(None, "fsdp"),
        P(None, "fsdp", None),
        P(None, "fsdp", None),
        P(None, "fsdp"),
        P(None, "fsdp"),
        P(None, "fsdp"),
    )
    return jax.shard_map(
        functools.partial(per_device, dict(mesh.shape) == {"dp": 2, "fsdp": 16}),
        mesh=mesh,
        in_specs=placed,
        out_specs=(
            P(None, ("dp", "fsdp"), None, None),
            P(None, ("dp", "fsdp"), None, None),
            P(None, "fsdp", None),
            P(None, "fsdp"),
            P(None, "fsdp"),
            P(None, "fsdp", None),
            P(None, "fsdp"),
            P(None, "fsdp"),
            P(None, "fsdp"),
            P(None, "fsdp", None),
            P(None, "fsdp", None),
            P(None, "fsdp"),
            P(None, "fsdp"),
            P(None, "fsdp"),
        ),
        check_vma=False,
    )
```
